32 devices in a mesh: row: 8 (over z, y), grp: 4 (over x, core).
Axes of the slice: x: 2, y: 2, z: 4, core: 2. Of those that a mesh axis runs over, the one named last changes fastest.
Arguments:
- image_rows: bfloat16 [8, 1024, 1024], P('grp', 'row'), may hold values from -6 to 6
- text_rows: bfloat16 [8, 128, 1024], P('grp'), may hold values from -6 to 6
- prompt_len: int32 [8], replicated, may hold values from 8 to 128, as said below
- prompt_slot: int32 [8], replicated, may hold values from 0 to 7, each once
- gain_self: float32 [1024], replicated, may hold values from 0.5 to 1.5
- w_query: bfloat16 [1024, 1024], replicated, may hold values from -0.1875 to 0.1875
- w_key: bfloat16 [1024, 1024], replicated, may hold values from -0.1875 to 0.1875
- w_value: bfloat16 [1024, 1024], replicated, may hold values from -0.1875 to 0.1875
- w_out: bfloat16 [1024, 1024], replicated, may hold values from -1 to 1
- gain_cross: float32 [1024], replicated, may hold values from 0.5 to 1.5
- w_query_text: bfloat16 [1024, 1024], replicated, may hold values from -0.1875 to 0.1875
- w_key_text: bfloat16 [1024, 1024], replicated, may hold values from -0.1875 to 0.1875
- w_value_text: bfloat16 [1024, 1024], replicated, may hold values from -0.1875 to 0.1875
- w_out_text: bfloat16 [1024, 1024], replicated, may hold values from -0.75 to 0.75
- gain_mlp: float32 [1024], replicated, may hold values from 0.5 to 1.5
- w_in: bfloat16 [1024, 4096], replicated, may hold values from -0.1875 to 0.1875
- w_mlp_out: bfloat16 [4096, 1024], replicated, may hold values from -0.125 to 0.125
- grad_out: bfloat16 [8, 1024, 1024], P('grp', 'row'), may hold values from -6 to 6
Outputs:
- out_block: bfloat16 [8, 1024, 1024], P('grp', 'row')
- grad_image: bfloat16 [8, 1024, 1024], P('grp', 'row')
- grad_text: bfloat16 [8, 128, 1024], P('grp')
- grad_gain_self: float32 [1024], P('row')
- grad_w_query: float32 [1024, 1024], P('row')
- grad_w_key: float32 [1024, 1024], P('row')
- grad_w_value: float32 [1024, 1024], P('row')
- grad_w_out: float32 [1024, 1024], P('row')
- grad_gain_cross: float32 [1024], P('row')
- grad_w_query_text: float32 [1024, 1024], P('row')
- grad_w_key_text: float32 [1024, 1024], P('row')
- grad_w_value_text: float32 [1024, 1024], P('row')
- grad_w_out_text: float32 [1024, 1024], P('row')
- grad_gain_mlp: float32 [1024], P('row')
- grad_w_in: float32 [1024, 4096], P('row')
- grad_w_mlp_out: float32 [4096, 1024], P('row')
The draws below stay inside these ranges and needn't reach their ends.
Inputs may be any that keep to these rules, and one draw needn't show every extreme that they name: prompt_len[s] counts the real text rows of prompt slot s; rows at and beyond it are padding. Some slot is full in every draw. prompt_slot[i] is the slot of text_rows that holds image i's prompt; each slot serves exactly one image.
All inputs are finite; a program needn't handle non-finite values.
Results may differ from the reference program's by a relative error of at most 0.025.
Values may be sent and summed in bfloat16 or wider, within the bound.
No kernel may reach another device: no remote copies, remote signals or barrier semaphores. Data moves between devices by JAX's collectives and lax.ppermute only.
A program may use at most 320 MiB of HBM per device.

```python
import jax
import jax.numpy as jnp
from jax import lax

D = 1024
HEADS = 16
HEAD_DIM = 64
FF = 4096
PROMPT = 128
LENGTH = 1024
IMAGES = 8


def draw_prompt_len(key, part):
    draw_key, place_key = jax.random.split(key)
    lengths = jax.random.randint(draw_key, (IMAGES,), 8, PROMPT + 1)
    chosen = jax.random.randint(place_key, (), 0, IMAGES)
    return jnp.where(jnp.arange(IMAGES) == chosen, PROMPT, lengths).astype(jnp.int32)


def shard_levels(rng, dims, pieces, low, largest):
    level, own = 1.0, jax.random.fold_in(rng, 6)
    for position, shards_of in pieces:
        draws = jnp.exp(jax.random.uniform(jax.random.fold_in(own, position), (shards_of,), jnp.float32, low / len(pieces), largest / len(pieces)))
        level = level * jnp.repeat(draws, dims[position] // shards_of).reshape([-1 if axis == position else 1 for axis in range(len(dims))])
    return level


def noise(rng, dims, width, bound, pieces=(), kind=jnp.bfloat16):
    level = shard_levels(rng, dims, pieces, -0.22, 0.18) if pieces else 1.0
    array = jax.random.normal(rng, dims, jnp.float32) * width * level
    return jnp.minimum(jnp.maximum(array, -bound), bound).astype(kind)


def setup_inputs(seed: int = 0) -> dict:
    arg_keys = jax.random.split(jax.random.key(seed), 19)
    return {
        "image_rows": noise(arg_keys[0], (IMAGES, LENGTH, D), 1.0, 6.0, ((0, 4), (1, 8))),
        "text_rows": noise(arg_keys[1], (IMAGES, PROMPT, D), 1.0, 6.0, ((0, 4),)),
        "prompt_len": draw_prompt_len(jax.random.fold_in(arg_keys[18], 71), 0),
        "prompt_slot": jax.random.permutation(arg_keys[3], IMAGES).astype(jnp.int32),
        "gain_self": jnp.clip(1.0 + 0.1 * jax.random.normal(arg_keys[4], (D,), jnp.float32), 0.5, 1.5),
        "w_query": noise(arg_keys[5], (D, D), D ** -0.5, 0.1875),
        "w_key": noise(arg_keys[6], (D, D), D ** -0.5, 0.1875),
        "w_value": noise(arg_keys[7], (D, D), D ** -0.5, 0.1875),
        "w_out": noise(arg_keys[8], (D, D), (D // 32) ** -0.5, 1.0),
        "gain_cross": jnp.clip(1.0 + 0.1 * jax.random.normal(arg_keys[9], (D,), jnp.float32), 0.5, 1.5),
        "w_query_text": noise(arg_keys[10], (D, D), D ** -0.5, 0.1875),
        "w_key_text": noise(arg_keys[11], (D, D), D ** -0.5, 0.1875),
        "w_value_text": noise(arg_keys[12], (D, D), D ** -0.5, 0.1875),
        "w_out_text": noise(arg_keys[13], (D, D), (D // 16) ** -0.5, 0.75),
        "gain_mlp": jnp.clip(1.0 + 0.1 * jax.random.normal(arg_keys[14], (D,), jnp.float32), 0.5, 1.5),
        "w_in": noise(arg_keys[15], (D, FF), D ** -0.5, 0.1875),
        "w_mlp_out": noise(arg_keys[16], (FF, D), (FF // 2) ** -0.5, 0.125),
        "grad_out": noise(arg_keys[17], (IMAGES, LENGTH, D), 1.0, 6.0, ((0, 4), (1, 8))),
    }


@jax.custom_vjp
def low(v):
    return lax.optimization_barrier(v.astype(jnp.bfloat16)).astype(jnp.float32)

@jax.custom_vjp
def low_back(v):
    return v

def low_keep(v):
    return (low(v), None)

def low_pass(kept, grad):
    return (grad,)

def back_keep(v):
    return (v, None)

def back_low(kept, grad):
    return (low(grad),)
low.defvjp(low_keep, low_pass)
low_back.defvjp(back_keep, back_low)
EPSILON = 1e-05
NEG_LARGE = -1e+30
HIGHEST = lax.Precision.HIGHEST

def norm_rows(values, gain):
    center = lax.optimization_barrier(jnp.mean(values, -1, keepdims=True))
    centered = values - center
    variance = lax.optimization_barrier(jnp.mean(centered * centered, -1, keepdims=True))
    return centered * lax.rsqrt(variance + EPSILON) * gain

def product(left, right):
    return jnp.dot(left, right, precision=HIGHEST)

def round_both(values):
    return low_back(low(values))

def split_heads(values):
    return values.reshape(values.shape[:-1] + (HEADS, HEAD_DIM))

def image_layer(inputs, text_keys, text_values, prompt_count, params):
    gain_self, w_query, w_key, w_value, w_out, gain_cross, w_query_text, w_out_text, gain_mlp, w_in, w_mlp_out = params
    scale_factor = HEAD_DIM ** (-0.5)
    normed = low(norm_rows(inputs, gain_self))
    queries = split_heads(round_both(product(normed, w_query)))
    keys = split_heads(round_both(product(normed, w_key)))
    values = split_heads(round_both(product(normed, w_value)))
    block_size = min(512, LENGTH)
    positions = jnp.arange(LENGTH, dtype=jnp.int32)

    def attend(block):
        start = block * block_size
        query_block = lax.dynamic_slice_in_dim(queries, start, block_size, 0)
        scores = low_back(jnp.einsum('qhd,khd->hqk', query_block, keys, precision=HIGHEST) * scale_factor)
        query_pos = start + jnp.arange(block_size, dtype=jnp.int32)
        allowed = positions[None, :] <= query_pos[:, None]
        probs = low(jax.nn.softmax(jnp.where(allowed[None], scores, NEG_LARGE), axis=-1))
        return jnp.einsum('hqk,khd->qhd', probs, values, precision=HIGHEST)
    context = lax.map(jax.checkpoint(attend), jnp.arange(LENGTH // block_size, dtype=jnp.int32))
    context = round_both(context.reshape(LENGTH, D))
    hidden = inputs + low_back(product(context, w_out))
    cross_normed = low(norm_rows(hidden, gain_cross))
    cross = split_heads(round_both(product(cross_normed, w_query_text)))
    cross_scores = low_back(jnp.einsum('qhd,khd->hqk', cross, text_keys, precision=HIGHEST) * scale_factor)
    text_mask = jnp.arange(PROMPT, dtype=jnp.int32) < prompt_count
    cross_probs = low(jax.nn.softmax(jnp.where(text_mask[None, None, :], cross_scores, NEG_LARGE), axis=-1))
    cross_context = jnp.einsum('hqk,khd->qhd', cross_probs, text_values, precision=HIGHEST)
    cross_context = round_both(cross_context.reshape(LENGTH, D))
    mixed = hidden + low_back(product(cross_context, w_out_text))
    mlp_normed = low(norm_rows(mixed, gain_mlp))
    pre_act = low_back(product(mlp_normed, w_in))
    activated = low(jax.nn.gelu(pre_act, approximate=True))
    return mixed + low_back(product(activated, w_mlp_out))

def layer_forward(inputs, text, gain_self, w_query, w_key, w_value, w_out, gain_cross, w_query_text, w_key_text, w_value_text, w_out_text, gain_mlp, w_in, w_mlp_out, prompt_len, prompt_slot):
    text_flat = text.reshape(IMAGES * PROMPT, D)
    text_keys = split_heads(round_both(product(text_flat, w_key_text)).reshape(IMAGES, PROMPT, D))
    text_values = split_heads(round_both(product(text_flat, w_value_text)).reshape(IMAGES, PROMPT, D))
    chosen_keys = jnp.take(text_keys, prompt_slot, axis=0)
    chosen_values = jnp.take(text_values, prompt_slot, axis=0)
    chosen_counts = jnp.take(prompt_len, prompt_slot)
    params = (gain_self, w_query, w_key, w_value, w_out, gain_cross, w_query_text, w_out_text, gain_mlp, w_in, w_mlp_out)

    def one_image(packed):
        return image_layer(packed[0], packed[1], packed[2], packed[3], params)
    return lax.map(jax.checkpoint(one_image), (inputs, chosen_keys, chosen_values, chosen_counts))

def reference(image_rows, text_rows, prompt_len, prompt_slot, gain_self, w_query, w_key, w_value, w_out, gain_cross, w_query_text, w_key_text, w_value_text, w_out_text, gain_mlp, w_in, w_mlp_out, grad_out):
    floats = [array_in.astype(jnp.float32) for array_in in (image_rows, text_rows, gain_self, w_query, w_key, w_value, w_out, gain_cross, w_query_text, w_key_text, w_value_text, w_out_text, gain_mlp, w_in, w_mlp_out)]

    def forward(*arrays):
        return layer_forward(*arrays, prompt_len, prompt_slot)
    block_out, pull_back = jax.vjp(forward, *floats)
    grads = pull_back(grad_out.astype(jnp.float32))
    return (block_out.astype(jnp.bfloat16), grads[0].astype(jnp.bfloat16), grads[1].astype(jnp.bfloat16), grads[2], grads[3], grads[4], grads[5], grads[6], grads[7], grads[8], grads[9], grads[10], grads[11], grads[12], grads[13], grads[14])
```

```python
import jax
import jax.numpy as jnp
from jax import lax
from jax.sharding import PartitionSpec as P
from jax.experimental import pallas as pl
from jax.experimental.pallas import tpu as pltpu

HEADS = 16
HEAD_DIM = 64


EPSILON = 1e-05
NEG_LARGE = -1e30
HIGHEST = lax.Precision.HIGHEST


def norm_rows(values, gain):
    center = jnp.mean(values, -1, keepdims=True)
    centered = values - center
    variance = jnp.mean(centered * centered, -1, keepdims=True)
    inverse = lax.rsqrt(variance + EPSILON)
    unit_rows = centered * inverse
    return (unit_rows * gain, unit_rows, inverse)


def norm_back(grad_normed, unit_rows, inverse, gain):
    grad_unit = grad_normed * gain
    first_mean = jnp.mean(grad_unit, -1, keepdims=True)
    second_mean = jnp.mean(grad_unit * unit_rows, -1, keepdims=True)
    grad_input = inverse * (grad_unit - first_mean - unit_rows * second_mean)
    return (grad_input, jnp.sum(grad_normed * unit_rows, 0))


def matmul(left, right):
    return jnp.dot(left, right, preferred_element_type=jnp.float32)


def matmul_left_t(left, right):
    return lax.dot_general(
        left, right, (((0,), (0,)), ((), ())), preferred_element_type=jnp.float32
    )


def matmul_right_t(left, right):
    return lax.dot_general(
        left, right, (((1,), (1,)), ((), ())), preferred_element_type=jnp.float32
    )


def split_heads(values):
    return values.reshape(values.shape[:-1] + (HEADS, HEAD_DIM))


def on_device_plain(
    image_rows,
    text_rows,
    prompt_len,
    prompt_slot,
    gain_self,
    w_query,
    w_key,
    w_value,
    w_out,
    gain_cross,
    w_query_text,
    w_key_text,
    w_value_text,
    w_out_text,
    gain_mlp,
    w_in,
    w_mlp_out,
    grad_out,
):
    images_here, rows_here, width = image_rows.shape
    prompt_rows = text_rows.shape[1]
    row_count = lax.axis_size("row")
    length = rows_here * row_count
    row_index = lax.axis_index("row")
    group_index = lax.axis_index("grp")
    scale_factor = HEAD_DIM ** (-0.5)
    block_size = min(512, length)
    block_count = length // block_size
    flat_rows = images_here * rows_here
    inputs = image_rows.astype(jnp.float32).reshape(flat_rows, width)
    normed_self, unit_self, inverse_self = norm_rows(inputs, gain_self)
    normed_low = normed_self.astype(jnp.bfloat16)
    query_low = (
        matmul(normed_low, w_query).astype(jnp.bfloat16).reshape(images_here, rows_here, width)
    )
    key_low = matmul(normed_low, w_key).astype(jnp.bfloat16).reshape(images_here, rows_here, width)
    value_low = (
        matmul(normed_low, w_value).astype(jnp.bfloat16).reshape(images_here, rows_here, width)
    )
    keys_all, values_all = (
        lax.all_gather(key_low, "row", axis=1, tiled=True),
        lax.all_gather(value_low, "row", axis=1, tiled=True),
    )
    query_heads = split_heads(query_low)
    query_pos = row_index * rows_here + jnp.arange(rows_here, dtype=jnp.int32)
    key_pos = jnp.arange(length, dtype=jnp.int32)
    causal = key_pos[None, :] <= query_pos[:, None]
    contexts = []
    totals = []
    for each_image in range(images_here):
        scores = (
            jnp.einsum(
                "qhd,khd->hqk",
                query_heads[each_image],
                split_heads(keys_all[each_image]),
                preferred_element_type=jnp.float32,
            )
            * scale_factor
        )
        scores = jnp.where(causal[None], scores, NEG_LARGE)
        largest = jnp.max(scores, -1, keepdims=True)
        expos = jnp.exp(scores - largest)
        denominator = jnp.sum(expos, -1, keepdims=True)
        probs_low = (expos / denominator).astype(jnp.bfloat16)
        contexts.append(
            jnp.einsum(
                "hqk,khd->qhd",
                probs_low,
                split_heads(values_all[each_image]),
                preferred_element_type=jnp.float32,
            )
        )
        totals.append((largest + jnp.log(denominator))[..., 0])
    context = jnp.stack(contexts).reshape(flat_rows, width)
    log_totals = jnp.stack(totals)
    context_low = context.astype(jnp.bfloat16)
    hidden = inputs + matmul(context_low, w_out)
    normed_cross, unit_cross, inverse_cross = norm_rows(hidden, gain_cross)
    cross_normed_low = normed_cross.astype(jnp.bfloat16)
    cross_low = (
        matmul(cross_normed_low, w_query_text)
        .astype(jnp.bfloat16)
        .reshape(images_here, rows_here, HEADS, HEAD_DIM)
    )
    text_flat = text_rows.reshape(-1, width)
    text_key = matmul(text_flat, w_key_text).astype(jnp.bfloat16).reshape(text_rows.shape)
    text_value = matmul(text_flat, w_value_text).astype(jnp.bfloat16).reshape(text_rows.shape)
    text_keys, text_values = (
        lax.all_gather(text_key, "grp", axis=0, tiled=True),
        lax.all_gather(text_value, "grp", axis=0, tiled=True),
    )
    image_total = prompt_slot.shape[0]
    slots = lax.dynamic_slice_in_dim(prompt_slot, group_index * images_here, images_here)
    keys_sel = split_heads(jnp.take(text_keys, slots, axis=0))
    values_sel = split_heads(jnp.take(text_values, slots, axis=0))
    lengths_sel = jnp.take(prompt_len, slots)
    text_mask = (jnp.arange(prompt_rows, dtype=jnp.int32)[None, :] < lengths_sel[:, None])[
        :, None, None, :
    ]
    cross_scores = (
        jnp.einsum("iqhd,ikhd->ihqk", cross_low, keys_sel, preferred_element_type=jnp.float32)
        * scale_factor
    )
    cross_probs = jax.nn.softmax(jnp.where(text_mask, cross_scores, NEG_LARGE), axis=-1)
    cross_probs_low = cross_probs.astype(jnp.bfloat16)
    cross_context = jnp.einsum(
        "ihqk,ikhd->iqhd", cross_probs_low, values_sel, preferred_element_type=jnp.float32
    )
    cross_context_low = cross_context.reshape(flat_rows, width).astype(jnp.bfloat16)
    mixed = hidden + matmul(cross_context_low, w_out_text)
    normed_mlp, unit_mlp, inverse_mlp = norm_rows(mixed, gain_mlp)
    mlp_low = normed_mlp.astype(jnp.bfloat16)
    pre_act = matmul(mlp_low, w_in)
    activated, gelu_back = jax.vjp(jax.nn.gelu, pre_act)
    activated_low = activated.astype(jnp.bfloat16)
    block_out = mixed + matmul(activated_low, w_mlp_out)
    out_block = block_out.astype(jnp.bfloat16).reshape(image_rows.shape)
    grad_low = grad_out.reshape(flat_rows, width)
    grad_w_mlp_out = matmul_left_t(activated_low, grad_low)
    grad_activated = matmul_right_t(grad_low, w_mlp_out)
    grad_pre_low = gelu_back(grad_activated)[0].astype(jnp.bfloat16)
    grad_w_in = matmul_left_t(mlp_low, grad_pre_low)
    grad_mlp_normed = matmul_right_t(grad_pre_low, w_in)
    grad_from_mlp, grad_gain_mlp = norm_back(grad_mlp_normed, unit_mlp, inverse_mlp, gain_mlp)
    grad_mixed = grad_low.astype(jnp.float32) + grad_from_mlp
    grad_mixed_low = grad_mixed.astype(jnp.bfloat16)
    grad_w_out_text = matmul_left_t(cross_context_low, grad_mixed_low)
    grad_cross_ctx = split_heads(
        matmul_right_t(grad_mixed_low, w_out_text)
        .astype(jnp.bfloat16)
        .reshape(images_here, rows_here, width)
    )
    grad_cross_probs = jnp.einsum(
        "iqhd,ikhd->ihqk", grad_cross_ctx, values_sel, preferred_element_type=jnp.float32
    )
    grad_values_sel = jnp.einsum(
        "ihqk,iqhd->ikhd", cross_probs_low, grad_cross_ctx, preferred_element_type=jnp.float32
    )
    grad_cross_scores = cross_probs * (
        grad_cross_probs - jnp.sum(cross_probs * grad_cross_probs, -1, keepdims=True)
    )
    grad_scores_low = grad_cross_scores.astype(jnp.bfloat16)
    grad_cross_query = (
        jnp.einsum("ihqk,ikhd->iqhd", grad_scores_low, keys_sel, preferred_element_type=jnp.float32)
        * scale_factor
    )
    grad_cross_query_low = grad_cross_query.astype(jnp.bfloat16).reshape(flat_rows, width)
    grad_keys_sel = (
        jnp.einsum(
            "ihqk,iqhd->ikhd", grad_scores_low, cross_low, preferred_element_type=jnp.float32
        )
        * scale_factor
    )
    grad_w_query_text = matmul_left_t(cross_normed_low, grad_cross_query_low)
    grad_cross_normed = matmul_right_t(grad_cross_query_low, w_query_text)
    grad_from_cross, grad_gain_cross = norm_back(
        grad_cross_normed, unit_cross, inverse_cross, gain_cross
    )
    grad_hidden = grad_mixed + grad_from_cross
    placing = (jnp.arange(image_total, dtype=jnp.int32)[:, None] == slots[None, :]).astype(
        jnp.float32
    )
    joined_text = jnp.concatenate(
        [
            grad_keys_sel.reshape(images_here, prompt_rows, width),
            grad_values_sel.reshape(images_here, prompt_rows, width),
        ],
        -1,
    )
    text_term = jnp.einsum("si,ipd->spd", placing, joined_text, precision=HIGHEST)
    text_grad = lax.psum_scatter(
        text_term.astype(jnp.bfloat16), "grp", scatter_dimension=0, tiled=True
    )
    share_rows = text_flat.shape[0] // row_count
    text_total = (
        lax.psum(text_grad, "row").astype(jnp.float32).reshape(-1, 2 * width).astype(jnp.bfloat16)
    )
    text_share = lax.dynamic_slice_in_dim(text_total, row_index * share_rows, share_rows, 0)
    text_grad_rows = (
        matmul_right_t(text_total[:, :width], w_key_text)
        + matmul_right_t(text_total[:, width:], w_value_text)
    ).astype(jnp.bfloat16)
    text_part = lax.dynamic_slice_in_dim(text_flat, row_index * share_rows, share_rows, 0)
    grad_w_key_text = matmul_left_t(text_part, text_share[:, :width])
    grad_w_value_text = matmul_left_t(text_part, text_share[:, width:])
    grad_text = text_grad_rows.reshape(text_rows.shape)
    grad_hidden_low = grad_hidden.astype(jnp.bfloat16)
    grad_w_out = matmul_left_t(context_low, grad_hidden_low)
    grad_context = (
        matmul_right_t(grad_hidden_low, w_out)
        .astype(jnp.bfloat16)
        .reshape(images_here, rows_here, width)
    )
    grad_context_heads = split_heads(grad_context)
    context_heads = split_heads(context.reshape(images_here, rows_here, width))
    delta = jnp.einsum(
        "iqhd,iqhd->ihq", grad_context_heads.astype(jnp.float32), context_heads, precision=HIGHEST
    )
    zero_query = jnp.zeros((images_here, rows_here, HEADS, HEAD_DIM), jnp.float32)

    def block_terms(block):
        start = block * block_size
        key_heads = split_heads(lax.dynamic_slice_in_dim(keys_all, start, block_size, 1))
        value_heads = split_heads(lax.dynamic_slice_in_dim(values_all, start, block_size, 1))
        block_pos = start + jnp.arange(block_size, dtype=jnp.int32)
        allowed = (block_pos[None, :] <= query_pos[:, None])[None, None]
        scores = (
            jnp.einsum(
                "iqhd,ikhd->ihqk", query_heads, key_heads, preferred_element_type=jnp.float32
            )
            * scale_factor
        )
        probs = jnp.where(allowed, jnp.exp(scores - log_totals[..., None]), 0.0)
        grad_probs = jnp.einsum(
            "iqhd,ikhd->ihqk", grad_context_heads, value_heads, preferred_element_type=jnp.float32
        )
        grad_scores = (probs * (grad_probs - delta[..., None])).astype(jnp.bfloat16)
        return (grad_scores, probs.astype(jnp.bfloat16), key_heads)

    def step_keys(block, carry):
        grad_query, term_buffer = carry
        grad_scores, probs_low, key_heads = block_terms(block)
        grad_query = (
            grad_query
            + jnp.einsum(
                "ihqk,ikhd->iqhd", grad_scores, key_heads, preferred_element_type=jnp.float32
            )
            * scale_factor
        )
        grad_key_part = (
            jnp.einsum(
                "ihqk,iqhd->ikhd", grad_scores, query_heads, preferred_element_type=jnp.float32
            )
            * scale_factor
        )
        grad_value_part = jnp.einsum(
            "ihqk,iqhd->ikhd", probs_low, grad_context_heads, preferred_element_type=jnp.float32
        )
        joined = jnp.concatenate(
            [
                grad_key_part.reshape(images_here, block_size, width),
                grad_value_part.reshape(images_here, block_size, width),
            ],
            -1,
        )
        term_buffer = lax.dynamic_update_slice_in_dim(term_buffer, joined, block * block_size, 1)
        return (grad_query, term_buffer)

    start_buffer = jnp.zeros((images_here, length, 2 * width), jnp.float32)
    grad_query, term_buffer = lax.fori_loop(0, block_count, step_keys, (zero_query, start_buffer))
    grad_kv = lax.psum_scatter(
        term_buffer.astype(jnp.bfloat16), "row", scatter_dimension=1, tiled=True
    ).astype(jnp.float32)
    grad_query_low = grad_query.reshape(flat_rows, width).astype(jnp.bfloat16)
    grad_kv_low = grad_kv.reshape(flat_rows, 2 * width).astype(jnp.bfloat16)
    grad_w_query = matmul_left_t(normed_low, grad_query_low)
    grad_w_key = matmul_left_t(normed_low, grad_kv_low[:, :width])
    grad_w_value = matmul_left_t(normed_low, grad_kv_low[:, width:])
    grad_normed_self = (
        matmul_right_t(grad_query_low, w_query)
        + matmul_right_t(grad_kv_low[:, :width], w_key)
        + matmul_right_t(grad_kv_low[:, width:], w_value)
    )
    grad_from_self, grad_gain_self = norm_back(grad_normed_self, unit_self, inverse_self, gain_self)
    grad_image = (grad_hidden + grad_from_self).astype(jnp.bfloat16).reshape(image_rows.shape)
    shares = (
        lax.psum_scatter(
            grad_gain_self.astype(jnp.bfloat16), "row", scatter_dimension=0, tiled=True
        ).astype(jnp.float32),
        lax.psum_scatter(
            grad_w_query.astype(jnp.bfloat16), "row", scatter_dimension=0, tiled=True
        ).astype(jnp.float32),
        lax.psum_scatter(
            grad_w_key.astype(jnp.bfloat16), "row", scatter_dimension=0, tiled=True
        ).astype(jnp.float32),
        lax.psum_scatter(
            grad_w_value.astype(jnp.bfloat16), "row", scatter_dimension=0, tiled=True
        ).astype(jnp.float32),
        lax.psum_scatter(
            grad_w_out.astype(jnp.bfloat16), "row", scatter_dimension=0, tiled=True
        ).astype(jnp.float32),
        lax.psum_scatter(
            grad_gain_cross.astype(jnp.bfloat16), "row", scatter_dimension=0, tiled=True
        ).astype(jnp.float32),
        lax.psum_scatter(
            grad_w_query_text.astype(jnp.bfloat16), "row", scatter_dimension=0, tiled=True
        ).astype(jnp.float32),
        lax.psum_scatter(
            grad_w_key_text.astype(jnp.bfloat16), "row", scatter_dimension=0, tiled=True
        ).astype(jnp.float32),
        lax.psum_scatter(
            grad_w_value_text.astype(jnp.bfloat16), "row", scatter_dimension=0, tiled=True
        ).astype(jnp.float32),
        lax.psum_scatter(
            grad_w_out_text.astype(jnp.bfloat16), "row", scatter_dimension=0, tiled=True
        ).astype(jnp.float32),
        lax.psum_scatter(
            grad_gain_mlp.astype(jnp.bfloat16), "row", scatter_dimension=0, tiled=True
        ).astype(jnp.float32),
        lax.psum_scatter(
            grad_w_in.astype(jnp.bfloat16), "row", scatter_dimension=0, tiled=True
        ).astype(jnp.float32),
        lax.psum_scatter(
            grad_w_mlp_out.astype(jnp.bfloat16), "row", scatter_dimension=0, tiled=True
        ).astype(jnp.float32),
    )
    summed = (
        lax.psum(shares[0].astype(jnp.bfloat16), "grp").astype(jnp.float32),
        lax.psum(shares[1].astype(jnp.bfloat16), "grp").astype(jnp.float32),
        lax.psum(shares[2].astype(jnp.bfloat16), "grp").astype(jnp.float32),
        lax.psum(shares[3].astype(jnp.bfloat16), "grp").astype(jnp.float32),
        lax.psum(shares[4].astype(jnp.bfloat16), "grp").astype(jnp.float32),
        lax.psum(shares[5].astype(jnp.bfloat16), "grp").astype(jnp.float32),
        lax.psum(shares[6].astype(jnp.bfloat16), "grp").astype(jnp.float32),
        lax.psum(shares[7].astype(jnp.bfloat16), "grp").astype(jnp.float32),
        lax.psum(shares[8].astype(jnp.bfloat16), "grp").astype(jnp.float32),
        lax.psum(shares[9].astype(jnp.bfloat16), "grp").astype(jnp.float32),
        lax.psum(shares[10].astype(jnp.bfloat16), "grp").astype(jnp.float32),
        lax.psum(shares[11].astype(jnp.bfloat16), "grp").astype(jnp.float32),
        lax.psum(shares[12].astype(jnp.bfloat16), "grp").astype(jnp.float32),
    )
    return (
        out_block,
        grad_image,
        grad_text,
        summed[0],
        summed[1],
        summed[2],
        summed[3],
        summed[4],
        summed[5],
        summed[6],
        summed[7],
        summed[8],
        summed[9],
        summed[10],
        summed[11],
        summed[12],
    )


AXES = ("row", "grp")
BF16 = jnp.bfloat16
F32 = jnp.float32
TEAM = 4
LINES = 4


def fits(mesh):
    return mesh.shape["row"] == 2 * LINES and mesh.shape["grp"] == 4


def moves(change):
    pairs = []
    for place in range(32):
        z, y, x, c = place // 8, place // 4 % 2, place // 2 % 2, place % 2
        z2, y2, x2, c2 = change(z, y, x, c)
        pairs.append((place, z2 * 8 + y2 * 4 + x2 * 2 + c2))
    return pairs


def move(values, change):
    return lax.ppermute(values, AXES, moves(change))


def to_member(values, member):
    flip_y, flip_c = member & 1, member >> 1
    return move(values, lambda z, y, x, c: (z, y ^ flip_y, x, c ^ flip_c))


def team_gather(values):
    side = to_member(values, 1)
    return [values, side, to_member(values, 2), to_member(side, 2)]


def hand_out(step):
    def change(z, y, x, c):
        which = z ^ step
        return (2 * c + (which & 1), y, x, which >> 1)

    return change


def hand_back(step):
    def change(z, y, x, c):
        return (step ^ ((z & 1) | (c << 1)), y, x, z >> 1)

    return change


def ring_groups():
    order = [(0, 0), (0, 1), (0, 2), (0, 3), (1, 3), (1, 2), (1, 1), (1, 0)]
    return [
        [z * 8 + y * 4 + x * 2 + c for x, z in order] for y in range(2) for c in range(2)
    ]


def ring_sum(blocks):
    flat = blocks.reshape(-1, blocks.shape[-1])
    return lax.psum_scatter(
        flat, AXES, scatter_dimension=0, axis_index_groups=ring_groups(), tiled=True
    )


def ring_blocks(left, right):
    return jnp.concatenate([left, right[::-1]], 0)


def lane_mask(rows, head):
    lane = lax.broadcasted_iota(jnp.int32, (rows, 128), 1)
    return (lane >= HEAD_DIM) if head else (lane < HEAD_DIM)


def only(values, head):
    return jnp.where(lane_mask(values.shape[0], head), values, jnp.zeros_like(values))


def dot_nt(left, right):
    return lax.dot_general(
        left, right, (((1,), (1,)), ((), ())), preferred_element_type=F32
    )


def dot_nn(left, right):
    return lax.dot_general(
        left, right, (((1,), (0,)), ((), ())), preferred_element_type=F32
    )


def dot_tn(left, right):
    return lax.dot_general(
        left, right, (((0,), (0,)), ((), ())), preferred_element_type=F32
    )


CHUNK = 64


def self_forward_kernel(table, *refs):
    parts, outs, lse_ref = refs[:TEAM], refs[TEAM : 2 * TEAM], refs[2 * TEAM]
    all_qkv, all_out = refs[2 * TEAM + 1 :]
    length, heads_width = all_out.shape
    chunks = parts[0].shape[0] // CHUNK
    for member in range(TEAM):
        for piece in range(chunks):
            at = pl.multiple_of(table[member * chunks + piece] * CHUNK, CHUNK)
            all_qkv[pl.ds(at, CHUNK), :] = parts[member][piece * CHUNK : (piece + 1) * CHUNK, :]
    block = 256
    pairs = heads_width // 128
    scale_factor = HEAD_DIM ** (-0.5)
    diagonal = lax.broadcasted_iota(jnp.int32, (block, block), 1) <= lax.broadcasted_iota(
        jnp.int32, (block, block), 0
    )
    for pair in range(pairs):
        q_cols = slice(128 * pair, 128 * pair + 128)
        k_cols = slice(heads_width + 128 * pair, heads_width + 128 * pair + 128)
        v_cols = slice(2 * heads_width + 128 * pair, 2 * heads_width + 128 * pair + 128)
        for block_at in range(length // block):
            rows = slice(block * block_at, block * (block_at + 1))
            q_block = all_qkv[rows, q_cols]
            joined = jnp.zeros((block, 128), F32)
            for head in range(2):
                q_one = only(q_block, head)
                near = dot_nt(q_one, all_qkv[rows, k_cols]) * scale_factor
                near = jnp.where(diagonal, near, NEG_LARGE)
                scores = near
                if block_at:
                    far = dot_nt(q_one, all_qkv[0 : block * block_at, k_cols]) * scale_factor
                    scores = jnp.concatenate([far, near], 1)
                largest = jnp.max(scores, -1, keepdims=True)
                expos = jnp.exp(scores - largest)
                denominator = jnp.sum(expos, -1, keepdims=True)
                probs_low = (expos / denominator).astype(BF16)
                mixed = dot_nn(probs_low, all_qkv[0 : block * (block_at + 1), v_cols])
                joined = jnp.where(lane_mask(block, head), mixed, joined)
                total = largest + jnp.log(denominator)
                lse_ref[2 * pair + head : 2 * pair + head + 1, rows] = jnp.transpose(
                    jnp.broadcast_to(total, (block, 128))
                )[0:1, :]
            all_out[rows, q_cols] = joined.astype(BF16)
    for member in range(TEAM):
        for piece in range(chunks):
            at = pl.multiple_of(table[member * chunks + piece] * CHUNK, CHUNK)
            outs[member][piece * CHUNK : (piece + 1) * CHUNK, :] = all_out[pl.ds(at, CHUNK), :]


def in_vmem(count):
    return [pl.BlockSpec(memory_space=pltpu.VMEM)] * count


def self_forward(table, parts):
    rows, width = parts[0].shape
    heads_width, length = width // 3, rows * TEAM
    outs = pl.pallas_call(
        self_forward_kernel,
        in_specs=[pl.BlockSpec(memory_space=pltpu.SMEM)] + in_vmem(TEAM),
        out_specs=in_vmem(TEAM + 1),
        out_shape=[jax.ShapeDtypeStruct((rows, heads_width), BF16)] * TEAM
        + [jax.ShapeDtypeStruct((8, length), F32)],
        scratch_shapes=[
            pltpu.VMEM((length, width), BF16),
            pltpu.VMEM((length, heads_width), BF16),
        ],
        name="self_forward",
        cost_estimate=pl.CostEstimate(
            flops=4 * length * length * heads_width,
            bytes_accessed=4 * length * width,
            transcendentals=4 * length * length,
        ),
    )(table, *parts)
    return outs[:TEAM], outs[TEAM]


def self_backward_kernel(table, *refs):
    parts, dparts, oparts = refs[:TEAM], refs[TEAM : 2 * TEAM], refs[2 * TEAM : 3 * TEAM]
    lse_ref = refs[3 * TEAM]
    outs = refs[3 * TEAM + 1 : 4 * TEAM + 1]
    all_qkv, all_do, delta_ref, sum_q, sum_k, sum_v = refs[4 * TEAM + 1 :]
    length, heads_width = all_do.shape
    chunks = parts[0].shape[0] // CHUNK
    head_row = lax.broadcasted_iota(jnp.int32, (8, heads_width), 0)
    head_col = lax.broadcasted_iota(jnp.int32, (8, heads_width), 1) // HEAD_DIM
    pick = (head_row == head_col).astype(F32)
    block = 256
    for member in range(TEAM):
        for piece in range(chunks):
            at = pl.multiple_of(table[member * chunks + piece] * CHUNK, CHUNK)
            here = slice(piece * CHUNK, (piece + 1) * CHUNK)
            all_qkv[pl.ds(at, CHUNK), :] = parts[member][here, :]
            all_do[pl.ds(at, CHUNK), :] = dparts[member][here, :]
            sum_q[pl.ds(at, CHUNK), :] = dparts[member][here, :].astype(F32) * oparts[member][
                here, :
            ].astype(F32)
    for block_at in range(length // block):
        rows = slice(block * block_at, block * (block_at + 1))
        delta_ref[:, rows] = lax.dot_general(
            pick,
            sum_q[rows, :],
            (((1,), (1,)), ((), ())),
            precision=HIGHEST,
            preferred_element_type=F32,
        )
    pairs = heads_width // 128
    scale_factor = HEAD_DIM ** (-0.5)
    diagonal = lax.broadcasted_iota(jnp.int32, (block, block), 0) <= lax.broadcasted_iota(
        jnp.int32, (block, block), 1
    )
    for pair in range(pairs):
        q_cols = slice(128 * pair, 128 * pair + 128)
        k_cols = slice(heads_width + 128 * pair, heads_width + 128 * pair + 128)
        v_cols = slice(2 * heads_width + 128 * pair, 2 * heads_width + 128 * pair + 128)
        for block_at in range(length // block):
            rows = slice(block * block_at, block * (block_at + 1))
            seen = slice(0, block * (block_at + 1))
            q_block = all_qkv[rows, q_cols]
            do_block = all_do[rows, q_cols]
            sum_q_block = jnp.zeros((block, 128), F32)
            for head in range(2):
                q_one, do_one = only(q_block, head), only(do_block, head)
                total = lse_ref[2 * pair + head : 2 * pair + head + 1, rows]
                delta = delta_ref[2 * pair + head : 2 * pair + head + 1, rows]
                scores = dot_nt(all_qkv[seen, k_cols], q_one) * scale_factor
                probs = jnp.exp(scores - total)
                near = jnp.where(diagonal, probs[block * block_at :, :], 0.0)
                if block_at:
                    probs = jnp.concatenate([probs[: block * block_at, :], near], 0)
                else:
                    probs = near
                grad_probs = dot_nt(all_qkv[seen, v_cols], do_one)
                grad_scores = (probs * (grad_probs - delta)).astype(BF16)
                term_v = dot_nn(probs.astype(BF16), do_one)
                term_k = dot_nn(grad_scores, q_one) * scale_factor
                if head == 0:
                    term_v_both, term_k_both = term_v, term_k
                else:
                    term_v_both, term_k_both = term_v_both + term_v, term_k_both + term_k
                term_q = dot_tn(grad_scores, all_qkv[seen, k_cols]) * scale_factor
                sum_q_block = jnp.where(lane_mask(block, head), term_q, sum_q_block)
            sum_q[rows, q_cols] = sum_q_block
            if block_at:
                before = slice(0, block * block_at)
                sum_k[before, q_cols] += term_k_both[before, :]
                sum_v[before, q_cols] += term_v_both[before, :]
            sum_k[rows, q_cols] = term_k_both[block * block_at :, :]
            sum_v[rows, q_cols] = term_v_both[block * block_at :, :]
    for member in range(TEAM):
        for piece in range(chunks):
            at = pl.multiple_of(table[member * chunks + piece] * CHUNK, CHUNK)
            here = slice(piece * CHUNK, (piece + 1) * CHUNK)
            outs[member][here, 0:heads_width] = sum_q[pl.ds(at, CHUNK), :].astype(BF16)
            outs[member][here, heads_width : 2 * heads_width] = sum_k[
                pl.ds(at, CHUNK), :
            ].astype(BF16)
            outs[member][here, 2 * heads_width : 3 * heads_width] = sum_v[
                pl.ds(at, CHUNK), :
            ].astype(BF16)


def self_backward(table, parts, dparts, oparts, lse):
    rows, width = parts[0].shape
    heads_width, length = width // 3, rows * TEAM
    return pl.pallas_call(
        self_backward_kernel,
        in_specs=[pl.BlockSpec(memory_space=pltpu.SMEM)] + in_vmem(3 * TEAM + 1),
        out_specs=in_vmem(TEAM),
        out_shape=[jax.ShapeDtypeStruct((rows, width), BF16)] * TEAM,
        scratch_shapes=[
            pltpu.VMEM((length, width), BF16),
            pltpu.VMEM((length, heads_width), BF16),
            pltpu.VMEM((8, length), F32),
            pltpu.VMEM((length, heads_width), F32),
            pltpu.VMEM((length, heads_width), F32),
            pltpu.VMEM((length, heads_width), F32),
        ],
        name="self_backward",
        cost_estimate=pl.CostEstimate(
            flops=10 * length * length * heads_width,
            bytes_accessed=8 * length * width,
            transcendentals=4 * length * length,
        ),
    )(table, *parts, *dparts, *oparts, lse)


def cross_probs_of(query_one, key_pair, allowed):
    scores = dot_nt(query_one, key_pair) * HEAD_DIM ** (-0.5)
    scores = jnp.where(allowed, scores, NEG_LARGE)
    expos = jnp.exp(scores - jnp.max(scores, -1, keepdims=True))
    return expos / jnp.sum(expos, -1, keepdims=True)


def cross_forward_kernel(count, c_ref, k_ref, v_ref, o_ref):
    rows, width = c_ref.shape
    allowed = lax.broadcasted_iota(jnp.int32, (rows, k_ref.shape[0]), 1) < count[0]
    for pair in range(width // 128):
        cols = slice(128 * pair, 128 * pair + 128)
        joined = jnp.zeros((rows, 128), F32)
        for head in range(2):
            probs = cross_probs_of(only(c_ref[:, cols], head), k_ref[:, cols], allowed)
            mixed = dot_nn(probs.astype(BF16), v_ref[:, cols])
            joined = jnp.where(lane_mask(rows, head), mixed, joined)
        o_ref[:, cols] = joined.astype(BF16)


def cross_forward(count, cross, keys, values):
    return pl.pallas_call(
        cross_forward_kernel,
        in_specs=[pl.BlockSpec(memory_space=pltpu.SMEM)] + in_vmem(3),
        out_specs=pl.BlockSpec(memory_space=pltpu.VMEM),
        out_shape=jax.ShapeDtypeStruct(cross.shape, BF16),
        name="cross_forward",
        cost_estimate=pl.CostEstimate(
            flops=8 * cross.shape[0] * keys.shape[0] * cross.shape[1],
            bytes_accessed=8 * cross.shape[0] * cross.shape[1],
            transcendentals=16 * cross.shape[0] * keys.shape[0],
        ),
    )(count, cross, keys, values)


def cross_backward_kernel(count, c_ref, k_ref, v_ref, do_ref, dc_ref, dkv_ref):
    rows, width = c_ref.shape
    scale_factor = HEAD_DIM ** (-0.5)
    allowed = lax.broadcasted_iota(jnp.int32, (rows, k_ref.shape[0]), 1) < count[0]
    for pair in range(width // 128):
        cols = slice(128 * pair, 128 * pair + 128)
        joined = jnp.zeros((rows, 128), F32)
        sum_k = jnp.zeros((k_ref.shape[0], 128), F32)
        sum_v = jnp.zeros((k_ref.shape[0], 128), F32)
        for head in range(2):
            c_one, do_one = only(c_ref[:, cols], head), only(do_ref[:, cols], head)
            probs = cross_probs_of(c_one, k_ref[:, cols], allowed)
            grad_probs = dot_nt(do_one, v_ref[:, cols])
            inner = jnp.sum(probs * grad_probs, -1, keepdims=True)
            grad_scores = (probs * (grad_probs - inner)).astype(BF16)
            term_c = dot_nn(grad_scores, k_ref[:, cols]) * scale_factor
            joined = jnp.where(lane_mask(rows, head), term_c, joined)
            sum_k += dot_tn(grad_scores, c_one) * scale_factor
            sum_v += dot_tn(probs.astype(BF16), do_one)
        dc_ref[:, cols] = joined.astype(BF16)
        dkv_ref[:, cols] = sum_k.astype(BF16)
        dkv_ref[:, width + 128 * pair : width + 128 * pair + 128] = sum_v.astype(BF16)


def cross_backward(count, cross, keys, values, grad_ctx):
    return pl.pallas_call(
        cross_backward_kernel,
        in_specs=[pl.BlockSpec(memory_space=pltpu.SMEM)] + in_vmem(4),
        out_specs=in_vmem(2),
        out_shape=[
            jax.ShapeDtypeStruct(cross.shape, BF16),
            jax.ShapeDtypeStruct((keys.shape[0], 2 * cross.shape[1]), BF16),
        ],
        name="cross_backward",
        cost_estimate=pl.CostEstimate(
            flops=20 * cross.shape[0] * keys.shape[0] * cross.shape[1],
            bytes_accessed=8 * cross.shape[0] * cross.shape[1],
            transcendentals=16 * cross.shape[0] * keys.shape[0],
        ),
    )(count, cross, keys, values, grad_ctx)


def low(values):
    return values.astype(BF16)


def in_order(first, own, other):
    return jnp.where(first == 0, jnp.stack([own, other]), jnp.stack([other, own]))


def on_device(
    image_rows,
    text_rows,
    prompt_len,
    prompt_slot,
    gain_self,
    w_query,
    w_key,
    w_value,
    w_out,
    gain_cross,
    w_query_text,
    w_key_text,
    w_value_text,
    w_out_text,
    gain_mlp,
    w_in,
    w_mlp_out,
    grad_out,
):
    width = image_rows.shape[-1]
    hidden_width = w_in.shape[-1]
    prompt_rows = text_rows.shape[1]
    row_index, group_index = lax.axis_index("row"), lax.axis_index("grp")
    z, y = row_index // 2, row_index % 2
    x, c = group_index // 2, group_index % 2
    mine = 2 * y + c
    part = width // TEAM
    slot_part = hidden_width // (LINES * TEAM)
    rows_here = image_rows.shape[1]
    half_rows = rows_here // 2
    members = [2 * (y ^ (k & 1)) + (c ^ (k >> 1)) for k in range(TEAM)]

    def take(values, start, size, dim):
        return lax.dynamic_slice_in_dim(values, start, size, dim)

    def hand_rows(values):
        pieces = []
        for step in range(LINES):
            which = z ^ step
            piece = lax.dynamic_slice(
                values, (which & 1, (which >> 1) * half_rows, 0), (1, half_rows, width)
            )[0]
            pieces.append(move(piece, hand_out(step)))
        return jnp.concatenate(pieces, 0)

    def return_rows(values):
        pieces = values.reshape(LINES, half_rows, width)
        back = jnp.stack([move(pieces[step], hand_back(step)) for step in range(LINES)])
        back = jnp.where(z & 1, back[jnp.array([1, 0, 3, 2])], back)
        back = jnp.where(z & 2, back[jnp.array([2, 3, 0, 1])], back)
        return (
            back.reshape(2, 2, half_rows, width)
            .transpose(1, 0, 2, 3)
            .reshape(2, rows_here, width)
        )

    chunk_list = []
    for k in range(TEAM):
        y_k, c_k = y ^ (k & 1), c ^ (k >> 1)
        turn = (z & 1) | (c_k << 1)
        for step in range(LINES):
            chunk_list.append(((step ^ turn) * 2 + y_k) * 2 + c_k)
    table = jnp.stack(chunk_list).astype(jnp.int32)

    image = 4 * x + z
    slot = lax.dynamic_index_in_dim(prompt_slot, image, keepdims=False)
    count = lax.dynamic_index_in_dim(prompt_len, slot, keepdims=True)

    rows_low = hand_rows(image_rows)
    inputs = rows_low.astype(F32)
    w_qkv_of = [
        jnp.concatenate([take(w, part * members[k], part, 1) for w in (w_query, w_key, w_value)], 1)
        for k in range(TEAM)
    ]
    normed_self, _, _ = norm_rows(inputs, gain_self)
    normed_parts = team_gather(low(normed_self))
    qkv_parts = [low(matmul(a, w_qkv_of[0])) for a in normed_parts]
    out_parts, log_totals = self_forward(table, qkv_parts)
    got = [out_parts[0]] + [to_member(out_parts[k], k) for k in range(1, TEAM)]

    def natural(parts):
        ordered = []
        for s in range(TEAM):
            apart = s ^ mine
            pick = (apart >> 1) | ((apart & 1) << 1)
            ordered.append(
                jnp.where(
                    pick & 2,
                    jnp.where(pick & 1, parts[3], parts[2]),
                    jnp.where(pick & 1, parts[1], parts[0]),
                )
            )
        return jnp.concatenate(ordered, 1)

    context_low = natural(got)
    hidden = inputs + matmul(context_low, w_out)
    normed_cross, unit_cross, inverse_cross = norm_rows(hidden, gain_cross)
    cross_normed_low = low(normed_cross)
    cross_low = low(matmul(cross_normed_low, w_query_text))

    text_all = lax.all_gather(text_rows, "grp", axis=0, tiled=True)
    text_mine = lax.dynamic_index_in_dim(text_all, slot, keepdims=False)
    text_key = low(matmul(text_mine, w_key_text))
    text_value = low(matmul(text_mine, w_value_text))
    cross_context_low = cross_forward(count, cross_low, text_key, text_value)
    mixed = hidden + matmul(cross_context_low, w_out_text)
    normed_mlp, unit_mlp, inverse_mlp = norm_rows(mixed, gain_mlp)
    mlp_low = low(normed_mlp)
    mlp_all = jnp.concatenate(team_gather(mlp_low), 0)

    grad_low = hand_rows(grad_out)
    grad_all = jnp.concatenate(team_gather(grad_low), 0)

    pre_act = matmul(mlp_low, w_in)
    activated, gelu_back = jax.vjp(jax.nn.gelu, pre_act)
    block_out = mixed + matmul(low(activated), w_mlp_out)
    out_block = return_rows(low(block_out))
    grad_activated = matmul_right_t(grad_low, w_mlp_out)
    grad_pre_low = low(gelu_back(grad_activated)[0])
    grad_mlp_normed = matmul_right_t(grad_pre_low, w_in)
    grad_from_mlp, grad_gain_mlp = norm_back(grad_mlp_normed, unit_mlp, inverse_mlp, gain_mlp)
    grad_mixed = grad_low.astype(F32) + grad_from_mlp
    grad_mixed_low = low(grad_mixed)
    grad_cross_ctx = low(matmul_right_t(grad_mixed_low, w_out_text))
    grad_cross_low, grad_text_kv = cross_backward(
        count, cross_low, text_key, text_value, grad_cross_ctx
    )
    grad_cross_normed = matmul_right_t(grad_cross_low, w_query_text)
    grad_from_cross, grad_gain_cross = norm_back(
        grad_cross_normed, unit_cross, inverse_cross, gain_cross
    )
    grad_hidden = grad_mixed + grad_from_cross
    grad_hidden_low = low(grad_hidden)
    hidden_all = jnp.concatenate(team_gather(grad_hidden_low), 0)

    w_in_mine = jnp.concatenate(
        [take(w_in, (b * TEAM + mine) * slot_part, slot_part, 1) for b in range(LINES)], 1
    )
    w_mlp_out_mine = jnp.concatenate(
        [take(w_mlp_out, (b * TEAM + mine) * slot_part, slot_part, 0) for b in range(LINES)], 0
    )
    pre_team = matmul(mlp_all, w_in_mine)
    act_team, back_team = jax.vjp(jax.nn.gelu, pre_team)
    grad_act_team = matmul_right_t(grad_all, w_mlp_out_mine)
    grad_pre_team = low(back_team(grad_act_team)[0])
    part_w_in = low(matmul_left_t(mlp_all, grad_pre_team))
    part_w_mlp_out = low(matmul_left_t(low(act_team), grad_all))
    half = width // 2
    joined = jnp.concatenate(
        [part_w_in.reshape(LINES, -1, width), part_w_mlp_out.reshape(LINES, -1, width)], 1
    )
    mlp_sum = ring_sum(ring_blocks(joined[:, :, :half], joined[:, :, half:]))

    grad_context = low(matmul_right_t(hidden_all, take(w_out, part * mine, part, 0)))
    rows_own = rows_low.shape[0]
    grad_context_parts = [grad_context[k * rows_own : (k + 1) * rows_own] for k in range(TEAM)]
    grad_qkv_parts = self_backward(table, qkv_parts, grad_context_parts, out_parts, log_totals)
    got_grads = [grad_qkv_parts[0]] + [
        to_member(grad_qkv_parts[k], k) for k in range(1, TEAM)
    ]
    grad_normed_self = sum(matmul_right_t(got_grads[k], w_qkv_of[k]) for k in range(TEAM))
    _, unit_self, inverse_self = norm_rows(inputs, gain_self)
    grad_from_self, grad_gain_self = norm_back(grad_normed_self, unit_self, inverse_self, gain_self)
    grad_image = return_rows(low(grad_hidden + grad_from_self))

    text_sum = low(grad_text_kv.astype(F32) + to_member(grad_text_kv, 2).astype(F32))
    text_total = low(text_sum.astype(F32) + to_member(text_sum, 1).astype(F32))
    text_left = lax.dynamic_index_in_dim(
        text_mine.reshape(prompt_rows, LINES, 2, width // 8), y, 2, keepdims=False
    ).reshape(prompt_rows, half)
    text_right = jnp.concatenate(
        [take(text_total, half * c, half, 1), take(text_total, width + half * c, half, 1)], 1
    )
    part_text = low(matmul_left_t(text_left, text_right))
    share = prompt_rows // TEAM
    text_share = take(text_total, share * mine, share, 0)
    grad_text_share = low(
        matmul_right_t(text_share[:, :width], w_key_text)
        + matmul_right_t(text_share[:, width:], w_value_text)
    )
    grad_text_all = lax.all_gather(grad_text_share, AXES, axis=0, tiled=False).reshape(
        LINES, 2, 2, 2, share, width
    )
    texts = []
    for each in range(text_rows.shape[0]):
        wanted = text_rows.shape[0] * group_index + each
        owner = jnp.sum(
            jnp.where(prompt_slot == wanted, jnp.arange(prompt_slot.shape[0]), 0)
        )
        texts.append(
            lax.dynamic_slice(
                grad_text_all,
                (owner % LINES, 0, owner // LINES, 0, 0, 0),
                (1, 2, 1, 2, share, width),
            ).reshape(prompt_rows, width)
        )
    grad_text = jnp.stack(texts)

    lefts = (cross_normed_low, cross_context_low, context_low)
    rights = (grad_cross_low, grad_mixed_low, grad_hidden_low)
    away = jnp.stack(
        [low(matmul_left_t(l, take(r, half * (1 - c), half, 1))) for l, r in zip(lefts, rights)]
    )
    away = to_member(away, 2)
    kept = jnp.stack([matmul_left_t(l, take(r, half * c, half, 1)) for l, r in zip(lefts, rights)])
    kept = low(kept + away.astype(F32)).reshape(3, LINES, 2, width // 8, half)
    away = to_member(lax.dynamic_index_in_dim(kept, 1 - y, 2, keepdims=False), 1)
    kept = lax.dynamic_index_in_dim(kept, y, 2, keepdims=False)
    kept = low(kept.astype(F32) + away.astype(F32))
    text_blocks = part_text.reshape(LINES, width // 8, 2, half).transpose(2, 0, 1, 3)
    small = jnp.concatenate([kept, text_blocks], 0).transpose(1, 0, 2, 3)
    small = small.reshape(LINES, 5 * (width // 8), half)
    quarter = half // 2
    small_sum = ring_sum(ring_blocks(small[:, :, :quarter], small[:, :, quarter:]))

    normed_all = jnp.concatenate(normed_parts, 0)
    part_qkv = low(matmul_left_t(normed_all, jnp.concatenate(grad_qkv_parts, 0)))
    part_qkv = part_qkv.reshape(LINES, 2, width // 8, 3 * part)
    gains = jnp.stack([grad_gain_self, grad_gain_cross, grad_gain_mlp])
    gains = low(gains).reshape(3, LINES, 2, width // 8).transpose(1, 2, 0, 3)
    gains = gains.reshape(LINES, 2, 1, 3 * (width // 8))
    gains = jnp.pad(gains, ((0, 0), (0, 0), (0, 15), (0, 0)))
    side = 3 * part // 2
    left = jnp.concatenate([part_qkv[..., :side], gains], 2).reshape(LINES, -1, side)
    right = jnp.concatenate([part_qkv[..., side:], jnp.zeros_like(gains)], 2)
    qkv_sum = ring_sum(ring_blocks(left, right.reshape(LINES, -1, side)))

    split = width // 4
    mlp_left = mlp_sum[:split].reshape(2, width // 8, half)
    other = to_member(lax.dynamic_index_in_dim(mlp_left, 1 - y, 0, keepdims=False), 1)
    own = lax.dynamic_index_in_dim(mlp_left, y, 0, keepdims=False)
    mlp_pack = jnp.concatenate([in_order(y, own, other).reshape(split, half), mlp_sum[split:]], 0)
    mlp_pack = lax.all_gather(mlp_pack, "grp", axis=0).reshape(2, 2, 2 * split, half)
    grad_w_in = (
        mlp_pack[:, :, :split]
        .reshape(2, 2, 2, width // 8, 2, slot_part)
        .transpose(3, 0, 4, 2, 1, 5)
        .reshape(width // 8, hidden_width)
        .astype(F32)
    )
    grad_w_mlp_out = (
        mlp_pack[:, :, split:].transpose(1, 2, 0, 3).reshape(2 * split, width).astype(F32)
    )
    small_all = lax.all_gather(small_sum, "grp", axis=0).reshape(2, 2, 5, width // 8, quarter)
    small_all = small_all.transpose(2, 3, 1, 0, 4).reshape(5, width // 8, width).astype(F32)

    qkv_half = qkv_sum.reshape(2, -1, side)
    other = to_member(lax.dynamic_index_in_dim(qkv_half, 1 - y, 0, keepdims=False), 1)
    own = lax.dynamic_index_in_dim(qkv_half, y, 0, keepdims=False)
    qkv_pack = lax.all_gather(in_order(y, own, other), "grp", axis=0)
    qkv_pack = qkv_pack.reshape(2, 2, 2, -1, side)
    gain_rows = jnp.sum(qkv_pack[:, :, :, width // 8].astype(F32), (0, 1, 2))
    gain_rows = gain_rows.reshape(3, width // 8)
    qkv_rows = qkv_pack[:, :, :, : width // 8].transpose(3, 2, 1, 0, 4)
    qkv_rows = qkv_rows.reshape(width // 8, TEAM, 3, part).transpose(2, 0, 1, 3)
    qkv_rows = qkv_rows.reshape(3, width // 8, width).astype(F32)
    return (
        out_block,
        grad_image,
        grad_text,
        gain_rows[0],
        qkv_rows[0],
        qkv_rows[1],
        qkv_rows[2],
        small_all[2],
        gain_rows[1],
        small_all[0],
        small_all[3],
        small_all[4],
        small_all[1],
        gain_rows[2],
        grad_w_in,
        grad_w_mlp_out,
    )


def solution(mesh):
    placed = (
        P("grp", "row", None),
        P("grp", None, None),
        P(),
        P(),
        P(),
        P(),
        P(),
        P(),
        P(),
        P(),
        P(),
        P(),
        P(),
        P(),
        P(),
        P(),
        P(),
        P("grp", "row", None),
    )
    return jax.shard_map(
        on_device if fits(mesh) else on_device_plain,
        mesh=mesh,
        in_specs=placed,
        out_specs=(
            P("grp", "row", None),
            P("grp", "row", None),
            P("grp", None, None),
            P("row"),
            P("row", None),
            P("row", None),
            P("row", None),
            P("row", None),
            P("row"),
            P("row", None),
            P("row", None),
            P("row", None),
            P("row", None),
            P("row"),
            P("row", None),
            P("row", None),
        ),
        check_vma=False,
    )
```

```python
import jax
import jax.numpy as jnp
import numpy as np
from jax import lax
from jax.sharding import PartitionSpec as P
from jax.experimental import pallas as pl
from jax.experimental.pallas import tpu as pltpu

HEADS = 16
HEAD_DIM = 64


EPSILON = 1e-05
NEG_LARGE = -1e30
HIGHEST = lax.Precision.HIGHEST


def norm_rows(values, gain):
    center = jnp.mean(values, -1, keepdims=True)
    centered = values - center
    variance = jnp.mean(centered * centered, -1, keepdims=True)
    inverse = lax.rsqrt(variance + EPSILON)
    unit_rows = centered * inverse
    return (unit_rows * gain, unit_rows, inverse)


def norm_back(grad_normed, unit_rows, inverse, gain):
    grad_unit = grad_normed * gain
    first_mean = jnp.mean(grad_unit, -1, keepdims=True)
    second_mean = jnp.mean(grad_unit * unit_rows, -1, keepdims=True)
    grad_input = inverse * (grad_unit - first_mean - unit_rows * second_mean)
    return (grad_input, jnp.sum(grad_normed * unit_rows, 0))


def matmul(left, right):
    return jnp.dot(left, right, preferred_element_type=jnp.float32)


def matmul_left_t(left, right):
    return lax.dot_general(
        left, right, (((0,), (0,)), ((), ())), preferred_element_type=jnp.float32
    )


def matmul_right_t(left, right):
    return lax.dot_general(
        left, right, (((1,), (1,)), ((), ())), preferred_element_type=jnp.float32
    )


def split_heads(values):
    return values.reshape(values.shape[:-1] + (HEADS, HEAD_DIM))


def on_device_plain(
    image_rows,
    text_rows,
    prompt_len,
    prompt_slot,
    gain_self,
    w_query,
    w_key,
    w_value,
    w_out,
    gain_cross,
    w_query_text,
    w_key_text,
    w_value_text,
    w_out_text,
    gain_mlp,
    w_in,
    w_mlp_out,
    grad_out,
):
    images_here, rows_here, width = image_rows.shape
    prompt_rows = text_rows.shape[1]
    row_count = lax.axis_size("row")
    length = rows_here * row_count
    row_index = lax.axis_index("row")
    group_index = lax.axis_index("grp")
    scale_factor = HEAD_DIM ** (-0.5)
    block_size = min(512, length)
    block_count = length // block_size
    flat_rows = images_here * rows_here
    inputs = image_rows.astype(jnp.float32).reshape(flat_rows, width)
    normed_self, unit_self, inverse_self = norm_rows(inputs, gain_self)
    normed_low = normed_self.astype(jnp.bfloat16)
    query_low = (
        matmul(normed_low, w_query).astype(jnp.bfloat16).reshape(images_here, rows_here, width)
    )
    key_low = matmul(normed_low, w_key).astype(jnp.bfloat16).reshape(images_here, rows_here, width)
    value_low = (
        matmul(normed_low, w_value).astype(jnp.bfloat16).reshape(images_here, rows_here, width)
    )
    keys_all, values_all = (
        lax.all_gather(key_low, "row", axis=1, tiled=True),
        lax.all_gather(value_low, "row", axis=1, tiled=True),
    )
    query_heads = split_heads(query_low)
    query_pos = row_index * rows_here + jnp.arange(rows_here, dtype=jnp.int32)
    key_pos = jnp.arange(length, dtype=jnp.int32)
    causal = key_pos[None, :] <= query_pos[:, None]
    contexts = []
    totals = []
    for each_image in range(images_here):
        scores = (
            jnp.einsum(
                "qhd,khd->hqk",
                query_heads[each_image],
                split_heads(keys_all[each_image]),
                preferred_element_type=jnp.float32,
            )
            * scale_factor
        )
        scores = jnp.where(causal[None], scores, NEG_LARGE)
        largest = jnp.max(scores, -1, keepdims=True)
        expos = jnp.exp(scores - largest)
        denominator = jnp.sum(expos, -1, keepdims=True)
        probs_low = (expos / denominator).astype(jnp.bfloat16)
        contexts.append(
            jnp.einsum(
                "hqk,khd->qhd",
                probs_low,
                split_heads(values_all[each_image]),
                preferred_element_type=jnp.float32,
            )
        )
        totals.append((largest + jnp.log(denominator))[..., 0])
    context = jnp.stack(contexts).reshape(flat_rows, width)
    log_totals = jnp.stack(totals)
    context_low = context.astype(jnp.bfloat16)
    hidden = inputs + matmul(context_low, w_out)
    normed_cross, unit_cross, inverse_cross = norm_rows(hidden, gain_cross)
    cross_normed_low = normed_cross.astype(jnp.bfloat16)
    cross_low = (
        matmul(cross_normed_low, w_query_text)
        .astype(jnp.bfloat16)
        .reshape(images_here, rows_here, HEADS, HEAD_DIM)
    )
    text_flat = text_rows.reshape(-1, width)
    text_key = matmul(text_flat, w_key_text).astype(jnp.bfloat16).reshape(text_rows.shape)
    text_value = matmul(text_flat, w_value_text).astype(jnp.bfloat16).reshape(text_rows.shape)
    text_keys, text_values = (
        lax.all_gather(text_key, "grp", axis=0, tiled=True),
        lax.all_gather(text_value, "grp", axis=0, tiled=True),
    )
    image_total = prompt_slot.shape[0]
    slots = lax.dynamic_slice_in_dim(prompt_slot, group_index * images_here, images_here)
    keys_sel = split_heads(jnp.take(text_keys, slots, axis=0))
    values_sel = split_heads(jnp.take(text_values, slots, axis=0))
    lengths_sel = jnp.take(prompt_len, slots)
    text_mask = (jnp.arange(prompt_rows, dtype=jnp.int32)[None, :] < lengths_sel[:, None])[
        :, None, None, :
    ]
    cross_scores = (
        jnp.einsum("iqhd,ikhd->ihqk", cross_low, keys_sel, preferred_element_type=jnp.float32)
        * scale_factor
    )
    cross_probs = jax.nn.softmax(jnp.where(text_mask, cross_scores, NEG_LARGE), axis=-1)
    cross_probs_low = cross_probs.astype(jnp.bfloat16)
    cross_context = jnp.einsum(
        "ihqk,ikhd->iqhd", cross_probs_low, values_sel, preferred_element_type=jnp.float32
    )
    cross_context_low = cross_context.reshape(flat_rows, width).astype(jnp.bfloat16)
    mixed = hidden + matmul(cross_context_low, w_out_text)
    normed_mlp, unit_mlp, inverse_mlp = norm_rows(mixed, gain_mlp)
    mlp_low = normed_mlp.astype(jnp.bfloat16)
    pre_act = matmul(mlp_low, w_in)
    activated, gelu_back = jax.vjp(jax.nn.gelu, pre_act)
    activated_low = activated.astype(jnp.bfloat16)
    block_out = mixed + matmul(activated_low, w_mlp_out)
    out_block = block_out.astype(jnp.bfloat16).reshape(image_rows.shape)
    grad_low = grad_out.reshape(flat_rows, width)
    grad_w_mlp_out = matmul_left_t(activated_low, grad_low)
    grad_activated = matmul_right_t(grad_low, w_mlp_out)
    grad_pre_low = gelu_back(grad_activated)[0].astype(jnp.bfloat16)
    grad_w_in = matmul_left_t(mlp_low, grad_pre_low)
    grad_mlp_normed = matmul_right_t(grad_pre_low, w_in)
    grad_from_mlp, grad_gain_mlp = norm_back(grad_mlp_normed, unit_mlp, inverse_mlp, gain_mlp)
    grad_mixed = grad_low.astype(jnp.float32) + grad_from_mlp
    grad_mixed_low = grad_mixed.astype(jnp.bfloat16)
    grad_w_out_text = matmul_left_t(cross_context_low, grad_mixed_low)
    grad_cross_ctx = split_heads(
        matmul_right_t(grad_mixed_low, w_out_text)
        .astype(jnp.bfloat16)
        .reshape(images_here, rows_here, width)
    )
    grad_cross_probs = jnp.einsum(
        "iqhd,ikhd->ihqk", grad_cross_ctx, values_sel, preferred_element_type=jnp.float32
    )
    grad_values_sel = jnp.einsum(
        "ihqk,iqhd->ikhd", cross_probs_low, grad_cross_ctx, preferred_element_type=jnp.float32
    )
    grad_cross_scores = cross_probs * (
        grad_cross_probs - jnp.sum(cross_probs * grad_cross_probs, -1, keepdims=True)
    )
    grad_scores_low = grad_cross_scores.astype(jnp.bfloat16)
    grad_cross_query = (
        jnp.einsum("ihqk,ikhd->iqhd", grad_scores_low, keys_sel, preferred_element_type=jnp.float32)
        * scale_factor
    )
    grad_cross_query_low = grad_cross_query.astype(jnp.bfloat16).reshape(flat_rows, width)
    grad_keys_sel = (
        jnp.einsum(
            "ihqk,iqhd->ikhd", grad_scores_low, cross_low, preferred_element_type=jnp.float32
        )
        * scale_factor
    )
    grad_w_query_text = matmul_left_t(cross_normed_low, grad_cross_query_low)
    grad_cross_normed = matmul_right_t(grad_cross_query_low, w_query_text)
    grad_from_cross, grad_gain_cross = norm_back(
        grad_cross_normed, unit_cross, inverse_cross, gain_cross
    )
    grad_hidden = grad_mixed + grad_from_cross
    placing = (jnp.arange(image_total, dtype=jnp.int32)[:, None] == slots[None, :]).astype(
        jnp.float32
    )
    joined_text = jnp.concatenate(
        [
            grad_keys_sel.reshape(images_here, prompt_rows, width),
            grad_values_sel.reshape(images_here, prompt_rows, width),
        ],
        -1,
    )
    text_term = jnp.einsum("si,ipd->spd", placing, joined_text, precision=HIGHEST)
    text_grad = lax.psum_scatter(
        text_term.astype(jnp.bfloat16), "grp", scatter_dimension=0, tiled=True
    )
    share_rows = text_flat.shape[0] // row_count
    text_total = (
        lax.psum(text_grad, "row").astype(jnp.float32).reshape(-1, 2 * width).astype(jnp.bfloat16)
    )
    text_share = lax.dynamic_slice_in_dim(text_total, row_index * share_rows, share_rows, 0)
    text_grad_rows = (
        matmul_right_t(text_total[:, :width], w_key_text)
        + matmul_right_t(text_total[:, width:], w_value_text)
    ).astype(jnp.bfloat16)
    text_part = lax.dynamic_slice_in_dim(text_flat, row_index * share_rows, share_rows, 0)
    grad_w_key_text = matmul_left_t(text_part, text_share[:, :width])
    grad_w_value_text = matmul_left_t(text_part, text_share[:, width:])
    grad_text = text_grad_rows.reshape(text_rows.shape)
    grad_hidden_low = grad_hidden.astype(jnp.bfloat16)
    grad_w_out = matmul_left_t(context_low, grad_hidden_low)
    grad_context = (
        matmul_right_t(grad_hidden_low, w_out)
        .astype(jnp.bfloat16)
        .reshape(images_here, rows_here, width)
    )
    grad_context_heads = split_heads(grad_context)
    context_heads = split_heads(context.reshape(images_here, rows_here, width))
    delta = jnp.einsum(
        "iqhd,iqhd->ihq", grad_context_heads.astype(jnp.float32), context_heads, precision=HIGHEST
    )
    zero_query = jnp.zeros((images_here, rows_here, HEADS, HEAD_DIM), jnp.float32)

    def block_terms(block):
        start = block * block_size
        key_heads = split_heads(lax.dynamic_slice_in_dim(keys_all, start, block_size, 1))
        value_heads = split_heads(lax.dynamic_slice_in_dim(values_all, start, block_size, 1))
        block_pos = start + jnp.arange(block_size, dtype=jnp.int32)
        allowed = (block_pos[None, :] <= query_pos[:, None])[None, None]
        scores = (
            jnp.einsum(
                "iqhd,ikhd->ihqk", query_heads, key_heads, preferred_element_type=jnp.float32
            )
            * scale_factor
        )
        probs = jnp.where(allowed, jnp.exp(scores - log_totals[..., None]), 0.0)
        grad_probs = jnp.einsum(
            "iqhd,ikhd->ihqk", grad_context_heads, value_heads, preferred_element_type=jnp.float32
        )
        grad_scores = (probs * (grad_probs - delta[..., None])).astype(jnp.bfloat16)
        return (grad_scores, probs.astype(jnp.bfloat16), key_heads)

    def step_keys(block, carry):
        grad_query, term_buffer = carry
        grad_scores, probs_low, key_heads = block_terms(block)
        grad_query = (
            grad_query
            + jnp.einsum(
                "ihqk,ikhd->iqhd", grad_scores, key_heads, preferred_element_type=jnp.float32
            )
            * scale_factor
        )
        grad_key_part = (
            jnp.einsum(
                "ihqk,iqhd->ikhd", grad_scores, query_heads, preferred_element_type=jnp.float32
            )
            * scale_factor
        )
        grad_value_part = jnp.einsum(
            "ihqk,iqhd->ikhd", probs_low, grad_context_heads, preferred_element_type=jnp.float32
        )
        joined = jnp.concatenate(
            [
                grad_key_part.reshape(images_here, block_size, width),
                grad_value_part.reshape(images_here, block_size, width),
            ],
            -1,
        )
        term_buffer = lax.dynamic_update_slice_in_dim(term_buffer, joined, block * block_size, 1)
        return (grad_query, term_buffer)

    start_buffer = jnp.zeros((images_here, length, 2 * width), jnp.float32)
    grad_query, term_buffer = lax.fori_loop(0, block_count, step_keys, (zero_query, start_buffer))
    grad_kv = lax.psum_scatter(
        term_buffer.astype(jnp.bfloat16), "row", scatter_dimension=1, tiled=True
    ).astype(jnp.float32)
    grad_query_low = grad_query.reshape(flat_rows, width).astype(jnp.bfloat16)
    grad_kv_low = grad_kv.reshape(flat_rows, 2 * width).astype(jnp.bfloat16)
    grad_w_query = matmul_left_t(normed_low, grad_query_low)
    grad_w_key = matmul_left_t(normed_low, grad_kv_low[:, :width])
    grad_w_value = matmul_left_t(normed_low, grad_kv_low[:, width:])
    grad_normed_self = (
        matmul_right_t(grad_query_low, w_query)
        + matmul_right_t(grad_kv_low[:, :width], w_key)
        + matmul_right_t(grad_kv_low[:, width:], w_value)
    )
    grad_from_self, grad_gain_self = norm_back(grad_normed_self, unit_self, inverse_self, gain_self)
    grad_image = (grad_hidden + grad_from_self).astype(jnp.bfloat16).reshape(image_rows.shape)
    shares = (
        lax.psum_scatter(
            grad_gain_self.astype(jnp.bfloat16), "row", scatter_dimension=0, tiled=True
        ).astype(jnp.float32),
        lax.psum_scatter(
            grad_w_query.astype(jnp.bfloat16), "row", scatter_dimension=0, tiled=True
        ).astype(jnp.float32),
        lax.psum_scatter(
            grad_w_key.astype(jnp.bfloat16), "row", scatter_dimension=0, tiled=True
        ).astype(jnp.float32),
        lax.psum_scatter(
            grad_w_value.astype(jnp.bfloat16), "row", scatter_dimension=0, tiled=True
        ).astype(jnp.float32),
        lax.psum_scatter(
            grad_w_out.astype(jnp.bfloat16), "row", scatter_dimension=0, tiled=True
        ).astype(jnp.float32),
        lax.psum_scatter(
            grad_gain_cross.astype(jnp.bfloat16), "row", scatter_dimension=0, tiled=True
        ).astype(jnp.float32),
        lax.psum_scatter(
            grad_w_query_text.astype(jnp.bfloat16), "row", scatter_dimension=0, tiled=True
        ).astype(jnp.float32),
        lax.psum_scatter(
            grad_w_key_text.astype(jnp.bfloat16), "row", scatter_dimension=0, tiled=True
        ).astype(jnp.float32),
        lax.psum_scatter(
            grad_w_value_text.astype(jnp.bfloat16), "row", scatter_dimension=0, tiled=True
        ).astype(jnp.float32),
        lax.psum_scatter(
            grad_w_out_text.astype(jnp.bfloat16), "row", scatter_dimension=0, tiled=True
        ).astype(jnp.float32),
        lax.psum_scatter(
            grad_gain_mlp.astype(jnp.bfloat16), "row", scatter_dimension=0, tiled=True
        ).astype(jnp.float32),
        lax.psum_scatter(
            grad_w_in.astype(jnp.bfloat16), "row", scatter_dimension=0, tiled=True
        ).astype(jnp.float32),
        lax.psum_scatter(
            grad_w_mlp_out.astype(jnp.bfloat16), "row", scatter_dimension=0, tiled=True
        ).astype(jnp.float32),
    )
    summed = (
        lax.psum(shares[0].astype(jnp.bfloat16), "grp").astype(jnp.float32),
        lax.psum(shares[1].astype(jnp.bfloat16), "grp").astype(jnp.float32),
        lax.psum(shares[2].astype(jnp.bfloat16), "grp").astype(jnp.float32),
        lax.psum(shares[3].astype(jnp.bfloat16), "grp").astype(jnp.float32),
        lax.psum(shares[4].astype(jnp.bfloat16), "grp").astype(jnp.float32),
        lax.psum(shares[5].astype(jnp.bfloat16), "grp").astype(jnp.float32),
        lax.psum(shares[6].astype(jnp.bfloat16), "grp").astype(jnp.float32),
        lax.psum(shares[7].astype(jnp.bfloat16), "grp").astype(jnp.float32),
        lax.psum(shares[8].astype(jnp.bfloat16), "grp").astype(jnp.float32),
        lax.psum(shares[9].astype(jnp.bfloat16), "grp").astype(jnp.float32),
        lax.psum(shares[10].astype(jnp.bfloat16), "grp").astype(jnp.float32),
        lax.psum(shares[11].astype(jnp.bfloat16), "grp").astype(jnp.float32),
        lax.psum(shares[12].astype(jnp.bfloat16), "grp").astype(jnp.float32),
    )
    return (
        out_block,
        grad_image,
        grad_text,
        summed[0],
        summed[1],
        summed[2],
        summed[3],
        summed[4],
        summed[5],
        summed[6],
        summed[7],
        summed[8],
        summed[9],
        summed[10],
        summed[11],
        summed[12],
    )


AXES = ("row", "grp")
SMALL_COST = pl.CostEstimate(flops=0, bytes_accessed=0, transcendentals=0)
BF16 = jnp.bfloat16
F32 = jnp.float32
TEAM = 4
LINES = 4


def fits(mesh):
    return mesh.shape["row"] == 2 * LINES and mesh.shape["grp"] == 4


def moves(change):
    pairs = []
    for place in range(32):
        z, y, x, c = place // 8, place // 4 % 2, place // 2 % 2, place % 2
        z2, y2, x2, c2 = change(z, y, x, c)
        pairs.append((place, z2 * 8 + y2 * 4 + x2 * 2 + c2))
    return pairs


def move(values, change):
    return lax.ppermute(values, AXES, moves(change))


def to_member(values, member):
    flip_y, flip_c = member & 1, member >> 1
    return move(values, lambda z, y, x, c: (z, y ^ flip_y, x, c ^ flip_c))


def team_gather(values):
    side = to_member(values, 1)
    return [values, side, to_member(values, 2), to_member(side, 2)]


def hand_out(step):
    def change(z, y, x, c):
        which = z ^ step
        return (2 * c + (which & 1), y, x, which >> 1)

    return change


def hand_back(step):
    def change(z, y, x, c):
        return (step ^ ((z & 1) | (c << 1)), y, x, z >> 1)

    return change


def ring_groups():
    order = [(0, 0), (0, 1), (0, 2), (0, 3), (1, 3), (1, 2), (1, 1), (1, 0)]
    return [
        [z * 8 + y * 4 + x * 2 + c for x, z in order] for y in range(2) for c in range(2)
    ]


def line_groups():
    return [[z * 8 + place for z in range(LINES)] for place in range(8)]


def ring_sum(blocks):
    flat = blocks.reshape(-1, blocks.shape[-1])
    return lax.psum_scatter(
        flat, AXES, scatter_dimension=0, axis_index_groups=ring_groups(), tiled=True
    )


def lane_mask(rows, head):
    lane = lax.broadcasted_iota(jnp.int32, (rows, 128), 1)
    return (lane >= HEAD_DIM) if head else (lane < HEAD_DIM)


def only(values, head):
    return jnp.where(lane_mask(values.shape[0], head), values, jnp.zeros_like(values))


def dot_nt(left, right):
    return lax.dot_general(
        left, right, (((1,), (1,)), ((), ())), preferred_element_type=F32
    )


def dot_nn(left, right):
    return lax.dot_general(
        left, right, (((1,), (0,)), ((), ())), preferred_element_type=F32
    )


def dot_tn(left, right):
    return lax.dot_general(
        left, right, (((0,), (0,)), ((), ())), preferred_element_type=F32
    )


CHUNK = 64


def self_forward_kernel(table, *refs):
    parts, outs, lse_ref = refs[:TEAM], refs[TEAM : 2 * TEAM], refs[2 * TEAM]
    all_qkv, all_out = refs[2 * TEAM + 1 :]
    length, heads_width = all_out.shape
    chunks = parts[0].shape[0] // CHUNK
    for member in range(TEAM):
        for piece in range(chunks):
            at = pl.multiple_of(table[member * chunks + piece] * CHUNK, CHUNK)
            all_qkv[pl.ds(at, CHUNK), :] = parts[member][piece * CHUNK : (piece + 1) * CHUNK, :]
    block = 256
    pairs = heads_width // 128
    scale_factor = HEAD_DIM ** (-0.5)
    diagonal = lax.broadcasted_iota(jnp.int32, (block, block), 1) <= lax.broadcasted_iota(
        jnp.int32, (block, block), 0
    )
    for pair in range(pairs):
        q_cols = slice(128 * pair, 128 * pair + 128)
        k_cols = slice(heads_width + 128 * pair, heads_width + 128 * pair + 128)
        v_cols = slice(2 * heads_width + 128 * pair, 2 * heads_width + 128 * pair + 128)
        for block_at in range(length // block):
            rows = slice(block * block_at, block * (block_at + 1))
            q_block = all_qkv[rows, q_cols]
            joined = jnp.zeros((block, 128), F32)
            for head in range(2):
                q_one = only(q_block, head)
                near = dot_nt(q_one, all_qkv[rows, k_cols]) * scale_factor
                near = jnp.where(diagonal, near, NEG_LARGE)
                scores = near
                if block_at:
                    far = dot_nt(q_one, all_qkv[0 : block * block_at, k_cols]) * scale_factor
                    scores = jnp.concatenate([far, near], 1)
                largest = jnp.max(scores, -1, keepdims=True)
                expos = jnp.exp(scores - largest)
                denominator = jnp.sum(expos, -1, keepdims=True)
                probs_low = (expos / denominator).astype(BF16)
                mixed = dot_nn(probs_low, all_qkv[0 : block * (block_at + 1), v_cols])
                joined = jnp.where(lane_mask(block, head), mixed, joined)
                total = largest + jnp.log(denominator)
                lse_ref[2 * pair + head : 2 * pair + head + 1, rows] = jnp.transpose(
                    jnp.broadcast_to(total, (block, 128))
                )[0:1, :]
            all_out[rows, q_cols] = joined.astype(BF16)
    for member in range(TEAM):
        for piece in range(chunks):
            at = pl.multiple_of(table[member * chunks + piece] * CHUNK, CHUNK)
            outs[member][piece * CHUNK : (piece + 1) * CHUNK, :] = all_out[pl.ds(at, CHUNK), :]


def in_vmem(count):
    return [pl.BlockSpec(memory_space=pltpu.VMEM)] * count


def self_forward(table, parts):
    rows, width = parts[0].shape
    heads_width, length = width // 3, rows * TEAM
    outs = pl.pallas_call(
        self_forward_kernel,
        in_specs=[pl.BlockSpec(memory_space=pltpu.SMEM)] + in_vmem(TEAM),
        out_specs=in_vmem(TEAM + 1),
        out_shape=[jax.ShapeDtypeStruct((rows, heads_width), BF16)] * TEAM
        + [jax.ShapeDtypeStruct((8, length), F32)],
        scratch_shapes=[
            pltpu.VMEM((length, width), BF16),
            pltpu.VMEM((length, heads_width), BF16),
        ],
        name="self_forward",
        cost_estimate=SMALL_COST,
    )(table, *parts)
    return outs[:TEAM], outs[TEAM]


def self_backward_kernel(table, *refs):
    parts, dparts, oparts = refs[:TEAM], refs[TEAM : 2 * TEAM], refs[2 * TEAM : 3 * TEAM]
    lse_ref = refs[3 * TEAM]
    outs = refs[3 * TEAM + 1 : 4 * TEAM + 1]
    all_qkv, all_do, delta_ref, sum_q, sum_k, sum_v = refs[4 * TEAM + 1 :]
    length, heads_width = all_do.shape
    chunks = parts[0].shape[0] // CHUNK
    head_row = lax.broadcasted_iota(jnp.int32, (8, heads_width), 0)
    head_col = lax.broadcasted_iota(jnp.int32, (8, heads_width), 1) // HEAD_DIM
    pick = (head_row == head_col).astype(F32)
    block = 256
    for member in range(TEAM):
        for piece in range(chunks):
            at = pl.multiple_of(table[member * chunks + piece] * CHUNK, CHUNK)
            here = slice(piece * CHUNK, (piece + 1) * CHUNK)
            all_qkv[pl.ds(at, CHUNK), :] = parts[member][here, :]
            all_do[pl.ds(at, CHUNK), :] = dparts[member][here, :]
            sum_q[pl.ds(at, CHUNK), :] = dparts[member][here, :].astype(F32) * oparts[member][
                here, :
            ].astype(F32)
    for block_at in range(length // block):
        rows = slice(block * block_at, block * (block_at + 1))
        delta_ref[:, rows] = lax.dot_general(
            pick,
            sum_q[rows, :],
            (((1,), (1,)), ((), ())),
            precision=HIGHEST,
            preferred_element_type=F32,
        )
    pairs = heads_width // 128
    scale_factor = HEAD_DIM ** (-0.5)
    diagonal = lax.broadcasted_iota(jnp.int32, (block, block), 0) <= lax.broadcasted_iota(
        jnp.int32, (block, block), 1
    )
    for pair in range(pairs):
        q_cols = slice(128 * pair, 128 * pair + 128)
        k_cols = slice(heads_width + 128 * pair, heads_width + 128 * pair + 128)
        v_cols = slice(2 * heads_width + 128 * pair, 2 * heads_width + 128 * pair + 128)
        for block_at in range(length // block):
            rows = slice(block * block_at, block * (block_at + 1))
            seen = slice(0, block * (block_at + 1))
            q_block = all_qkv[rows, q_cols]
            do_block = all_do[rows, q_cols]
            sum_q_block = jnp.zeros((block, 128), F32)
            for head in range(2):
                q_one, do_one = only(q_block, head), only(do_block, head)
                total = lse_ref[2 * pair + head : 2 * pair + head + 1, rows]
                delta = delta_ref[2 * pair + head : 2 * pair + head + 1, rows]
                scores = dot_nt(all_qkv[seen, k_cols], q_one) * scale_factor
                probs = jnp.exp(scores - total)
                near = jnp.where(diagonal, probs[block * block_at :, :], 0.0)
                if block_at:
                    probs = jnp.concatenate([probs[: block * block_at, :], near], 0)
                else:
                    probs = near
                grad_probs = dot_nt(all_qkv[seen, v_cols], do_one)
                grad_scores = (probs * (grad_probs - delta)).astype(BF16)
                term_v = dot_nn(probs.astype(BF16), do_one)
                term_k = dot_nn(grad_scores, q_one) * scale_factor
                if head == 0:
                    term_v_both, term_k_both = term_v, term_k
                else:
                    term_v_both, term_k_both = term_v_both + term_v, term_k_both + term_k
                term_q = dot_tn(grad_scores, all_qkv[seen, k_cols]) * scale_factor
                sum_q_block = jnp.where(lane_mask(block, head), term_q, sum_q_block)
            sum_q[rows, q_cols] = sum_q_block
            if block_at:
                before = slice(0, block * block_at)
                sum_k[before, q_cols] += term_k_both[before, :]
                sum_v[before, q_cols] += term_v_both[before, :]
            sum_k[rows, q_cols] = term_k_both[block * block_at :, :]
            sum_v[rows, q_cols] = term_v_both[block * block_at :, :]
    for member in range(TEAM):
        for piece in range(chunks):
            at = pl.multiple_of(table[member * chunks + piece] * CHUNK, CHUNK)
            here = slice(piece * CHUNK, (piece + 1) * CHUNK)
            outs[member][here, 0:heads_width] = sum_q[pl.ds(at, CHUNK), :].astype(BF16)
            outs[member][here, heads_width : 2 * heads_width] = sum_k[
                pl.ds(at, CHUNK), :
            ].astype(BF16)
            outs[member][here, 2 * heads_width : 3 * heads_width] = sum_v[
                pl.ds(at, CHUNK), :
            ].astype(BF16)


def self_backward(table, parts, dparts, oparts, lse):
    rows, width = parts[0].shape
    heads_width, length = width // 3, rows * TEAM
    return pl.pallas_call(
        self_backward_kernel,
        in_specs=[pl.BlockSpec(memory_space=pltpu.SMEM)] + in_vmem(3 * TEAM + 1),
        out_specs=in_vmem(TEAM),
        out_shape=[jax.ShapeDtypeStruct((rows, width), BF16)] * TEAM,
        scratch_shapes=[
            pltpu.VMEM((length, width), BF16),
            pltpu.VMEM((length, heads_width), BF16),
            pltpu.VMEM((8, length), F32),
            pltpu.VMEM((length, heads_width), F32),
            pltpu.VMEM((length, heads_width), F32),
            pltpu.VMEM((length, heads_width), F32),
        ],
        name="self_backward",
        cost_estimate=SMALL_COST,
    )(table, *parts, *dparts, *oparts, lse)


def cross_probs_of(query_one, key_pair, allowed):
    scores = dot_nt(query_one, key_pair) * HEAD_DIM ** (-0.5)
    scores = jnp.where(allowed, scores, NEG_LARGE)
    expos = jnp.exp(scores - jnp.max(scores, -1, keepdims=True))
    return expos / jnp.sum(expos, -1, keepdims=True)


def cross_forward_kernel(count, c_ref, k_ref, v_ref, o_ref):
    rows, width = c_ref.shape
    allowed = lax.broadcasted_iota(jnp.int32, (rows, k_ref.shape[0]), 1) < count[0]
    for pair in range(width // 128):
        cols = slice(128 * pair, 128 * pair + 128)
        joined = jnp.zeros((rows, 128), F32)
        for head in range(2):
            probs = cross_probs_of(only(c_ref[:, cols], head), k_ref[:, cols], allowed)
            mixed = dot_nn(probs.astype(BF16), v_ref[:, cols])
            joined = jnp.where(lane_mask(rows, head), mixed, joined)
        o_ref[:, cols] = joined.astype(BF16)


def cross_forward(count, cross, keys, values):
    return pl.pallas_call(
        cross_forward_kernel,
        in_specs=[pl.BlockSpec(memory_space=pltpu.SMEM)] + in_vmem(3),
        out_specs=pl.BlockSpec(memory_space=pltpu.VMEM),
        out_shape=jax.ShapeDtypeStruct(cross.shape, BF16),
        name="cross_forward",
        cost_estimate=SMALL_COST,
    )(count, cross, keys, values)


def cross_backward_kernel(count, c_ref, k_ref, v_ref, do_ref, dc_ref, dkv_ref):
    rows, width = c_ref.shape
    scale_factor = HEAD_DIM ** (-0.5)
    allowed = lax.broadcasted_iota(jnp.int32, (rows, k_ref.shape[0]), 1) < count[0]
    for pair in range(width // 128):
        cols = slice(128 * pair, 128 * pair + 128)
        joined = jnp.zeros((rows, 128), F32)
        sum_k = jnp.zeros((k_ref.shape[0], 128), F32)
        sum_v = jnp.zeros((k_ref.shape[0], 128), F32)
        for head in range(2):
            c_one, do_one = only(c_ref[:, cols], head), only(do_ref[:, cols], head)
            probs = cross_probs_of(c_one, k_ref[:, cols], allowed)
            grad_probs = dot_nt(do_one, v_ref[:, cols])
            inner = jnp.sum(probs * grad_probs, -1, keepdims=True)
            grad_scores = (probs * (grad_probs - inner)).astype(BF16)
            term_c = dot_nn(grad_scores, k_ref[:, cols]) * scale_factor
            joined = jnp.where(lane_mask(rows, head), term_c, joined)
            sum_k += dot_tn(grad_scores, c_one) * scale_factor
            sum_v += dot_tn(probs.astype(BF16), do_one)
        dc_ref[:, cols] = joined.astype(BF16)
        dkv_ref[:, cols] = sum_k.astype(BF16)
        dkv_ref[:, width + 128 * pair : width + 128 * pair + 128] = sum_v.astype(BF16)


def cross_backward(count, cross, keys, values, grad_ctx):
    return pl.pallas_call(
        cross_backward_kernel,
        in_specs=[pl.BlockSpec(memory_space=pltpu.SMEM)] + in_vmem(4),
        out_specs=in_vmem(2),
        out_shape=[
            jax.ShapeDtypeStruct(cross.shape, BF16),
            jax.ShapeDtypeStruct((keys.shape[0], 2 * cross.shape[1]), BF16),
        ],
        name="cross_backward",
        cost_estimate=SMALL_COST,
    )(count, cross, keys, values, grad_ctx)


GELU_SCALE = (2.0 / jnp.pi) ** 0.5
GELU_CUBE = 0.044715


def gelu_both(values):
    square = values * values
    slope = jnp.tanh(GELU_SCALE * (values + GELU_CUBE * (square * values)))
    half_up = 0.5 * (1.0 + slope)
    steep = GELU_SCALE * (1.0 + 3.0 * GELU_CUBE * square)
    return (values * half_up, half_up + 0.5 * values * (1.0 - slope * slope) * steep)


def norm_back_rows(grad_normed, values, gain):
    centered = values - jnp.mean(values, -1, keepdims=True)
    inverse = lax.rsqrt(jnp.mean(centered * centered, -1, keepdims=True) + EPSILON)
    unit_rows = centered * inverse
    grad_unit = grad_normed * gain
    first_mean = jnp.mean(grad_unit, -1, keepdims=True)
    second_mean = jnp.mean(grad_unit * unit_rows, -1, keepdims=True)
    return inverse * (grad_unit - first_mean - unit_rows * second_mean)


def sort_chunks(table, first, count, source, target):
    for piece in range(count):
        at = pl.multiple_of(table[first + piece] * CHUNK, CHUNK)
        target[piece * CHUNK : (piece + 1) * CHUNK, :] = source[pl.ds(at, CHUNK), :]


def mlp_rows_kernel(
    table, m_ref, g_ref, mixed_ref, gain_ref, in_ref, out_ref, block_ref, grad_ref, low_ref,
    total, back, grad_rows
):
    step = pl.program_id(0)

    @pl.when(step == 0)
    def _():
        sort_chunks(table, 0, LINES, g_ref, grad_rows)

    activated, slope = gelu_both(dot_nn(m_ref[...], in_ref[...]))
    term = dot_nn(activated.astype(BF16), out_ref[...])
    grad_pre = (dot_nt(grad_rows[...], out_ref[...]) * slope).astype(BF16)
    back_term = dot_nt(grad_pre, in_ref[...])

    @pl.when(step == 0)
    def _():
        total[...] = mixed_ref[...] + term
        back[...] = back_term

    @pl.when(step > 0)
    def _():
        total[...] += term
        back[...] += back_term

    @pl.when(step == pl.num_programs(0) - 1)
    def _():
        block_ref[...] = total[...].astype(BF16)
        grad_mixed = grad_rows[...].astype(F32) + norm_back_rows(
            back[...], mixed_ref[...], gain_ref[...]
        )
        grad_ref[...] = grad_mixed
        low_ref[...] = grad_mixed.astype(BF16)


def mlp_rows(table, mlp_low, grad_low, mixed, gain, w_in, w_mlp_out):
    rows, width = mlp_low.shape
    hidden_width = w_in.shape[1]
    block = 512
    whole = pl.BlockSpec((rows, width), lambda i, t: (0, 0))
    return pl.pallas_call(
        mlp_rows_kernel,
        grid_spec=pltpu.PrefetchScalarGridSpec(
            num_scalar_prefetch=1,
            grid=(hidden_width // block,),
            in_specs=[
                whole,
                pl.BlockSpec(grad_low.shape, lambda i, t: (0, 0)),
                whole,
                pl.BlockSpec((1, width), lambda i, t: (0, 0)),
                pl.BlockSpec((width, block), lambda i, t: (0, i)),
                pl.BlockSpec((block, width), lambda i, t: (i, 0)),
            ],
            out_specs=[whole, whole, whole],
            scratch_shapes=[
                pltpu.VMEM((rows, width), F32),
                pltpu.VMEM((rows, width), F32),
                pltpu.VMEM((rows, width), BF16),
            ],
        ),
        out_shape=[
            jax.ShapeDtypeStruct((rows, width), BF16),
            jax.ShapeDtypeStruct((rows, width), F32),
            jax.ShapeDtypeStruct((rows, width), BF16),
        ],
        name="mlp_rows",
        cost_estimate=SMALL_COST,
    )(table, mlp_low, grad_low, mixed, gain, w_in, w_mlp_out)


def mlp_team_kernel(table, *refs):
    parts, grad_parts = refs[:TEAM], refs[TEAM : 2 * TEAM]
    in_ref, out_ref, sum_ref, m_all, g_all = refs[2 * TEAM :]
    step = pl.program_id(0)
    block = in_ref.shape[1]
    rows = parts[0].shape[0]

    @pl.when(step == 0)
    def _():
        for member in range(TEAM):
            here = pl.ds(member * rows, rows)
            sort_chunks(table, 1 + member * LINES, LINES, grad_parts[member], g_all.at[here])
            m_all[here, :] = parts[member][...]

    activated, slope = gelu_both(dot_nn(m_all[...], in_ref[...]))
    grad_pre = (dot_nt(g_all[...], out_ref[...]) * slope).astype(BF16)
    part_in = dot_tn(m_all[...], grad_pre).astype(BF16)
    part_out = dot_tn(activated.astype(BF16), g_all[...]).astype(BF16)
    right = step // 2
    cols = pl.ds(pl.multiple_of((step % 2) * block, block), block)
    for line in range(LINES):
        place = jnp.where(right == 0, line, 2 * LINES - 1 - line)
        sum_ref[place, 0:block, cols] = part_in[line * block : (line + 1) * block, :]
    half = part_out.shape[1] // 2
    sum_ref[step, block : 2 * block, :] = part_out[:, :half]
    sum_ref[2 * LINES - 1 - step, block : 2 * block, :] = part_out[:, half:]


def mlp_team(table, parts, grad_parts, w_in, w_mlp_out):
    rows, width = TEAM * parts[0].shape[0], parts[0].shape[1]
    block = w_in.shape[1] // (LINES * TEAM)
    return pl.pallas_call(
        mlp_team_kernel,
        grid_spec=pltpu.PrefetchScalarGridSpec(
            num_scalar_prefetch=1,
            grid=(LINES,),
            in_specs=[pl.BlockSpec(parts[0].shape, lambda i, t: (0, 0))] * (2 * TEAM)
            + [
                pl.BlockSpec((width, block), lambda i, t: (0, i * TEAM + t[0])),
                pl.BlockSpec((block, width), lambda i, t: (i * TEAM + t[0], 0)),
            ],
            out_specs=pl.BlockSpec((2 * LINES, 2 * block, width // 2), lambda i, t: (0, 0, 0)),
            scratch_shapes=[pltpu.VMEM((rows, width), BF16), pltpu.VMEM((rows, width), BF16)],
        ),
        out_shape=jax.ShapeDtypeStruct((2 * LINES, 2 * block, width // 2), BF16),
        name="mlp_team",
        cost_estimate=SMALL_COST,
    )(table, *parts, *grad_parts, w_in, w_mlp_out)


def small_sums_kernel(core, *refs):
    lefts, rights = refs[:TEAM], refs[TEAM : TEAM + 10]
    text_ref, grad_ref, sum_ref, left_all, right_all = refs[TEAM + 10 :]
    step = pl.program_id(0)
    rows, half = lefts[0].shape[1], right_all.shape[2]
    quarter = sum_ref.shape[2]
    block = text_ref.shape[1]
    cols = pl.ds(pl.multiple_of(core[0] * half, half), half)

    @pl.when(step == 0)
    def _():
        for member in range(TEAM):
            here = slice(member * rows, (member + 1) * rows)
            for at in range(3):
                left_all[at, here, :] = lefts[member][at]
            right_all[2, here, :] = rights[6 + member][:, cols]
        for at, first in ((0, 0), (1, 3)):
            right_all[at, 0:rows, :] = rights[first][...]
            right_all[at, rows : 2 * rows, :] = rights[first + 1][...]
            right_all[at, 2 * rows :, :] = rights[first + 2][...]

    mine = pl.ds(pl.multiple_of(step * block, block), block)
    pairs = [(left_all[at, :, mine], right_all[at]) for at in range(3)]
    pairs += [(text_ref[...], grad_ref[at]) for at in range(2)]
    for at, (left, right) in enumerate(pairs):
        part = dot_tn(left, right).astype(BF16)
        sum_ref[step, at * block : (at + 1) * block, :] = part[:, :quarter]
        sum_ref[2 * LINES - 1 - step, at * block : (at + 1) * block, :] = part[:, quarter:]


def small_sums(core, lefts, rights, text_left, text_right):
    rows, half = rights[0].shape
    block, quarter = text_left.shape[1] // LINES, half // 2

    def whole(values):
        return pl.BlockSpec(values.shape, lambda i, t: (0,) * values.ndim)

    return pl.pallas_call(
        small_sums_kernel,
        grid_spec=pltpu.PrefetchScalarGridSpec(
            num_scalar_prefetch=1,
            grid=(LINES,),
            in_specs=[whole(values) for values in (*lefts, *rights)]
            + [
                pl.BlockSpec((text_left.shape[0], block), lambda i, t: (0, i)),
                whole(text_right),
            ],
            out_specs=pl.BlockSpec((2 * LINES, 5 * block, quarter), lambda i, t: (0, 0, 0)),
            scratch_shapes=[
                pltpu.VMEM((3, TEAM * rows, LINES * block), BF16),
                pltpu.VMEM((3, TEAM * rows, half), BF16),
            ],
        ),
        out_shape=jax.ShapeDtypeStruct((2 * LINES, 5 * block, quarter), BF16),
        name="small_sums",
        cost_estimate=SMALL_COST,
    )(core, *lefts, *rights, text_left, text_right)


def qkv_products_kernel(*refs):
    lefts, rights, (sum_ref, left_all, right_all) = refs[:TEAM], refs[TEAM : 2 * TEAM], refs[2 * TEAM :]
    step = pl.program_id(0)
    rows, (block, side) = lefts[0].shape[0], sum_ref.shape[1:]

    @pl.when(step == 0)
    def _():
        for member in range(TEAM):
            left_all[member * rows : (member + 1) * rows, :] = lefts[member][...]
            right_all[member * rows : (member + 1) * rows, :] = rights[member][...]

    left = left_all[:, pl.ds(pl.multiple_of(step * block, block), block)]
    part = dot_tn(left, right_all[...]).astype(BF16)
    sum_ref[step] = part[:, :side]
    sum_ref[2 * LINES - 1 - step] = part[:, side:]


def qkv_products_of(lefts, rights):
    (rows, width), (_, wide) = lefts[0].shape, rights[0].shape
    block, side = width // LINES, wide // 2
    return pl.pallas_call(
        qkv_products_kernel,
        grid=(LINES,),
        in_specs=[pl.BlockSpec((rows, width), lambda i: (0, 0))] * TEAM
        + [pl.BlockSpec((rows, wide), lambda i: (0, 0))] * TEAM,
        out_specs=pl.BlockSpec((2 * LINES, block, side), lambda i: (0, 0, 0)),
        out_shape=jax.ShapeDtypeStruct((2 * LINES, block, side), BF16),
        scratch_shapes=[
            pltpu.VMEM((TEAM * rows, width), BF16),
            pltpu.VMEM((TEAM * rows, wide), BF16),
        ],
        name="qkv_products",
        cost_estimate=SMALL_COST,
    )(*lefts, *rights)


def place_of(place, piece):
    return (place[0] ^ (piece & 1), place[1] ^ (piece >> 1))


def gain_row(total, gain_ref):
    wide = jnp.transpose(jnp.broadcast_to(total, (total.shape[0], 128)))
    return wide[0:1, :] / gain_ref[...]


def mlp_spread_kernel(place, *refs):
    pieces, (gain_in, w_ref), (in_ref, out_ref, gain_ref) = refs[:4], refs[4:6], refs[6:]
    rows, block = in_ref.shape[0], pieces[0].shape[1] // 2
    for piece in range(4):
        right, core = place_of(place, piece)
        for flip in range(2):
            side = place[2] ^ flip
            for low_line in range(2):
                at = (((2 * right + low_line) * 2 + side) * 2 + core) * block
                in_ref[:, pl.ds(pl.multiple_of(at, block), block)] = pieces[piece][
                    flip * rows : (flip + 1) * rows, low_line * block : (low_line + 1) * block
                ].astype(F32)
        tall = out_ref.shape[0] // 2
        out_ref[
            pl.ds(pl.multiple_of(core * tall, tall), tall),
            pl.ds(pl.multiple_of(right * 2 * block, 2 * block), 2 * block),
        ] = pieces[piece][2 * rows :, :].astype(F32)
    total = jnp.sum(in_ref[...] * w_ref[...].astype(F32), -1, keepdims=True)
    gain_ref[...] = gain_row(total, gain_in)


def small_spread_kernel(place, *refs):
    pieces, (gain_in, w_ref), outs, gain_ref = refs[:4], refs[4:6], refs[6:11], refs[11]
    rows, quarter = outs[0].shape[0], pieces[0].shape[1]
    for piece in range(4):
        right, core = place_of(place, piece)
        at = pl.multiple_of((2 * core + right) * quarter, quarter)
        for which in range(5):
            outs[which][:, pl.ds(at, quarter)] = pieces[piece][
                which * rows : (which + 1) * rows, :
            ].astype(F32)
    total = jnp.sum(outs[0][...] * w_ref[...].astype(F32), -1, keepdims=True)
    gain_ref[...] = gain_row(total, gain_in)


def qkv_spread_kernel(place, *refs):
    pieces, gain_in, w_refs, outs, gain_ref = refs[:4], refs[4], refs[5:8], refs[8:11], refs[11]
    rows, part = outs[0].shape[0], outs[0].shape[1] // TEAM
    for far in range(2):
        core = place[1] ^ far
        for flip in range(2):
            side = place[2] ^ flip
            one, two = pieces[2 * far][flip], pieces[2 * far + 1][flip]
            straight = place[0] == 0
            left = jnp.where(straight, one, two).astype(F32)
            right = jnp.where(straight, two, one).astype(F32)
            both = jnp.concatenate([left, right], 1)
            at = pl.multiple_of((2 * side + core) * part, part)
            for which in range(3):
                outs[which][:, pl.ds(at, part)] = both[:, which * part : (which + 1) * part]
    total = jnp.zeros((rows, 1), F32)
    for which in range(3):
        total += jnp.sum(outs[which][...] * w_refs[which][...].astype(F32), -1, keepdims=True)
    gain_ref[...] = gain_row(total, gain_in)


def spread(kernel, place, pieces, gain, weights, shapes, name):
    block = shapes[0][0]

    def whole(shape):
        return pl.BlockSpec(shape, lambda i, p: (0,) * len(shape))

    return pl.pallas_call(
        kernel,
        grid_spec=pltpu.PrefetchScalarGridSpec(
            num_scalar_prefetch=1,
            grid=(1,),
            in_specs=[whole(v.shape) for v in pieces]
            + [pl.BlockSpec((1, block), lambda i, p: (0, p[3]))]
            + [pl.BlockSpec((block, w.shape[1]), lambda i, p: (p[3], 0)) for w in weights],
            out_specs=[whole(shape) for shape in shapes + [(1, block)]],
        ),
        out_shape=[jax.ShapeDtypeStruct(shape, F32) for shape in shapes + [(1, block)]],
        name=name,
        cost_estimate=SMALL_COST,
    )(place, *pieces, gain, *weights)


def text_share_kernel(place, total_ref, key_ref, value_ref, own_ref, far_ref, part_ref):
    half, share = key_ref.shape[1], own_ref.shape[0]
    rows = total_ref[pl.ds(pl.multiple_of(place[2] * 2 * share, 2 * share), 2 * share), :]
    part_ref[...] = dot_nt(rows[:, :half], key_ref[...]) + dot_nt(rows[:, half:], value_ref[...])
    own_ref[...] = part_ref[pl.ds(pl.multiple_of(place[1] * share, share), share), :]
    away = (1 - place[1]) * share
    far_ref[...] = part_ref[pl.ds(pl.multiple_of(away, share), share), :].astype(BF16)


def text_share(place, total, w_key_text, w_value_text):
    prompt_rows, width = total.shape
    share, half = prompt_rows // TEAM, width // 2
    side = pl.BlockSpec((width, half), lambda i, p: (0, p[1]))
    out = pl.BlockSpec((share, width), lambda i, p: (0, 0))
    return pl.pallas_call(
        text_share_kernel,
        grid_spec=pltpu.PrefetchScalarGridSpec(
            num_scalar_prefetch=1,
            grid=(1,),
            in_specs=[pl.BlockSpec((prompt_rows, width), lambda i, p: (0, 0)), side, side],
            out_specs=[out, out],
            scratch_shapes=[pltpu.VMEM((2 * share, width), F32)],
        ),
        out_shape=[
            jax.ShapeDtypeStruct((share, width), F32),
            jax.ShapeDtypeStruct((share, width), BF16),
        ],
        name="text_share",
        cost_estimate=SMALL_COST,
    )(place, total, w_key_text, w_value_text)


def text_choose_kernel(owners, shares_ref, near_ref, far_ref):
    count = near_ref.shape[0]
    for each in range(count):
        near_ref[each] = shares_ref[owners[each]]
        far_ref[each] = shares_ref[owners[count + each]]


def text_choose(owners, shares):
    shape = (owners.shape[0] // 2,) + shares.shape[1:]
    return pl.pallas_call(
        text_choose_kernel,
        in_specs=[pl.BlockSpec(memory_space=pltpu.SMEM)] + in_vmem(1),
        out_specs=in_vmem(2),
        out_shape=[jax.ShapeDtypeStruct(shape, BF16)] * 2,
        name="text_choose",
        cost_estimate=SMALL_COST,
    )(owners, shares)


def text_place_kernel(place, *refs):
    pieces, out_ref = refs[:4], refs[4]
    share = pieces[0].shape[1]
    for piece in range(4):
        at = (2 * (place[2] ^ (piece & 1)) + (place[1] ^ (piece >> 1))) * share
        for each in range(out_ref.shape[0]):
            out_ref[each, pl.ds(pl.multiple_of(at, share), share), :] = pieces[piece][each]


def text_place(place, pieces):
    count, share, width = pieces[0].shape
    return pl.pallas_call(
        text_place_kernel,
        in_specs=[pl.BlockSpec(memory_space=pltpu.SMEM)] + in_vmem(4),
        out_specs=in_vmem(1)[0],
        out_shape=jax.ShapeDtypeStruct((count, TEAM * share, width), BF16),
        name="text_place",
        cost_estimate=SMALL_COST,
    )(place, *pieces)


def input_grad_kernel(turn, *refs):
    parts, (q_ref, k_ref, v_ref) = refs[:TEAM], refs[TEAM : TEAM + 3]
    rows_ref, gain_ref, hidden_ref, block_ref, out_ref, kept, total = refs[TEAM + 3 :]
    step = pl.program_id(0)
    part = q_ref.shape[1]

    @pl.when(step == 0)
    def _():
        for member in range(TEAM):
            kept[member] = parts[member][...]
        total[...] = jnp.zeros_like(total)

    grads = kept[step]
    for at, w_ref in enumerate((q_ref, k_ref, v_ref)):
        total[...] += dot_nt(grads[:, at * part : (at + 1) * part], w_ref[...])

    @pl.when(step == TEAM - 1)
    def _():
        grad = hidden_ref[...] + norm_back_rows(
            total[...], rows_ref[...].astype(F32), gain_ref[...]
        )
        tall = out_ref.shape[2]
        for line in range(LINES):
            here = slice(line * tall, (line + 1) * tall)
            out_ref[line, 0] = grad[here, :].astype(BF16)
            out_ref[line, 1] = block_ref[here, :]


def input_grad(turn, parts, weights, rows_low, gain, grad_hidden, block_out):
    rows, width = rows_low.shape
    wide = parts[0].shape[1]
    part = wide // 3

    def whole(values):
        return pl.BlockSpec(values.shape, lambda i, t: (0,) * values.ndim)

    shape = (LINES, 2, rows // LINES, width)
    return pl.pallas_call(
        input_grad_kernel,
        grid_spec=pltpu.PrefetchScalarGridSpec(
            num_scalar_prefetch=1,
            grid=(TEAM,),
            in_specs=[whole(v) for v in parts]
            + [pl.BlockSpec((width, part), lambda i, t: (0, t[i]))] * 3
            + [whole(v) for v in (rows_low, gain, grad_hidden, block_out)],
            out_specs=pl.BlockSpec(shape, lambda i, t: (0, 0, 0, 0)),
            scratch_shapes=[
                pltpu.VMEM((TEAM, rows, wide), BF16),
                pltpu.VMEM((rows, width), F32),
            ],
        ),
        out_shape=jax.ShapeDtypeStruct(shape, BF16),
        name="input_grad",
        cost_estimate=SMALL_COST,
    )(turn, *parts, *weights, rows_low, gain, grad_hidden, block_out)


def return_place_kernel(place, *refs):
    pieces, outs = refs[:LINES], refs[LINES:]
    tall = pieces[0].shape[1]
    for step in range(LINES):
        which = place[4] ^ step
        at = pl.multiple_of((which >> 1) * tall, tall)
        for each in range(2):
            outs[each][which & 1, pl.ds(at, tall), :] = pieces[step][each]


def return_place(place, pieces):
    _, tall, width = pieces[0].shape
    return pl.pallas_call(
        return_place_kernel,
        in_specs=[pl.BlockSpec(memory_space=pltpu.SMEM)] + in_vmem(LINES),
        out_specs=in_vmem(2),
        out_shape=[jax.ShapeDtypeStruct((2, 2 * tall, width), BF16)] * 2,
        name="return_place",
        cost_estimate=SMALL_COST,
    )(place, *pieces)


def across(values):
    return move(values, lambda z, y, x, c: (z, y, 1 - x, c))


def together(*values):
    return lax.optimization_barrier(values)


def after(values, *others):
    return lax.optimization_barrier((values, others))[0]


def low(values):
    return values.astype(BF16)


def in_order(first, own, other):
    return jnp.where(first == 0, jnp.stack([own, other]), jnp.stack([other, own]))


def on_device(
    image_rows,
    text_rows,
    prompt_len,
    prompt_slot,
    gain_self,
    w_query,
    w_key,
    w_value,
    w_out,
    gain_cross,
    w_query_text,
    w_key_text,
    w_value_text,
    w_out_text,
    gain_mlp,
    w_in,
    w_mlp_out,
    grad_out,
):
    width = image_rows.shape[-1]
    hidden_width = w_in.shape[-1]
    prompt_rows = text_rows.shape[1]
    rows_here = image_rows.shape[1]
    half_rows = rows_here // 2
    part, half = width // TEAM, width // 2
    block = width // (2 * LINES)
    row_index, group_index = lax.axis_index("row"), lax.axis_index("grp")
    z, y, x, c = row_index >> 1, row_index & 1, group_index >> 1, group_index & 1
    mine = 2 * y + c

    def take(values, start, size, dim):
        return lax.dynamic_slice_in_dim(values, start, size, dim, allow_negative_indices=False)

    def pick_row(values, index, dim=0):
        return lax.dynamic_index_in_dim(
            values, index, dim, keepdims=False, allow_negative_indices=False
        )

    def halves(values, side):
        near = jnp.where(side == 0, values[:, :half], values[:, half:])
        return near, jnp.where(side == 0, values[:, half:], values[:, :half])

    def line_columns(values):
        pairs = [values[:, b * block : (b + 1) * block] for b in range(2 * LINES)]
        near = [jnp.where(y == 0, pairs[2 * b], pairs[2 * b + 1]) for b in range(LINES)]
        far = [jnp.where(y == 0, pairs[2 * b + 1], pairs[2 * b]) for b in range(LINES)]
        return jnp.concatenate(near, 1), jnp.concatenate(far, 1)

    def line_stack(arrays):
        sides = [line_columns(values) for values in arrays]
        return jnp.stack([s[0] for s in sides]), jnp.stack([s[1] for s in sides])

    def hand_rows(values):
        pieces = []
        for step in range(LINES):
            which = z ^ step
            piece = lax.dynamic_slice(
                values,
                (which & 1, (which >> 1) * half_rows, 0),
                (1, half_rows, width),
                allow_negative_indices=False,
            )[0]
            pieces.append(move(piece, hand_out(step)))
        return jnp.concatenate(pieces, 0)

    def natural(parts):
        odd, high = c == 1, y == 1
        parts = [parts[0], parts[2], parts[1], parts[3]]
        parts = [jnp.where(odd, parts[m ^ 1], parts[m]) for m in range(TEAM)]
        return jnp.concatenate([jnp.where(high, parts[m ^ 2], parts[m]) for m in range(TEAM)], 1)

    def right_parts(values, side):
        near, far = halves(values, c)
        side_near, side_far = halves(side, c)
        return [near, side_near, to_member(jnp.concatenate([far, side_far], 0), 2)]

    member = np.repeat(np.arange(TEAM), LINES)
    core_of = c ^ (member >> 1)
    line_of = np.tile(np.arange(LINES), TEAM) ^ ((z & 1) | (core_of << 1))
    table = ((line_of * 2 + (y ^ (member & 1))) * 2 + core_of).astype(jnp.int32)
    grad_table = jnp.concatenate([mine[None], line_of]).astype(jnp.int32)
    turn = (mine ^ np.array([0, 2, 1, 3])).astype(jnp.int32)
    place = jnp.stack([x, c, y, row_index, z]).astype(jnp.int32)
    slots = np.arange(prompt_slot.shape[0])
    wanted = text_rows.shape[0] * group_index + np.arange(text_rows.shape[0])
    wanted = jnp.concatenate([wanted, wanted ^ 2])
    owners = jnp.sum(jnp.where(prompt_slot[None, :] == wanted[:, None], slots[None, :], 0), 1)
    owners = ((((owners & 3) ^ z) << 1) | ((owners >> 2) ^ x)).astype(jnp.int32)

    image = 4 * x + z
    slot = pick_row(prompt_slot, image)
    count = take(prompt_len, slot, 1, 0)

    rows_low = hand_rows(image_rows)
    text_all = lax.all_gather(text_rows, "grp", axis=0, tiled=True)
    grad_rows = lax.all_gather(
        after(grad_out, rows_low), AXES, axis=0, axis_index_groups=line_groups()
    )
    inputs = rows_low.astype(F32)
    start = part * mine
    w_qkv = jnp.concatenate([take(w, start, part, 1) for w in (w_query, w_key, w_value)], 1)
    normed_self, _, _ = norm_rows(inputs, gain_self)
    normed_parts = team_gather(low(normed_self))
    qkv_parts = [low(matmul(a, w_qkv)) for a in normed_parts]
    out_parts, log_totals = self_forward(table, qkv_parts)
    got = [out_parts[0]] + [to_member(out_parts[k], k) for k in range(1, TEAM)]
    text_mine = pick_row(text_all, slot)
    text_now = after(text_mine, out_parts[0])
    text_key = low(matmul(text_now, w_key_text))
    text_value = low(matmul(text_now, w_value_text))

    context_low = natural(after(got, text_key, text_value))
    hidden = inputs + matmul(context_low, w_out)
    normed_cross, unit_cross, inverse_cross = norm_rows(hidden, gain_cross)
    cross_normed_low = low(normed_cross)
    cross_low = low(matmul(cross_normed_low, w_query_text))
    cross_context_low = cross_forward(count, cross_low, text_key, text_value)
    grad_rows = pick_row(after(grad_rows, cross_low), z & 1, 1)
    tops, bottoms = grad_rows[:, :half_rows], grad_rows[:, half_rows:]
    grad_far = to_member(jnp.where(c == 0, bottoms, tops), 2)
    grad_low = jnp.where(
        c == z >> 1, jnp.where(c == 0, tops, bottoms), grad_far
    ).reshape(-1, width)
    grad_side, grad_core = to_member(grad_low, 1), to_member(grad_low, 2)
    mixed = hidden + matmul(cross_context_low, w_out_text)
    normed_mlp, _, _ = norm_rows(mixed, gain_mlp)
    mlp_low = low(normed_mlp)
    mlp_side, mlp_core = to_member(mlp_low, 1), to_member(mlp_low, 2)
    left_near, left_far = line_stack(
        after([cross_normed_low, cross_context_low, context_low], mlp_low)
    )
    left_side = to_member(left_far, 1)

    block_out, grad_mixed, grad_mixed_low = mlp_rows(
        grad_table[1:], mlp_low, grad_low, mixed, gain_mlp.reshape(1, width), w_in, w_mlp_out
    )
    mlp_side, mlp_core, grad_side, grad_core = after(
        (mlp_side, mlp_core, grad_side, grad_core), grad_mixed_low
    )
    mlp_parts = [mlp_low, mlp_side, mlp_core, to_member(mlp_side, 2)]
    grad_parts = [grad_low, grad_side, grad_core, to_member(grad_side, 2)]
    mlp_blocks = mlp_team(grad_table, after(mlp_parts, left_far), grad_parts, w_in, w_mlp_out)
    mlp_blocks, left_side = lax.optimization_barrier((mlp_blocks, left_side))
    mlp_sum = ring_sum(mlp_blocks)

    grad_mixed_low = after(grad_mixed_low, mlp_blocks)
    mixed_side = to_member(grad_mixed_low, 1)
    grad_cross_ctx = low(matmul_right_t(grad_mixed_low, w_out_text))
    grad_cross_low, grad_text_kv = cross_backward(
        count, cross_low, text_key, text_value, grad_cross_ctx
    )
    grad_cross_low, grad_text_kv, mixed_side = lax.optimization_barrier(
        (grad_cross_low, grad_text_kv, mixed_side)
    )
    cross_side = to_member(grad_cross_low, 1)
    grad_cross_normed = matmul_right_t(grad_cross_low, w_query_text)
    grad_from_cross, _ = norm_back(grad_cross_normed, unit_cross, inverse_cross, gain_cross)
    grad_hidden = grad_mixed + grad_from_cross
    grad_hidden_low = low(grad_hidden)
    hidden_side, hidden_core = to_member(grad_hidden_low, 1), to_member(grad_hidden_low, 2)
    key_near, key_far = halves(after(grad_text_kv, grad_hidden_low)[:, :width], c)
    value_near, value_far = halves(after(grad_text_kv, grad_hidden_low)[:, width:], c)
    kv_far = to_member(jnp.concatenate([key_far, value_far], 1), 2)
    kv_near = jnp.concatenate([key_near, value_near], 1)
    kv_near = low(kv_near.astype(F32) + kv_far.astype(F32))
    kv_side = to_member(kv_near, 1)
    hidden_side = after(hidden_side, kv_near)
    hidden_parts = [grad_hidden_low, hidden_side, hidden_core, to_member(hidden_side, 2)]
    text_total = low(kv_near.astype(F32) + kv_side.astype(F32))
    text_left = line_columns(text_mine)[0]
    share_own, share_far = text_share(place, text_total, w_key_text, w_value_text)
    split = width // 4
    first, second = mlp_sum[:block], mlp_sum[block:split]
    own, send = jnp.where(y == 0, first, second), jnp.where(y == 0, second, first)
    small_blocks = small_sums(
        c.reshape(1),
        [left_near, left_side, to_member(left_near, 2), to_member(left_side, 2)],
        right_parts(grad_cross_low, cross_side)
        + right_parts(grad_mixed_low, mixed_side)
        + hidden_parts,
        text_left,
        after(jnp.stack([text_total[:, :half], text_total[:, half:]]), share_far, send),
    )
    small_blocks, share_far, other = together(
        small_blocks, to_member(share_far, 2), to_member(send, 1)
    )
    small_sum = ring_sum(small_blocks)

    shares = low(share_own + share_far.astype(F32))[None]
    mlp_pack = jnp.concatenate([own, other, mlp_sum[split:]], 0)
    w_out_mine = take(w_out, start, part, 0)
    grad_context_parts = [
        low(matmul_right_t(v, w_out_mine)) for v in after(hidden_parts, shares, mlp_pack)
    ]
    grad_qkv_parts = self_backward(table, qkv_parts, grad_context_parts, out_parts, log_totals)
    grad_qkv_parts, shares_two, mlp_across = together(
        grad_qkv_parts, across(shares), across(mlp_pack)
    )
    got_grads = [grad_qkv_parts[0]] + [
        to_member(grad_qkv_parts[k], k) for k in range(1, TEAM)
    ]
    shares = jnp.concatenate([shares, shares_two], 0)
    qkv_products = qkv_products_of(normed_parts, after(grad_qkv_parts, shares))
    qkv_products, mlp_core, mlp_far = together(
        qkv_products, to_member(mlp_pack, 2), to_member(mlp_across, 2)
    )
    qkv_sum = ring_sum(qkv_products)
    grad_w_in, grad_w_mlp_out, grad_gain_mlp = spread(
        mlp_spread_kernel,
        place,
        [mlp_pack, mlp_across, mlp_core, mlp_far],
        gain_mlp.reshape(1, width),
        [w_in],
        [(block, hidden_width), (2 * split, width)],
        "mlp_spread",
    )
    grad_w_in, got_grads, shares_two = together(
        grad_w_in, got_grads, move(shares, lambda z, y, x, c: (z ^ 1, y, x, c))
    )
    shares = jnp.concatenate([shares, shares_two], 0)
    back_pieces = input_grad(
        turn,
        after(got_grads, shares, small_sum),
        (w_query, w_key, w_value),
        rows_low,
        gain_self.reshape(1, width),
        grad_hidden,
        block_out,
    )
    back_pieces, shares_two, small_across = together(
        back_pieces, move(shares, lambda z, y, x, c: (z ^ 2, y, x, c)), across(small_sum)
    )
    back = [move(back_pieces[step], hand_back(step)) for step in range(LINES)]
    near, far = text_choose(owners, jnp.concatenate([shares, shares_two], 0))
    grad_text = text_place(
        place, [near, to_member(near, 1), to_member(far, 2), to_member(far, 3)]
    )
    small_all = spread(
        small_spread_kernel,
        place,
        [small_sum, small_across, to_member(small_sum, 2), to_member(small_across, 2)],
        gain_cross.reshape(1, width),
        [w_query_text],
        [(block, width)] * 5,
        "small_spread",
    )
    grad_image, out_block = return_place(place, after(back, grad_text, small_all[0]))
    qkv_half = after(qkv_sum, grad_image).reshape(2, block, -1)
    own, send = (
        jnp.where(y == 0, qkv_half[0], qkv_half[1]),
        jnp.where(y == 0, qkv_half[1], qkv_half[0]),
    )
    qkv_pack = jnp.stack([own, to_member(send, 1)])
    qkv_across = across(qkv_pack)
    grad_w_query, grad_w_key, grad_w_value, grad_gain_self = spread(
        qkv_spread_kernel,
        place,
        [qkv_pack, qkv_across, to_member(qkv_pack, 2), to_member(qkv_across, 2)],
        gain_self.reshape(1, width),
        [w_query, w_key, w_value],
        [(block, width)] * 3,
        "qkv_spread",
    )
    return (
        out_block,
        grad_image,
        grad_text,
        grad_gain_self.reshape(block),
        grad_w_query,
        grad_w_key,
        grad_w_value,
        small_all[2],
        small_all[5].reshape(block),
        small_all[0],
        small_all[3],
        small_all[4],
        small_all[1],
        grad_gain_mlp.reshape(block),
        grad_w_in,
        grad_w_mlp_out,
    )


def solution(mesh):
    placed = (
        P("grp", "row", None),
        P("grp", None, None),
        P(),
        P(),
        P(),
        P(),
        P(),
        P(),
        P(),
        P(),
        P(),
        P(),
        P(),
        P(),
        P(),
        P(),
        P(),
        P("grp", "row", None),
    )
    return jax.shard_map(
        on_device if fits(mesh) else on_device_plain,
        mesh=mesh,
        in_specs=placed,
        out_specs=(
            P("grp", "row", None),
            P("grp", "row", None),
            P("grp", None, None),
            P("row"),
            P("row", None),
            P("row", None),
            P("row", None),
            P("row", None),
            P("row"),
            P("row", None),
            P("row", None),
            P("row", None),
            P("row", None),
            P("row"),
            P("row", None),
            P("row", None),
        ),
        check_vma=False,
    )
```

```python
import functools

import jax
import jax.numpy as jnp
import numpy as np
from jax import lax
from jax.sharding import PartitionSpec as P
from jax.experimental import pallas as pl
from jax.experimental.pallas import tpu as pltpu

HEADS = 16
HEAD_DIM = 64


EPSILON = 1e-05
NEG_LARGE = -1e30
HIGHEST = lax.Precision.HIGHEST


def norm_rows(values, gain):
    center = jnp.mean(values, -1, keepdims=True)
    centered = values - center
    variance = jnp.mean(centered * centered, -1, keepdims=True)
    inverse = lax.rsqrt(variance + EPSILON)
    unit_rows = centered * inverse
    return (unit_rows * gain, unit_rows, inverse)


def norm_back(grad_normed, unit_rows, inverse, gain):
    grad_unit = grad_normed * gain
    first_mean = jnp.mean(grad_unit, -1, keepdims=True)
    second_mean = jnp.mean(grad_unit * unit_rows, -1, keepdims=True)
    grad_input = inverse * (grad_unit - first_mean - unit_rows * second_mean)
    return (grad_input, jnp.sum(grad_normed * unit_rows, 0))


def matmul(left, right):
    return jnp.dot(left, right, preferred_element_type=jnp.float32)


def matmul_left_t(left, right):
    return lax.dot_general(
        left, right, (((0,), (0,)), ((), ())), preferred_element_type=jnp.float32
    )


def matmul_right_t(left, right):
    return lax.dot_general(
        left, right, (((1,), (1,)), ((), ())), preferred_element_type=jnp.float32
    )


def split_heads(values):
    return values.reshape(values.shape[:-1] + (HEADS, HEAD_DIM))


def on_device_plain(
    image_rows,
    text_rows,
    prompt_len,
    prompt_slot,
    gain_self,
    w_query,
    w_key,
    w_value,
    w_out,
    gain_cross,
    w_query_text,
    w_key_text,
    w_value_text,
    w_out_text,
    gain_mlp,
    w_in,
    w_mlp_out,
    grad_out,
):
    images_here, rows_here, width = image_rows.shape
    prompt_rows = text_rows.shape[1]
    row_count = lax.axis_size("row")
    length = rows_here * row_count
    row_index = lax.axis_index("row")
    group_index = lax.axis_index("grp")
    scale_factor = HEAD_DIM ** (-0.5)
    block_size = min(512, length)
    block_count = length // block_size
    flat_rows = images_here * rows_here
    inputs = image_rows.astype(jnp.float32).reshape(flat_rows, width)
    normed_self, unit_self, inverse_self = norm_rows(inputs, gain_self)
    normed_low = normed_self.astype(jnp.bfloat16)
    query_low = (
        matmul(normed_low, w_query).astype(jnp.bfloat16).reshape(images_here, rows_here, width)
    )
    key_low = matmul(normed_low, w_key).astype(jnp.bfloat16).reshape(images_here, rows_here, width)
    value_low = (
        matmul(normed_low, w_value).astype(jnp.bfloat16).reshape(images_here, rows_here, width)
    )
    keys_all, values_all = (
        lax.all_gather(key_low, "row", axis=1, tiled=True),
        lax.all_gather(value_low, "row", axis=1, tiled=True),
    )
    query_heads = split_heads(query_low)
    query_pos = row_index * rows_here + jnp.arange(rows_here, dtype=jnp.int32)
    key_pos = jnp.arange(length, dtype=jnp.int32)
    causal = key_pos[None, :] <= query_pos[:, None]
    contexts = []
    totals = []
    for each_image in range(images_here):
        scores = (
            jnp.einsum(
                "qhd,khd->hqk",
                query_heads[each_image],
                split_heads(keys_all[each_image]),
                preferred_element_type=jnp.float32,
            )
            * scale_factor
        )
        scores = jnp.where(causal[None], scores, NEG_LARGE)
        largest = jnp.max(scores, -1, keepdims=True)
        expos = jnp.exp(scores - largest)
        denominator = jnp.sum(expos, -1, keepdims=True)
        probs_low = (expos / denominator).astype(jnp.bfloat16)
        contexts.append(
            jnp.einsum(
                "hqk,khd->qhd",
                probs_low,
                split_heads(values_all[each_image]),
                preferred_element_type=jnp.float32,
            )
        )
        totals.append((largest + jnp.log(denominator))[..., 0])
    context = jnp.stack(contexts).reshape(flat_rows, width)
    log_totals = jnp.stack(totals)
    context_low = context.astype(jnp.bfloat16)
    hidden = inputs + matmul(context_low, w_out)
    normed_cross, unit_cross, inverse_cross = norm_rows(hidden, gain_cross)
    cross_normed_low = normed_cross.astype(jnp.bfloat16)
    cross_low = (
        matmul(cross_normed_low, w_query_text)
        .astype(jnp.bfloat16)
        .reshape(images_here, rows_here, HEADS, HEAD_DIM)
    )
    text_flat = text_rows.reshape(-1, width)
    text_key = matmul(text_flat, w_key_text).astype(jnp.bfloat16).reshape(text_rows.shape)
    text_value = matmul(text_flat, w_value_text).astype(jnp.bfloat16).reshape(text_rows.shape)
    text_keys, text_values = (
        lax.all_gather(text_key, "grp", axis=0, tiled=True),
        lax.all_gather(text_value, "grp", axis=0, tiled=True),
    )
    image_total = prompt_slot.shape[0]
    slots = lax.dynamic_slice_in_dim(prompt_slot, group_index * images_here, images_here)
    keys_sel = split_heads(jnp.take(text_keys, slots, axis=0))
    values_sel = split_heads(jnp.take(text_values, slots, axis=0))
    lengths_sel = jnp.take(prompt_len, slots)
    text_mask = (jnp.arange(prompt_rows, dtype=jnp.int32)[None, :] < lengths_sel[:, None])[
        :, None, None, :
    ]
    cross_scores = (
        jnp.einsum("iqhd,ikhd->ihqk", cross_low, keys_sel, preferred_element_type=jnp.float32)
        * scale_factor
    )
    cross_probs = jax.nn.softmax(jnp.where(text_mask, cross_scores, NEG_LARGE), axis=-1)
    cross_probs_low = cross_probs.astype(jnp.bfloat16)
    cross_context = jnp.einsum(
        "ihqk,ikhd->iqhd", cross_probs_low, values_sel, preferred_element_type=jnp.float32
    )
    cross_context_low = cross_context.reshape(flat_rows, width).astype(jnp.bfloat16)
    mixed = hidden + matmul(cross_context_low, w_out_text)
    normed_mlp, unit_mlp, inverse_mlp = norm_rows(mixed, gain_mlp)
    mlp_low = normed_mlp.astype(jnp.bfloat16)
    pre_act = matmul(mlp_low, w_in)
    activated, gelu_back = jax.vjp(jax.nn.gelu, pre_act)
    activated_low = activated.astype(jnp.bfloat16)
    block_out = mixed + matmul(activated_low, w_mlp_out)
    out_block = block_out.astype(jnp.bfloat16).reshape(image_rows.shape)
    grad_low = grad_out.reshape(flat_rows, width)
    grad_w_mlp_out = matmul_left_t(activated_low, grad_low)
    grad_activated = matmul_right_t(grad_low, w_mlp_out)
    grad_pre_low = gelu_back(grad_activated)[0].astype(jnp.bfloat16)
    grad_w_in = matmul_left_t(mlp_low, grad_pre_low)
    grad_mlp_normed = matmul_right_t(grad_pre_low, w_in)
    grad_from_mlp, grad_gain_mlp = norm_back(grad_mlp_normed, unit_mlp, inverse_mlp, gain_mlp)
    grad_mixed = grad_low.astype(jnp.float32) + grad_from_mlp
    grad_mixed_low = grad_mixed.astype(jnp.bfloat16)
    grad_w_out_text = matmul_left_t(cross_context_low, grad_mixed_low)
    grad_cross_ctx = split_heads(
        matmul_right_t(grad_mixed_low, w_out_text)
        .astype(jnp.bfloat16)
        .reshape(images_here, rows_here, width)
    )
    grad_cross_probs = jnp.einsum(
        "iqhd,ikhd->ihqk", grad_cross_ctx, values_sel, preferred_element_type=jnp.float32
    )
    grad_values_sel = jnp.einsum(
        "ihqk,iqhd->ikhd", cross_probs_low, grad_cross_ctx, preferred_element_type=jnp.float32
    )
    grad_cross_scores = cross_probs * (
        grad_cross_probs - jnp.sum(cross_probs * grad_cross_probs, -1, keepdims=True)
    )
    grad_scores_low = grad_cross_scores.astype(jnp.bfloat16)
    grad_cross_query = (
        jnp.einsum("ihqk,ikhd->iqhd", grad_scores_low, keys_sel, preferred_element_type=jnp.float32)
        * scale_factor
    )
    grad_cross_query_low = grad_cross_query.astype(jnp.bfloat16).reshape(flat_rows, width)
    grad_keys_sel = (
        jnp.einsum(
            "ihqk,iqhd->ikhd", grad_scores_low, cross_low, preferred_element_type=jnp.float32
        )
        * scale_factor
    )
    grad_w_query_text = matmul_left_t(cross_normed_low, grad_cross_query_low)
    grad_cross_normed = matmul_right_t(grad_cross_query_low, w_query_text)
    grad_from_cross, grad_gain_cross = norm_back(
        grad_cross_normed, unit_cross, inverse_cross, gain_cross
    )
    grad_hidden = grad_mixed + grad_from_cross
    placing = (jnp.arange(image_total, dtype=jnp.int32)[:, None] == slots[None, :]).astype(
        jnp.float32
    )
    joined_text = jnp.concatenate(
        [
            grad_keys_sel.reshape(images_here, prompt_rows, width),
            grad_values_sel.reshape(images_here, prompt_rows, width),
        ],
        -1,
    )
    text_term = jnp.einsum("si,ipd->spd", placing, joined_text, precision=HIGHEST)
    text_grad = lax.psum_scatter(
        text_term.astype(jnp.bfloat16), "grp", scatter_dimension=0, tiled=True
    )
    share_rows = text_flat.shape[0] // row_count
    text_total = (
        lax.psum(text_grad, "row").astype(jnp.float32).reshape(-1, 2 * width).astype(jnp.bfloat16)
    )
    text_share = lax.dynamic_slice_in_dim(text_total, row_index * share_rows, share_rows, 0)
    text_grad_rows = (
        matmul_right_t(text_total[:, :width], w_key_text)
        + matmul_right_t(text_total[:, width:], w_value_text)
    ).astype(jnp.bfloat16)
    text_part = lax.dynamic_slice_in_dim(text_flat, row_index * share_rows, share_rows, 0)
    grad_w_key_text = matmul_left_t(text_part, text_share[:, :width])
    grad_w_value_text = matmul_left_t(text_part, text_share[:, width:])
    grad_text = text_grad_rows.reshape(text_rows.shape)
    grad_hidden_low = grad_hidden.astype(jnp.bfloat16)
    grad_w_out = matmul_left_t(context_low, grad_hidden_low)
    grad_context = (
        matmul_right_t(grad_hidden_low, w_out)
        .astype(jnp.bfloat16)
        .reshape(images_here, rows_here, width)
    )
    grad_context_heads = split_heads(grad_context)
    context_heads = split_heads(context.reshape(images_here, rows_here, width))
    delta = jnp.einsum(
        "iqhd,iqhd->ihq", grad_context_heads.astype(jnp.float32), context_heads, precision=HIGHEST
    )
    zero_query = jnp.zeros((images_here, rows_here, HEADS, HEAD_DIM), jnp.float32)

    def block_terms(block):
        start = block * block_size
        key_heads = split_heads(lax.dynamic_slice_in_dim(keys_all, start, block_size, 1))
        value_heads = split_heads(lax.dynamic_slice_in_dim(values_all, start, block_size, 1))
        block_pos = start + jnp.arange(block_size, dtype=jnp.int32)
        allowed = (block_pos[None, :] <= query_pos[:, None])[None, None]
        scores = (
            jnp.einsum(
                "iqhd,ikhd->ihqk", query_heads, key_heads, preferred_element_type=jnp.float32
            )
            * scale_factor
        )
        probs = jnp.where(allowed, jnp.exp(scores - log_totals[..., None]), 0.0)
        grad_probs = jnp.einsum(
            "iqhd,ikhd->ihqk", grad_context_heads, value_heads, preferred_element_type=jnp.float32
        )
        grad_scores = (probs * (grad_probs - delta[..., None])).astype(jnp.bfloat16)
        return (grad_scores, probs.astype(jnp.bfloat16), key_heads)

    def step_keys(block, carry):
        grad_query, term_buffer = carry
        grad_scores, probs_low, key_heads = block_terms(block)
        grad_query = (
            grad_query
            + jnp.einsum(
                "ihqk,ikhd->iqhd", grad_scores, key_heads, preferred_element_type=jnp.float32
            )
            * scale_factor
        )
        grad_key_part = (
            jnp.einsum(
                "ihqk,iqhd->ikhd", grad_scores, query_heads, preferred_element_type=jnp.float32
            )
            * scale_factor
        )
        grad_value_part = jnp.einsum(
            "ihqk,iqhd->ikhd", probs_low, grad_context_heads, preferred_element_type=jnp.float32
        )
        joined = jnp.concatenate(
            [
                grad_key_part.reshape(images_here, block_size, width),
                grad_value_part.reshape(images_here, block_size, width),
            ],
            -1,
        )
        term_buffer = lax.dynamic_update_slice_in_dim(term_buffer, joined, block * block_size, 1)
        return (grad_query, term_buffer)

    start_buffer = jnp.zeros((images_here, length, 2 * width), jnp.float32)
    grad_query, term_buffer = lax.fori_loop(0, block_count, step_keys, (zero_query, start_buffer))
    grad_kv = lax.psum_scatter(
        term_buffer.astype(jnp.bfloat16), "row", scatter_dimension=1, tiled=True
    ).astype(jnp.float32)
    grad_query_low = grad_query.reshape(flat_rows, width).astype(jnp.bfloat16)
    grad_kv_low = grad_kv.reshape(flat_rows, 2 * width).astype(jnp.bfloat16)
    grad_w_query = matmul_left_t(normed_low, grad_query_low)
    grad_w_key = matmul_left_t(normed_low, grad_kv_low[:, :width])
    grad_w_value = matmul_left_t(normed_low, grad_kv_low[:, width:])
    grad_normed_self = (
        matmul_right_t(grad_query_low, w_query)
        + matmul_right_t(grad_kv_low[:, :width], w_key)
        + matmul_right_t(grad_kv_low[:, width:], w_value)
    )
    grad_from_self, grad_gain_self = norm_back(grad_normed_self, unit_self, inverse_self, gain_self)
    grad_image = (grad_hidden + grad_from_self).astype(jnp.bfloat16).reshape(image_rows.shape)
    shares = (
        lax.psum_scatter(
            grad_gain_self.astype(jnp.bfloat16), "row", scatter_dimension=0, tiled=True
        ).astype(jnp.float32),
        lax.psum_scatter(
            grad_w_query.astype(jnp.bfloat16), "row", scatter_dimension=0, tiled=True
        ).astype(jnp.float32),
        lax.psum_scatter(
            grad_w_key.astype(jnp.bfloat16), "row", scatter_dimension=0, tiled=True
        ).astype(jnp.float32),
        lax.psum_scatter(
            grad_w_value.astype(jnp.bfloat16), "row", scatter_dimension=0, tiled=True
        ).astype(jnp.float32),
        lax.psum_scatter(
            grad_w_out.astype(jnp.bfloat16), "row", scatter_dimension=0, tiled=True
        ).astype(jnp.float32),
        lax.psum_scatter(
            grad_gain_cross.astype(jnp.bfloat16), "row", scatter_dimension=0, tiled=True
        ).astype(jnp.float32),
        lax.psum_scatter(
            grad_w_query_text.astype(jnp.bfloat16), "row", scatter_dimension=0, tiled=True
        ).astype(jnp.float32),
        lax.psum_scatter(
            grad_w_key_text.astype(jnp.bfloat16), "row", scatter_dimension=0, tiled=True
        ).astype(jnp.float32),
        lax.psum_scatter(
            grad_w_value_text.astype(jnp.bfloat16), "row", scatter_dimension=0, tiled=True
        ).astype(jnp.float32),
        lax.psum_scatter(
            grad_w_out_text.astype(jnp.bfloat16), "row", scatter_dimension=0, tiled=True
        ).astype(jnp.float32),
        lax.psum_scatter(
            grad_gain_mlp.astype(jnp.bfloat16), "row", scatter_dimension=0, tiled=True
        ).astype(jnp.float32),
        lax.psum_scatter(
            grad_w_in.astype(jnp.bfloat16), "row", scatter_dimension=0, tiled=True
        ).astype(jnp.float32),
        lax.psum_scatter(
            grad_w_mlp_out.astype(jnp.bfloat16), "row", scatter_dimension=0, tiled=True
        ).astype(jnp.float32),
    )
    summed = (
        lax.psum(shares[0].astype(jnp.bfloat16), "grp").astype(jnp.float32),
        lax.psum(shares[1].astype(jnp.bfloat16), "grp").astype(jnp.float32),
        lax.psum(shares[2].astype(jnp.bfloat16), "grp").astype(jnp.float32),
        lax.psum(shares[3].astype(jnp.bfloat16), "grp").astype(jnp.float32),
        lax.psum(shares[4].astype(jnp.bfloat16), "grp").astype(jnp.float32),
        lax.psum(shares[5].astype(jnp.bfloat16), "grp").astype(jnp.float32),
        lax.psum(shares[6].astype(jnp.bfloat16), "grp").astype(jnp.float32),
        lax.psum(shares[7].astype(jnp.bfloat16), "grp").astype(jnp.float32),
        lax.psum(shares[8].astype(jnp.bfloat16), "grp").astype(jnp.float32),
        lax.psum(shares[9].astype(jnp.bfloat16), "grp").astype(jnp.float32),
        lax.psum(shares[10].astype(jnp.bfloat16), "grp").astype(jnp.float32),
        lax.psum(shares[11].astype(jnp.bfloat16), "grp").astype(jnp.float32),
        lax.psum(shares[12].astype(jnp.bfloat16), "grp").astype(jnp.float32),
    )
    return (
        out_block,
        grad_image,
        grad_text,
        summed[0],
        summed[1],
        summed[2],
        summed[3],
        summed[4],
        summed[5],
        summed[6],
        summed[7],
        summed[8],
        summed[9],
        summed[10],
        summed[11],
        summed[12],
    )


AXES = ("row", "grp")
SMALL_COST = pl.CostEstimate(flops=0, bytes_accessed=0, transcendentals=0)
BF16 = jnp.bfloat16
F32 = jnp.float32
TEAM = 4
LINES = 4


def fits(mesh):
    return mesh.shape["row"] == 2 * LINES and mesh.shape["grp"] == 4


def moves(change):
    pairs = []
    for place in range(32):
        z, y, x, c = place // 8, place // 4 % 2, place // 2 % 2, place % 2
        z2, y2, x2, c2 = change(z, y, x, c)
        pairs.append((place, z2 * 8 + y2 * 4 + x2 * 2 + c2))
    return pairs


def move(values, change):
    return lax.ppermute(values, AXES, moves(change))


def to_member(values, member):
    flip_y, flip_c = member & 1, member >> 1
    return move(values, lambda z, y, x, c: (z, y ^ flip_y, x, c ^ flip_c))


def team_gather(values):
    side = to_member(values, 1)
    return [values, side, to_member(values, 2), to_member(side, 2)]


def hand_out(step):
    def change(z, y, x, c):
        which = z ^ step
        return (2 * c + (which & 1), y, x, which >> 1)

    return change


def hand_back(step):
    def change(z, y, x, c):
        return (step ^ ((z & 1) | (c << 1)), y, x, z >> 1)

    return change


def ring_groups():
    order = [(0, 0), (0, 1), (0, 2), (0, 3), (1, 3), (1, 2), (1, 1), (1, 0)]
    return [
        [z * 8 + y * 4 + x * 2 + c for x, z in order] for y in range(2) for c in range(2)
    ]


def line_groups():
    return [[z * 8 + place for z in range(LINES)] for place in range(8)]


def ring_sum(blocks):
    flat = blocks.reshape(-1, blocks.shape[-1])
    return lax.psum_scatter(
        flat, AXES, scatter_dimension=0, axis_index_groups=ring_groups(), tiled=True
    )


def lane_mask(rows, head):
    lane = lax.broadcasted_iota(jnp.int32, (rows, 128), 1)
    return (lane >= HEAD_DIM) if head else (lane < HEAD_DIM)


def only(values, head):
    return jnp.where(lane_mask(values.shape[0], head), values, jnp.zeros_like(values))


def dot_nt(left, right):
    return lax.dot_general(
        left, right, (((1,), (1,)), ((), ())), preferred_element_type=F32
    )


def dot_nn(left, right):
    return lax.dot_general(
        left, right, (((1,), (0,)), ((), ())), preferred_element_type=F32
    )


def dot_tn(left, right):
    return lax.dot_general(
        left, right, (((0,), (0,)), ((), ())), preferred_element_type=F32
    )


CHUNK = 64


def self_forward_kernel(table, *refs):
    parts, outs, lse_ref = refs[:TEAM], refs[TEAM : 2 * TEAM], refs[2 * TEAM]
    all_qkv, all_out = refs[2 * TEAM + 1 :]
    length, heads_width = all_out.shape
    chunks = parts[0].shape[0] // CHUNK
    for member in range(TEAM):
        for piece in range(chunks):
            at = pl.multiple_of(table[member * chunks + piece] * CHUNK, CHUNK)
            all_qkv[pl.ds(at, CHUNK), :] = parts[member][piece * CHUNK : (piece + 1) * CHUNK, :]
    block = 256
    pairs = heads_width // 128
    scale_factor = HEAD_DIM ** (-0.5)
    diagonal = lax.broadcasted_iota(jnp.int32, (block, block), 1) <= lax.broadcasted_iota(
        jnp.int32, (block, block), 0
    )
    for pair in range(pairs):
        q_cols = slice(128 * pair, 128 * pair + 128)
        k_cols = slice(heads_width + 128 * pair, heads_width + 128 * pair + 128)
        v_cols = slice(2 * heads_width + 128 * pair, 2 * heads_width + 128 * pair + 128)
        for block_at in range(length // block):
            rows = slice(block * block_at, block * (block_at + 1))
            q_block = all_qkv[rows, q_cols]
            joined = jnp.zeros((block, 128), F32)
            for head in range(2):
                q_one = only(q_block, head)
                near = dot_nt(q_one, all_qkv[rows, k_cols]) * scale_factor
                near = jnp.where(diagonal, near, NEG_LARGE)
                scores = near
                if block_at:
                    far = dot_nt(q_one, all_qkv[0 : block * block_at, k_cols]) * scale_factor
                    scores = jnp.concatenate([far, near], 1)
                largest = jnp.max(scores, -1, keepdims=True)
                expos = jnp.exp(scores - largest)
                denominator = jnp.sum(expos, -1, keepdims=True)
                probs_low = (expos / denominator).astype(BF16)
                mixed = dot_nn(probs_low, all_qkv[0 : block * (block_at + 1), v_cols])
                joined = jnp.where(lane_mask(block, head), mixed, joined)
                total = largest + jnp.log(denominator)
                lse_ref[2 * pair + head : 2 * pair + head + 1, rows] = jnp.transpose(
                    jnp.broadcast_to(total, (block, 128))
                )[0:1, :]
            all_out[rows, q_cols] = joined.astype(BF16)
    for member in range(TEAM):
        for piece in range(chunks):
            at = pl.multiple_of(table[member * chunks + piece] * CHUNK, CHUNK)
            outs[member][piece * CHUNK : (piece + 1) * CHUNK, :] = all_out[pl.ds(at, CHUNK), :]


def in_vmem(count):
    return [pl.BlockSpec(memory_space=pltpu.VMEM)] * count


def self_forward(table, parts):
    rows, width = parts[0].shape
    heads_width, length = width // 3, rows * TEAM
    outs = pl.pallas_call(
        self_forward_kernel,
        in_specs=[pl.BlockSpec(memory_space=pltpu.SMEM)] + in_vmem(TEAM),
        out_specs=in_vmem(TEAM + 1),
        out_shape=[jax.ShapeDtypeStruct((rows, heads_width), BF16)] * TEAM
        + [jax.ShapeDtypeStruct((8, length), F32)],
        scratch_shapes=[
            pltpu.VMEM((length, width), BF16),
            pltpu.VMEM((length, heads_width), BF16),
        ],
        name="self_forward",
        cost_estimate=SMALL_COST,
    )(table, *parts)
    return outs[:TEAM], outs[TEAM]


def self_backward_kernel(table, *refs):
    parts, hidden, oparts = refs[:TEAM], refs[TEAM : 2 * TEAM], refs[2 * TEAM : 3 * TEAM]
    lse_ref, w_ref = refs[3 * TEAM : 3 * TEAM + 2]
    outs = refs[3 * TEAM + 2 : 4 * TEAM + 2]
    all_qkv, all_do, delta_ref, sum_q, sum_k, sum_v = refs[4 * TEAM + 2 :]
    length, heads_width = all_do.shape
    chunks = parts[0].shape[0] // CHUNK
    head_row = lax.broadcasted_iota(jnp.int32, (8, heads_width), 0)
    head_col = lax.broadcasted_iota(jnp.int32, (8, heads_width), 1) // HEAD_DIM
    pick = (head_row == head_col).astype(F32)
    block = 256
    for member in range(TEAM):
        grad_out = dot_nt(hidden[member][...], w_ref[...]).astype(BF16)
        products = grad_out.astype(F32) * oparts[member][...].astype(F32)
        for piece in range(chunks):
            at = pl.multiple_of(table[member * chunks + piece] * CHUNK, CHUNK)
            here = slice(piece * CHUNK, (piece + 1) * CHUNK)
            all_qkv[pl.ds(at, CHUNK), :] = parts[member][here, :]
            all_do[pl.ds(at, CHUNK), :] = grad_out[here, :]
            sum_q[pl.ds(at, CHUNK), :] = products[here, :]
    for block_at in range(length // block):
        rows = slice(block * block_at, block * (block_at + 1))
        delta_ref[:, rows] = lax.dot_general(
            pick,
            sum_q[rows, :],
            (((1,), (1,)), ((), ())),
            precision=HIGHEST,
            preferred_element_type=F32,
        )
    pairs = heads_width // 128
    scale_factor = HEAD_DIM ** (-0.5)
    diagonal = lax.broadcasted_iota(jnp.int32, (block, block), 0) <= lax.broadcasted_iota(
        jnp.int32, (block, block), 1
    )
    for pair in range(pairs):
        q_cols = slice(128 * pair, 128 * pair + 128)
        k_cols = slice(heads_width + 128 * pair, heads_width + 128 * pair + 128)
        v_cols = slice(2 * heads_width + 128 * pair, 2 * heads_width + 128 * pair + 128)
        for block_at in range(length // block):
            rows = slice(block * block_at, block * (block_at + 1))
            seen = slice(0, block * (block_at + 1))
            q_block = all_qkv[rows, q_cols]
            do_block = all_do[rows, q_cols]
            sum_q_block = jnp.zeros((block, 128), F32)
            for head in range(2):
                q_one, do_one = only(q_block, head), only(do_block, head)
                total = lse_ref[2 * pair + head : 2 * pair + head + 1, rows]
                delta = delta_ref[2 * pair + head : 2 * pair + head + 1, rows]
                scores = dot_nt(all_qkv[seen, k_cols], q_one) * scale_factor
                probs = jnp.exp(scores - total)
                near = jnp.where(diagonal, probs[block * block_at :, :], 0.0)
                if block_at:
                    probs = jnp.concatenate([probs[: block * block_at, :], near], 0)
                else:
                    probs = near
                grad_probs = dot_nt(all_qkv[seen, v_cols], do_one)
                grad_scores = (probs * (grad_probs - delta)).astype(BF16)
                term_v = dot_nn(probs.astype(BF16), do_one)
                term_k = dot_nn(grad_scores, q_one) * scale_factor
                if head == 0:
                    term_v_both, term_k_both = term_v, term_k
                else:
                    term_v_both, term_k_both = term_v_both + term_v, term_k_both + term_k
                term_q = dot_tn(grad_scores, all_qkv[seen, k_cols]) * scale_factor
                sum_q_block = jnp.where(lane_mask(block, head), term_q, sum_q_block)
            sum_q[rows, q_cols] = sum_q_block
            if block_at:
                before = slice(0, block * block_at)
                sum_k[before, q_cols] += term_k_both[before, :]
                sum_v[before, q_cols] += term_v_both[before, :]
            sum_k[rows, q_cols] = term_k_both[block * block_at :, :]
            sum_v[rows, q_cols] = term_v_both[block * block_at :, :]
    for member in range(TEAM):
        for piece in range(chunks):
            at = pl.multiple_of(table[member * chunks + piece] * CHUNK, CHUNK)
            here = slice(piece * CHUNK, (piece + 1) * CHUNK)
            outs[member][here, 0:heads_width] = sum_q[pl.ds(at, CHUNK), :].astype(BF16)
            outs[member][here, heads_width : 2 * heads_width] = sum_k[
                pl.ds(at, CHUNK), :
            ].astype(BF16)
            outs[member][here, 2 * heads_width : 3 * heads_width] = sum_v[
                pl.ds(at, CHUNK), :
            ].astype(BF16)


def whole_spec(values):
    return pl.BlockSpec(values.shape, lambda *_: (0,) * len(values.shape))


def self_backward(table, parts, hidden, oparts, lse, w_out):
    rows, width = parts[0].shape
    heads_width, length = width // 3, rows * TEAM
    last = TEAM * LINES
    out = jax.ShapeDtypeStruct((rows, width), BF16)
    return pl.pallas_call(
        self_backward_kernel,
        grid_spec=pltpu.PrefetchScalarGridSpec(
            num_scalar_prefetch=1,
            grid=(1,),
            in_specs=[whole_spec(v) for v in (*parts, *hidden, *oparts, lse)]
            + [pl.BlockSpec((heads_width, w_out.shape[1]), lambda i, t: (t[last], 0))],
            out_specs=[whole_spec(out)] * TEAM,
            scratch_shapes=[
                pltpu.VMEM((length, width), BF16),
                pltpu.VMEM((length, heads_width), BF16),
                pltpu.VMEM((8, length), F32),
                pltpu.VMEM((length, heads_width), F32),
                pltpu.VMEM((length, heads_width), F32),
                pltpu.VMEM((length, heads_width), F32),
            ],
        ),
        out_shape=[out] * TEAM,
        name="self_backward",
        cost_estimate=SMALL_COST,
    )(table, *parts, *hidden, *oparts, lse, w_out)


def cross_probs_of(query_one, key_pair, allowed):
    scores = dot_nt(query_one, key_pair) * HEAD_DIM ** (-0.5)
    scores = jnp.where(allowed, scores, NEG_LARGE)
    expos = jnp.exp(scores - jnp.max(scores, -1, keepdims=True))
    return expos / jnp.sum(expos, -1, keepdims=True)


def cross_forward_kernel(count, c_ref, k_ref, v_ref, o_ref):
    rows, width = c_ref.shape
    allowed = lax.broadcasted_iota(jnp.int32, (rows, k_ref.shape[0]), 1) < count[0]
    for pair in range(width // 128):
        cols = slice(128 * pair, 128 * pair + 128)
        joined = jnp.zeros((rows, 128), F32)
        for head in range(2):
            probs = cross_probs_of(only(c_ref[:, cols], head), k_ref[:, cols], allowed)
            mixed = dot_nn(probs.astype(BF16), v_ref[:, cols])
            joined = jnp.where(lane_mask(rows, head), mixed, joined)
        o_ref[:, cols] = joined.astype(BF16)


def cross_forward(count, cross, keys, values):
    return pl.pallas_call(
        cross_forward_kernel,
        in_specs=[pl.BlockSpec(memory_space=pltpu.SMEM)] + in_vmem(3),
        out_specs=pl.BlockSpec(memory_space=pltpu.VMEM),
        out_shape=jax.ShapeDtypeStruct(cross.shape, BF16),
        name="cross_forward",
        cost_estimate=SMALL_COST,
    )(count, cross, keys, values)


def cross_backward_kernel(count, c_ref, k_ref, v_ref, do_ref, dc_ref, near_ref, far_ref):
    rows, width = c_ref.shape
    scale_factor = HEAD_DIM ** (-0.5)
    allowed = lax.broadcasted_iota(jnp.int32, (rows, k_ref.shape[0]), 1) < count[0]
    for pair in range(width // 128):
        cols = slice(128 * pair, 128 * pair + 128)
        joined = jnp.zeros((rows, 128), F32)
        sum_k = jnp.zeros((k_ref.shape[0], 128), F32)
        sum_v = jnp.zeros((k_ref.shape[0], 128), F32)
        for head in range(2):
            c_one, do_one = only(c_ref[:, cols], head), only(do_ref[:, cols], head)
            probs = cross_probs_of(c_one, k_ref[:, cols], allowed)
            grad_probs = dot_nt(do_one, v_ref[:, cols])
            inner = jnp.sum(probs * grad_probs, -1, keepdims=True)
            grad_scores = (probs * (grad_probs - inner)).astype(BF16)
            term_c = dot_nn(grad_scores, k_ref[:, cols]) * scale_factor
            joined = jnp.where(lane_mask(rows, head), term_c, joined)
            sum_k += dot_tn(grad_scores, c_one) * scale_factor
            sum_v += dot_tn(probs.astype(BF16), do_one)
        dc_ref[:, cols] = joined.astype(BF16)
        half = width // 2
        side, first = 128 * pair // half, 128 * pair % half

        def keep(ref, sums=(sum_k, sum_v), first=first, half=half):
            ref[:, first : first + 128] = sums[0].astype(BF16)
            ref[:, half + first : half + first + 128] = sums[1].astype(BF16)

        pl.when(count[1] == side)(functools.partial(keep, near_ref))
        pl.when(count[1] != side)(functools.partial(keep, far_ref))


def cross_backward(count, cross, keys, values, grad_ctx):
    side = jax.ShapeDtypeStruct((keys.shape[0], cross.shape[1]), BF16)
    return pl.pallas_call(
        cross_backward_kernel,
        in_specs=[pl.BlockSpec(memory_space=pltpu.SMEM)] + in_vmem(4),
        out_specs=in_vmem(3),
        out_shape=[jax.ShapeDtypeStruct(cross.shape, BF16), side, side],
        name="cross_backward",
        cost_estimate=SMALL_COST,
    )(count, cross, keys, values, grad_ctx)


GELU_SCALE = (2.0 / jnp.pi) ** 0.5
GELU_CUBE = 0.044715


def gelu_both(values):
    square = values * values
    slope = jnp.tanh(GELU_SCALE * (values + GELU_CUBE * (square * values)))
    half_up = 0.5 * (1.0 + slope)
    steep = GELU_SCALE * (1.0 + 3.0 * GELU_CUBE * square)
    return (values * half_up, half_up + 0.5 * values * (1.0 - slope * slope) * steep)


def norm_back_rows(grad_normed, values, gain):
    centered = values - jnp.mean(values, -1, keepdims=True)
    inverse = lax.rsqrt(jnp.mean(centered * centered, -1, keepdims=True) + EPSILON)
    unit_rows = centered * inverse
    grad_unit = grad_normed * gain
    first_mean = jnp.mean(grad_unit, -1, keepdims=True)
    second_mean = jnp.mean(grad_unit * unit_rows, -1, keepdims=True)
    return inverse * (grad_unit - first_mean - unit_rows * second_mean)


def sort_chunks(table, first, count, source, target):
    for piece in range(count):
        at = pl.multiple_of(table[first + piece] * CHUNK, CHUNK)
        target[piece * CHUNK : (piece + 1) * CHUNK, :] = source[pl.ds(at, CHUNK), :]


def mlp_rows_kernel(
    table, m_ref, g_ref, mixed_ref, gain_ref, in_ref, out_ref, block_ref, grad_ref, low_ref,
    total, back, grad_rows
):
    step = pl.program_id(0)

    @pl.when(step == 0)
    def _():
        sort_chunks(table, 0, LINES, g_ref, grad_rows)

    block = in_ref.shape[1]
    acts, grads = [], []
    for first in (0, block // 2):
        here = slice(first, first + block // 2)
        activated, slope = gelu_both(dot_nn(m_ref[...], in_ref[:, here]))
        acts.append(activated.astype(BF16))
        grads.append((dot_nt(grad_rows[...], out_ref[here, :]) * slope).astype(BF16))
    term = dot_nn(jnp.concatenate(acts, 1), out_ref[...])
    back_term = dot_nt(jnp.concatenate(grads, 1), in_ref[...])

    @pl.when(step == 0)
    def _():
        total[...] = mixed_ref[...] + term
        back[...] = back_term

    @pl.when(step > 0)
    def _():
        total[...] += term
        back[...] += back_term

    @pl.when(step == pl.num_programs(0) - 1)
    def _():
        block_ref[...] = total[...].astype(BF16)
        grad_mixed = grad_rows[...].astype(F32) + norm_back_rows(
            back[...], mixed_ref[...], gain_ref[...]
        )
        grad_ref[...] = grad_mixed
        low_ref[...] = grad_mixed.astype(BF16)


def mlp_rows(table, mlp_low, grad_low, mixed, gain, w_in, w_mlp_out):
    rows, width = mlp_low.shape
    hidden_width = w_in.shape[1]
    block = hidden_width // LINES
    whole = pl.BlockSpec((rows, width), lambda i, t: (0, 0))
    return pl.pallas_call(
        mlp_rows_kernel,
        grid_spec=pltpu.PrefetchScalarGridSpec(
            num_scalar_prefetch=1,
            grid=(hidden_width // block,),
            in_specs=[
                whole,
                pl.BlockSpec(grad_low.shape, lambda i, t: (0, 0)),
                whole,
                pl.BlockSpec((1, width), lambda i, t: (0, 0)),
                pl.BlockSpec((width, block), lambda i, t: (0, i)),
                pl.BlockSpec((block, width), lambda i, t: (i, 0)),
            ],
            out_specs=[whole, whole, whole],
            scratch_shapes=[
                pltpu.VMEM((rows, width), F32),
                pltpu.VMEM((rows, width), F32),
                pltpu.VMEM((rows, width), BF16),
            ],
        ),
        out_shape=[
            jax.ShapeDtypeStruct((rows, width), BF16),
            jax.ShapeDtypeStruct((rows, width), F32),
            jax.ShapeDtypeStruct((rows, width), BF16),
        ],
        name="mlp_rows",
        cost_estimate=SMALL_COST,
    )(table, mlp_low, grad_low, mixed, gain, w_in, w_mlp_out)


def mlp_team_kernel(table, *refs):
    parts, grad_parts = refs[:TEAM], refs[TEAM : 2 * TEAM]
    in_ref, out_ref, sum_ref, m_all, g_all = refs[2 * TEAM :]
    step = pl.program_id(0)
    block = in_ref.shape[1]
    rows = parts[0].shape[0]

    @pl.when(step == 0)
    def _():
        for member in range(TEAM):
            here = pl.ds(member * rows, rows)
            sort_chunks(table, 1 + member * LINES, LINES, grad_parts[member], g_all.at[here])
            m_all[here, :] = parts[member][...]

    activated, slope = gelu_both(dot_nn(m_all[...], in_ref[...]))
    grad_pre = (dot_nt(g_all[...], out_ref[...]) * slope).astype(BF16)
    part_in = dot_tn(m_all[...], grad_pre).astype(BF16)
    part_out = dot_tn(activated.astype(BF16), g_all[...]).astype(BF16)
    right = step // 2
    cols = pl.ds(pl.multiple_of((step % 2) * block, block), block)
    for line in range(LINES):
        place = jnp.where(right == 0, line, 2 * LINES - 1 - line)
        sum_ref[place, 0:block, cols] = part_in[line * block : (line + 1) * block, :]
    half = part_out.shape[1] // 2
    sum_ref[step, block : 2 * block, :] = part_out[:, :half]
    sum_ref[2 * LINES - 1 - step, block : 2 * block, :] = part_out[:, half:]


def mlp_team(table, parts, grad_parts, w_in, w_mlp_out):
    rows, width = TEAM * parts[0].shape[0], parts[0].shape[1]
    block = w_in.shape[1] // (LINES * TEAM)
    return pl.pallas_call(
        mlp_team_kernel,
        grid_spec=pltpu.PrefetchScalarGridSpec(
            num_scalar_prefetch=1,
            grid=(LINES,),
            in_specs=[pl.BlockSpec(parts[0].shape, lambda i, t: (0, 0))] * (2 * TEAM)
            + [
                pl.BlockSpec((width, block), lambda i, t: (0, i * TEAM + t[0])),
                pl.BlockSpec((block, width), lambda i, t: (i * TEAM + t[0], 0)),
            ],
            out_specs=pl.BlockSpec((2 * LINES, 2 * block, width // 2), lambda i, t: (0, 0, 0)),
            scratch_shapes=[pltpu.VMEM((rows, width), BF16), pltpu.VMEM((rows, width), BF16)],
        ),
        out_shape=jax.ShapeDtypeStruct((2 * LINES, 2 * block, width // 2), BF16),
        name="mlp_team",
        cost_estimate=SMALL_COST,
    )(table, *parts, *grad_parts, w_in, w_mlp_out)


def small_sums_kernel(core, *refs):
    lefts, rights = refs[:TEAM], refs[TEAM : TEAM + 7]
    text_ref, grad_ref, sum_ref, left_all, right_all = refs[TEAM + 7 :]
    step = pl.program_id(0)
    rows, half = lefts[0].shape[1], right_all.shape[2]
    quarter = sum_ref.shape[2]
    block = text_ref.shape[1]
    cols = pl.ds(pl.multiple_of(core[0] * half, half), half)

    @pl.when(step == 0)
    def _():
        for member in range(TEAM):
            here = slice(member * rows, (member + 1) * rows)
            for at in range(2):
                left_all[at, here, :] = lefts[member][at]
            right_all[1, here, :] = rights[3 + member][:, cols]
        right_all[0, 0:rows, :] = rights[0][:, cols]
        right_all[0, rows : 2 * rows, :] = rights[1][:, cols]
        right_all[0, 2 * rows :, :] = rights[2][...]

    mine = pl.ds(pl.multiple_of(step * block, block), block)
    pairs = [(left_all[at, :, mine], right_all[at]) for at in range(2)]
    pairs += [(text_ref[...], grad_ref[:, at * half : (at + 1) * half]) for at in range(2)]
    for at, (left, right) in enumerate(pairs):
        part = dot_tn(left, right).astype(BF16)
        sum_ref[step, at * block : (at + 1) * block, :] = part[:, :quarter]
        sum_ref[2 * LINES - 1 - step, at * block : (at + 1) * block, :] = part[:, quarter:]


def small_sums(core, lefts, rights, text_left, text_right):
    rows, half = rights[0].shape[0], rights[0].shape[1] // 2
    block, quarter = text_left.shape[1] // LINES, half // 2
    return pl.pallas_call(
        small_sums_kernel,
        grid_spec=pltpu.PrefetchScalarGridSpec(
            num_scalar_prefetch=1,
            grid=(LINES,),
            in_specs=[pl.BlockSpec((2,) + v.shape[1:], lambda i, t: (0, 0, 0)) for v in lefts]
            + [whole_spec(v) for v in rights]
            + [pl.BlockSpec((text_left.shape[0], block), lambda i, t: (0, i))]
            + [whole_spec(text_right)],
            out_specs=pl.BlockSpec((2 * LINES, 4 * block, quarter), lambda i, t: (0, 0, 0)),
            scratch_shapes=[
                pltpu.VMEM((2, TEAM * rows, LINES * block), BF16),
                pltpu.VMEM((2, TEAM * rows, half), BF16),
            ],
        ),
        out_shape=jax.ShapeDtypeStruct((2 * LINES, 4 * block, quarter), BF16),
        name="small_sums",
        cost_estimate=SMALL_COST,
    )(core, *lefts, *rights, text_left, text_right)


def qkv_products_kernel(core, *refs):
    lefts, rights = refs[:TEAM], refs[TEAM : 2 * TEAM]
    cross_lefts, cross_rights = refs[2 * TEAM : 3 * TEAM], refs[3 * TEAM : 3 * TEAM + 3]
    sum_ref, left_all, right_all, cross_left, cross_right = refs[3 * TEAM + 3 :]
    step = pl.program_id(0)
    rows, lanes = lefts[0].shape[0], sum_ref.shape[2]
    block = left_all.shape[1] // LINES

    @pl.when(step == 0)
    def _():
        for member in range(TEAM):
            here = slice(member * rows, (member + 1) * rows)
            left_all[here, :] = lefts[member][...]
            right_all[here, :] = rights[member][...]
            cross_left[here, :] = cross_lefts[member][0]
        half = cross_right.shape[1]
        cols = pl.ds(pl.multiple_of(core[0] * half, half), half)
        cross_right[0:rows, :] = cross_rights[0][:, cols]
        cross_right[rows : 2 * rows, :] = cross_rights[1][:, cols]
        cross_right[2 * rows :, :] = cross_rights[2][...]

    left = left_all[:, pl.ds(pl.multiple_of(step * block, block), block)]
    part = dot_tn(left, right_all[...]).astype(BF16)
    small = cross_left[:, pl.ds(pl.multiple_of(step * lanes, lanes), lanes)]
    cross = dot_tn(small, cross_right[...]).astype(BF16)
    for right, to in enumerate((step, 2 * LINES - 1 - step)):
        for side in range(2):
            for at in range(3):
                first = (3 * side + at) * lanes
                col = (3 * right + at) * lanes
                sum_ref[to, first : first + lanes, :] = part[
                    side * lanes : (side + 1) * lanes, col : col + lanes
                ]
        for at in range(2):
            first, col = (6 + at) * lanes, (2 * right + at) * lanes
            sum_ref[to, first : first + lanes, :] = cross[:, col : col + lanes]


def qkv_products_of(core, lefts, rights, cross_lefts, cross_rights):
    (rows, width), (_, wide) = lefts[0].shape, rights[0].shape
    lanes = width // (2 * LINES)
    half = cross_rights[0].shape[1] // 2
    return pl.pallas_call(
        qkv_products_kernel,
        grid_spec=pltpu.PrefetchScalarGridSpec(
            num_scalar_prefetch=1,
            grid=(LINES,),
            in_specs=[whole_spec(v) for v in (*lefts, *rights)]
            + [pl.BlockSpec((1,) + v.shape[1:], lambda i, t: (2, 0, 0)) for v in cross_lefts]
            + [whole_spec(v) for v in cross_rights],
            out_specs=pl.BlockSpec((2 * LINES, 8 * lanes, lanes), lambda i, t: (0, 0, 0)),
            scratch_shapes=[
                pltpu.VMEM((TEAM * rows, width), BF16),
                pltpu.VMEM((TEAM * rows, wide), BF16),
                pltpu.VMEM((TEAM * rows, LINES * lanes), BF16),
                pltpu.VMEM((TEAM * rows, half), BF16),
            ],
        ),
        out_shape=jax.ShapeDtypeStruct((2 * LINES, 8 * lanes, lanes), BF16),
        name="qkv_products",
        cost_estimate=SMALL_COST,
    )(core, *lefts, *rights, *cross_lefts, *cross_rights)


def place_of(place, piece):
    return (place[0] ^ (piece & 1), place[1] ^ (piece >> 1))


def gain_row(total, gain_ref):
    wide = jnp.transpose(jnp.broadcast_to(total, (total.shape[0], 128)))
    return wide[0:1, :] / gain_ref[...]


def mlp_spread_kernel(place, *refs):
    pieces, (gain_in, w_ref), (in_ref, out_ref, gain_ref) = refs[:4], refs[4:6], refs[6:]
    rows, block = in_ref.shape[0], pieces[0].shape[1] // 2
    for piece in range(4):
        right, core = place_of(place, piece)
        for flip in range(2):
            side = place[2] ^ flip
            for low_line in range(2):
                at = (((2 * right + low_line) * 2 + side) * 2 + core) * block
                in_ref[:, pl.ds(pl.multiple_of(at, block), block)] = pieces[piece][
                    flip * rows : (flip + 1) * rows, low_line * block : (low_line + 1) * block
                ].astype(F32)
        tall = out_ref.shape[0] // 2
        out_ref[
            pl.ds(pl.multiple_of(core * tall, tall), tall),
            pl.ds(pl.multiple_of(right * 2 * block, 2 * block), 2 * block),
        ] = pieces[piece][2 * rows :, :].astype(F32)
    total = jnp.sum(in_ref[...] * w_ref[...].astype(F32), -1, keepdims=True)
    gain_ref[...] = gain_row(total, gain_in)


def small_spread_kernel(place, *refs):
    pieces, outs = refs[:4], refs[4:]
    rows, quarter = outs[0].shape[0], pieces[0].shape[1]
    for piece in range(4):
        right, core = place_of(place, piece)
        at = pl.multiple_of((2 * core + right) * quarter, quarter)
        for which in range(4):
            outs[which][:, pl.ds(at, quarter)] = pieces[piece][
                which * rows : (which + 1) * rows, :
            ].astype(F32)


def qkv_spread_kernel(place, *refs):
    pieces, gains, w_refs, outs, gain_outs = refs[:4], refs[4:6], refs[6:10], refs[10:14], refs[14:]
    rows, part = outs[0].shape[0], outs[0].shape[1] // TEAM
    lanes = pieces[0].shape[1]
    for far in range(2):
        core = place[1] ^ far
        straight = place[0] == 0
        for flip in range(2):
            side = place[2] ^ flip
            tiles = []
            for at in range(3):
                first = (3 * flip + at) * rows
                tiles.append([pieces[2 * far + far_x][first : first + rows, :] for far_x in (0, 1)])
            left = [jnp.where(straight, one, two).astype(F32) for one, two in tiles]
            right = [jnp.where(straight, two, one).astype(F32) for one, two in tiles]
            columns = left + right
            for at in range(6):
                to = (2 * side + core) * part + (at % 2) * lanes
                outs[at // 2][:, pl.ds(pl.multiple_of(to, lanes), lanes)] = columns[at]
        for far_x in range(2):
            for at in range(2):
                to = core * 2 * part + (place[0] ^ far_x) * part + at * lanes
                outs[3][:, pl.ds(pl.multiple_of(to, lanes), lanes)] = pieces[2 * far + far_x][
                    (6 + at) * rows : (7 + at) * rows, :
                ].astype(F32)
    totals = [
        jnp.sum(outs[which][...] * w_refs[which][...].astype(F32), -1, keepdims=True)
        for which in range(4)
    ]
    gain_outs[0][...] = gain_row(totals[0] + totals[1] + totals[2], gains[0])
    gain_outs[1][...] = gain_row(totals[3], gains[1])


def spread(kernel, place, pieces, gains, weights, shapes, name):
    block = shapes[0][0] if not gains else gains[0].shape[1] // (2 * LINES)
    shapes = shapes + [(1, block)] * len(gains)
    return pl.pallas_call(
        kernel,
        grid_spec=pltpu.PrefetchScalarGridSpec(
            num_scalar_prefetch=1,
            grid=(1,),
            in_specs=[whole_spec(v) for v in pieces]
            + [pl.BlockSpec((1, block), lambda i, p: (0, p[3]))] * len(gains)
            + [pl.BlockSpec((block, w.shape[1]), lambda i, p: (p[3], 0)) for w in weights],
            out_specs=[pl.BlockSpec(shape, lambda i, p: (0, 0)) for shape in shapes],
        ),
        out_shape=[jax.ShapeDtypeStruct(shape, F32) for shape in shapes],
        name=name,
        cost_estimate=SMALL_COST,
    )(place, *pieces, *gains, *weights)


def text_share_kernel(place, total_ref, key_ref, value_ref, own_ref, far_ref, part_ref):
    half, share = key_ref.shape[1], own_ref.shape[0]
    rows = total_ref[pl.ds(pl.multiple_of(place[2] * 2 * share, 2 * share), 2 * share), :]
    part_ref[...] = dot_nt(rows[:, :half], key_ref[...]) + dot_nt(rows[:, half:], value_ref[...])
    own_ref[...] = part_ref[pl.ds(pl.multiple_of(place[1] * share, share), share), :]
    away = (1 - place[1]) * share
    far_ref[...] = part_ref[pl.ds(pl.multiple_of(away, share), share), :].astype(BF16)


def text_share(place, total, w_key_text, w_value_text):
    prompt_rows, width = total.shape
    share, half = prompt_rows // TEAM, width // 2
    side = pl.BlockSpec((width, half), lambda i, p: (0, p[1]))
    out = pl.BlockSpec((share, width), lambda i, p: (0, 0))
    return pl.pallas_call(
        text_share_kernel,
        grid_spec=pltpu.PrefetchScalarGridSpec(
            num_scalar_prefetch=1,
            grid=(1,),
            in_specs=[pl.BlockSpec((prompt_rows, width), lambda i, p: (0, 0)), side, side],
            out_specs=[out, out],
            scratch_shapes=[pltpu.VMEM((2 * share, width), F32)],
        ),
        out_shape=[
            jax.ShapeDtypeStruct((share, width), F32),
            jax.ShapeDtypeStruct((share, width), BF16),
        ],
        name="text_share",
        cost_estimate=SMALL_COST,
    )(place, total, w_key_text, w_value_text)


def text_choose_kernel(owners, shares_ref, near_ref, far_ref):
    count = near_ref.shape[0]
    for each in range(count):
        near_ref[each] = shares_ref[owners[each]]
        far_ref[each] = shares_ref[owners[count + each]]


def text_choose(owners, shares):
    shape = (owners.shape[0] // 2,) + shares.shape[1:]
    return pl.pallas_call(
        text_choose_kernel,
        in_specs=[pl.BlockSpec(memory_space=pltpu.SMEM)] + in_vmem(1),
        out_specs=in_vmem(2),
        out_shape=[jax.ShapeDtypeStruct(shape, BF16)] * 2,
        name="text_choose",
        cost_estimate=SMALL_COST,
    )(owners, shares)


def text_place_kernel(place, *refs):
    pieces, out_ref = refs[:4], refs[4]
    share = pieces[0].shape[1]
    for piece in range(4):
        at = (2 * (place[2] ^ (piece & 1)) + (place[1] ^ (piece >> 1))) * share
        for each in range(out_ref.shape[0]):
            out_ref[each, pl.ds(pl.multiple_of(at, share), share), :] = pieces[piece][each]


def text_place(place, pieces):
    count, share, width = pieces[0].shape
    return pl.pallas_call(
        text_place_kernel,
        in_specs=[pl.BlockSpec(memory_space=pltpu.SMEM)] + in_vmem(4),
        out_specs=in_vmem(1)[0],
        out_shape=jax.ShapeDtypeStruct((count, TEAM * share, width), BF16),
        name="text_place",
        cost_estimate=SMALL_COST,
    )(place, *pieces)


def input_grad_kernel(turn, *refs):
    parts, (q_ref, k_ref, v_ref) = refs[:TEAM], refs[TEAM : TEAM + 3]
    rows_ref, gain_ref, hidden_ref, block_ref, out_ref, kept, total = refs[TEAM + 3 :]
    step = pl.program_id(0)
    part = q_ref.shape[1]

    @pl.when(step == 0)
    def _():
        for member in range(TEAM):
            kept[member] = parts[member][...]
        total[...] = jnp.zeros_like(total)

    grads = kept[step]
    for at, w_ref in enumerate((q_ref, k_ref, v_ref)):
        total[...] += dot_nt(grads[:, at * part : (at + 1) * part], w_ref[...])

    @pl.when(step == TEAM - 1)
    def _():
        grad = hidden_ref[...] + norm_back_rows(
            total[...], rows_ref[...].astype(F32), gain_ref[...]
        )
        tall = out_ref.shape[2]
        for line in range(LINES):
            here = slice(line * tall, (line + 1) * tall)
            out_ref[line, 0] = grad[here, :].astype(BF16)
            out_ref[line, 1] = block_ref[here, :]


def input_grad(turn, parts, weights, rows_low, gain, grad_hidden, block_out):
    rows, width = rows_low.shape
    wide = parts[0].shape[1]
    part = wide // 3

    def whole(values):
        return pl.BlockSpec(values.shape, lambda i, t: (0,) * values.ndim)

    shape = (LINES, 2, rows // LINES, width)
    return pl.pallas_call(
        input_grad_kernel,
        grid_spec=pltpu.PrefetchScalarGridSpec(
            num_scalar_prefetch=1,
            grid=(TEAM,),
            in_specs=[whole(v) for v in parts]
            + [pl.BlockSpec((width, part), lambda i, t: (0, t[i]))] * 3
            + [whole(v) for v in (rows_low, gain, grad_hidden, block_out)],
            out_specs=pl.BlockSpec(shape, lambda i, t: (0, 0, 0, 0)),
            scratch_shapes=[
                pltpu.VMEM((TEAM, rows, wide), BF16),
                pltpu.VMEM((rows, width), F32),
            ],
        ),
        out_shape=jax.ShapeDtypeStruct(shape, BF16),
        name="input_grad",
        cost_estimate=SMALL_COST,
    )(turn, *parts, *weights, rows_low, gain, grad_hidden, block_out)


def return_place_kernel(place, *refs):
    pieces, outs = refs[:LINES], refs[LINES:]
    tall = pieces[0].shape[1]
    for step in range(LINES):
        which = place[4] ^ step
        at = pl.multiple_of((which >> 1) * tall, tall)
        for each in range(2):
            outs[each][which & 1, pl.ds(at, tall), :] = pieces[step][each]


def return_place(place, pieces):
    _, tall, width = pieces[0].shape
    return pl.pallas_call(
        return_place_kernel,
        in_specs=[pl.BlockSpec(memory_space=pltpu.SMEM)] + in_vmem(LINES),
        out_specs=in_vmem(2),
        out_shape=[jax.ShapeDtypeStruct((2, 2 * tall, width), BF16)] * 2,
        name="return_place",
        cost_estimate=SMALL_COST,
    )(place, *pieces)


def across(values):
    return move(values, lambda z, y, x, c: (z, y, 1 - x, c))


def together(*values):
    return lax.optimization_barrier(values)


def after(values, *others):
    return lax.optimization_barrier((values, others))[0]


def low(values):
    return values.astype(BF16)


def in_order(first, own, other):
    return jnp.where(first == 0, jnp.stack([own, other]), jnp.stack([other, own]))


def on_device(
    image_rows,
    text_rows,
    prompt_len,
    prompt_slot,
    gain_self,
    w_query,
    w_key,
    w_value,
    w_out,
    gain_cross,
    w_query_text,
    w_key_text,
    w_value_text,
    w_out_text,
    gain_mlp,
    w_in,
    w_mlp_out,
    grad_out,
):
    width = image_rows.shape[-1]
    hidden_width = w_in.shape[-1]
    prompt_rows = text_rows.shape[1]
    rows_here = image_rows.shape[1]
    half_rows = rows_here // 2
    part, half = width // TEAM, width // 2
    block = width // (2 * LINES)
    row_index, group_index = lax.axis_index("row"), lax.axis_index("grp")
    z, y, x, c = row_index >> 1, row_index & 1, group_index >> 1, group_index & 1
    mine = 2 * y + c

    def take(values, start, size, dim):
        return lax.dynamic_slice_in_dim(values, start, size, dim, allow_negative_indices=False)

    def pick_row(values, index, dim=0):
        return lax.dynamic_index_in_dim(
            values, index, dim, keepdims=False, allow_negative_indices=False
        )

    def line_columns(values):
        pairs = [values[:, b * block : (b + 1) * block] for b in range(2 * LINES)]
        near = [jnp.where(y == 0, pairs[2 * b], pairs[2 * b + 1]) for b in range(LINES)]
        far = [jnp.where(y == 0, pairs[2 * b + 1], pairs[2 * b]) for b in range(LINES)]
        return jnp.concatenate(near, 1), jnp.concatenate(far, 1)

    def line_stack(arrays):
        sides = [line_columns(values) for values in arrays]
        return jnp.stack([s[0] for s in sides]), jnp.stack([s[1] for s in sides])

    def hand_rows(values):
        pieces = []
        for step in range(LINES):
            which = z ^ step
            piece = lax.dynamic_slice(
                values,
                (which & 1, (which >> 1) * half_rows, 0),
                (1, half_rows, width),
                allow_negative_indices=False,
            )[0]
            pieces.append(move(piece, hand_out(step)))
        return jnp.concatenate(pieces, 0)

    def natural(parts):
        odd, high = c == 1, y == 1
        parts = [parts[0], parts[2], parts[1], parts[3]]
        parts = [jnp.where(odd, parts[m ^ 1], parts[m]) for m in range(TEAM)]
        return jnp.concatenate([jnp.where(high, parts[m ^ 2], parts[m]) for m in range(TEAM)], 1)

    def right_parts(values, side):
        parts = (values, side)
        away = [jnp.where(c == 0, v[:, half:], v[:, :half]) for v in parts]
        return [values, side, to_member(jnp.concatenate(away, 0), 2)]

    member = np.repeat(np.arange(TEAM), LINES)
    core_of = c ^ (member >> 1)
    line_of = np.tile(np.arange(LINES), TEAM) ^ ((z & 1) | (core_of << 1))
    table = (line_of * 2 + (y ^ (member & 1))) * 2 + core_of
    table = jnp.concatenate([table, mine[None]]).astype(jnp.int32)
    grad_table = jnp.concatenate([mine[None], line_of]).astype(jnp.int32)
    turn = (mine ^ np.array([0, 2, 1, 3])).astype(jnp.int32)
    place = jnp.stack([x, c, y, row_index, z]).astype(jnp.int32)
    slots = np.arange(prompt_slot.shape[0])
    wanted = text_rows.shape[0] * group_index + np.arange(text_rows.shape[0])
    wanted = jnp.concatenate([wanted, wanted ^ 2])
    owners = jnp.sum(jnp.where(prompt_slot[None, :] == wanted[:, None], slots[None, :], 0), 1)
    owners = ((((owners & 3) ^ z) << 1) | ((owners >> 2) ^ x)).astype(jnp.int32)

    image = 4 * x + z
    slot = pick_row(prompt_slot, image)
    count = take(prompt_len, slot, 1, 0)

    start = part * mine
    w_qkv = jnp.concatenate([take(w, start, part, 1) for w in (w_query, w_key, w_value)], 1)
    rows_low, w_qkv, count = together(hand_rows(image_rows), w_qkv, count)
    count_core = jnp.concatenate([count, c[None]])
    inputs = rows_low.astype(F32)
    text_across = across(text_rows)
    wanted_x, wanted_c = slot >> 2, (slot >> 1) & 1
    text_mine = pick_row(jnp.where(wanted_x == x, text_rows, text_across), slot & 1)
    text_mine = jnp.where(wanted_c == c, text_mine, to_member(text_mine, 2))
    grad_rows = lax.all_gather(
        after(grad_out, rows_low), AXES, axis=0, axis_index_groups=line_groups()
    )
    normed_self, _, _ = norm_rows(inputs, gain_self)
    normed_parts = team_gather(low(normed_self))
    qkv_parts = [low(matmul(a, w_qkv)) for a in normed_parts]
    out_parts, log_totals = self_forward(table, qkv_parts)
    got = [out_parts[0]] + [to_member(out_parts[k], k) for k in range(1, TEAM)]
    text_now = after(text_mine, out_parts[0])
    text_key = low(matmul(text_now, w_key_text))
    text_value = low(matmul(text_now, w_value_text))

    context_low = natural(after(got, text_key, text_value))
    hidden = inputs + matmul(context_low, w_out)
    normed_cross, unit_cross, inverse_cross = norm_rows(hidden, gain_cross)
    cross_normed_low = low(normed_cross)
    cross_low = low(matmul(cross_normed_low, w_query_text))
    cross_context_low = cross_forward(count, cross_low, text_key, text_value)
    grad_rows = after(grad_rows, cross_low)
    image_side = z & 1

    def half_image(core):
        return lax.dynamic_slice(
            grad_rows,
            (0, image_side, half_rows * core, 0),
            (LINES, 1, half_rows, width),
            allow_negative_indices=False,
        ).reshape(-1, width)

    grad_far = to_member(half_image(1 - c), 2)
    grad_low = jnp.where(c == z >> 1, half_image(c), grad_far)
    grad_side, grad_core = to_member(grad_low, 1), to_member(grad_low, 2)
    mixed = hidden + matmul(cross_context_low, w_out_text)
    normed_mlp, _, _ = norm_rows(mixed, gain_mlp)
    mlp_low = low(normed_mlp)
    mlp_side, mlp_core = to_member(mlp_low, 1), to_member(mlp_low, 2)
    left_rows = [cross_context_low, context_low, cross_normed_low]
    left_far = line_stack(after(left_rows, mlp_low))[1]
    left_side = to_member(left_far, 1)

    block_out, grad_mixed, grad_mixed_low = mlp_rows(
        grad_table[1:], mlp_low, grad_low, mixed, gain_mlp.reshape(1, width), w_in, w_mlp_out
    )
    mlp_side, mlp_core, grad_side, grad_core = after(
        (mlp_side, mlp_core, grad_side, grad_core), grad_mixed_low
    )
    mlp_parts = [mlp_low, mlp_side, mlp_core, to_member(mlp_side, 2)]
    grad_parts = [grad_low, grad_side, grad_core, to_member(grad_side, 2)]
    mlp_blocks = mlp_team(grad_table, after(mlp_parts, left_far), grad_parts, w_in, w_mlp_out)
    mlp_blocks, left_side = lax.optimization_barrier((mlp_blocks, left_side))
    mlp_sum = ring_sum(mlp_blocks)

    grad_mixed_low = after(grad_mixed_low, mlp_blocks)
    mixed_side = to_member(grad_mixed_low, 1)
    grad_cross_ctx = low(matmul_right_t(grad_mixed_low, w_out_text))
    grad_cross_low, kv_near, kv_far = cross_backward(
        count_core, cross_low, text_key, text_value, grad_cross_ctx
    )
    grad_cross_low, kv_near, kv_far, mixed_side = together(
        grad_cross_low, kv_near, kv_far, mixed_side
    )
    kv_near = low(kv_near.astype(F32) + to_member(kv_far, 2).astype(F32))
    kv_side = to_member(kv_near, 1)
    grad_cross_normed = matmul_right_t(after(grad_cross_low, kv_near), w_query_text)
    grad_from_cross, _ = norm_back(grad_cross_normed, unit_cross, inverse_cross, gain_cross)
    grad_hidden = grad_mixed + grad_from_cross
    grad_hidden_low = low(grad_hidden)
    text_total = low(kv_near.astype(F32) + kv_side.astype(F32))
    hidden_side = to_member(after(grad_hidden_low, text_total), 1)
    hidden_core = to_member(grad_hidden_low, 2)
    left_rows, left_side, mixed_side, text_left = after(
        (left_rows, left_side, mixed_side, text_mine), text_total
    )
    left_near = line_stack(left_rows)[0]
    mixed_parts = right_parts(grad_mixed_low, mixed_side)
    lefts = [left_near, left_side, to_member(left_near, 2), to_member(left_side, 2)]
    text_left = line_columns(text_left)[0]
    share_own, share_far = text_share(
        place, after(text_total, text_left, mixed_parts[1]), w_key_text, w_value_text
    )
    share_own, share_far, hidden_side, lefts = together(share_own, share_far, hidden_side, lefts)
    share_far = to_member(share_far, 2)
    hidden_parts = [grad_hidden_low, hidden_side, hidden_core, to_member(hidden_side, 2)]
    cross_side = to_member(after(grad_cross_low, hidden_side), 1)
    split = width // 4
    first, second = mlp_sum[:block], mlp_sum[block:split]
    own, send = jnp.where(y == 0, first, second), jnp.where(y == 0, second, first)
    small_blocks = small_sums(
        c.reshape(1), lefts, mixed_parts + hidden_parts, text_left, text_total
    )
    small_blocks, share_far = together(small_blocks, share_far)
    small_sum = ring_sum(small_blocks)

    shares = low(share_own + share_far.astype(F32))[None]
    grad_qkv_parts = self_backward(
        table,
        qkv_parts,
        after(hidden_parts, small_blocks, send, shares),
        out_parts,
        log_totals,
        w_out,
    )
    grad_qkv_parts, cross_side, other, shares_two = together(
        grad_qkv_parts, cross_side, to_member(send, 1), across(shares)
    )
    got_grads = [grad_qkv_parts[0]] + [
        to_member(grad_qkv_parts[k], k) for k in range(1, TEAM)
    ]
    mlp_pack = jnp.concatenate([own, other, mlp_sum[split:]], 0)
    cross_parts = right_parts(grad_cross_low, cross_side)
    qkv_products = qkv_products_of(
        c.reshape(1), normed_parts, after(grad_qkv_parts, mlp_pack, shares_two), lefts, cross_parts
    )
    shares = jnp.concatenate([shares, shares_two], 0)
    qkv_products, got_grads, shares_two = together(
        qkv_products, got_grads, move(shares, lambda z, y, x, c: (z ^ 1, y, x, c))
    )
    shares = jnp.concatenate([shares, shares_two], 0)
    qkv_sum = ring_sum(qkv_products)
    back_pieces = input_grad(
        turn,
        after(got_grads, small_sum, shares),
        (w_query, w_key, w_value),
        rows_low,
        gain_self.reshape(1, width),
        grad_hidden,
        block_out,
    )
    back_pieces, small_across, shares_two = together(
        back_pieces, across(small_sum), move(shares, lambda z, y, x, c: (z ^ 2, y, x, c))
    )
    back = [move(back_pieces[step], hand_back(step)) for step in range(LINES)]
    near, far = text_choose(owners, jnp.concatenate([shares, shares_two], 0))
    small_core, small_far, near = together(
        to_member(small_sum, 2), to_member(small_across, 2), near
    )
    small_all = spread(
        small_spread_kernel,
        place,
        [small_sum, small_across, small_core, small_far],
        [],
        [],
        [(block, width)] * 4,
        "small_spread",
    )
    small_all, mlp_across, text_back = together(
        small_all,
        across(mlp_pack),
        [near, to_member(near, 1), to_member(far, 2), to_member(far, 3)],
    )
    grad_text = text_place(place, text_back)
    grad_text, mlp_core, mlp_far = together(
        grad_text, to_member(mlp_pack, 2), to_member(mlp_across, 2)
    )
    grad_w_in, grad_w_mlp_out, grad_gain_mlp = spread(
        mlp_spread_kernel,
        place,
        [mlp_pack, mlp_across, mlp_core, mlp_far],
        [gain_mlp.reshape(1, width)],
        [w_in],
        [(block, hidden_width), (2 * split, width)],
        "mlp_spread",
    )
    grad_w_in, back = together(grad_w_in, back)
    grad_image, out_block = return_place(place, back)
    qkv_done = after(qkv_sum, back)
    own, send = qkv_done[: 3 * block], qkv_done[3 * block : 6 * block]
    own, send = jnp.where(y == 0, own, send), jnp.where(y == 0, send, own)
    qkv_pack = jnp.concatenate([own, to_member(send, 1), qkv_done[6 * block :]], 0)
    qkv_across = across(qkv_pack)
    grad_w_query, grad_w_key, grad_w_value, grad_w_query_text, gain_one, gain_two = spread(
        qkv_spread_kernel,
        place,
        [qkv_pack, qkv_across, to_member(qkv_pack, 2), to_member(qkv_across, 2)],
        [gain_self.reshape(1, width), gain_cross.reshape(1, width)],
        [w_query, w_key, w_value, w_query_text],
        [(block, width)] * 4,
        "qkv_spread",
    )
    return (
        out_block,
        grad_image,
        grad_text,
        gain_one.reshape(block),
        grad_w_query,
        grad_w_key,
        grad_w_value,
        small_all[1],
        gain_two.reshape(block),
        grad_w_query_text,
        small_all[2],
        small_all[3],
        small_all[0],
        grad_gain_mlp.reshape(block),
        grad_w_in,
        grad_w_mlp_out,
    )


def solution(mesh):
    placed = (
        P("grp", "row", None),
        P("grp", None, None),
        P(),
        P(),
        P(),
        P(),
        P(),
        P(),
        P(),
        P(),
        P(),
        P(),
        P(),
        P(),
        P(),
        P(),
        P(),
        P("grp", "row", None),
    )
    return jax.shard_map(
        on_device if fits(mesh) else on_device_plain,
        mesh=mesh,
        in_specs=placed,
        out_specs=(
            P("grp", "row", None),
            P("grp", "row", None),
            P("grp", None, None),
            P("row"),
            P("row", None),
            P("row", None),
            P("row", None),
            P("row", None),
            P("row"),
            P("row", None),
            P("row", None),
            P("row", None),
            P("row", None),
            P("row"),
            P("row", None),
            P("row", None),
        ),
        check_vma=False,
    )
```

```python
import functools

import jax
import jax.numpy as jnp
import numpy as np
from jax import lax
from jax.sharding import PartitionSpec as P
from jax.experimental import pallas as pl
from jax.experimental.pallas import tpu as pltpu

HEADS = 16
HEAD_DIM = 64


EPSILON = 1e-05
NEG_LARGE = -1e30
HIGHEST = lax.Precision.HIGHEST


def norm_rows(values, gain):
    center = jnp.mean(values, -1, keepdims=True)
    centered = values - center
    variance = jnp.mean(centered * centered, -1, keepdims=True)
    inverse = lax.rsqrt(variance + EPSILON)
    unit_rows = centered * inverse
    return (unit_rows * gain, unit_rows, inverse)


def norm_back(grad_normed, unit_rows, inverse, gain):
    grad_unit = grad_normed * gain
    first_mean = jnp.mean(grad_unit, -1, keepdims=True)
    second_mean = jnp.mean(grad_unit * unit_rows, -1, keepdims=True)
    grad_input = inverse * (grad_unit - first_mean - unit_rows * second_mean)
    return (grad_input, jnp.sum(grad_normed * unit_rows, 0))


def matmul(left, right):
    return jnp.dot(left, right, preferred_element_type=jnp.float32)


def matmul_left_t(left, right):
    return lax.dot_general(
        left, right, (((0,), (0,)), ((), ())), preferred_element_type=jnp.float32
    )


def matmul_right_t(left, right):
    return lax.dot_general(
        left, right, (((1,), (1,)), ((), ())), preferred_element_type=jnp.float32
    )


def split_heads(values):
    return values.reshape(values.shape[:-1] + (HEADS, HEAD_DIM))


def on_device_plain(
    image_rows,
    text_rows,
    prompt_len,
    prompt_slot,
    gain_self,
    w_query,
    w_key,
    w_value,
    w_out,
    gain_cross,
    w_query_text,
    w_key_text,
    w_value_text,
    w_out_text,
    gain_mlp,
    w_in,
    w_mlp_out,
    grad_out,
):
    images_here, rows_here, width = image_rows.shape
    prompt_rows = text_rows.shape[1]
    row_count = lax.axis_size("row")
    length = rows_here * row_count
    row_index = lax.axis_index("row")
    group_index = lax.axis_index("grp")
    scale_factor = HEAD_DIM ** (-0.5)
    block_size = min(512, length)
    block_count = length // block_size
    flat_rows = images_here * rows_here
    inputs = image_rows.astype(jnp.float32).reshape(flat_rows, width)
    normed_self, unit_self, inverse_self = norm_rows(inputs, gain_self)
    normed_low = normed_self.astype(jnp.bfloat16)
    query_low = (
        matmul(normed_low, w_query).astype(jnp.bfloat16).reshape(images_here, rows_here, width)
    )
    key_low = matmul(normed_low, w_key).astype(jnp.bfloat16).reshape(images_here, rows_here, width)
    value_low = (
        matmul(normed_low, w_value).astype(jnp.bfloat16).reshape(images_here, rows_here, width)
    )
    keys_all, values_all = (
        lax.all_gather(key_low, "row", axis=1, tiled=True),
        lax.all_gather(value_low, "row", axis=1, tiled=True),
    )
    query_heads = split_heads(query_low)
    query_pos = row_index * rows_here + jnp.arange(rows_here, dtype=jnp.int32)
    key_pos = jnp.arange(length, dtype=jnp.int32)
    causal = key_pos[None, :] <= query_pos[:, None]
    contexts = []
    totals = []
    for each_image in range(images_here):
        scores = (
            jnp.einsum(
                "qhd,khd->hqk",
                query_heads[each_image],
                split_heads(keys_all[each_image]),
                preferred_element_type=jnp.float32,
            )
            * scale_factor
        )
        scores = jnp.where(causal[None], scores, NEG_LARGE)
        largest = jnp.max(scores, -1, keepdims=True)
        expos = jnp.exp(scores - largest)
        denominator = jnp.sum(expos, -1, keepdims=True)
        probs_low = (expos / denominator).astype(jnp.bfloat16)
        contexts.append(
            jnp.einsum(
                "hqk,khd->qhd",
                probs_low,
                split_heads(values_all[each_image]),
                preferred_element_type=jnp.float32,
            )
        )
        totals.append((largest + jnp.log(denominator))[..., 0])
    context = jnp.stack(contexts).reshape(flat_rows, width)
    log_totals = jnp.stack(totals)
    context_low = context.astype(jnp.bfloat16)
    hidden = inputs + matmul(context_low, w_out)
    normed_cross, unit_cross, inverse_cross = norm_rows(hidden, gain_cross)
    cross_normed_low = normed_cross.astype(jnp.bfloat16)
    cross_low = (
        matmul(cross_normed_low, w_query_text)
        .astype(jnp.bfloat16)
        .reshape(images_here, rows_here, HEADS, HEAD_DIM)
    )
    text_flat = text_rows.reshape(-1, width)
    text_key = matmul(text_flat, w_key_text).astype(jnp.bfloat16).reshape(text_rows.shape)
    text_value = matmul(text_flat, w_value_text).astype(jnp.bfloat16).reshape(text_rows.shape)
    text_keys, text_values = (
        lax.all_gather(text_key, "grp", axis=0, tiled=True),
        lax.all_gather(text_value, "grp", axis=0, tiled=True),
    )
    image_total = prompt_slot.shape[0]
    slots = lax.dynamic_slice_in_dim(prompt_slot, group_index * images_here, images_here)
    keys_sel = split_heads(jnp.take(text_keys, slots, axis=0))
    values_sel = split_heads(jnp.take(text_values, slots, axis=0))
    lengths_sel = jnp.take(prompt_len, slots)
    text_mask = (jnp.arange(prompt_rows, dtype=jnp.int32)[None, :] < lengths_sel[:, None])[
        :, None, None, :
    ]
    cross_scores = (
        jnp.einsum("iqhd,ikhd->ihqk", cross_low, keys_sel, preferred_element_type=jnp.float32)
        * scale_factor
    )
    cross_probs = jax.nn.softmax(jnp.where(text_mask, cross_scores, NEG_LARGE), axis=-1)
    cross_probs_low = cross_probs.astype(jnp.bfloat16)
    cross_context = jnp.einsum(
        "ihqk,ikhd->iqhd", cross_probs_low, values_sel, preferred_element_type=jnp.float32
    )
    cross_context_low = cross_context.reshape(flat_rows, width).astype(jnp.bfloat16)
    mixed = hidden + matmul(cross_context_low, w_out_text)
    normed_mlp, unit_mlp, inverse_mlp = norm_rows(mixed, gain_mlp)
    mlp_low = normed_mlp.astype(jnp.bfloat16)
    pre_act = matmul(mlp_low, w_in)
    activated, gelu_back = jax.vjp(jax.nn.gelu, pre_act)
    activated_low = activated.astype(jnp.bfloat16)
    block_out = mixed + matmul(activated_low, w_mlp_out)
    out_block = block_out.astype(jnp.bfloat16).reshape(image_rows.shape)
    grad_low = grad_out.reshape(flat_rows, width)
    grad_w_mlp_out = matmul_left_t(activated_low, grad_low)
    grad_activated = matmul_right_t(grad_low, w_mlp_out)
    grad_pre_low = gelu_back(grad_activated)[0].astype(jnp.bfloat16)
    grad_w_in = matmul_left_t(mlp_low, grad_pre_low)
    grad_mlp_normed = matmul_right_t(grad_pre_low, w_in)
    grad_from_mlp, grad_gain_mlp = norm_back(grad_mlp_normed, unit_mlp, inverse_mlp, gain_mlp)
    grad_mixed = grad_low.astype(jnp.float32) + grad_from_mlp
    grad_mixed_low = grad_mixed.astype(jnp.bfloat16)
    grad_w_out_text = matmul_left_t(cross_context_low, grad_mixed_low)
    grad_cross_ctx = split_heads(
        matmul_right_t(grad_mixed_low, w_out_text)
        .astype(jnp.bfloat16)
        .reshape(images_here, rows_here, width)
    )
    grad_cross_probs = jnp.einsum(
        "iqhd,ikhd->ihqk", grad_cross_ctx, values_sel, preferred_element_type=jnp.float32
    )
    grad_values_sel = jnp.einsum(
        "ihqk,iqhd->ikhd", cross_probs_low, grad_cross_ctx, preferred_element_type=jnp.float32
    )
    grad_cross_scores = cross_probs * (
        grad_cross_probs - jnp.sum(cross_probs * grad_cross_probs, -1, keepdims=True)
    )
    grad_scores_low = grad_cross_scores.astype(jnp.bfloat16)
    grad_cross_query = (
        jnp.einsum("ihqk,ikhd->iqhd", grad_scores_low, keys_sel, preferred_element_type=jnp.float32)
        * scale_factor
    )
    grad_cross_query_low = grad_cross_query.astype(jnp.bfloat16).reshape(flat_rows, width)
    grad_keys_sel = (
        jnp.einsum(
            "ihqk,iqhd->ikhd", grad_scores_low, cross_low, preferred_element_type=jnp.float32
        )
        * scale_factor
    )
    grad_w_query_text = matmul_left_t(cross_normed_low, grad_cross_query_low)
    grad_cross_normed = matmul_right_t(grad_cross_query_low, w_query_text)
    grad_from_cross, grad_gain_cross = norm_back(
        grad_cross_normed, unit_cross, inverse_cross, gain_cross
    )
    grad_hidden = grad_mixed + grad_from_cross
    placing = (jnp.arange(image_total, dtype=jnp.int32)[:, None] == slots[None, :]).astype(
        jnp.float32
    )
    joined_text = jnp.concatenate(
        [
            grad_keys_sel.reshape(images_here, prompt_rows, width),
            grad_values_sel.reshape(images_here, prompt_rows, width),
        ],
        -1,
    )
    text_term = jnp.einsum("si,ipd->spd", placing, joined_text, precision=HIGHEST)
    text_grad = lax.psum_scatter(
        text_term.astype(jnp.bfloat16), "grp", scatter_dimension=0, tiled=True
    )
    share_rows = text_flat.shape[0] // row_count
    text_total = (
        lax.psum(text_grad, "row").astype(jnp.float32).reshape(-1, 2 * width).astype(jnp.bfloat16)
    )
    text_share = lax.dynamic_slice_in_dim(text_total, row_index * share_rows, share_rows, 0)
    text_grad_rows = (
        matmul_right_t(text_total[:, :width], w_key_text)
        + matmul_right_t(text_total[:, width:], w_value_text)
    ).astype(jnp.bfloat16)
    text_part = lax.dynamic_slice_in_dim(text_flat, row_index * share_rows, share_rows, 0)
    grad_w_key_text = matmul_left_t(text_part, text_share[:, :width])
    grad_w_value_text = matmul_left_t(text_part, text_share[:, width:])
    grad_text = text_grad_rows.reshape(text_rows.shape)
    grad_hidden_low = grad_hidden.astype(jnp.bfloat16)
    grad_w_out = matmul_left_t(context_low, grad_hidden_low)
    grad_context = (
        matmul_right_t(grad_hidden_low, w_out)
        .astype(jnp.bfloat16)
        .reshape(images_here, rows_here, width)
    )
    grad_context_heads = split_heads(grad_context)
    context_heads = split_heads(context.reshape(images_here, rows_here, width))
    delta = jnp.einsum(
        "iqhd,iqhd->ihq", grad_context_heads.astype(jnp.float32), context_heads, precision=HIGHEST
    )
    zero_query = jnp.zeros((images_here, rows_here, HEADS, HEAD_DIM), jnp.float32)

    def block_terms(block):
        start = block * block_size
        key_heads = split_heads(lax.dynamic_slice_in_dim(keys_all, start, block_size, 1))
        value_heads = split_heads(lax.dynamic_slice_in_dim(values_all, start, block_size, 1))
        block_pos = start + jnp.arange(block_size, dtype=jnp.int32)
        allowed = (block_pos[None, :] <= query_pos[:, None])[None, None]
        scores = (
            jnp.einsum(
                "iqhd,ikhd->ihqk", query_heads, key_heads, preferred_element_type=jnp.float32
            )
            * scale_factor
        )
        probs = jnp.where(allowed, jnp.exp(scores - log_totals[..., None]), 0.0)
        grad_probs = jnp.einsum(
            "iqhd,ikhd->ihqk", grad_context_heads, value_heads, preferred_element_type=jnp.float32
        )
        grad_scores = (probs * (grad_probs - delta[..., None])).astype(jnp.bfloat16)
        return (grad_scores, probs.astype(jnp.bfloat16), key_heads)

    def step_keys(block, carry):
        grad_query, term_buffer = carry
        grad_scores, probs_low, key_heads = block_terms(block)
        grad_query = (
            grad_query
            + jnp.einsum(
                "ihqk,ikhd->iqhd", grad_scores, key_heads, preferred_element_type=jnp.float32
            )
            * scale_factor
        )
        grad_key_part = (
            jnp.einsum(
                "ihqk,iqhd->ikhd", grad_scores, query_heads, preferred_element_type=jnp.float32
            )
            * scale_factor
        )
        grad_value_part = jnp.einsum(
            "ihqk,iqhd->ikhd", probs_low, grad_context_heads, preferred_element_type=jnp.float32
        )
        joined = jnp.concatenate(
            [
                grad_key_part.reshape(images_here, block_size, width),
                grad_value_part.reshape(images_here, block_size, width),
            ],
            -1,
        )
        term_buffer = lax.dynamic_update_slice_in_dim(term_buffer, joined, block * block_size, 1)
        return (grad_query, term_buffer)

    start_buffer = jnp.zeros((images_here, length, 2 * width), jnp.float32)
    grad_query, term_buffer = lax.fori_loop(0, block_count, step_keys, (zero_query, start_buffer))
    grad_kv = lax.psum_scatter(
        term_buffer.astype(jnp.bfloat16), "row", scatter_dimension=1, tiled=True
    ).astype(jnp.float32)
    grad_query_low = grad_query.reshape(flat_rows, width).astype(jnp.bfloat16)
    grad_kv_low = grad_kv.reshape(flat_rows, 2 * width).astype(jnp.bfloat16)
    grad_w_query = matmul_left_t(normed_low, grad_query_low)
    grad_w_key = matmul_left_t(normed_low, grad_kv_low[:, :width])
    grad_w_value = matmul_left_t(normed_low, grad_kv_low[:, width:])
    grad_normed_self = (
        matmul_right_t(grad_query_low, w_query)
        + matmul_right_t(grad_kv_low[:, :width], w_key)
        + matmul_right_t(grad_kv_low[:, width:], w_value)
    )
    grad_from_self, grad_gain_self = norm_back(grad_normed_self, unit_self, inverse_self, gain_self)
    grad_image = (grad_hidden + grad_from_self).astype(jnp.bfloat16).reshape(image_rows.shape)
    shares = (
        lax.psum_scatter(
            grad_gain_self.astype(jnp.bfloat16), "row", scatter_dimension=0, tiled=True
        ).astype(jnp.float32),
        lax.psum_scatter(
            grad_w_query.astype(jnp.bfloat16), "row", scatter_dimension=0, tiled=True
        ).astype(jnp.float32),
        lax.psum_scatter(
            grad_w_key.astype(jnp.bfloat16), "row", scatter_dimension=0, tiled=True
        ).astype(jnp.float32),
        lax.psum_scatter(
            grad_w_value.astype(jnp.bfloat16), "row", scatter_dimension=0, tiled=True
        ).astype(jnp.float32),
        lax.psum_scatter(
            grad_w_out.astype(jnp.bfloat16), "row", scatter_dimension=0, tiled=True
        ).astype(jnp.float32),
        lax.psum_scatter(
            grad_gain_cross.astype(jnp.bfloat16), "row", scatter_dimension=0, tiled=True
        ).astype(jnp.float32),
        lax.psum_scatter(
            grad_w_query_text.astype(jnp.bfloat16), "row", scatter_dimension=0, tiled=True
        ).astype(jnp.float32),
        lax.psum_scatter(
            grad_w_key_text.astype(jnp.bfloat16), "row", scatter_dimension=0, tiled=True
        ).astype(jnp.float32),
        lax.psum_scatter(
            grad_w_value_text.astype(jnp.bfloat16), "row", scatter_dimension=0, tiled=True
        ).astype(jnp.float32),
        lax.psum_scatter(
            grad_w_out_text.astype(jnp.bfloat16), "row", scatter_dimension=0, tiled=True
        ).astype(jnp.float32),
        lax.psum_scatter(
            grad_gain_mlp.astype(jnp.bfloat16), "row", scatter_dimension=0, tiled=True
        ).astype(jnp.float32),
        lax.psum_scatter(
            grad_w_in.astype(jnp.bfloat16), "row", scatter_dimension=0, tiled=True
        ).astype(jnp.float32),
        lax.psum_scatter(
            grad_w_mlp_out.astype(jnp.bfloat16), "row", scatter_dimension=0, tiled=True
        ).astype(jnp.float32),
    )
    summed = (
        lax.psum(shares[0].astype(jnp.bfloat16), "grp").astype(jnp.float32),
        lax.psum(shares[1].astype(jnp.bfloat16), "grp").astype(jnp.float32),
        lax.psum(shares[2].astype(jnp.bfloat16), "grp").astype(jnp.float32),
        lax.psum(shares[3].astype(jnp.bfloat16), "grp").astype(jnp.float32),
        lax.psum(shares[4].astype(jnp.bfloat16), "grp").astype(jnp.float32),
        lax.psum(shares[5].astype(jnp.bfloat16), "grp").astype(jnp.float32),
        lax.psum(shares[6].astype(jnp.bfloat16), "grp").astype(jnp.float32),
        lax.psum(shares[7].astype(jnp.bfloat16), "grp").astype(jnp.float32),
        lax.psum(shares[8].astype(jnp.bfloat16), "grp").astype(jnp.float32),
        lax.psum(shares[9].astype(jnp.bfloat16), "grp").astype(jnp.float32),
        lax.psum(shares[10].astype(jnp.bfloat16), "grp").astype(jnp.float32),
        lax.psum(shares[11].astype(jnp.bfloat16), "grp").astype(jnp.float32),
        lax.psum(shares[12].astype(jnp.bfloat16), "grp").astype(jnp.float32),
    )
    return (
        out_block,
        grad_image,
        grad_text,
        summed[0],
        summed[1],
        summed[2],
        summed[3],
        summed[4],
        summed[5],
        summed[6],
        summed[7],
        summed[8],
        summed[9],
        summed[10],
        summed[11],
        summed[12],
    )


AXES = ("row", "grp")
SMALL_COST = pl.CostEstimate(flops=0, bytes_accessed=0, transcendentals=0)
BF16 = jnp.bfloat16
F32 = jnp.float32
TEAM = 4
LINES = 4


def fits(mesh):
    return mesh.shape["row"] == 2 * LINES and mesh.shape["grp"] == 4


def moves(change):
    pairs = []
    for place in range(32):
        z, y, x, c = place // 8, place // 4 % 2, place // 2 % 2, place % 2
        z2, y2, x2, c2 = change(z, y, x, c)
        pairs.append((place, z2 * 8 + y2 * 4 + x2 * 2 + c2))
    return pairs


def move(values, change):
    return lax.ppermute(values, AXES, moves(change))


def to_member(values, member):
    flip_y, flip_c = member & 1, member >> 1
    return move(values, lambda z, y, x, c: (z, y ^ flip_y, x, c ^ flip_c))


def team_gather(values):
    side = to_member(values, 1)
    return [values, side, to_member(values, 2), to_member(side, 2)]


def hand_out(step):
    def change(z, y, x, c):
        which = z ^ step
        return (2 * c + (which & 1), y, x, which >> 1)

    return change


def hand_back(step):
    def change(z, y, x, c):
        return (step ^ ((z & 1) | (c << 1)), y, x, z >> 1)

    return change


def ring_groups():
    order = [(0, 0), (0, 1), (0, 2), (0, 3), (1, 3), (1, 2), (1, 1), (1, 0)]
    return [
        [z * 8 + y * 4 + x * 2 + c for x, z in order] for y in range(2) for c in range(2)
    ]


def line_groups():
    return [[z * 8 + place for z in range(LINES)] for place in range(8)]


def ring_sum(blocks):
    flat = blocks.reshape(-1, blocks.shape[-1])
    return lax.psum_scatter(
        flat, AXES, scatter_dimension=0, axis_index_groups=ring_groups(), tiled=True
    )


def lane_mask(rows, head):
    lane = lax.broadcasted_iota(jnp.int32, (rows, 128), 1)
    return (lane >= HEAD_DIM) if head else (lane < HEAD_DIM)


def only(values, head):
    return jnp.where(lane_mask(values.shape[0], head), values, jnp.zeros_like(values))


def dot_nt(left, right):
    return lax.dot_general(
        left, right, (((1,), (1,)), ((), ())), preferred_element_type=F32
    )


def dot_nn(left, right):
    return lax.dot_general(
        left, right, (((1,), (0,)), ((), ())), preferred_element_type=F32
    )


def dot_tn(left, right):
    return lax.dot_general(
        left, right, (((0,), (0,)), ((), ())), preferred_element_type=F32
    )


CHUNK = 64


def self_forward_kernel(table, *refs):
    parts, outs, lse_ref = refs[:TEAM], refs[TEAM : 2 * TEAM], refs[2 * TEAM]
    all_qkv, all_out = refs[2 * TEAM + 1 :]
    length, heads_width = all_out.shape
    chunks = parts[0].shape[0] // CHUNK
    for member in range(TEAM):
        for piece in range(chunks):
            at = pl.multiple_of(table[member * chunks + piece] * CHUNK, CHUNK)
            all_qkv[pl.ds(at, CHUNK), :] = parts[member][piece * CHUNK : (piece + 1) * CHUNK, :]
    block = 256
    pairs = heads_width // 128
    scale_factor = HEAD_DIM ** (-0.5)
    diagonal = lax.broadcasted_iota(jnp.int32, (block, block), 1) <= lax.broadcasted_iota(
        jnp.int32, (block, block), 0
    )
    for pair in range(pairs):
        q_cols = slice(128 * pair, 128 * pair + 128)
        k_cols = slice(heads_width + 128 * pair, heads_width + 128 * pair + 128)
        v_cols = slice(2 * heads_width + 128 * pair, 2 * heads_width + 128 * pair + 128)
        for block_at in range(length // block):
            rows = slice(block * block_at, block * (block_at + 1))
            q_block = all_qkv[rows, q_cols]
            joined = jnp.zeros((block, 128), F32)
            for head in range(2):
                q_one = only(q_block, head)
                near = dot_nt(q_one, all_qkv[rows, k_cols]) * scale_factor
                near = jnp.where(diagonal, near, NEG_LARGE)
                scores = near
                if block_at:
                    far = dot_nt(q_one, all_qkv[0 : block * block_at, k_cols]) * scale_factor
                    scores = jnp.concatenate([far, near], 1)
                largest = jnp.max(scores, -1, keepdims=True)
                expos = jnp.exp(scores - largest)
                denominator = jnp.sum(expos, -1, keepdims=True)
                probs_low = (expos / denominator).astype(BF16)
                mixed = dot_nn(probs_low, all_qkv[0 : block * (block_at + 1), v_cols])
                joined = jnp.where(lane_mask(block, head), mixed, joined)
                total = largest + jnp.log(denominator)
                lse_ref[2 * pair + head : 2 * pair + head + 1, rows] = jnp.transpose(
                    jnp.broadcast_to(total, (block, 128))
                )[0:1, :]
            all_out[rows, q_cols] = joined.astype(BF16)
    for member in range(TEAM):
        for piece in range(chunks):
            at = pl.multiple_of(table[member * chunks + piece] * CHUNK, CHUNK)
            outs[member][piece * CHUNK : (piece + 1) * CHUNK, :] = all_out[pl.ds(at, CHUNK), :]


def in_vmem(count):
    return [pl.BlockSpec(memory_space=pltpu.VMEM)] * count


def self_forward(table, parts):
    rows, width = parts[0].shape
    heads_width, length = width // 3, rows * TEAM
    outs = pl.pallas_call(
        self_forward_kernel,
        in_specs=[pl.BlockSpec(memory_space=pltpu.SMEM)] + in_vmem(TEAM),
        out_specs=in_vmem(TEAM + 1),
        out_shape=[jax.ShapeDtypeStruct((rows, heads_width), BF16)] * TEAM
        + [jax.ShapeDtypeStruct((8, length), F32)],
        scratch_shapes=[
            pltpu.VMEM((length, width), BF16),
            pltpu.VMEM((length, heads_width), BF16),
        ],
        name="self_forward",
        cost_estimate=SMALL_COST,
    )(table, *parts)
    return outs[:TEAM], outs[TEAM]


def self_backward_kernel(table, *refs):
    parts, hidden, oparts = refs[:TEAM], refs[TEAM : 2 * TEAM], refs[2 * TEAM : 3 * TEAM]
    lse_ref, w_ref = refs[3 * TEAM : 3 * TEAM + 2]
    outs = refs[3 * TEAM + 2 : 4 * TEAM + 2]
    all_qkv, all_do, delta_ref, sum_q, sum_k, sum_v = refs[4 * TEAM + 2 :]
    length, heads_width = all_do.shape
    chunks = parts[0].shape[0] // CHUNK
    head_row = lax.broadcasted_iota(jnp.int32, (8, heads_width), 0)
    head_col = lax.broadcasted_iota(jnp.int32, (8, heads_width), 1) // HEAD_DIM
    pick = (head_row == head_col).astype(F32)
    block = 256
    for member in range(TEAM):
        grad_out = dot_nt(hidden[member][...], w_ref[...]).astype(BF16)
        products = grad_out.astype(F32) * oparts[member][...].astype(F32)
        for piece in range(chunks):
            at = pl.multiple_of(table[member * chunks + piece] * CHUNK, CHUNK)
            here = slice(piece * CHUNK, (piece + 1) * CHUNK)
            all_qkv[pl.ds(at, CHUNK), :] = parts[member][here, :]
            all_do[pl.ds(at, CHUNK), :] = grad_out[here, :]
            sum_q[pl.ds(at, CHUNK), :] = products[here, :]
    for block_at in range(length // block):
        rows = slice(block * block_at, block * (block_at + 1))
        delta_ref[:, rows] = lax.dot_general(
            pick,
            sum_q[rows, :],
            (((1,), (1,)), ((), ())),
            precision=HIGHEST,
            preferred_element_type=F32,
        )
    pairs = heads_width // 128
    scale_factor = HEAD_DIM ** (-0.5)
    diagonal = lax.broadcasted_iota(jnp.int32, (block, block), 0) <= lax.broadcasted_iota(
        jnp.int32, (block, block), 1
    )
    for pair in range(pairs):
        q_cols = slice(128 * pair, 128 * pair + 128)
        k_cols = slice(heads_width + 128 * pair, heads_width + 128 * pair + 128)
        v_cols = slice(2 * heads_width + 128 * pair, 2 * heads_width + 128 * pair + 128)
        for block_at in range(length // block):
            rows = slice(block * block_at, block * (block_at + 1))
            seen = slice(0, block * (block_at + 1))
            q_block = all_qkv[rows, q_cols]
            do_block = all_do[rows, q_cols]
            sum_q_block = jnp.zeros((block, 128), F32)
            for head in range(2):
                q_one, do_one = only(q_block, head), only(do_block, head)
                total = lse_ref[2 * pair + head : 2 * pair + head + 1, rows]
                delta = delta_ref[2 * pair + head : 2 * pair + head + 1, rows]
                scores = dot_nt(all_qkv[seen, k_cols], q_one) * scale_factor
                probs = jnp.exp(scores - total)
                near = jnp.where(diagonal, probs[block * block_at :, :], 0.0)
                if block_at:
                    probs = jnp.concatenate([probs[: block * block_at, :], near], 0)
                else:
                    probs = near
                grad_probs = dot_nt(all_qkv[seen, v_cols], do_one)
                grad_scores = (probs * (grad_probs - delta)).astype(BF16)
                term_v = dot_nn(probs.astype(BF16), do_one)
                term_k = dot_nn(grad_scores, q_one) * scale_factor
                if head == 0:
                    term_v_both, term_k_both = term_v, term_k
                else:
                    term_v_both, term_k_both = term_v_both + term_v, term_k_both + term_k
                term_q = dot_tn(grad_scores, all_qkv[seen, k_cols]) * scale_factor
                sum_q_block = jnp.where(lane_mask(block, head), term_q, sum_q_block)
            sum_q[rows, q_cols] = sum_q_block
            if block_at:
                before = slice(0, block * block_at)
                sum_k[before, q_cols] += term_k_both[before, :]
                sum_v[before, q_cols] += term_v_both[before, :]
            sum_k[rows, q_cols] = term_k_both[block * block_at :, :]
            sum_v[rows, q_cols] = term_v_both[block * block_at :, :]
    for member in range(TEAM):
        for piece in range(chunks):
            at = pl.multiple_of(table[member * chunks + piece] * CHUNK, CHUNK)
            here = slice(piece * CHUNK, (piece + 1) * CHUNK)
            outs[member][here, 0:heads_width] = sum_q[pl.ds(at, CHUNK), :].astype(BF16)
            outs[member][here, heads_width : 2 * heads_width] = sum_k[
                pl.ds(at, CHUNK), :
            ].astype(BF16)
            outs[member][here, 2 * heads_width : 3 * heads_width] = sum_v[
                pl.ds(at, CHUNK), :
            ].astype(BF16)


def whole_spec(values):
    return pl.BlockSpec(values.shape, lambda *_: (0,) * len(values.shape))


def self_backward(table, parts, hidden, oparts, lse, w_out):
    rows, width = parts[0].shape
    heads_width, length = width // 3, rows * TEAM
    last = TEAM * LINES
    out = jax.ShapeDtypeStruct((rows, width), BF16)
    return pl.pallas_call(
        self_backward_kernel,
        grid_spec=pltpu.PrefetchScalarGridSpec(
            num_scalar_prefetch=1,
            grid=(1,),
            in_specs=[whole_spec(v) for v in (*parts, *hidden, *oparts, lse)]
            + [pl.BlockSpec((heads_width, w_out.shape[1]), lambda i, t: (t[last], 0))],
            out_specs=[whole_spec(out)] * TEAM,
            scratch_shapes=[
                pltpu.VMEM((length, width), BF16),
                pltpu.VMEM((length, heads_width), BF16),
                pltpu.VMEM((8, length), F32),
                pltpu.VMEM((length, heads_width), F32),
                pltpu.VMEM((length, heads_width), F32),
                pltpu.VMEM((length, heads_width), F32),
            ],
        ),
        out_shape=[out] * TEAM,
        name="self_backward",
        cost_estimate=SMALL_COST,
    )(table, *parts, *hidden, *oparts, lse, w_out)


def cross_probs_of(query_one, key_pair, allowed):
    scores = dot_nt(query_one, key_pair) * HEAD_DIM ** (-0.5)
    scores = jnp.where(allowed, scores, NEG_LARGE)
    expos = jnp.exp(scores - jnp.max(scores, -1, keepdims=True))
    return expos / jnp.sum(expos, -1, keepdims=True)


def cross_forward_kernel(count, c_ref, k_ref, v_ref, o_ref):
    rows, width = c_ref.shape
    allowed = lax.broadcasted_iota(jnp.int32, (rows, k_ref.shape[0]), 1) < count[0]
    for pair in range(width // 128):
        cols = slice(128 * pair, 128 * pair + 128)
        joined = jnp.zeros((rows, 128), F32)
        for head in range(2):
            probs = cross_probs_of(only(c_ref[:, cols], head), k_ref[:, cols], allowed)
            mixed = dot_nn(probs.astype(BF16), v_ref[:, cols])
            joined = jnp.where(lane_mask(rows, head), mixed, joined)
        o_ref[:, cols] = joined.astype(BF16)


def cross_forward(count, cross, keys, values):
    return pl.pallas_call(
        cross_forward_kernel,
        in_specs=[pl.BlockSpec(memory_space=pltpu.SMEM)] + in_vmem(3),
        out_specs=pl.BlockSpec(memory_space=pltpu.VMEM),
        out_shape=jax.ShapeDtypeStruct(cross.shape, BF16),
        name="cross_forward",
        cost_estimate=SMALL_COST,
    )(count, cross, keys, values)


def cross_backward_kernel(count, c_ref, k_ref, v_ref, do_ref, dc_ref, near_ref, far_ref):
    rows, width = c_ref.shape
    half = width // 2
    scale_factor = HEAD_DIM ** (-0.5)
    allowed = lax.broadcasted_iota(jnp.int32, (rows, k_ref.shape[0]), 1) < count[0]

    @pl.loop(0, width // 128)
    def _(step):
        for at in range(1):
            first = (step + at) * 128
            cols = pl.ds(pl.multiple_of(first, 128), 128)
            joined = jnp.zeros((rows, 128), F32)
            sum_k = jnp.zeros((k_ref.shape[0], 128), F32)
            sum_v = jnp.zeros((k_ref.shape[0], 128), F32)
            for head in range(2):
                c_one, do_one = only(c_ref[:, cols], head), only(do_ref[:, cols], head)
                probs = cross_probs_of(c_one, k_ref[:, cols], allowed)
                grad_probs = dot_nt(do_one, v_ref[:, cols])
                inner = jnp.sum(probs * grad_probs, -1, keepdims=True)
                grad_scores = (probs * (grad_probs - inner)).astype(BF16)
                term_c = dot_nn(grad_scores, k_ref[:, cols]) * scale_factor
                joined = jnp.where(lane_mask(rows, head), term_c, joined)
                sum_k += dot_tn(grad_scores, c_one) * scale_factor
                sum_v += dot_tn(probs.astype(BF16), do_one)
            dc_ref[:, cols] = joined.astype(BF16)
            side = (first >= half).astype(jnp.int32)
            within = first - half * side
            key_cols = pl.ds(pl.multiple_of(within, 128), 128)
            value_cols = pl.ds(pl.multiple_of(half + within, 128), 128)

            def keep(ref, sums=(sum_k, sum_v), cols=(key_cols, value_cols)):
                for values, where in zip(sums, cols):
                    ref[:, where] = values.astype(BF16)

            pl.when(count[1] == side)(functools.partial(keep, near_ref))
            pl.when(count[1] != side)(functools.partial(keep, far_ref))


def cross_backward(count, cross, keys, values, grad_ctx):
    side = jax.ShapeDtypeStruct((keys.shape[0], cross.shape[1]), BF16)
    return pl.pallas_call(
        cross_backward_kernel,
        in_specs=[pl.BlockSpec(memory_space=pltpu.SMEM)] + in_vmem(4),
        out_specs=in_vmem(3),
        out_shape=[jax.ShapeDtypeStruct(cross.shape, BF16), side, side],
        name="cross_backward",
        cost_estimate=SMALL_COST,
    )(count, cross, keys, values, grad_ctx)


GELU_SCALE = (2.0 / jnp.pi) ** 0.5
GELU_CUBE = 0.044715


def gelu_both(values):
    square = values * values
    slope = jnp.tanh(GELU_SCALE * (values + GELU_CUBE * (square * values)))
    half_up = 0.5 * (1.0 + slope)
    steep = GELU_SCALE * (1.0 + 3.0 * GELU_CUBE * square)
    return (values * half_up, half_up + 0.5 * values * (1.0 - slope * slope) * steep)


def norm_back_rows(grad_normed, values, gain):
    centered = values - jnp.mean(values, -1, keepdims=True)
    inverse = lax.rsqrt(jnp.mean(centered * centered, -1, keepdims=True) + EPSILON)
    unit_rows = centered * inverse
    grad_unit = grad_normed * gain
    first_mean = jnp.mean(grad_unit, -1, keepdims=True)
    second_mean = jnp.mean(grad_unit * unit_rows, -1, keepdims=True)
    return inverse * (grad_unit - first_mean - unit_rows * second_mean)


def sort_chunks(table, first, count, source, target):
    for piece in range(count):
        at = pl.multiple_of(table[first + piece] * CHUNK, CHUNK)
        target[piece * CHUNK : (piece + 1) * CHUNK, :] = source[pl.ds(at, CHUNK), :]


def mlp_rows_kernel(
    table, m_ref, g_ref, mixed_ref, gain_ref, in_ref, out_ref, *refs
):
    block_refs, (grad_ref, low_ref, total, back, grad_rows) = refs[:LINES], refs[LINES:]
    step = pl.program_id(0)

    @pl.when(step == 0)
    def _():
        sort_chunks(table, 0, LINES, g_ref, grad_rows)

    block = in_ref.shape[1]
    acts, grads = [], []
    for first in (0, block // 2):
        here = slice(first, first + block // 2)
        activated, slope = gelu_both(dot_nn(m_ref[...], in_ref[:, here]))
        acts.append(activated.astype(BF16))
        grads.append((dot_nt(grad_rows[...], out_ref[here, :]) * slope).astype(BF16))
    term = dot_nn(jnp.concatenate(acts, 1), out_ref[...])
    back_term = dot_nt(jnp.concatenate(grads, 1), in_ref[...])

    @pl.when(step == 0)
    def _():
        total[...] = mixed_ref[...] + term
        back[...] = back_term

    @pl.when(step > 0)
    def _():
        total[...] += term
        back[...] += back_term

    @pl.when(step == pl.num_programs(0) - 1)
    def _():
        for line in range(LINES):
            block_refs[line][...] = total[line * CHUNK : (line + 1) * CHUNK, :].astype(BF16)
        grad_mixed = grad_rows[...].astype(F32) + norm_back_rows(
            back[...], mixed_ref[...], gain_ref[...]
        )
        grad_ref[...] = grad_mixed
        low_ref[...] = grad_mixed.astype(BF16)


def mlp_rows(table, mlp_low, grad_low, mixed, gain, w_in, w_mlp_out):
    rows, width = mlp_low.shape
    hidden_width = w_in.shape[1]
    block = hidden_width // LINES
    whole = pl.BlockSpec((rows, width), lambda i, t: (0, 0))
    return pl.pallas_call(
        mlp_rows_kernel,
        grid_spec=pltpu.PrefetchScalarGridSpec(
            num_scalar_prefetch=1,
            grid=(hidden_width // block,),
            in_specs=[
                whole,
                pl.BlockSpec(grad_low.shape, lambda i, t: (0, 0)),
                whole,
                pl.BlockSpec((1, width), lambda i, t: (0, 0)),
                pl.BlockSpec((width, block), lambda i, t: (0, i)),
                pl.BlockSpec((block, width), lambda i, t: (i, 0)),
            ],
            out_specs=[pl.BlockSpec((rows // LINES, width), lambda i, t: (0, 0))] * LINES
            + [whole, whole],
            scratch_shapes=[
                pltpu.VMEM((rows, width), F32),
                pltpu.VMEM((rows, width), F32),
                pltpu.VMEM((rows, width), BF16),
            ],
        ),
        out_shape=[jax.ShapeDtypeStruct((rows // LINES, width), BF16)] * LINES
        + [
            jax.ShapeDtypeStruct((rows, width), F32),
            jax.ShapeDtypeStruct((rows, width), BF16),
        ],
        name="mlp_rows",
        cost_estimate=SMALL_COST,
    )(table, mlp_low, grad_low, mixed, gain, w_in, w_mlp_out)


def mlp_team_kernel(table, *refs):
    parts, grad_parts = refs[:TEAM], refs[TEAM : 2 * TEAM]
    in_ref, out_ref, sum_ref, m_all, g_all = refs[2 * TEAM :]
    step = pl.program_id(0)
    block = in_ref.shape[1]
    rows = parts[0].shape[0]

    @pl.when(step == 0)
    def _():
        for member in range(TEAM):
            here = pl.ds(member * rows, rows)
            sort_chunks(table, 1 + member * LINES, LINES, grad_parts[member], g_all.at[here])
            m_all[here, :] = parts[member][...]

    activated, slope = gelu_both(dot_nn(m_all[...], in_ref[...]))
    grad_pre = (dot_nt(g_all[...], out_ref[...]) * slope).astype(BF16)
    part_in = dot_tn(m_all[...], grad_pre).astype(BF16)
    part_out = dot_tn(activated.astype(BF16), g_all[...]).astype(BF16)
    right = step // 2
    cols = pl.ds(pl.multiple_of((step % 2) * block, block), block)
    for line in range(LINES):
        place = jnp.where(right == 0, line, 2 * LINES - 1 - line)
        sum_ref[place, 0:block, cols] = part_in[line * block : (line + 1) * block, :]
    half = part_out.shape[1] // 2
    sum_ref[step, block : 2 * block, :] = part_out[:, :half]
    sum_ref[2 * LINES - 1 - step, block : 2 * block, :] = part_out[:, half:]


def mlp_team(table, parts, grad_parts, w_in, w_mlp_out):
    rows, width = TEAM * parts[0].shape[0], parts[0].shape[1]
    block = w_in.shape[1] // (LINES * TEAM)
    return pl.pallas_call(
        mlp_team_kernel,
        grid_spec=pltpu.PrefetchScalarGridSpec(
            num_scalar_prefetch=1,
            grid=(LINES,),
            in_specs=[pl.BlockSpec(parts[0].shape, lambda i, t: (0, 0))] * (2 * TEAM)
            + [
                pl.BlockSpec((width, block), lambda i, t: (0, i * TEAM + t[0])),
                pl.BlockSpec((block, width), lambda i, t: (i * TEAM + t[0], 0)),
            ],
            out_specs=pl.BlockSpec((2 * LINES, 2 * block, width // 2), lambda i, t: (0, 0, 0)),
            scratch_shapes=[pltpu.VMEM((rows, width), BF16), pltpu.VMEM((rows, width), BF16)],
        ),
        out_shape=jax.ShapeDtypeStruct((2 * LINES, 2 * block, width // 2), BF16),
        name="mlp_team",
        cost_estimate=SMALL_COST,
    )(table, *parts, *grad_parts, w_in, w_mlp_out)


def small_sums_kernel(core, *refs):
    lefts, rights = refs[:TEAM], refs[TEAM : TEAM + 7]
    text_ref, grad_ref, sum_ref, left_all, right_all = refs[TEAM + 7 :]
    step = pl.program_id(0)
    rows, half = lefts[0].shape[1], right_all.shape[2]
    quarter = sum_ref.shape[2]
    block = text_ref.shape[1]
    cols = pl.ds(pl.multiple_of(core[0] * half, half), half)

    @pl.when(step == 0)
    def _():
        for member in range(TEAM):
            here = slice(member * rows, (member + 1) * rows)
            for at in range(2):
                left_all[at, here, :] = lefts[member][at]
            right_all[1, here, :] = rights[3 + member][:, cols]
        right_all[0, 0:rows, :] = rights[0][:, cols]
        right_all[0, rows : 2 * rows, :] = rights[1][:, cols]
        right_all[0, 2 * rows :, :] = rights[2][...]

    mine = pl.ds(pl.multiple_of(step * block, block), block)
    pairs = [(left_all[at, :, mine], right_all[at]) for at in range(2)]
    pairs += [(text_ref[...], grad_ref[:, at * half : (at + 1) * half]) for at in range(2)]
    for at, (left, right) in enumerate(pairs):
        part = dot_tn(left, right).astype(BF16)
        sum_ref[step, at * block : (at + 1) * block, :] = part[:, :quarter]
        sum_ref[2 * LINES - 1 - step, at * block : (at + 1) * block, :] = part[:, quarter:]


def small_sums(core, lefts, rights, text_left, text_right):
    rows, half = rights[0].shape[0], rights[0].shape[1] // 2
    block, quarter = text_left.shape[1] // LINES, half // 2
    return pl.pallas_call(
        small_sums_kernel,
        grid_spec=pltpu.PrefetchScalarGridSpec(
            num_scalar_prefetch=1,
            grid=(LINES,),
            in_specs=[pl.BlockSpec((2,) + v.shape[1:], lambda i, t: (0, 0, 0)) for v in lefts]
            + [whole_spec(v) for v in rights]
            + [pl.BlockSpec((text_left.shape[0], block), lambda i, t: (0, i))]
            + [whole_spec(text_right)],
            out_specs=pl.BlockSpec((2 * LINES, 4 * block, quarter), lambda i, t: (0, 0, 0)),
            scratch_shapes=[
                pltpu.VMEM((2, TEAM * rows, LINES * block), BF16),
                pltpu.VMEM((2, TEAM * rows, half), BF16),
            ],
        ),
        out_shape=jax.ShapeDtypeStruct((2 * LINES, 4 * block, quarter), BF16),
        name="small_sums",
        cost_estimate=SMALL_COST,
    )(core, *lefts, *rights, text_left, text_right)


def qkv_products_kernel(core, *refs):
    lefts, rights = refs[:TEAM], refs[TEAM : 2 * TEAM]
    cross_lefts, cross_rights = refs[2 * TEAM : 3 * TEAM], refs[3 * TEAM : 3 * TEAM + 3]
    sum_ref, left_all, right_all, cross_left, cross_right = refs[3 * TEAM + 3 :]
    step = pl.program_id(0)
    rows, lanes = lefts[0].shape[0], sum_ref.shape[2]
    block = left_all.shape[1] // LINES

    @pl.when(step == 0)
    def _():
        for member in range(TEAM):
            here = slice(member * rows, (member + 1) * rows)
            left_all[here, :] = lefts[member][...]
            right_all[here, :] = rights[member][...]
            cross_left[here, :] = cross_lefts[member][0]
        half = cross_right.shape[1]
        cols = pl.ds(pl.multiple_of(core[0] * half, half), half)
        cross_right[0:rows, :] = cross_rights[0][:, cols]
        cross_right[rows : 2 * rows, :] = cross_rights[1][:, cols]
        cross_right[2 * rows :, :] = cross_rights[2][...]

    left = left_all[:, pl.ds(pl.multiple_of(step * block, block), block)]
    part = dot_tn(left, right_all[...]).astype(BF16)
    small = cross_left[:, pl.ds(pl.multiple_of(step * lanes, lanes), lanes)]
    cross = dot_tn(small, cross_right[...]).astype(BF16)
    for right, to in enumerate((step, 2 * LINES - 1 - step)):
        for side in range(2):
            for at in range(3):
                first = (3 * side + at) * lanes
                col = (3 * right + at) * lanes
                sum_ref[to, first : first + lanes, :] = part[
                    side * lanes : (side + 1) * lanes, col : col + lanes
                ]
        for at in range(2):
            first, col = (6 + at) * lanes, (2 * right + at) * lanes
            sum_ref[to, first : first + lanes, :] = cross[:, col : col + lanes]


def qkv_products_of(core, lefts, rights, cross_lefts, cross_rights):
    (rows, width), (_, wide) = lefts[0].shape, rights[0].shape
    lanes = width // (2 * LINES)
    half = cross_rights[0].shape[1] // 2
    return pl.pallas_call(
        qkv_products_kernel,
        grid_spec=pltpu.PrefetchScalarGridSpec(
            num_scalar_prefetch=1,
            grid=(LINES,),
            in_specs=[whole_spec(v) for v in (*lefts, *rights)]
            + [pl.BlockSpec((1,) + v.shape[1:], lambda i, t: (2, 0, 0)) for v in cross_lefts]
            + [whole_spec(v) for v in cross_rights],
            out_specs=pl.BlockSpec((2 * LINES, 8 * lanes, lanes), lambda i, t: (0, 0, 0)),
            scratch_shapes=[
                pltpu.VMEM((TEAM * rows, width), BF16),
                pltpu.VMEM((TEAM * rows, wide), BF16),
                pltpu.VMEM((TEAM * rows, LINES * lanes), BF16),
                pltpu.VMEM((TEAM * rows, half), BF16),
            ],
        ),
        out_shape=jax.ShapeDtypeStruct((2 * LINES, 8 * lanes, lanes), BF16),
        name="qkv_products",
        cost_estimate=SMALL_COST,
    )(core, *lefts, *rights, *cross_lefts, *cross_rights)


def place_of(place, piece):
    return (place[0] ^ (piece & 1), place[1] ^ (piece >> 1))


def gain_row(total, gain_ref):
    wide = jnp.transpose(jnp.broadcast_to(total, (total.shape[0], 128)))
    return wide[0:1, :] / gain_ref[...]


def mlp_spread_kernel(place, *refs):
    wholes, (side_ref, core_ref, far_ref), (gain_in, w_ref) = refs[:2], refs[2:5], refs[5:7]
    in_ref, out_ref, gain_ref = refs[7:]
    rows, block = in_ref.shape[0], wholes[0].shape[1] // 2
    tall = out_ref.shape[0] // 2
    mine = pl.ds(pl.multiple_of(place[2] * rows, rows), rows)
    for flip_x in range(2):
        right = place[0] ^ flip_x
        tiles = (
            (0, 0, wholes[flip_x][mine, :]),
            (1, 0, side_ref[flip_x]),
            (0, 1, core_ref[flip_x, :rows, :]),
            (1, 1, far_ref[flip_x]),
        )
        for flip_y, flip_c, tile in tiles:
            for low_line in range(2):
                at = ((2 * right + low_line) * 2 + (place[2] ^ flip_y)) * 2 + (place[1] ^ flip_c)
                in_ref[:, pl.ds(pl.multiple_of(at * block, block), block)] = tile[
                    :, low_line * block : (low_line + 1) * block
                ].astype(F32)
        for flip_c, tile in ((0, wholes[flip_x][2 * rows :, :]), (1, core_ref[flip_x, rows:, :])):
            out_ref[
                pl.ds(pl.multiple_of((place[1] ^ flip_c) * tall, tall), tall),
                pl.ds(pl.multiple_of(right * 2 * block, 2 * block), 2 * block),
            ] = tile.astype(F32)
    total = jnp.sum(in_ref[...] * w_ref[...].astype(F32), -1, keepdims=True)
    gain_ref[...] = gain_row(total, gain_in)


def small_spread_kernel(place, *refs):
    pieces, outs = refs[:4], refs[4:]
    rows, quarter = outs[0].shape[0], pieces[0].shape[1]
    for piece in range(4):
        right, core = place_of(place, piece)
        at = pl.multiple_of((2 * core + right) * quarter, quarter)
        for which in range(4):
            outs[which][:, pl.ds(at, quarter)] = pieces[piece][
                which * rows : (which + 1) * rows, :
            ].astype(F32)


def qkv_spread_kernel(place, *refs):
    wholes, (side_ref, core_ref, far_ref) = refs[:2], refs[2:5]
    gains, w_refs, outs, gain_outs = refs[5:7], refs[7:11], refs[11:15], refs[15:]
    rows, part = outs[0].shape[0], outs[0].shape[1] // TEAM
    lanes = wholes[0].shape[1]

    def tile(flip_x, flip_y, flip_c, at):
        here = slice(at * rows, (at + 1) * rows)
        if flip_c:
            return far_ref[flip_x, here, :] if flip_y else core_ref[flip_x, here, :]
        if flip_y:
            return side_ref[flip_x, here, :]
        first = pl.multiple_of((3 * place[2] + at) * rows, rows)
        return wholes[flip_x][pl.ds(first, rows), :]

    straight = place[0] == 0
    for flip_c in range(2):
        core = place[1] ^ flip_c
        for flip_y in range(2):
            tiles = [[tile(flip_x, flip_y, flip_c, at) for flip_x in (0, 1)] for at in range(3)]
            left = [jnp.where(straight, one, two).astype(F32) for one, two in tiles]
            right = [jnp.where(straight, two, one).astype(F32) for one, two in tiles]
            columns = left + right
            for at in range(6):
                to = (2 * (place[2] ^ flip_y) + core) * part + (at % 2) * lanes
                outs[at // 2][:, pl.ds(pl.multiple_of(to, lanes), lanes)] = columns[at]
        for flip_x in range(2):
            for at in range(2):
                to = core * 2 * part + (place[0] ^ flip_x) * part + at * lanes
                if flip_c:
                    values = core_ref[flip_x, (3 + at) * rows : (4 + at) * rows, :]
                else:
                    values = wholes[flip_x][(6 + at) * rows : (7 + at) * rows, :]
                outs[3][:, pl.ds(pl.multiple_of(to, lanes), lanes)] = values.astype(F32)
    totals = [
        jnp.sum(outs[which][...] * w_refs[which][...].astype(F32), -1, keepdims=True)
        for which in range(4)
    ]
    gain_outs[0][...] = gain_row(totals[0] + totals[1] + totals[2], gains[0])
    gain_outs[1][...] = gain_row(totals[3], gains[1])


def spread(kernel, place, pieces, gains, weights, shapes, name):
    block = shapes[0][0] if not gains else gains[0].shape[1] // (2 * LINES)
    shapes = shapes + [(1, block)] * len(gains)
    return pl.pallas_call(
        kernel,
        grid_spec=pltpu.PrefetchScalarGridSpec(
            num_scalar_prefetch=1,
            grid=(1,),
            in_specs=[whole_spec(v) for v in pieces]
            + [pl.BlockSpec((1, block), lambda i, p: (0, p[3]))] * len(gains)
            + [pl.BlockSpec((block, w.shape[1]), lambda i, p: (p[3], 0)) for w in weights],
            out_specs=[pl.BlockSpec(shape, lambda i, p: (0, 0)) for shape in shapes],
        ),
        out_shape=[jax.ShapeDtypeStruct(shape, F32) for shape in shapes],
        name=name,
        cost_estimate=SMALL_COST,
    )(place, *pieces, *gains, *weights)


def text_share_kernel(place, total_ref, key_ref, value_ref, own_ref, far_ref, part_ref):
    half, share = key_ref.shape[1], own_ref.shape[0]
    rows = total_ref[pl.ds(pl.multiple_of(place[2] * 2 * share, 2 * share), 2 * share), :]
    part_ref[...] = dot_nt(rows[:, :half], key_ref[...]) + dot_nt(rows[:, half:], value_ref[...])
    own_ref[...] = part_ref[pl.ds(pl.multiple_of(place[1] * share, share), share), :]
    away = (1 - place[1]) * share
    far_ref[...] = part_ref[pl.ds(pl.multiple_of(away, share), share), :].astype(BF16)


def text_share(place, total, w_key_text, w_value_text):
    prompt_rows, width = total.shape
    share, half = prompt_rows // TEAM, width // 2
    side = pl.BlockSpec((width, half), lambda i, p: (0, p[1]))
    out = pl.BlockSpec((share, width), lambda i, p: (0, 0))
    return pl.pallas_call(
        text_share_kernel,
        grid_spec=pltpu.PrefetchScalarGridSpec(
            num_scalar_prefetch=1,
            grid=(1,),
            in_specs=[pl.BlockSpec((prompt_rows, width), lambda i, p: (0, 0)), side, side],
            out_specs=[out, out],
            scratch_shapes=[pltpu.VMEM((2 * share, width), F32)],
        ),
        out_shape=[
            jax.ShapeDtypeStruct((share, width), F32),
            jax.ShapeDtypeStruct((share, width), BF16),
        ],
        name="text_share",
        cost_estimate=SMALL_COST,
    )(place, total, w_key_text, w_value_text)


def text_choose_kernel(owners, shares_ref, near_ref, far_ref):
    count = near_ref.shape[0]
    for each in range(count):
        near_ref[each] = shares_ref[owners[each]]
        far_ref[each] = shares_ref[owners[count + each]]


def text_choose(owners, shares):
    shape = (owners.shape[0] // 2,) + shares.shape[1:]
    return pl.pallas_call(
        text_choose_kernel,
        in_specs=[pl.BlockSpec(memory_space=pltpu.SMEM)] + in_vmem(1),
        out_specs=in_vmem(2),
        out_shape=[jax.ShapeDtypeStruct(shape, BF16)] * 2,
        name="text_choose",
        cost_estimate=SMALL_COST,
    )(owners, shares)


def text_place_kernel(place, *refs):
    pieces, out_ref = refs[:4], refs[4]
    share = pieces[0].shape[1]
    for piece in range(4):
        at = (2 * (place[2] ^ (piece & 1)) + (place[1] ^ (piece >> 1))) * share
        for each in range(out_ref.shape[0]):
            out_ref[each, pl.ds(pl.multiple_of(at, share), share), :] = pieces[piece][each]


def text_place(place, pieces):
    count, share, width = pieces[0].shape
    return pl.pallas_call(
        text_place_kernel,
        in_specs=[pl.BlockSpec(memory_space=pltpu.SMEM)] + in_vmem(4),
        out_specs=in_vmem(1)[0],
        out_shape=jax.ShapeDtypeStruct((count, TEAM * share, width), BF16),
        name="text_place",
        cost_estimate=SMALL_COST,
    )(place, *pieces)


def input_grad_kernel(turn, *refs):
    parts, (q_ref, k_ref, v_ref) = refs[:TEAM], refs[TEAM : TEAM + 3]
    rows_ref, gain_ref, hidden_ref = refs[TEAM + 3 : TEAM + 6]
    blocks, refs = refs[TEAM + 6 : TEAM + 6 + LINES], refs[TEAM + 6 + LINES :]
    outs, (kept, total) = refs[:LINES], refs[LINES:]
    step = pl.program_id(0)
    part = q_ref.shape[1]

    @pl.when(step == 0)
    def _():
        for member in range(TEAM):
            kept[member] = parts[member][...]
        total[...] = jnp.zeros_like(total)

    grads = kept[step]
    for at, w_ref in enumerate((q_ref, k_ref, v_ref)):
        total[...] += dot_nt(grads[:, at * part : (at + 1) * part], w_ref[...])

    @pl.when(step == TEAM - 1)
    def _():
        grad = hidden_ref[...] + norm_back_rows(
            total[...], rows_ref[...].astype(F32), gain_ref[...]
        )
        for line in range(LINES):
            outs[line][0] = grad[line * CHUNK : (line + 1) * CHUNK, :].astype(BF16)
            outs[line][1] = blocks[line][...]


def input_grad(turn, parts, weights, rows_low, gain, grad_hidden, block_out):
    rows, width = rows_low.shape
    wide = parts[0].shape[1]
    part = wide // 3
    out = jax.ShapeDtypeStruct((2, rows // LINES, width), BF16)
    return pl.pallas_call(
        input_grad_kernel,
        grid_spec=pltpu.PrefetchScalarGridSpec(
            num_scalar_prefetch=1,
            grid=(TEAM,),
            in_specs=[whole_spec(v) for v in parts]
            + [pl.BlockSpec((width, part), lambda i, t: (0, t[i]))] * 3
            + [whole_spec(v) for v in (rows_low, gain, grad_hidden, *block_out)],
            out_specs=[whole_spec(out)] * LINES,
            scratch_shapes=[
                pltpu.VMEM((TEAM, rows, wide), BF16),
                pltpu.VMEM((rows, width), F32),
            ],
        ),
        out_shape=[out] * LINES,
        name="input_grad",
        cost_estimate=SMALL_COST,
    )(turn, *parts, *weights, rows_low, gain, grad_hidden, *block_out)


def return_place_kernel(place, *refs):
    pieces, outs = refs[:LINES], refs[LINES:]
    tall = pieces[0].shape[1]
    for step in range(LINES):
        which = place[4] ^ step
        at = pl.multiple_of((which >> 1) * tall, tall)
        for each in range(2):
            outs[each][which & 1, pl.ds(at, tall), :] = pieces[step][each]


def return_place(place, pieces):
    _, tall, width = pieces[0].shape
    return pl.pallas_call(
        return_place_kernel,
        in_specs=[pl.BlockSpec(memory_space=pltpu.SMEM)] + in_vmem(LINES),
        out_specs=in_vmem(2),
        out_shape=[jax.ShapeDtypeStruct((2, 2 * tall, width), BF16)] * 2,
        name="return_place",
        cost_estimate=SMALL_COST,
    )(place, *pieces)


def across(values):
    return move(values, lambda z, y, x, c: (z, y, 1 - x, c))


def together(*values):
    return lax.optimization_barrier(values)


def after(values, *others):
    return lax.optimization_barrier((values, others))[0]


def low(values):
    return values.astype(BF16)


def in_order(first, own, other):
    return jnp.where(first == 0, jnp.stack([own, other]), jnp.stack([other, own]))


def on_device(
    image_rows,
    text_rows,
    prompt_len,
    prompt_slot,
    gain_self,
    w_query,
    w_key,
    w_value,
    w_out,
    gain_cross,
    w_query_text,
    w_key_text,
    w_value_text,
    w_out_text,
    gain_mlp,
    w_in,
    w_mlp_out,
    grad_out,
):
    width = image_rows.shape[-1]
    hidden_width = w_in.shape[-1]
    prompt_rows = text_rows.shape[1]
    rows_here = image_rows.shape[1]
    half_rows = rows_here // 2
    part, half = width // TEAM, width // 2
    block = width // (2 * LINES)
    row_index, group_index = lax.axis_index("row"), lax.axis_index("grp")
    z, y, x, c = row_index >> 1, row_index & 1, group_index >> 1, group_index & 1
    mine = 2 * y + c

    def take(values, start, size, dim):
        return lax.dynamic_slice_in_dim(values, start, size, dim, allow_negative_indices=False)

    def pick_row(values, index, dim=0):
        return lax.dynamic_index_in_dim(
            values, index, dim, keepdims=False, allow_negative_indices=False
        )

    def line_columns(values):
        pairs = [values[:, b * block : (b + 1) * block] for b in range(2 * LINES)]
        near = [jnp.where(y == 0, pairs[2 * b], pairs[2 * b + 1]) for b in range(LINES)]
        far = [jnp.where(y == 0, pairs[2 * b + 1], pairs[2 * b]) for b in range(LINES)]
        return jnp.concatenate(near, 1), jnp.concatenate(far, 1)

    def line_stack(arrays):
        sides = [line_columns(values) for values in arrays]
        return jnp.stack([s[0] for s in sides]), jnp.stack([s[1] for s in sides])

    def hand_rows(values):
        pieces = []
        for step in range(LINES):
            which = z ^ step
            piece = lax.dynamic_slice(
                values,
                (which & 1, (which >> 1) * half_rows, 0),
                (1, half_rows, width),
                allow_negative_indices=False,
            )[0]
            pieces.append(move(piece, hand_out(step)))
        return jnp.concatenate(pieces, 0)

    def natural(parts):
        odd, high = c == 1, y == 1
        parts = [parts[0], parts[2], parts[1], parts[3]]
        parts = [jnp.where(odd, parts[m ^ 1], parts[m]) for m in range(TEAM)]
        return jnp.concatenate([jnp.where(high, parts[m ^ 2], parts[m]) for m in range(TEAM)], 1)

    def side_rows(values, far_values, rows):
        both = jnp.stack([values, far_values])
        first, second, rest = both[:, :rows], both[:, rows : 2 * rows], both[:, 2 * rows :]
        kept = jnp.where(y == 0, first, second)
        return jnp.where(y == 0, second, first), jnp.concatenate([kept, rest], 1)

    def right_parts(values, side):
        parts = (values, side)
        away = [jnp.where(c == 0, v[:, half:], v[:, :half]) for v in parts]
        return [values, side, to_member(jnp.concatenate(away, 0), 2)]

    member = np.repeat(np.arange(TEAM), LINES)
    core_of = c ^ (member >> 1)
    line_of = np.tile(np.arange(LINES), TEAM) ^ ((z & 1) | (core_of << 1))
    table = (line_of * 2 + (y ^ (member & 1))) * 2 + core_of
    table = jnp.concatenate([table, mine[None]]).astype(jnp.int32)
    grad_table = jnp.concatenate([mine[None], line_of]).astype(jnp.int32)
    turn = (mine ^ np.array([0, 2, 1, 3])).astype(jnp.int32)
    place = jnp.stack([x, c, y, row_index, z]).astype(jnp.int32)
    slots = np.arange(prompt_slot.shape[0])
    wanted = text_rows.shape[0] * group_index + np.arange(text_rows.shape[0])
    wanted = jnp.concatenate([wanted, wanted ^ 2])
    owners = jnp.sum(jnp.where(prompt_slot[None, :] == wanted[:, None], slots[None, :], 0), 1)
    apart = (owners & 3) ^ z
    owners = (((apart & 1) << 2) | (apart & 2) | ((owners >> 2) ^ x)).astype(jnp.int32)

    image = 4 * x + z
    slot = pick_row(prompt_slot, image)
    count = take(prompt_len, slot, 1, 0)

    start = part * mine
    w_qkv = jnp.concatenate([take(w, start, part, 1) for w in (w_query, w_key, w_value)], 1)
    rows_low, w_qkv, count = together(hand_rows(image_rows), w_qkv, count)
    count_core = jnp.concatenate([count, c[None]])
    inputs = rows_low.astype(F32)
    text_across = across(text_rows)
    wanted_x, wanted_c = slot >> 2, (slot >> 1) & 1
    text_mine = pick_row(jnp.where(wanted_x == x, text_rows, text_across), slot & 1)
    text_mine = jnp.where(wanted_c == c, text_mine, to_member(text_mine, 2))
    grad_rows = lax.all_gather(
        after(grad_out, rows_low), AXES, axis=0, axis_index_groups=line_groups()
    )
    normed_self, _, _ = norm_rows(inputs, gain_self)
    normed_parts = team_gather(low(normed_self))
    qkv_parts = [low(matmul(a, w_qkv)) for a in normed_parts]
    out_parts, log_totals = self_forward(table, qkv_parts)
    got = [out_parts[0]] + [to_member(out_parts[k], k) for k in range(1, TEAM)]
    text_now = after(text_mine, out_parts[0])
    text_key = low(matmul(text_now, w_key_text))
    text_value = low(matmul(text_now, w_value_text))

    context_low = natural(after(got, text_key, text_value))
    hidden = inputs + matmul(context_low, w_out)
    normed_cross, unit_cross, inverse_cross = norm_rows(hidden, gain_cross)
    cross_normed_low = low(normed_cross)
    cross_low = low(matmul(cross_normed_low, w_query_text))
    cross_context_low = cross_forward(count, cross_low, text_key, text_value)
    grad_rows = after(grad_rows, cross_low)
    image_side = z & 1

    def half_image(core):
        return lax.dynamic_slice(
            grad_rows,
            (0, image_side, half_rows * core, 0),
            (LINES, 1, half_rows, width),
            allow_negative_indices=False,
        ).reshape(-1, width)

    grad_far = to_member(half_image(1 - c), 2)
    grad_low = jnp.where(c == z >> 1, half_image(c), grad_far)
    grad_side, grad_core = to_member(grad_low, 1), to_member(grad_low, 2)
    mixed = hidden + matmul(cross_context_low, w_out_text)
    normed_mlp, _, _ = norm_rows(mixed, gain_mlp)
    mlp_low = low(normed_mlp)
    mlp_side, mlp_core = to_member(mlp_low, 1), to_member(mlp_low, 2)
    left_rows = [cross_context_low, context_low, cross_normed_low]
    left_far = line_stack(after(left_rows, mlp_low))[1]
    left_side = to_member(left_far, 1)

    *block_out, grad_mixed, grad_mixed_low = mlp_rows(
        grad_table[1:], mlp_low, grad_low, mixed, gain_mlp.reshape(1, width), w_in, w_mlp_out
    )
    mlp_side, mlp_core, grad_side, grad_core = after(
        (mlp_side, mlp_core, grad_side, grad_core), grad_mixed_low
    )
    mlp_parts = [mlp_low, mlp_side, mlp_core, to_member(mlp_side, 2)]
    grad_parts = [grad_low, grad_side, grad_core, to_member(grad_side, 2)]
    mlp_blocks = mlp_team(grad_table, after(mlp_parts, left_far), grad_parts, w_in, w_mlp_out)
    mlp_blocks, left_side = lax.optimization_barrier((mlp_blocks, left_side))
    mlp_sum = ring_sum(mlp_blocks)

    grad_mixed_low = after(grad_mixed_low, mlp_blocks)
    mixed_side = to_member(grad_mixed_low, 1)
    grad_cross_ctx = low(matmul_right_t(grad_mixed_low, w_out_text))
    grad_cross_low, kv_near, kv_far = cross_backward(
        count_core, cross_low, text_key, text_value, grad_cross_ctx
    )
    grad_cross_low, kv_near, kv_far, mixed_side = together(
        grad_cross_low, kv_near, kv_far, mixed_side
    )
    kv_near = low(kv_near.astype(F32) + to_member(kv_far, 2).astype(F32))
    kv_side = to_member(kv_near, 1)
    grad_cross_normed = matmul_right_t(after(grad_cross_low, kv_near), w_query_text)
    grad_from_cross, _ = norm_back(grad_cross_normed, unit_cross, inverse_cross, gain_cross)
    grad_hidden = grad_mixed + grad_from_cross
    grad_hidden_low = low(grad_hidden)
    text_total = low(kv_near.astype(F32) + kv_side.astype(F32))
    hidden_side = to_member(after(grad_hidden_low, text_total), 1)
    hidden_core = to_member(grad_hidden_low, 2)
    left_rows, left_side, mixed_side, text_left = after(
        (left_rows, left_side, mixed_side, text_mine), text_total
    )
    left_near = line_stack(left_rows)[0]
    mixed_parts = right_parts(grad_mixed_low, mixed_side)
    lefts = [left_near, left_side, to_member(left_near, 2), to_member(left_side, 2)]
    text_left = line_columns(text_left)[0]
    share_own, share_far = text_share(
        place, after(text_total, text_left, mixed_parts[1]), w_key_text, w_value_text
    )
    share_own, share_far, hidden_side, lefts = together(share_own, share_far, hidden_side, lefts)
    share_far = to_member(share_far, 2)
    hidden_parts = [grad_hidden_low, hidden_side, hidden_core, to_member(hidden_side, 2)]
    cross_side = to_member(after(grad_cross_low, hidden_side), 1)
    split = width // 4
    small_blocks = small_sums(
        c.reshape(1), lefts, mixed_parts + hidden_parts, text_left, text_total
    )
    small_blocks, share_far = together(small_blocks, share_far)
    small_sum = ring_sum(small_blocks)

    shares = low(share_own + share_far.astype(F32))[None]
    grad_qkv_parts = self_backward(
        table,
        qkv_parts,
        after(hidden_parts, small_blocks, mlp_sum, shares),
        out_parts,
        log_totals,
        w_out,
    )
    grad_qkv_parts, cross_side, shares_two = together(
        grad_qkv_parts, cross_side, across(shares)
    )
    got_grads = [grad_qkv_parts[0]] + [
        to_member(grad_qkv_parts[k], k) for k in range(1, TEAM)
    ]
    cross_parts = right_parts(grad_cross_low, cross_side)
    qkv_products = qkv_products_of(
        c.reshape(1), normed_parts, after(grad_qkv_parts, shares_two), lefts, cross_parts
    )
    shares = jnp.concatenate([shares, shares_two], 0)
    qkv_products, got_grads, shares_two, mlp_across = together(
        qkv_products,
        got_grads,
        move(shares, lambda z, y, x, c: (z ^ 2, y, x, c)),
        across(mlp_sum),
    )
    mlp_send, mlp_keep = side_rows(mlp_sum, mlp_across, block)
    shares = jnp.concatenate([shares, shares_two], 0)
    qkv_sum = ring_sum(qkv_products)
    back_pieces = input_grad(
        turn,
        after(got_grads, small_sum, shares, mlp_keep),
        (w_query, w_key, w_value),
        rows_low,
        gain_self.reshape(1, width),
        grad_hidden,
        block_out,
    )
    back_pieces, mlp_parts = together(
        back_pieces, [to_member(mlp_send, 1), to_member(mlp_keep, 2), to_member(mlp_send, 3)]
    )
    back = [move(back_pieces[step], hand_back(step)) for step in range(LINES)]
    grad_w_in, grad_w_mlp_out, grad_gain_mlp = spread(
        mlp_spread_kernel,
        place,
        [mlp_sum, mlp_across, *mlp_parts],
        [gain_mlp.reshape(1, width)],
        [w_in],
        [(block, hidden_width), (2 * split, width)],
        "mlp_spread",
    )
    grad_w_in, small_across, shares_two = together(
        grad_w_in, across(small_sum), move(shares, lambda z, y, x, c: (z ^ 1, y, x, c))
    )
    small_core, small_far = to_member(small_sum, 2), to_member(small_across, 2)
    near, far = text_choose(owners, jnp.concatenate([shares, shares_two], 0))
    small_all = spread(
        small_spread_kernel,
        place,
        after([small_sum, small_across, small_core, small_far], near),
        [],
        [],
        [(block, width)] * 4,
        "small_spread",
    )
    qkv_done = after(qkv_sum, near)
    small_all, back[0], back[1], text_back, qkv_across = together(
        small_all,
        back[0],
        back[1],
        [near, to_member(near, 1), to_member(far, 2), to_member(far, 3)],
        across(qkv_done),
    )
    qkv_send, qkv_keep = side_rows(qkv_done, qkv_across, 3 * block)
    grad_text = text_place(place, after(text_back, qkv_send, qkv_keep))
    grad_text, back, qkv_parts_back = together(
        grad_text,
        back,
        [to_member(qkv_send, 1), to_member(qkv_keep, 2), to_member(qkv_send, 3)],
    )
    grad_image, out_block = return_place(place, back)
    grad_w_query, grad_w_key, grad_w_value, grad_w_query_text, gain_one, gain_two = spread(
        qkv_spread_kernel,
        place,
        [qkv_done, qkv_across, *qkv_parts_back],
        [gain_self.reshape(1, width), gain_cross.reshape(1, width)],
        [w_query, w_key, w_value, w_query_text],
        [(block, width)] * 4,
        "qkv_spread",
    )
    return (
        out_block,
        grad_image,
        grad_text,
        gain_one.reshape(block),
        grad_w_query,
        grad_w_key,
        grad_w_value,
        small_all[1],
        gain_two.reshape(block),
        grad_w_query_text,
        small_all[2],
        small_all[3],
        small_all[0],
        grad_gain_mlp.reshape(block),
        grad_w_in,
        grad_w_mlp_out,
    )


def solution(mesh):
    placed = (
        P("grp", "row", None),
        P("grp", None, None),
        P(),
        P(),
        P(),
        P(),
        P(),
        P(),
        P(),
        P(),
        P(),
        P(),
        P(),
        P(),
        P(),
        P(),
        P(),
        P("grp", "row", None),
    )
    return jax.shard_map(
        on_device if fits(mesh) else on_device_plain,
        mesh=mesh,
        in_specs=placed,
        out_specs=(
            P("grp", "row", None),
            P("grp", "row", None),
            P("grp", None, None),
            P("row"),
            P("row", None),
            P("row", None),
            P("row", None),
            P("row", None),
            P("row"),
            P("row", None),
            P("row", None),
            P("row", None),
            P("row", None),
            P("row"),
            P("row", None),
            P("row", None),
        ),
        check_vma=False,
    )
```

```python
import functools

import jax
import jax.numpy as jnp
import numpy as np
from jax import lax
from jax.sharding import PartitionSpec as P
from jax.experimental import pallas as pl
from jax.experimental.pallas import tpu as pltpu

HEADS = 16
HEAD_DIM = 64


EPSILON = 1e-05
NEG_LARGE = -1e30
HIGHEST = lax.Precision.HIGHEST


def norm_rows(values, gain):
    center = jnp.mean(values, -1, keepdims=True)
    centered = values - center
    variance = jnp.mean(centered * centered, -1, keepdims=True)
    inverse = lax.rsqrt(variance + EPSILON)
    unit_rows = centered * inverse
    return (unit_rows * gain, unit_rows, inverse)


def norm_back(grad_normed, unit_rows, inverse, gain):
    grad_unit = grad_normed * gain
    first_mean = jnp.mean(grad_unit, -1, keepdims=True)
    second_mean = jnp.mean(grad_unit * unit_rows, -1, keepdims=True)
    grad_input = inverse * (grad_unit - first_mean - unit_rows * second_mean)
    return (grad_input, jnp.sum(grad_normed * unit_rows, 0))


def matmul(left, right):
    return jnp.dot(left, right, preferred_element_type=jnp.float32)


def matmul_left_t(left, right):
    return lax.dot_general(
        left, right, (((0,), (0,)), ((), ())), preferred_element_type=jnp.float32
    )


def matmul_right_t(left, right):
    return lax.dot_general(
        left, right, (((1,), (1,)), ((), ())), preferred_element_type=jnp.float32
    )


def split_heads(values):
    return values.reshape(values.shape[:-1] + (HEADS, HEAD_DIM))


def on_device_plain(
    image_rows,
    text_rows,
    prompt_len,
    prompt_slot,
    gain_self,
    w_query,
    w_key,
    w_value,
    w_out,
    gain_cross,
    w_query_text,
    w_key_text,
    w_value_text,
    w_out_text,
    gain_mlp,
    w_in,
    w_mlp_out,
    grad_out,
):
    images_here, rows_here, width = image_rows.shape
    prompt_rows = text_rows.shape[1]
    row_count = lax.axis_size("row")
    length = rows_here * row_count
    row_index = lax.axis_index("row")
    group_index = lax.axis_index("grp")
    scale_factor = HEAD_DIM ** (-0.5)
    block_size = min(512, length)
    block_count = length // block_size
    flat_rows = images_here * rows_here
    inputs = image_rows.astype(jnp.float32).reshape(flat_rows, width)
    normed_self, unit_self, inverse_self = norm_rows(inputs, gain_self)
    normed_low = normed_self.astype(jnp.bfloat16)
    query_low = (
        matmul(normed_low, w_query).astype(jnp.bfloat16).reshape(images_here, rows_here, width)
    )
    key_low = matmul(normed_low, w_key).astype(jnp.bfloat16).reshape(images_here, rows_here, width)
    value_low = (
        matmul(normed_low, w_value).astype(jnp.bfloat16).reshape(images_here, rows_here, width)
    )
    keys_all, values_all = (
        lax.all_gather(key_low, "row", axis=1, tiled=True),
        lax.all_gather(value_low, "row", axis=1, tiled=True),
    )
    query_heads = split_heads(query_low)
    query_pos = row_index * rows_here + jnp.arange(rows_here, dtype=jnp.int32)
    key_pos = jnp.arange(length, dtype=jnp.int32)
    causal = key_pos[None, :] <= query_pos[:, None]
    contexts = []
    totals = []
    for each_image in range(images_here):
        scores = (
            jnp.einsum(
                "qhd,khd->hqk",
                query_heads[each_image],
                split_heads(keys_all[each_image]),
                preferred_element_type=jnp.float32,
            )
            * scale_factor
        )
        scores = jnp.where(causal[None], scores, NEG_LARGE)
        largest = jnp.max(scores, -1, keepdims=True)
        expos = jnp.exp(scores - largest)
        denominator = jnp.sum(expos, -1, keepdims=True)
        probs_low = (expos / denominator).astype(jnp.bfloat16)
        contexts.append(
            jnp.einsum(
                "hqk,khd->qhd",
                probs_low,
                split_heads(values_all[each_image]),
                preferred_element_type=jnp.float32,
            )
        )
        totals.append((largest + jnp.log(denominator))[..., 0])
    context = jnp.stack(contexts).reshape(flat_rows, width)
    log_totals = jnp.stack(totals)
    context_low = context.astype(jnp.bfloat16)
    hidden = inputs + matmul(context_low, w_out)
    normed_cross, unit_cross, inverse_cross = norm_rows(hidden, gain_cross)
    cross_normed_low = normed_cross.astype(jnp.bfloat16)
    cross_low = (
        matmul(cross_normed_low, w_query_text)
        .astype(jnp.bfloat16)
        .reshape(images_here, rows_here, HEADS, HEAD_DIM)
    )
    text_flat = text_rows.reshape(-1, width)
    text_key = matmul(text_flat, w_key_text).astype(jnp.bfloat16).reshape(text_rows.shape)
    text_value = matmul(text_flat, w_value_text).astype(jnp.bfloat16).reshape(text_rows.shape)
    text_keys, text_values = (
        lax.all_gather(text_key, "grp", axis=0, tiled=True),
        lax.all_gather(text_value, "grp", axis=0, tiled=True),
    )
    image_total = prompt_slot.shape[0]
    slots = lax.dynamic_slice_in_dim(prompt_slot, group_index * images_here, images_here)
    keys_sel = split_heads(jnp.take(text_keys, slots, axis=0))
    values_sel = split_heads(jnp.take(text_values, slots, axis=0))
    lengths_sel = jnp.take(prompt_len, slots)
    text_mask = (jnp.arange(prompt_rows, dtype=jnp.int32)[None, :] < lengths_sel[:, None])[
        :, None, None, :
    ]
    cross_scores = (
        jnp.einsum("iqhd,ikhd->ihqk", cross_low, keys_sel, preferred_element_type=jnp.float32)
        * scale_factor
    )
    cross_probs = jax.nn.softmax(jnp.where(text_mask, cross_scores, NEG_LARGE), axis=-1)
    cross_probs_low = cross_probs.astype(jnp.bfloat16)
    cross_context = jnp.einsum(
        "ihqk,ikhd->iqhd", cross_probs_low, values_sel, preferred_element_type=jnp.float32
    )
    cross_context_low = cross_context.reshape(flat_rows, width).astype(jnp.bfloat16)
    mixed = hidden + matmul(cross_context_low, w_out_text)
    normed_mlp, unit_mlp, inverse_mlp = norm_rows(mixed, gain_mlp)
    mlp_low = normed_mlp.astype(jnp.bfloat16)
    pre_act = matmul(mlp_low, w_in)
    activated, gelu_back = jax.vjp(jax.nn.gelu, pre_act)
    activated_low = activated.astype(jnp.bfloat16)
    block_out = mixed + matmul(activated_low, w_mlp_out)
    out_block = block_out.astype(jnp.bfloat16).reshape(image_rows.shape)
    grad_low = grad_out.reshape(flat_rows, width)
    grad_w_mlp_out = matmul_left_t(activated_low, grad_low)
    grad_activated = matmul_right_t(grad_low, w_mlp_out)
    grad_pre_low = gelu_back(grad_activated)[0].astype(jnp.bfloat16)
    grad_w_in = matmul_left_t(mlp_low, grad_pre_low)
    grad_mlp_normed = matmul_right_t(grad_pre_low, w_in)
    grad_from_mlp, grad_gain_mlp = norm_back(grad_mlp_normed, unit_mlp, inverse_mlp, gain_mlp)
    grad_mixed = grad_low.astype(jnp.float32) + grad_from_mlp
    grad_mixed_low = grad_mixed.astype(jnp.bfloat16)
    grad_w_out_text = matmul_left_t(cross_context_low, grad_mixed_low)
    grad_cross_ctx = split_heads(
        matmul_right_t(grad_mixed_low, w_out_text)
        .astype(jnp.bfloat16)
        .reshape(images_here, rows_here, width)
    )
    grad_cross_probs = jnp.einsum(
        "iqhd,ikhd->ihqk", grad_cross_ctx, values_sel, preferred_element_type=jnp.float32
    )
    grad_values_sel = jnp.einsum(
        "ihqk,iqhd->ikhd", cross_probs_low, grad_cross_ctx, preferred_element_type=jnp.float32
    )
    grad_cross_scores = cross_probs * (
        grad_cross_probs - jnp.sum(cross_probs * grad_cross_probs, -1, keepdims=True)
    )
    grad_scores_low = grad_cross_scores.astype(jnp.bfloat16)
    grad_cross_query = (
        jnp.einsum("ihqk,ikhd->iqhd", grad_scores_low, keys_sel, preferred_element_type=jnp.float32)
        * scale_factor
    )
    grad_cross_query_low = grad_cross_query.astype(jnp.bfloat16).reshape(flat_rows, width)
    grad_keys_sel = (
        jnp.einsum(
            "ihqk,iqhd->ikhd", grad_scores_low, cross_low, preferred_element_type=jnp.float32
        )
        * scale_factor
    )
    grad_w_query_text = matmul_left_t(cross_normed_low, grad_cross_query_low)
    grad_cross_normed = matmul_right_t(grad_cross_query_low, w_query_text)
    grad_from_cross, grad_gain_cross = norm_back(
        grad_cross_normed, unit_cross, inverse_cross, gain_cross
    )
    grad_hidden = grad_mixed + grad_from_cross
    placing = (jnp.arange(image_total, dtype=jnp.int32)[:, None] == slots[None, :]).astype(
        jnp.float32
    )
    joined_text = jnp.concatenate(
        [
            grad_keys_sel.reshape(images_here, prompt_rows, width),
            grad_values_sel.reshape(images_here, prompt_rows, width),
        ],
        -1,
    )
    text_term = jnp.einsum("si,ipd->spd", placing, joined_text, precision=HIGHEST)
    text_grad = lax.psum_scatter(
        text_term.astype(jnp.bfloat16), "grp", scatter_dimension=0, tiled=True
    )
    share_rows = text_flat.shape[0] // row_count
    text_total = (
        lax.psum(text_grad, "row").astype(jnp.float32).reshape(-1, 2 * width).astype(jnp.bfloat16)
    )
    text_share = lax.dynamic_slice_in_dim(text_total, row_index * share_rows, share_rows, 0)
    text_grad_rows = (
        matmul_right_t(text_total[:, :width], w_key_text)
        + matmul_right_t(text_total[:, width:], w_value_text)
    ).astype(jnp.bfloat16)
    text_part = lax.dynamic_slice_in_dim(text_flat, row_index * share_rows, share_rows, 0)
    grad_w_key_text = matmul_left_t(text_part, text_share[:, :width])
    grad_w_value_text = matmul_left_t(text_part, text_share[:, width:])
    grad_text = text_grad_rows.reshape(text_rows.shape)
    grad_hidden_low = grad_hidden.astype(jnp.bfloat16)
    grad_w_out = matmul_left_t(context_low, grad_hidden_low)
    grad_context = (
        matmul_right_t(grad_hidden_low, w_out)
        .astype(jnp.bfloat16)
        .reshape(images_here, rows_here, width)
    )
    grad_context_heads = split_heads(grad_context)
    context_heads = split_heads(context.reshape(images_here, rows_here, width))
    delta = jnp.einsum(
        "iqhd,iqhd->ihq", grad_context_heads.astype(jnp.float32), context_heads, precision=HIGHEST
    )
    zero_query = jnp.zeros((images_here, rows_here, HEADS, HEAD_DIM), jnp.float32)

    def block_terms(block):
        start = block * block_size
        key_heads = split_heads(lax.dynamic_slice_in_dim(keys_all, start, block_size, 1))
        value_heads = split_heads(lax.dynamic_slice_in_dim(values_all, start, block_size, 1))
        block_pos = start + jnp.arange(block_size, dtype=jnp.int32)
        allowed = (block_pos[None, :] <= query_pos[:, None])[None, None]
        scores = (
            jnp.einsum(
                "iqhd,ikhd->ihqk", query_heads, key_heads, preferred_element_type=jnp.float32
            )
            * scale_factor
        )
        probs = jnp.where(allowed, jnp.exp(scores - log_totals[..., None]), 0.0)
        grad_probs = jnp.einsum(
            "iqhd,ikhd->ihqk", grad_context_heads, value_heads, preferred_element_type=jnp.float32
        )
        grad_scores = (probs * (grad_probs - delta[..., None])).astype(jnp.bfloat16)
        return (grad_scores, probs.astype(jnp.bfloat16), key_heads)

    def step_keys(block, carry):
        grad_query, term_buffer = carry
        grad_scores, probs_low, key_heads = block_terms(block)
        grad_query = (
            grad_query
            + jnp.einsum(
                "ihqk,ikhd->iqhd", grad_scores, key_heads, preferred_element_type=jnp.float32
            )
            * scale_factor
        )
        grad_key_part = (
            jnp.einsum(
                "ihqk,iqhd->ikhd", grad_scores, query_heads, preferred_element_type=jnp.float32
            )
            * scale_factor
        )
        grad_value_part = jnp.einsum(
            "ihqk,iqhd->ikhd", probs_low, grad_context_heads, preferred_element_type=jnp.float32
        )
        joined = jnp.concatenate(
            [
                grad_key_part.reshape(images_here, block_size, width),
                grad_value_part.reshape(images_here, block_size, width),
            ],
            -1,
        )
        term_buffer = lax.dynamic_update_slice_in_dim(term_buffer, joined, block * block_size, 1)
        return (grad_query, term_buffer)

    start_buffer = jnp.zeros((images_here, length, 2 * width), jnp.float32)
    grad_query, term_buffer = lax.fori_loop(0, block_count, step_keys, (zero_query, start_buffer))
    grad_kv = lax.psum_scatter(
        term_buffer.astype(jnp.bfloat16), "row", scatter_dimension=1, tiled=True
    ).astype(jnp.float32)
    grad_query_low = grad_query.reshape(flat_rows, width).astype(jnp.bfloat16)
    grad_kv_low = grad_kv.reshape(flat_rows, 2 * width).astype(jnp.bfloat16)
    grad_w_query = matmul_left_t(normed_low, grad_query_low)
    grad_w_key = matmul_left_t(normed_low, grad_kv_low[:, :width])
    grad_w_value = matmul_left_t(normed_low, grad_kv_low[:, width:])
    grad_normed_self = (
        matmul_right_t(grad_query_low, w_query)
        + matmul_right_t(grad_kv_low[:, :width], w_key)
        + matmul_right_t(grad_kv_low[:, width:], w_value)
    )
    grad_from_self, grad_gain_self = norm_back(grad_normed_self, unit_self, inverse_self, gain_self)
    grad_image = (grad_hidden + grad_from_self).astype(jnp.bfloat16).reshape(image_rows.shape)
    shares = (
        lax.psum_scatter(
            grad_gain_self.astype(jnp.bfloat16), "row", scatter_dimension=0, tiled=True
        ).astype(jnp.float32),
        lax.psum_scatter(
            grad_w_query.astype(jnp.bfloat16), "row", scatter_dimension=0, tiled=True
        ).astype(jnp.float32),
        lax.psum_scatter(
            grad_w_key.astype(jnp.bfloat16), "row", scatter_dimension=0, tiled=True
        ).astype(jnp.float32),
        lax.psum_scatter(
            grad_w_value.astype(jnp.bfloat16), "row", scatter_dimension=0, tiled=True
        ).astype(jnp.float32),
        lax.psum_scatter(
            grad_w_out.astype(jnp.bfloat16), "row", scatter_dimension=0, tiled=True
        ).astype(jnp.float32),
        lax.psum_scatter(
            grad_gain_cross.astype(jnp.bfloat16), "row", scatter_dimension=0, tiled=True
        ).astype(jnp.float32),
        lax.psum_scatter(
            grad_w_query_text.astype(jnp.bfloat16), "row", scatter_dimension=0, tiled=True
        ).astype(jnp.float32),
        lax.psum_scatter(
            grad_w_key_text.astype(jnp.bfloat16), "row", scatter_dimension=0, tiled=True
        ).astype(jnp.float32),
        lax.psum_scatter(
            grad_w_value_text.astype(jnp.bfloat16), "row", scatter_dimension=0, tiled=True
        ).astype(jnp.float32),
        lax.psum_scatter(
            grad_w_out_text.astype(jnp.bfloat16), "row", scatter_dimension=0, tiled=True
        ).astype(jnp.float32),
        lax.psum_scatter(
            grad_gain_mlp.astype(jnp.bfloat16), "row", scatter_dimension=0, tiled=True
        ).astype(jnp.float32),
        lax.psum_scatter(
            grad_w_in.astype(jnp.bfloat16), "row", scatter_dimension=0, tiled=True
        ).astype(jnp.float32),
        lax.psum_scatter(
            grad_w_mlp_out.astype(jnp.bfloat16), "row", scatter_dimension=0, tiled=True
        ).astype(jnp.float32),
    )
    summed = (
        lax.psum(shares[0].astype(jnp.bfloat16), "grp").astype(jnp.float32),
        lax.psum(shares[1].astype(jnp.bfloat16), "grp").astype(jnp.float32),
        lax.psum(shares[2].astype(jnp.bfloat16), "grp").astype(jnp.float32),
        lax.psum(shares[3].astype(jnp.bfloat16), "grp").astype(jnp.float32),
        lax.psum(shares[4].astype(jnp.bfloat16), "grp").astype(jnp.float32),
        lax.psum(shares[5].astype(jnp.bfloat16), "grp").astype(jnp.float32),
        lax.psum(shares[6].astype(jnp.bfloat16), "grp").astype(jnp.float32),
        lax.psum(shares[7].astype(jnp.bfloat16), "grp").astype(jnp.float32),
        lax.psum(shares[8].astype(jnp.bfloat16), "grp").astype(jnp.float32),
        lax.psum(shares[9].astype(jnp.bfloat16), "grp").astype(jnp.float32),
        lax.psum(shares[10].astype(jnp.bfloat16), "grp").astype(jnp.float32),
        lax.psum(shares[11].astype(jnp.bfloat16), "grp").astype(jnp.float32),
        lax.psum(shares[12].astype(jnp.bfloat16), "grp").astype(jnp.float32),
    )
    return (
        out_block,
        grad_image,
        grad_text,
        summed[0],
        summed[1],
        summed[2],
        summed[3],
        summed[4],
        summed[5],
        summed[6],
        summed[7],
        summed[8],
        summed[9],
        summed[10],
        summed[11],
        summed[12],
    )


AXES = ("row", "grp")
SMALL_COST = pl.CostEstimate(flops=0, bytes_accessed=0, transcendentals=0)
BF16 = jnp.bfloat16
F32 = jnp.float32
TEAM = 4
LINES = 4


def fits(mesh):
    return mesh.shape["row"] == 2 * LINES and mesh.shape["grp"] == 4


def moves(change):
    pairs = []
    for place in range(32):
        z, y, x, c = place // 8, place // 4 % 2, place // 2 % 2, place % 2
        z2, y2, x2, c2 = change(z, y, x, c)
        pairs.append((place, z2 * 8 + y2 * 4 + x2 * 2 + c2))
    return pairs


def move(values, change):
    return lax.ppermute(values, AXES, moves(change))


def to_member(values, member):
    flip_y, flip_c = member & 1, member >> 1
    return move(values, lambda z, y, x, c: (z, y ^ flip_y, x, c ^ flip_c))


def team_gather(values):
    side = to_member(values, 1)
    return [values, side, to_member(values, 2), to_member(side, 2)]


def hand_out(step):
    def change(z, y, x, c):
        which = z ^ step
        return (2 * c + (which & 1), y, x, which >> 1)

    return change


def hand_back(step):
    def change(z, y, x, c):
        return (step ^ ((z & 1) | (c << 1)), y, x, z >> 1)

    return change


def ring_groups():
    order = [(0, 0), (0, 1), (0, 2), (0, 3), (1, 3), (1, 2), (1, 1), (1, 0)]
    return [
        [z * 8 + y * 4 + x * 2 + c for x, z in order] for y in range(2) for c in range(2)
    ]


def line_groups():
    return [[z * 8 + place for z in range(LINES)] for place in range(8)]


def ring_sum(blocks):
    flat = blocks.reshape(-1, blocks.shape[-1])
    return lax.psum_scatter(
        flat, AXES, scatter_dimension=0, axis_index_groups=ring_groups(), tiled=True
    )


def lane_mask(rows, head):
    lane = lax.broadcasted_iota(jnp.int32, (rows, 128), 1)
    return (lane >= HEAD_DIM) if head else (lane < HEAD_DIM)


def only(values, head):
    return jnp.where(lane_mask(values.shape[0], head), values, jnp.zeros_like(values))


def dot_nt(left, right):
    return lax.dot_general(
        left, right, (((1,), (1,)), ((), ())), preferred_element_type=F32
    )


def dot_nn(left, right):
    return lax.dot_general(
        left, right, (((1,), (0,)), ((), ())), preferred_element_type=F32
    )


def dot_tn(left, right):
    return lax.dot_general(
        left, right, (((0,), (0,)), ((), ())), preferred_element_type=F32
    )


CHUNK = 64


def self_forward_kernel(table, *refs):
    parts, outs, lse_ref = refs[:TEAM], refs[TEAM : 2 * TEAM], refs[2 * TEAM]
    all_qkv, all_out = refs[2 * TEAM + 1 :]
    length, heads_width = all_out.shape
    chunks = parts[0].shape[0] // CHUNK
    for member in range(TEAM):
        for piece in range(chunks):
            at = pl.multiple_of(table[member * chunks + piece] * CHUNK, CHUNK)
            all_qkv[pl.ds(at, CHUNK), :] = parts[member][piece * CHUNK : (piece + 1) * CHUNK, :]
    block = 256
    pairs = heads_width // 128
    scale_factor = HEAD_DIM ** (-0.5)
    diagonal = lax.broadcasted_iota(jnp.int32, (block, block), 1) <= lax.broadcasted_iota(
        jnp.int32, (block, block), 0
    )
    for pair in range(pairs):
        q_cols = slice(128 * pair, 128 * pair + 128)
        k_cols = slice(heads_width + 128 * pair, heads_width + 128 * pair + 128)
        v_cols = slice(2 * heads_width + 128 * pair, 2 * heads_width + 128 * pair + 128)
        for block_at in range(length // block):
            rows = slice(block * block_at, block * (block_at + 1))
            q_block = all_qkv[rows, q_cols]
            joined = jnp.zeros((block, 128), F32)
            for head in range(2):
                q_one = only(q_block, head)
                near = dot_nt(q_one, all_qkv[rows, k_cols]) * scale_factor
                near = jnp.where(diagonal, near, NEG_LARGE)
                scores = near
                if block_at:
                    far = dot_nt(q_one, all_qkv[0 : block * block_at, k_cols]) * scale_factor
                    scores = jnp.concatenate([far, near], 1)
                largest = jnp.max(scores, -1, keepdims=True)
                expos = jnp.exp(scores - largest)
                denominator = jnp.sum(expos, -1, keepdims=True)
                probs_low = (expos / denominator).astype(BF16)
                mixed = dot_nn(probs_low, all_qkv[0 : block * (block_at + 1), v_cols])
                joined = jnp.where(lane_mask(block, head), mixed, joined)
                total = largest + jnp.log(denominator)
                lse_ref[2 * pair + head : 2 * pair + head + 1, rows] = jnp.transpose(
                    jnp.broadcast_to(total, (block, 128))
                )[0:1, :]
            all_out[rows, q_cols] = joined.astype(BF16)
    for member in range(TEAM):
        for piece in range(chunks):
            at = pl.multiple_of(table[member * chunks + piece] * CHUNK, CHUNK)
            outs[member][piece * CHUNK : (piece + 1) * CHUNK, :] = all_out[pl.ds(at, CHUNK), :]


def in_vmem(count):
    return [pl.BlockSpec(memory_space=pltpu.VMEM)] * count


def self_forward(table, parts):
    rows, width = parts[0].shape
    heads_width, length = width // 3, rows * TEAM
    outs = pl.pallas_call(
        self_forward_kernel,
        in_specs=[pl.BlockSpec(memory_space=pltpu.SMEM)] + in_vmem(TEAM),
        out_specs=in_vmem(TEAM + 1),
        out_shape=[jax.ShapeDtypeStruct((rows, heads_width), BF16)] * TEAM
        + [jax.ShapeDtypeStruct((8, length), F32)],
        scratch_shapes=[
            pltpu.VMEM((length, width), BF16),
            pltpu.VMEM((length, heads_width), BF16),
        ],
        name="self_forward",
        cost_estimate=SMALL_COST,
    )(table, *parts)
    return outs[:TEAM], outs[TEAM]


def self_backward_kernel(table, *refs):
    parts, hidden, oparts = refs[:TEAM], refs[TEAM : 2 * TEAM], refs[2 * TEAM : 3 * TEAM]
    lse_ref, w_ref = refs[3 * TEAM : 3 * TEAM + 2]
    outs = refs[3 * TEAM + 2 : 4 * TEAM + 2]
    all_qkv, all_do, delta_ref, sum_q, sum_k, sum_v = refs[4 * TEAM + 2 :]
    length, heads_width = all_do.shape
    chunks = parts[0].shape[0] // CHUNK
    head_row = lax.broadcasted_iota(jnp.int32, (8, heads_width), 0)
    head_col = lax.broadcasted_iota(jnp.int32, (8, heads_width), 1) // HEAD_DIM
    pick = (head_row == head_col).astype(F32)
    block = 256
    for member in range(TEAM):
        grad_out = dot_nt(hidden[member][...], w_ref[...]).astype(BF16)
        products = grad_out.astype(F32) * oparts[member][...].astype(F32)
        for piece in range(chunks):
            at = pl.multiple_of(table[member * chunks + piece] * CHUNK, CHUNK)
            here = slice(piece * CHUNK, (piece + 1) * CHUNK)
            all_qkv[pl.ds(at, CHUNK), :] = parts[member][here, :]
            all_do[pl.ds(at, CHUNK), :] = grad_out[here, :]
            sum_q[pl.ds(at, CHUNK), :] = products[here, :]
    for block_at in range(length // block):
        rows = slice(block * block_at, block * (block_at + 1))
        delta_ref[:, rows] = lax.dot_general(
            pick,
            sum_q[rows, :],
            (((1,), (1,)), ((), ())),
            precision=HIGHEST,
            preferred_element_type=F32,
        )
    pairs = heads_width // 128
    scale_factor = HEAD_DIM ** (-0.5)
    diagonal = lax.broadcasted_iota(jnp.int32, (block, block), 0) <= lax.broadcasted_iota(
        jnp.int32, (block, block), 1
    )
    for pair in range(pairs):
        q_cols = slice(128 * pair, 128 * pair + 128)
        k_cols = slice(heads_width + 128 * pair, heads_width + 128 * pair + 128)
        v_cols = slice(2 * heads_width + 128 * pair, 2 * heads_width + 128 * pair + 128)
        for block_at in range(length // block):
            rows = slice(block * block_at, block * (block_at + 1))
            seen = slice(0, block * (block_at + 1))
            q_block = all_qkv[rows, q_cols]
            do_block = all_do[rows, q_cols]
            sum_q_block = jnp.zeros((block, 128), F32)
            for head in range(2):
                q_one, do_one = only(q_block, head), only(do_block, head)
                total = lse_ref[2 * pair + head : 2 * pair + head + 1, rows]
                delta = delta_ref[2 * pair + head : 2 * pair + head + 1, rows]
                scores = dot_nt(all_qkv[seen, k_cols], q_one) * scale_factor
                probs = jnp.exp(scores - total)
                near = jnp.where(diagonal, probs[block * block_at :, :], 0.0)
                if block_at:
                    probs = jnp.concatenate([probs[: block * block_at, :], near], 0)
                else:
                    probs = near
                grad_probs = dot_nt(all_qkv[seen, v_cols], do_one)
                grad_scores = (probs * (grad_probs - delta)).astype(BF16)
                term_v = dot_nn(probs.astype(BF16), do_one)
                term_k = dot_nn(grad_scores, q_one) * scale_factor
                if head == 0:
                    term_v_both, term_k_both = term_v, term_k
                else:
                    term_v_both, term_k_both = term_v_both + term_v, term_k_both + term_k
                term_q = dot_tn(grad_scores, all_qkv[seen, k_cols]) * scale_factor
                sum_q_block = jnp.where(lane_mask(block, head), term_q, sum_q_block)
            sum_q[rows, q_cols] = sum_q_block
            if block_at:
                before = slice(0, block * block_at)
                sum_k[before, q_cols] += term_k_both[before, :]
                sum_v[before, q_cols] += term_v_both[before, :]
            sum_k[rows, q_cols] = term_k_both[block * block_at :, :]
            sum_v[rows, q_cols] = term_v_both[block * block_at :, :]
    for member in range(TEAM):
        for piece in range(chunks):
            at = pl.multiple_of(table[member * chunks + piece] * CHUNK, CHUNK)
            here = slice(piece * CHUNK, (piece + 1) * CHUNK)
            outs[member][here, 0:heads_width] = sum_q[pl.ds(at, CHUNK), :].astype(BF16)
            outs[member][here, heads_width : 2 * heads_width] = sum_k[
                pl.ds(at, CHUNK), :
            ].astype(BF16)
            outs[member][here, 2 * heads_width : 3 * heads_width] = sum_v[
                pl.ds(at, CHUNK), :
            ].astype(BF16)


def whole_spec(values):
    return pl.BlockSpec(values.shape, lambda *_: (0,) * len(values.shape))


def self_backward(table, parts, hidden, oparts, lse, w_out):
    rows, width = parts[0].shape
    heads_width, length = width // 3, rows * TEAM
    last = TEAM * LINES
    out = jax.ShapeDtypeStruct((rows, width), BF16)
    return pl.pallas_call(
        self_backward_kernel,
        grid_spec=pltpu.PrefetchScalarGridSpec(
            num_scalar_prefetch=1,
            grid=(1,),
            in_specs=[whole_spec(v) for v in (*parts, *hidden, *oparts, lse)]
            + [pl.BlockSpec((heads_width, w_out.shape[1]), lambda i, t: (t[last], 0))],
            out_specs=[whole_spec(out)] * TEAM,
            scratch_shapes=[
                pltpu.VMEM((length, width), BF16),
                pltpu.VMEM((length, heads_width), BF16),
                pltpu.VMEM((8, length), F32),
                pltpu.VMEM((length, heads_width), F32),
                pltpu.VMEM((length, heads_width), F32),
                pltpu.VMEM((length, heads_width), F32),
            ],
        ),
        out_shape=[out] * TEAM,
        name="self_backward",
        cost_estimate=SMALL_COST,
    )(table, *parts, *hidden, *oparts, lse, w_out)


def cross_probs_of(query_one, key_pair, allowed):
    scores = dot_nt(query_one, key_pair) * HEAD_DIM ** (-0.5)
    scores = jnp.where(allowed, scores, NEG_LARGE)
    expos = jnp.exp(scores - jnp.max(scores, -1, keepdims=True))
    return expos / jnp.sum(expos, -1, keepdims=True)


def cross_forward_kernel(count, c_ref, k_ref, v_ref, o_ref):
    rows, width = c_ref.shape
    allowed = lax.broadcasted_iota(jnp.int32, (rows, k_ref.shape[0]), 1) < count[0]
    for pair in range(width // 128):
        cols = slice(128 * pair, 128 * pair + 128)
        joined = jnp.zeros((rows, 128), F32)
        for head in range(2):
            probs = cross_probs_of(only(c_ref[:, cols], head), k_ref[:, cols], allowed)
            mixed = dot_nn(probs.astype(BF16), v_ref[:, cols])
            joined = jnp.where(lane_mask(rows, head), mixed, joined)
        o_ref[:, cols] = joined.astype(BF16)


def cross_forward(count, cross, keys, values):
    return pl.pallas_call(
        cross_forward_kernel,
        in_specs=[pl.BlockSpec(memory_space=pltpu.SMEM)] + in_vmem(3),
        out_specs=pl.BlockSpec(memory_space=pltpu.VMEM),
        out_shape=jax.ShapeDtypeStruct(cross.shape, BF16),
        name="cross_forward",
        cost_estimate=SMALL_COST,
    )(count, cross, keys, values)


def cross_backward_kernel(count, c_ref, k_ref, v_ref, do_ref, dc_ref, near_ref, far_ref):
    rows, width = c_ref.shape
    half = width // 2
    scale_factor = HEAD_DIM ** (-0.5)
    allowed = lax.broadcasted_iota(jnp.int32, (rows, k_ref.shape[0]), 1) < count[0]

    @pl.loop(0, width // 128)
    def _(step):
        for at in range(1):
            first = (step + at) * 128
            cols = pl.ds(pl.multiple_of(first, 128), 128)
            joined = jnp.zeros((rows, 128), F32)
            sum_k = jnp.zeros((k_ref.shape[0], 128), F32)
            sum_v = jnp.zeros((k_ref.shape[0], 128), F32)
            for head in range(2):
                c_one, do_one = only(c_ref[:, cols], head), only(do_ref[:, cols], head)
                probs = cross_probs_of(c_one, k_ref[:, cols], allowed)
                grad_probs = dot_nt(do_one, v_ref[:, cols])
                inner = jnp.sum(probs * grad_probs, -1, keepdims=True)
                grad_scores = (probs * (grad_probs - inner)).astype(BF16)
                term_c = dot_nn(grad_scores, k_ref[:, cols]) * scale_factor
                joined = jnp.where(lane_mask(rows, head), term_c, joined)
                sum_k += dot_tn(grad_scores, c_one) * scale_factor
                sum_v += dot_tn(probs.astype(BF16), do_one)
            dc_ref[:, cols] = joined.astype(BF16)
            side = (first >= half).astype(jnp.int32)
            within = first - half * side
            key_cols = pl.ds(pl.multiple_of(within, 128), 128)
            value_cols = pl.ds(pl.multiple_of(half + within, 128), 128)

            def keep(ref, sums=(sum_k, sum_v), cols=(key_cols, value_cols)):
                for values, where in zip(sums, cols):
                    ref[:, where] = values.astype(BF16)

            pl.when(count[1] == side)(functools.partial(keep, near_ref))
            pl.when(count[1] != side)(functools.partial(keep, far_ref))


def cross_backward(count, cross, keys, values, grad_ctx):
    side = jax.ShapeDtypeStruct((keys.shape[0], cross.shape[1]), BF16)
    return pl.pallas_call(
        cross_backward_kernel,
        in_specs=[pl.BlockSpec(memory_space=pltpu.SMEM)] + in_vmem(4),
        out_specs=in_vmem(3),
        out_shape=[jax.ShapeDtypeStruct(cross.shape, BF16), side, side],
        name="cross_backward",
        cost_estimate=SMALL_COST,
    )(count, cross, keys, values, grad_ctx)


GELU_SCALE = (2.0 / jnp.pi) ** 0.5
GELU_CUBE = 0.044715


def gelu_both(values):
    square = values * values
    slope = jnp.tanh(GELU_SCALE * (values + GELU_CUBE * (square * values)))
    half_up = 0.5 * (1.0 + slope)
    steep = GELU_SCALE * (1.0 + 3.0 * GELU_CUBE * square)
    return (values * half_up, half_up + 0.5 * values * (1.0 - slope * slope) * steep)


def norm_back_rows(grad_normed, values, gain):
    centered = values - jnp.mean(values, -1, keepdims=True)
    inverse = lax.rsqrt(jnp.mean(centered * centered, -1, keepdims=True) + EPSILON)
    unit_rows = centered * inverse
    grad_unit = grad_normed * gain
    first_mean = jnp.mean(grad_unit, -1, keepdims=True)
    second_mean = jnp.mean(grad_unit * unit_rows, -1, keepdims=True)
    return inverse * (grad_unit - first_mean - unit_rows * second_mean)


def sort_chunks(table, first, count, source, target):
    for piece in range(count):
        at = pl.multiple_of(table[first + piece] * CHUNK, CHUNK)
        target[piece * CHUNK : (piece + 1) * CHUNK, :] = source[pl.ds(at, CHUNK), :]


def mlp_rows_kernel(
    table, m_ref, g_ref, mixed_ref, gain_ref, in_ref, out_ref, *refs
):
    block_refs, (grad_ref, low_ref, total, back, grad_rows) = refs[:LINES], refs[LINES:]
    step = pl.program_id(0)

    @pl.when(step == 0)
    def _():
        sort_chunks(table, 0, LINES, g_ref, grad_rows)

    block = in_ref.shape[1]
    acts, grads = [], []
    for first in (0, block // 2):
        here = slice(first, first + block // 2)
        activated, slope = gelu_both(dot_nn(m_ref[...], in_ref[:, here]))
        acts.append(activated.astype(BF16))
        grads.append((dot_nt(grad_rows[...], out_ref[here, :]) * slope).astype(BF16))
    term = dot_nn(jnp.concatenate(acts, 1), out_ref[...])
    back_term = dot_nt(jnp.concatenate(grads, 1), in_ref[...])

    @pl.when(step == 0)
    def _():
        total[...] = mixed_ref[...] + term
        back[...] = back_term

    @pl.when(step > 0)
    def _():
        total[...] += term
        back[...] += back_term

    @pl.when(step == pl.num_programs(0) - 1)
    def _():
        for line in range(LINES):
            block_refs[line][...] = total[line * CHUNK : (line + 1) * CHUNK, :].astype(BF16)
        grad_mixed = grad_rows[...].astype(F32) + norm_back_rows(
            back[...], mixed_ref[...], gain_ref[...]
        )
        grad_ref[...] = grad_mixed
        low_ref[...] = grad_mixed.astype(BF16)


def mlp_rows(table, mlp_low, grad_low, mixed, gain, w_in, w_mlp_out):
    rows, width = mlp_low.shape
    hidden_width = w_in.shape[1]
    block = hidden_width // LINES
    whole = pl.BlockSpec((rows, width), lambda i, t: (0, 0))
    return pl.pallas_call(
        mlp_rows_kernel,
        grid_spec=pltpu.PrefetchScalarGridSpec(
            num_scalar_prefetch=1,
            grid=(hidden_width // block,),
            in_specs=[
                whole,
                pl.BlockSpec(grad_low.shape, lambda i, t: (0, 0)),
                whole,
                pl.BlockSpec((1, width), lambda i, t: (0, 0)),
                pl.BlockSpec((width, block), lambda i, t: (0, i)),
                pl.BlockSpec((block, width), lambda i, t: (i, 0)),
            ],
            out_specs=[pl.BlockSpec((rows // LINES, width), lambda i, t: (0, 0))] * LINES
            + [whole, whole],
            scratch_shapes=[
                pltpu.VMEM((rows, width), F32),
                pltpu.VMEM((rows, width), F32),
                pltpu.VMEM((rows, width), BF16),
            ],
        ),
        out_shape=[jax.ShapeDtypeStruct((rows // LINES, width), BF16)] * LINES
        + [
            jax.ShapeDtypeStruct((rows, width), F32),
            jax.ShapeDtypeStruct((rows, width), BF16),
        ],
        name="mlp_rows",
        cost_estimate=SMALL_COST,
    )(table, mlp_low, grad_low, mixed, gain, w_in, w_mlp_out)


def mlp_team_kernel(table, *refs):
    parts, grad_parts = refs[:TEAM], refs[TEAM : 2 * TEAM]
    in_ref, out_ref, sum_ref, m_all, g_all = refs[2 * TEAM :]
    step = pl.program_id(0)
    block = in_ref.shape[1]
    rows = parts[0].shape[0]

    @pl.when(step == 0)
    def _():
        for member in range(TEAM):
            here = pl.ds(member * rows, rows)
            sort_chunks(table, 1 + member * LINES, LINES, grad_parts[member], g_all.at[here])
            m_all[here, :] = parts[member][...]

    activated, slope = gelu_both(dot_nn(m_all[...], in_ref[...]))
    grad_pre = (dot_nt(g_all[...], out_ref[...]) * slope).astype(BF16)
    part_in = dot_tn(m_all[...], grad_pre).astype(BF16)
    part_out = dot_tn(activated.astype(BF16), g_all[...]).astype(BF16)
    right = step // 2
    cols = pl.ds(pl.multiple_of((step % 2) * block, block), block)
    for line in range(LINES):
        place = jnp.where(right == 0, line, 2 * LINES - 1 - line)
        sum_ref[place, 0:block, cols] = part_in[line * block : (line + 1) * block, :]
    half = part_out.shape[1] // 2
    sum_ref[step, block : 2 * block, :] = part_out[:, :half]
    sum_ref[2 * LINES - 1 - step, block : 2 * block, :] = part_out[:, half:]


def mlp_team(table, parts, grad_parts, w_in, w_mlp_out):
    rows, width = TEAM * parts[0].shape[0], parts[0].shape[1]
    block = w_in.shape[1] // (LINES * TEAM)
    return pl.pallas_call(
        mlp_team_kernel,
        grid_spec=pltpu.PrefetchScalarGridSpec(
            num_scalar_prefetch=1,
            grid=(LINES,),
            in_specs=[pl.BlockSpec(parts[0].shape, lambda i, t: (0, 0))] * (2 * TEAM)
            + [
                pl.BlockSpec((width, block), lambda i, t: (0, i * TEAM + t[0])),
                pl.BlockSpec((block, width), lambda i, t: (i * TEAM + t[0], 0)),
            ],
            out_specs=pl.BlockSpec((2 * LINES, 2 * block, width // 2), lambda i, t: (0, 0, 0)),
            scratch_shapes=[pltpu.VMEM((rows, width), BF16), pltpu.VMEM((rows, width), BF16)],
        ),
        out_shape=jax.ShapeDtypeStruct((2 * LINES, 2 * block, width // 2), BF16),
        name="mlp_team",
        cost_estimate=SMALL_COST,
    )(table, *parts, *grad_parts, w_in, w_mlp_out)


def small_sums_kernel(core, *refs):
    lefts, rights = refs[:TEAM], refs[TEAM : TEAM + 7]
    text_ref, grad_ref, sum_ref, left_all, right_all = refs[TEAM + 7 :]
    step = pl.program_id(0)
    rows, half = lefts[0].shape[1], right_all.shape[2]
    quarter = sum_ref.shape[2]
    block = text_ref.shape[1]
    cols = pl.ds(pl.multiple_of(core[0] * half, half), half)

    @pl.when(step == 0)
    def _():
        for member in range(TEAM):
            here = slice(member * rows, (member + 1) * rows)
            for at in range(2):
                left_all[at, here, :] = lefts[member][at]
            right_all[1, here, :] = rights[3 + member][:, cols]
        right_all[0, 0:rows, :] = rights[0][:, cols]
        right_all[0, rows : 2 * rows, :] = rights[1][:, cols]
        right_all[0, 2 * rows :, :] = rights[2][...]

    mine = pl.ds(pl.multiple_of(step * block, block), block)
    pairs = [(left_all[at, :, mine], right_all[at]) for at in range(2)]
    pairs += [(text_ref[...], grad_ref[:, at * half : (at + 1) * half]) for at in range(2)]
    for at, (left, right) in enumerate(pairs):
        part = dot_tn(left, right).astype(BF16)
        sum_ref[step, at * block : (at + 1) * block, :] = part[:, :quarter]
        sum_ref[2 * LINES - 1 - step, at * block : (at + 1) * block, :] = part[:, quarter:]


def small_sums(core, lefts, rights, text_left, text_right):
    rows, half = rights[0].shape[0], rights[0].shape[1] // 2
    block, quarter = text_left.shape[1] // LINES, half // 2
    return pl.pallas_call(
        small_sums_kernel,
        grid_spec=pltpu.PrefetchScalarGridSpec(
            num_scalar_prefetch=1,
            grid=(LINES,),
            in_specs=[pl.BlockSpec((2,) + v.shape[1:], lambda i, t: (0, 0, 0)) for v in lefts]
            + [whole_spec(v) for v in rights]
            + [pl.BlockSpec((text_left.shape[0], block), lambda i, t: (0, i))]
            + [whole_spec(text_right)],
            out_specs=pl.BlockSpec((2 * LINES, 4 * block, quarter), lambda i, t: (0, 0, 0)),
            scratch_shapes=[
                pltpu.VMEM((2, TEAM * rows, LINES * block), BF16),
                pltpu.VMEM((2, TEAM * rows, half), BF16),
            ],
        ),
        out_shape=jax.ShapeDtypeStruct((2 * LINES, 4 * block, quarter), BF16),
        name="small_sums",
        cost_estimate=SMALL_COST,
    )(core, *lefts, *rights, text_left, text_right)


def qkv_products_kernel(core, *refs):
    lefts, rights = refs[:TEAM], refs[TEAM : 2 * TEAM]
    cross_lefts, cross_rights = refs[2 * TEAM : 3 * TEAM], refs[3 * TEAM : 3 * TEAM + 3]
    sum_ref, left_all, right_all, cross_left, cross_right = refs[3 * TEAM + 3 :]
    step = pl.program_id(0)
    rows, lanes = lefts[0].shape[0], sum_ref.shape[2]
    block = left_all.shape[1] // LINES

    @pl.when(step == 0)
    def _():
        for member in range(TEAM):
            here = slice(member * rows, (member + 1) * rows)
            left_all[here, :] = lefts[member][...]
            right_all[here, :] = rights[member][...]
            cross_left[here, :] = cross_lefts[member][0]
        half = cross_right.shape[1]
        cols = pl.ds(pl.multiple_of(core[0] * half, half), half)
        cross_right[0:rows, :] = cross_rights[0][:, cols]
        cross_right[rows : 2 * rows, :] = cross_rights[1][:, cols]
        cross_right[2 * rows :, :] = cross_rights[2][...]

    left = left_all[:, pl.ds(pl.multiple_of(step * block, block), block)]
    part = dot_tn(left, right_all[...]).astype(BF16)
    small = cross_left[:, pl.ds(pl.multiple_of(step * lanes, lanes), lanes)]
    cross = dot_tn(small, cross_right[...]).astype(BF16)
    for right, to in enumerate((step, 2 * LINES - 1 - step)):
        for side in range(2):
            for at in range(3):
                first = (3 * side + at) * lanes
                col = (3 * right + at) * lanes
                sum_ref[to, first : first + lanes, :] = part[
                    side * lanes : (side + 1) * lanes, col : col + lanes
                ]
        for at in range(2):
            first, col = (6 + at) * lanes, (2 * right + at) * lanes
            sum_ref[to, first : first + lanes, :] = cross[:, col : col + lanes]


def qkv_products_of(core, lefts, rights, cross_lefts, cross_rights):
    (rows, width), (_, wide) = lefts[0].shape, rights[0].shape
    lanes = width // (2 * LINES)
    half = cross_rights[0].shape[1] // 2
    return pl.pallas_call(
        qkv_products_kernel,
        grid_spec=pltpu.PrefetchScalarGridSpec(
            num_scalar_prefetch=1,
            grid=(LINES,),
            in_specs=[whole_spec(v) for v in (*lefts, *rights)]
            + [pl.BlockSpec((1,) + v.shape[1:], lambda i, t: (2, 0, 0)) for v in cross_lefts]
            + [whole_spec(v) for v in cross_rights],
            out_specs=pl.BlockSpec((2 * LINES, 8 * lanes, lanes), lambda i, t: (0, 0, 0)),
            scratch_shapes=[
                pltpu.VMEM((TEAM * rows, width), BF16),
                pltpu.VMEM((TEAM * rows, wide), BF16),
                pltpu.VMEM((TEAM * rows, LINES * lanes), BF16),
                pltpu.VMEM((TEAM * rows, half), BF16),
            ],
        ),
        out_shape=jax.ShapeDtypeStruct((2 * LINES, 8 * lanes, lanes), BF16),
        name="qkv_products",
        cost_estimate=SMALL_COST,
    )(core, *lefts, *rights, *cross_lefts, *cross_rights)


def place_of(place, piece):
    return (place[0] ^ (piece & 1), place[1] ^ (piece >> 1))


def gain_row(total, gain_ref):
    wide = jnp.transpose(jnp.broadcast_to(total, (total.shape[0], 128)))
    return wide[0:1, :] / gain_ref[...]


def mlp_spread_kernel(place, *refs):
    wholes, (side_ref, core_ref, far_ref), (gain_in, w_ref) = refs[:2], refs[2:5], refs[5:7]
    in_ref, out_ref, gain_ref = refs[7:]
    rows, block = in_ref.shape[0], wholes[0].shape[1] // 2
    tall = out_ref.shape[0] // 2
    mine = pl.ds(pl.multiple_of(place[2] * rows, rows), rows)
    for flip_x in range(2):
        right = place[0] ^ flip_x
        tiles = (
            (0, 0, wholes[flip_x][mine, :]),
            (1, 0, side_ref[flip_x]),
            (0, 1, core_ref[flip_x, :rows, :]),
            (1, 1, far_ref[flip_x]),
        )
        for flip_y, flip_c, tile in tiles:
            for low_line in range(2):
                at = ((2 * right + low_line) * 2 + (place[2] ^ flip_y)) * 2 + (place[1] ^ flip_c)
                in_ref[:, pl.ds(pl.multiple_of(at * block, block), block)] = tile[
                    :, low_line * block : (low_line + 1) * block
                ].astype(F32)
        for flip_c, tile in ((0, wholes[flip_x][2 * rows :, :]), (1, core_ref[flip_x, rows:, :])):
            out_ref[
                pl.ds(pl.multiple_of((place[1] ^ flip_c) * tall, tall), tall),
                pl.ds(pl.multiple_of(right * 2 * block, 2 * block), 2 * block),
            ] = tile.astype(F32)
    total = jnp.sum(in_ref[...] * w_ref[...].astype(F32), -1, keepdims=True)
    gain_ref[...] = gain_row(total, gain_in)


def small_spread_kernel(place, *refs):
    pieces, outs = refs[:4], refs[4:]
    rows, quarter = outs[0].shape[0], pieces[0].shape[1]
    for piece in range(4):
        right, core = place_of(place, piece)
        at = pl.multiple_of((2 * core + right) * quarter, quarter)
        for which in range(4):
            outs[which][:, pl.ds(at, quarter)] = pieces[piece][
                which * rows : (which + 1) * rows, :
            ].astype(F32)


def qkv_spread_kernel(place, *refs):
    wholes, (side_ref, core_ref, far_ref) = refs[:2], refs[2:5]
    gains, w_refs, outs, gain_outs = refs[5:7], refs[7:11], refs[11:15], refs[15:]
    rows, part = outs[0].shape[0], outs[0].shape[1] // TEAM
    lanes = wholes[0].shape[1]

    def tile(flip_x, flip_y, flip_c, at):
        here = slice(at * rows, (at + 1) * rows)
        if flip_c:
            return far_ref[flip_x, here, :] if flip_y else core_ref[flip_x, here, :]
        if flip_y:
            return side_ref[flip_x, here, :]
        first = pl.multiple_of((3 * place[2] + at) * rows, rows)
        return wholes[flip_x][pl.ds(first, rows), :]

    straight = place[0] == 0
    for flip_c in range(2):
        core = place[1] ^ flip_c
        for flip_y in range(2):
            tiles = [[tile(flip_x, flip_y, flip_c, at) for flip_x in (0, 1)] for at in range(3)]
            left = [jnp.where(straight, one, two).astype(F32) for one, two in tiles]
            right = [jnp.where(straight, two, one).astype(F32) for one, two in tiles]
            columns = left + right
            for at in range(6):
                to = (2 * (place[2] ^ flip_y) + core) * part + (at % 2) * lanes
                outs[at // 2][:, pl.ds(pl.multiple_of(to, lanes), lanes)] = columns[at]
        for flip_x in range(2):
            for at in range(2):
                to = core * 2 * part + (place[0] ^ flip_x) * part + at * lanes
                if flip_c:
                    values = core_ref[flip_x, (3 + at) * rows : (4 + at) * rows, :]
                else:
                    values = wholes[flip_x][(6 + at) * rows : (7 + at) * rows, :]
                outs[3][:, pl.ds(pl.multiple_of(to, lanes), lanes)] = values.astype(F32)
    totals = [
        jnp.sum(outs[which][...] * w_refs[which][...].astype(F32), -1, keepdims=True)
        for which in range(4)
    ]
    gain_outs[0][...] = gain_row(totals[0] + totals[1] + totals[2], gains[0])
    gain_outs[1][...] = gain_row(totals[3], gains[1])


def spread(kernel, place, pieces, gains, weights, shapes, name):
    block = shapes[0][0] if not gains else gains[0].shape[1] // (2 * LINES)
    shapes = shapes + [(1, block)] * len(gains)
    return pl.pallas_call(
        kernel,
        grid_spec=pltpu.PrefetchScalarGridSpec(
            num_scalar_prefetch=1,
            grid=(1,),
            in_specs=[whole_spec(v) for v in pieces]
            + [pl.BlockSpec((1, block), lambda i, p: (0, p[3]))] * len(gains)
            + [pl.BlockSpec((block, w.shape[1]), lambda i, p: (p[3], 0)) for w in weights],
            out_specs=[pl.BlockSpec(shape, lambda i, p: (0, 0)) for shape in shapes],
        ),
        out_shape=[jax.ShapeDtypeStruct(shape, F32) for shape in shapes],
        name=name,
        cost_estimate=SMALL_COST,
    )(place, *pieces, *gains, *weights)


def text_share_kernel(place, total_ref, key_ref, value_ref, own_ref, far_ref, part_ref):
    half, share = key_ref.shape[1], own_ref.shape[0]
    rows = total_ref[pl.ds(pl.multiple_of(place[2] * 2 * share, 2 * share), 2 * share), :]
    part_ref[...] = dot_nt(rows[:, :half], key_ref[...]) + dot_nt(rows[:, half:], value_ref[...])
    own_ref[...] = part_ref[pl.ds(pl.multiple_of(place[1] * share, share), share), :]
    away = (1 - place[1]) * share
    far_ref[...] = part_ref[pl.ds(pl.multiple_of(away, share), share), :].astype(BF16)


def text_share(place, total, w_key_text, w_value_text):
    prompt_rows, width = total.shape
    share, half = prompt_rows // TEAM, width // 2
    side = pl.BlockSpec((width, half), lambda i, p: (0, p[1]))
    out = pl.BlockSpec((share, width), lambda i, p: (0, 0))
    return pl.pallas_call(
        text_share_kernel,
        grid_spec=pltpu.PrefetchScalarGridSpec(
            num_scalar_prefetch=1,
            grid=(1,),
            in_specs=[pl.BlockSpec((prompt_rows, width), lambda i, p: (0, 0)), side, side],
            out_specs=[out, out],
            scratch_shapes=[pltpu.VMEM((2 * share, width), F32)],
        ),
        out_shape=[
            jax.ShapeDtypeStruct((share, width), F32),
            jax.ShapeDtypeStruct((share, width), BF16),
        ],
        name="text_share",
        cost_estimate=SMALL_COST,
    )(place, total, w_key_text, w_value_text)


def text_choose_kernel(owners, shares_ref, near_ref, far_ref):
    count = near_ref.shape[0]
    for each in range(count):
        near_ref[each] = shares_ref[owners[each]]
        far_ref[each] = shares_ref[owners[count + each]]


def text_choose(owners, shares):
    shape = (owners.shape[0] // 2,) + shares.shape[1:]
    return pl.pallas_call(
        text_choose_kernel,
        in_specs=[pl.BlockSpec(memory_space=pltpu.SMEM)] + in_vmem(1),
        out_specs=in_vmem(2),
        out_shape=[jax.ShapeDtypeStruct(shape, BF16)] * 2,
        name="text_choose",
        cost_estimate=SMALL_COST,
    )(owners, shares)


def text_place_kernel(place, *refs):
    pieces, out_ref = refs[:4], refs[4]
    share = pieces[0].shape[1]
    for piece in range(4):
        at = (2 * (place[2] ^ (piece & 1)) + (place[1] ^ (piece >> 1))) * share
        for each in range(out_ref.shape[0]):
            out_ref[each, pl.ds(pl.multiple_of(at, share), share), :] = pieces[piece][each]


def text_place(place, pieces):
    count, share, width = pieces[0].shape
    return pl.pallas_call(
        text_place_kernel,
        in_specs=[pl.BlockSpec(memory_space=pltpu.SMEM)] + in_vmem(4),
        out_specs=in_vmem(1)[0],
        out_shape=jax.ShapeDtypeStruct((count, TEAM * share, width), BF16),
        name="text_place",
        cost_estimate=SMALL_COST,
    )(place, *pieces)


def input_grad_kernel(turn, *refs):
    parts, (q_ref, k_ref, v_ref) = refs[:TEAM], refs[TEAM : TEAM + 3]
    rows_ref, gain_ref, hidden_ref = refs[TEAM + 3 : TEAM + 6]
    blocks, refs = refs[TEAM + 6 : TEAM + 6 + LINES], refs[TEAM + 6 + LINES :]
    outs, (kept, total) = refs[:LINES], refs[LINES:]
    step = pl.program_id(0)
    part = q_ref.shape[1]

    @pl.when(step == 0)
    def _():
        for member in range(TEAM):
            kept[member] = parts[member][...]
        total[...] = jnp.zeros_like(total)

    grads = kept[step]
    for at, w_ref in enumerate((q_ref, k_ref, v_ref)):
        total[...] += dot_nt(grads[:, at * part : (at + 1) * part], w_ref[...])

    @pl.when(step == TEAM - 1)
    def _():
        grad = hidden_ref[...] + norm_back_rows(
            total[...], rows_ref[...].astype(F32), gain_ref[...]
        )
        for line in range(LINES):
            outs[line][0] = grad[line * CHUNK : (line + 1) * CHUNK, :].astype(BF16)
            outs[line][1] = blocks[line][...]


def input_grad(turn, parts, weights, rows_low, gain, grad_hidden, block_out):
    rows, width = rows_low.shape
    wide = parts[0].shape[1]
    part = wide // 3
    out = jax.ShapeDtypeStruct((2, rows // LINES, width), BF16)
    return pl.pallas_call(
        input_grad_kernel,
        grid_spec=pltpu.PrefetchScalarGridSpec(
            num_scalar_prefetch=1,
            grid=(TEAM,),
            in_specs=[whole_spec(v) for v in parts]
            + [pl.BlockSpec((width, part), lambda i, t: (0, t[i]))] * 3
            + [whole_spec(v) for v in (rows_low, gain, grad_hidden, *block_out)],
            out_specs=[whole_spec(out)] * LINES,
            scratch_shapes=[
                pltpu.VMEM((TEAM, rows, wide), BF16),
                pltpu.VMEM((rows, width), F32),
            ],
        ),
        out_shape=[out] * LINES,
        name="input_grad",
        cost_estimate=SMALL_COST,
    )(turn, *parts, *weights, rows_low, gain, grad_hidden, *block_out)


def return_place_kernel(place, *refs):
    pieces, outs = refs[:LINES], refs[LINES:]
    tall = pieces[0].shape[1]
    for step in range(LINES):
        which = place[4] ^ step
        at = pl.multiple_of((which >> 1) * tall, tall)
        for each in range(2):
            outs[each][which & 1, pl.ds(at, tall), :] = pieces[step][each]


def return_place(place, pieces):
    _, tall, width = pieces[0].shape
    return pl.pallas_call(
        return_place_kernel,
        in_specs=[pl.BlockSpec(memory_space=pltpu.SMEM)] + in_vmem(LINES),
        out_specs=in_vmem(2),
        out_shape=[jax.ShapeDtypeStruct((2, 2 * tall, width), BF16)] * 2,
        name="return_place",
        cost_estimate=SMALL_COST,
    )(place, *pieces)


def across(values):
    return move(values, lambda z, y, x, c: (z, y, 1 - x, c))


def together(*values):
    return lax.optimization_barrier(values)


def after(values, *others):
    return lax.optimization_barrier((values, others))[0]


def low(values):
    return values.astype(BF16)


def in_order(first, own, other):
    return jnp.where(first == 0, jnp.stack([own, other]), jnp.stack([other, own]))


def on_device(
    image_rows,
    text_rows,
    prompt_len,
    prompt_slot,
    gain_self,
    w_query,
    w_key,
    w_value,
    w_out,
    gain_cross,
    w_query_text,
    w_key_text,
    w_value_text,
    w_out_text,
    gain_mlp,
    w_in,
    w_mlp_out,
    grad_out,
):
    width = image_rows.shape[-1]
    hidden_width = w_in.shape[-1]
    prompt_rows = text_rows.shape[1]
    rows_here = image_rows.shape[1]
    half_rows = rows_here // 2
    part, half = width // TEAM, width // 2
    block = width // (2 * LINES)
    row_index, group_index = lax.axis_index("row"), lax.axis_index("grp")
    z, y, x, c = row_index >> 1, row_index & 1, group_index >> 1, group_index & 1
    mine = 2 * y + c

    def take(values, start, size, dim):
        return lax.dynamic_slice_in_dim(values, start, size, dim, allow_negative_indices=False)

    def pick_row(values, index, dim=0):
        return lax.dynamic_index_in_dim(
            values, index, dim, keepdims=False, allow_negative_indices=False
        )

    def line_columns(values):
        pairs = [values[:, b * block : (b + 1) * block] for b in range(2 * LINES)]
        near = [jnp.where(y == 0, pairs[2 * b], pairs[2 * b + 1]) for b in range(LINES)]
        far = [jnp.where(y == 0, pairs[2 * b + 1], pairs[2 * b]) for b in range(LINES)]
        return jnp.concatenate(near, 1), jnp.concatenate(far, 1)

    def line_stack(arrays):
        sides = [line_columns(values) for values in arrays]
        return jnp.stack([s[0] for s in sides]), jnp.stack([s[1] for s in sides])

    def hand_rows(values):
        pieces = []
        for step in range(LINES):
            which = z ^ step
            piece = lax.dynamic_slice(
                values,
                (which & 1, (which >> 1) * half_rows, 0),
                (1, half_rows, width),
                allow_negative_indices=False,
            )[0]
            pieces.append(move(piece, hand_out(step)))
        return jnp.concatenate(pieces, 0)

    def natural(parts):
        odd, high = c == 1, y == 1
        parts = [parts[0], parts[2], parts[1], parts[3]]
        parts = [jnp.where(odd, parts[m ^ 1], parts[m]) for m in range(TEAM)]
        return jnp.concatenate([jnp.where(high, parts[m ^ 2], parts[m]) for m in range(TEAM)], 1)

    def side_rows(values, far_values, rows):
        both = jnp.stack([values, far_values])
        first, second, rest = both[:, :rows], both[:, rows : 2 * rows], both[:, 2 * rows :]
        kept = jnp.where(y == 0, first, second)
        return jnp.where(y == 0, second, first), jnp.concatenate([kept, rest], 1)

    def right_parts(values, side):
        parts = (values, side)
        away = [jnp.where(c == 0, v[:, half:], v[:, :half]) for v in parts]
        return [values, side, to_member(jnp.concatenate(away, 0), 2)]

    member = np.repeat(np.arange(TEAM), LINES)
    core_of = c ^ (member >> 1)
    line_of = np.tile(np.arange(LINES), TEAM) ^ ((z & 1) | (core_of << 1))
    table = (line_of * 2 + (y ^ (member & 1))) * 2 + core_of
    table = jnp.concatenate([table, mine[None]]).astype(jnp.int32)
    grad_table = jnp.concatenate([mine[None], line_of]).astype(jnp.int32)
    turn = (mine ^ np.array([0, 2, 1, 3])).astype(jnp.int32)
    place = jnp.stack([x, c, y, row_index, z]).astype(jnp.int32)
    slots = np.arange(prompt_slot.shape[0])
    wanted = text_rows.shape[0] * group_index + np.arange(text_rows.shape[0])
    wanted = jnp.concatenate([wanted, wanted ^ 2])
    owners = jnp.sum(jnp.where(prompt_slot[None, :] == wanted[:, None], slots[None, :], 0), 1)
    apart = (owners & 3) ^ z
    owners = (((apart & 1) << 2) | (apart & 2) | ((owners >> 2) ^ x)).astype(jnp.int32)

    image = 4 * x + z
    slot = pick_row(prompt_slot, image)
    count = take(prompt_len, slot, 1, 0)

    start = part * mine
    w_qkv = jnp.concatenate([take(w, start, part, 1) for w in (w_query, w_key, w_value)], 1)
    rows_low, w_qkv, count = together(hand_rows(image_rows), w_qkv, count)
    count_core = jnp.concatenate([count, c[None]])
    inputs = rows_low.astype(F32)
    text_across = across(text_rows)
    wanted_x, wanted_c = slot >> 2, (slot >> 1) & 1
    text_mine = pick_row(jnp.where(wanted_x == x, text_rows, text_across), slot & 1)
    text_mine = jnp.where(wanted_c == c, text_mine, to_member(text_mine, 2))
    grad_rows = lax.all_gather(
        after(grad_out, rows_low), AXES, axis=0, axis_index_groups=line_groups()
    )
    normed_self, _, _ = norm_rows(inputs, gain_self)
    normed_parts = team_gather(low(normed_self))
    qkv_parts = [low(matmul(a, w_qkv)) for a in normed_parts]
    out_parts, log_totals = self_forward(table, qkv_parts)
    got = [out_parts[0]] + [to_member(out_parts[k], k) for k in range(1, TEAM)]
    text_now = after(text_mine, out_parts[0])
    text_key = low(matmul(text_now, w_key_text))
    text_value = low(matmul(text_now, w_value_text))

    context_low = natural(after(got, text_key, text_value))
    hidden = inputs + matmul(context_low, w_out)
    normed_cross, unit_cross, inverse_cross = norm_rows(hidden, gain_cross)
    cross_normed_low = low(normed_cross)
    cross_low = low(matmul(cross_normed_low, w_query_text))
    cross_context_low = cross_forward(count, cross_low, text_key, text_value)
    grad_rows = after(grad_rows, cross_low)
    image_side = z & 1

    def half_image(core):
        return lax.dynamic_slice(
            grad_rows,
            (0, image_side, half_rows * core, 0),
            (LINES, 1, half_rows, width),
            allow_negative_indices=False,
        ).reshape(-1, width)

    grad_far = to_member(half_image(1 - c), 2)
    grad_low = jnp.where(c == z >> 1, half_image(c), grad_far)
    grad_side, grad_core = to_member(grad_low, 1), to_member(grad_low, 2)
    mixed = hidden + matmul(cross_context_low, w_out_text)
    normed_mlp, _, _ = norm_rows(mixed, gain_mlp)
    mlp_low = low(normed_mlp)
    mlp_side, mlp_core = to_member(mlp_low, 1), to_member(mlp_low, 2)
    left_rows = [cross_context_low, context_low, cross_normed_low]
    left_far = line_stack(after(left_rows, mlp_low))[1]
    left_side = to_member(left_far, 1)

    *block_out, grad_mixed, grad_mixed_low = mlp_rows(
        grad_table[1:], mlp_low, grad_low, mixed, gain_mlp.reshape(1, width), w_in, w_mlp_out
    )
    mlp_side, mlp_core, grad_side, grad_core = after(
        (mlp_side, mlp_core, grad_side, grad_core), grad_mixed_low
    )
    mlp_parts = [mlp_low, mlp_side, mlp_core, to_member(mlp_side, 2)]
    grad_parts = [grad_low, grad_side, grad_core, to_member(grad_side, 2)]
    mlp_blocks = mlp_team(grad_table, after(mlp_parts, left_far), grad_parts, w_in, w_mlp_out)
    mlp_blocks, left_side = lax.optimization_barrier((mlp_blocks, left_side))
    mlp_sum = ring_sum(mlp_blocks)

    grad_mixed_low = after(grad_mixed_low, mlp_blocks)
    mixed_side = to_member(grad_mixed_low, 1)
    grad_cross_ctx = low(matmul_right_t(grad_mixed_low, w_out_text))
    grad_cross_low, kv_near, kv_far = cross_backward(
        count_core, cross_low, text_key, text_value, grad_cross_ctx
    )
    grad_cross_low, kv_near, kv_far, mixed_side = together(
        grad_cross_low, kv_near, kv_far, mixed_side
    )
    kv_near = low(kv_near.astype(F32) + to_member(kv_far, 2).astype(F32))
    kv_side = to_member(kv_near, 1)
    grad_cross_normed = matmul_right_t(after(grad_cross_low, kv_near), w_query_text)
    grad_from_cross, _ = norm_back(grad_cross_normed, unit_cross, inverse_cross, gain_cross)
    grad_hidden = grad_mixed + grad_from_cross
    grad_hidden_low = low(grad_hidden)
    text_total = low(kv_near.astype(F32) + after(kv_side, grad_hidden_low).astype(F32))
    hidden_side = to_member(after(grad_hidden_low, text_total), 1)
    hidden_core = to_member(grad_hidden_low, 2)
    left_rows, left_side, mixed_side, text_left = after(
        (left_rows, left_side, mixed_side, text_mine), text_total
    )
    left_near = line_stack(left_rows)[0]
    mixed_parts = right_parts(grad_mixed_low, mixed_side)
    lefts = [left_near, left_side, to_member(left_near, 2), to_member(left_side, 2)]
    text_left = line_columns(text_left)[0]
    share_own, share_far = text_share(
        place, after(text_total, text_left, mixed_parts[1]), w_key_text, w_value_text
    )
    share_own, share_far, hidden_side, lefts = together(share_own, share_far, hidden_side, lefts)
    share_far = to_member(share_far, 2)
    hidden_parts = [grad_hidden_low, hidden_side, hidden_core, to_member(hidden_side, 2)]
    cross_side = to_member(after(grad_cross_low, hidden_side), 1)
    split = width // 4
    small_blocks = small_sums(
        c.reshape(1), lefts, mixed_parts + hidden_parts, text_left, text_total
    )
    small_blocks, share_far = together(small_blocks, share_far)
    small_sum = ring_sum(small_blocks)

    shares = low(share_own + share_far.astype(F32))[None]
    grad_qkv_parts = self_backward(
        table,
        qkv_parts,
        after(hidden_parts, small_blocks, mlp_sum, shares),
        out_parts,
        log_totals,
        w_out,
    )
    grad_qkv_parts, cross_side, shares_two = together(
        grad_qkv_parts, cross_side, across(shares)
    )
    got_grads = [grad_qkv_parts[0]] + [
        to_member(grad_qkv_parts[k], k) for k in range(1, TEAM)
    ]
    cross_parts = right_parts(grad_cross_low, cross_side)
    qkv_products = qkv_products_of(
        c.reshape(1), normed_parts, after(grad_qkv_parts, shares_two), lefts, cross_parts
    )
    shares = jnp.concatenate([shares, shares_two], 0)
    qkv_products, got_grads, shares_two, mlp_across = together(
        qkv_products,
        got_grads,
        move(shares, lambda z, y, x, c: (z ^ 2, y, x, c)),
        across(mlp_sum),
    )
    mlp_send, mlp_keep = side_rows(mlp_sum, mlp_across, block)
    shares = jnp.concatenate([shares, shares_two], 0)
    qkv_sum = ring_sum(qkv_products)
    back_pieces = input_grad(
        turn,
        after(got_grads, small_sum, shares, mlp_keep),
        (w_query, w_key, w_value),
        rows_low,
        gain_self.reshape(1, width),
        grad_hidden,
        block_out,
    )
    back_pieces, mlp_parts = together(
        back_pieces, [to_member(mlp_send, 1), to_member(mlp_keep, 2), to_member(mlp_send, 3)]
    )
    back = [move(back_pieces[step], hand_back(step)) for step in range(LINES)]
    grad_w_in, grad_w_mlp_out, grad_gain_mlp = spread(
        mlp_spread_kernel,
        place,
        [mlp_sum, mlp_across, *mlp_parts],
        [gain_mlp.reshape(1, width)],
        [w_in],
        [(block, hidden_width), (2 * split, width)],
        "mlp_spread",
    )
    grad_w_in, small_across, shares_two = together(
        grad_w_in, across(small_sum), move(shares, lambda z, y, x, c: (z ^ 1, y, x, c))
    )
    small_core, small_far = to_member(small_sum, 2), to_member(small_across, 2)
    near, far = text_choose(owners, jnp.concatenate([shares, shares_two], 0))
    small_all = spread(
        small_spread_kernel,
        place,
        after([small_sum, small_across, small_core, small_far], near),
        [],
        [],
        [(block, width)] * 4,
        "small_spread",
    )
    qkv_done = after(qkv_sum, near)
    small_all, back[0], back[1], text_back, qkv_across = together(
        small_all,
        back[0],
        back[1],
        [near, to_member(near, 1), to_member(far, 2), to_member(far, 3)],
        across(qkv_done),
    )
    qkv_send, qkv_keep = side_rows(qkv_done, qkv_across, 3 * block)
    grad_text = text_place(place, after(text_back, qkv_send, qkv_keep))
    grad_text, back, qkv_parts_back = together(
        grad_text,
        back,
        [to_member(qkv_send, 1), to_member(qkv_keep, 2), to_member(qkv_send, 3)],
    )
    grad_image, out_block = return_place(place, back)
    grad_w_query, grad_w_key, grad_w_value, grad_w_query_text, gain_one, gain_two = spread(
        qkv_spread_kernel,
        place,
        [qkv_done, qkv_across, *qkv_parts_back],
        [gain_self.reshape(1, width), gain_cross.reshape(1, width)],
        [w_query, w_key, w_value, w_query_text],
        [(block, width)] * 4,
        "qkv_spread",
    )
    return (
        out_block,
        grad_image,
        grad_text,
        gain_one.reshape(block),
        grad_w_query,
        grad_w_key,
        grad_w_value,
        small_all[1],
        gain_two.reshape(block),
        grad_w_query_text,
        small_all[2],
        small_all[3],
        small_all[0],
        grad_gain_mlp.reshape(block),
        grad_w_in,
        grad_w_mlp_out,
    )


def solution(mesh):
    placed = (
        P("grp", "row", None),
        P("grp", None, None),
        P(),
        P(),
        P(),
        P(),
        P(),
        P(),
        P(),
        P(),
        P(),
        P(),
        P(),
        P(),
        P(),
        P(),
        P(),
        P("grp", "row", None),
    )
    return jax.shard_map(
        on_device if fits(mesh) else on_device_plain,
        mesh=mesh,
        in_specs=placed,
        out_specs=(
            P("grp", "row", None),
            P("grp", "row", None),
            P("grp", None, None),
            P("row"),
            P("row", None),
            P("row", None),
            P("row", None),
            P("row", None),
            P("row"),
            P("row", None),
            P("row", None),
            P("row", None),
            P("row", None),
            P("row"),
            P("row", None),
            P("row", None),
        ),
        check_vma=False,
    )
```

```python
import functools

import jax
import jax.numpy as jnp
import numpy as np
from jax import lax
from jax.sharding import PartitionSpec as P
from jax.experimental import pallas as pl
from jax.experimental.pallas import tpu as pltpu

HEADS = 16
HEAD_DIM = 64


EPSILON = 1e-05
NEG_LARGE = -1e30
HIGHEST = lax.Precision.HIGHEST


def norm_rows(values, gain):
    center = jnp.mean(values, -1, keepdims=True)
    centered = values - center
    variance = jnp.mean(centered * centered, -1, keepdims=True)
    inverse = lax.rsqrt(variance + EPSILON)
    unit_rows = centered * inverse
    return (unit_rows * gain, unit_rows, inverse)


def norm_back(grad_normed, unit_rows, inverse, gain):
    grad_unit = grad_normed * gain
    first_mean = jnp.mean(grad_unit, -1, keepdims=True)
    second_mean = jnp.mean(grad_unit * unit_rows, -1, keepdims=True)
    grad_input = inverse * (grad_unit - first_mean - unit_rows * second_mean)
    return (grad_input, jnp.sum(grad_normed * unit_rows, 0))


def matmul(left, right):
    return jnp.dot(left, right, preferred_element_type=jnp.float32)


def matmul_left_t(left, right):
    return lax.dot_general(
        left, right, (((0,), (0,)), ((), ())), preferred_element_type=jnp.float32
    )


def matmul_right_t(left, right):
    return lax.dot_general(
        left, right, (((1,), (1,)), ((), ())), preferred_element_type=jnp.float32
    )


def split_heads(values):
    return values.reshape(values.shape[:-1] + (HEADS, HEAD_DIM))


def on_device_plain(
    image_rows,
    text_rows,
    prompt_len,
    prompt_slot,
    gain_self,
    w_query,
    w_key,
    w_value,
    w_out,
    gain_cross,
    w_query_text,
    w_key_text,
    w_value_text,
    w_out_text,
    gain_mlp,
    w_in,
    w_mlp_out,
    grad_out,
):
    images_here, rows_here, width = image_rows.shape
    prompt_rows = text_rows.shape[1]
    row_count = lax.axis_size("row")
    length = rows_here * row_count
    row_index = lax.axis_index("row")
    group_index = lax.axis_index("grp")
    scale_factor = HEAD_DIM ** (-0.5)
    block_size = min(512, length)
    block_count = length // block_size
    flat_rows = images_here * rows_here
    inputs = image_rows.astype(jnp.float32).reshape(flat_rows, width)
    normed_self, unit_self, inverse_self = norm_rows(inputs, gain_self)
    normed_low = normed_self.astype(jnp.bfloat16)
    query_low = (
        matmul(normed_low, w_query).astype(jnp.bfloat16).reshape(images_here, rows_here, width)
    )
    key_low = matmul(normed_low, w_key).astype(jnp.bfloat16).reshape(images_here, rows_here, width)
    value_low = (
        matmul(normed_low, w_value).astype(jnp.bfloat16).reshape(images_here, rows_here, width)
    )
    keys_all, values_all = (
        lax.all_gather(key_low, "row", axis=1, tiled=True),
        lax.all_gather(value_low, "row", axis=1, tiled=True),
    )
    query_heads = split_heads(query_low)
    query_pos = row_index * rows_here + jnp.arange(rows_here, dtype=jnp.int32)
    key_pos = jnp.arange(length, dtype=jnp.int32)
    causal = key_pos[None, :] <= query_pos[:, None]
    contexts = []
    totals = []
    for each_image in range(images_here):
        scores = (
            jnp.einsum(
                "qhd,khd->hqk",
                query_heads[each_image],
                split_heads(keys_all[each_image]),
                preferred_element_type=jnp.float32,
            )
            * scale_factor
        )
        scores = jnp.where(causal[None], scores, NEG_LARGE)
        largest = jnp.max(scores, -1, keepdims=True)
        expos = jnp.exp(scores - largest)
        denominator = jnp.sum(expos, -1, keepdims=True)
        probs_low = (expos / denominator).astype(jnp.bfloat16)
        contexts.append(
            jnp.einsum(
                "hqk,khd->qhd",
                probs_low,
                split_heads(values_all[each_image]),
                preferred_element_type=jnp.float32,
            )
        )
        totals.append((largest + jnp.log(denominator))[..., 0])
    context = jnp.stack(contexts).reshape(flat_rows, width)
    log_totals = jnp.stack(totals)
    context_low = context.astype(jnp.bfloat16)
    hidden = inputs + matmul(context_low, w_out)
    normed_cross, unit_cross, inverse_cross = norm_rows(hidden, gain_cross)
    cross_normed_low = normed_cross.astype(jnp.bfloat16)
    cross_low = (
        matmul(cross_normed_low, w_query_text)
        .astype(jnp.bfloat16)
        .reshape(images_here, rows_here, HEADS, HEAD_DIM)
    )
    text_flat = text_rows.reshape(-1, width)
    text_key = matmul(text_flat, w_key_text).astype(jnp.bfloat16).reshape(text_rows.shape)
    text_value = matmul(text_flat, w_value_text).astype(jnp.bfloat16).reshape(text_rows.shape)
    text_keys, text_values = (
        lax.all_gather(text_key, "grp", axis=0, tiled=True),
        lax.all_gather(text_value, "grp", axis=0, tiled=True),
    )
    image_total = prompt_slot.shape[0]
    slots = lax.dynamic_slice_in_dim(prompt_slot, group_index * images_here, images_here)
    keys_sel = split_heads(jnp.take(text_keys, slots, axis=0))
    values_sel = split_heads(jnp.take(text_values, slots, axis=0))
    lengths_sel = jnp.take(prompt_len, slots)
    text_mask = (jnp.arange(prompt_rows, dtype=jnp.int32)[None, :] < lengths_sel[:, None])[
        :, None, None, :
    ]
    cross_scores = (
        jnp.einsum("iqhd,ikhd->ihqk", cross_low, keys_sel, preferred_element_type=jnp.float32)
        * scale_factor
    )
    cross_probs = jax.nn.softmax(jnp.where(text_mask, cross_scores, NEG_LARGE), axis=-1)
    cross_probs_low = cross_probs.astype(jnp.bfloat16)
    cross_context = jnp.einsum(
        "ihqk,ikhd->iqhd", cross_probs_low, values_sel, preferred_element_type=jnp.float32
    )
    cross_context_low = cross_context.reshape(flat_rows, width).astype(jnp.bfloat16)
    mixed = hidden + matmul(cross_context_low, w_out_text)
    normed_mlp, unit_mlp, inverse_mlp = norm_rows(mixed, gain_mlp)
    mlp_low = normed_mlp.astype(jnp.bfloat16)
    pre_act = matmul(mlp_low, w_in)
    activated, gelu_back = jax.vjp(jax.nn.gelu, pre_act)
    activated_low = activated.astype(jnp.bfloat16)
    block_out = mixed + matmul(activated_low, w_mlp_out)
    out_block = block_out.astype(jnp.bfloat16).reshape(image_rows.shape)
    grad_low = grad_out.reshape(flat_rows, width)
    grad_w_mlp_out = matmul_left_t(activated_low, grad_low)
    grad_activated = matmul_right_t(grad_low, w_mlp_out)
    grad_pre_low = gelu_back(grad_activated)[0].astype(jnp.bfloat16)
    grad_w_in = matmul_left_t(mlp_low, grad_pre_low)
    grad_mlp_normed = matmul_right_t(grad_pre_low, w_in)
    grad_from_mlp, grad_gain_mlp = norm_back(grad_mlp_normed, unit_mlp, inverse_mlp, gain_mlp)
    grad_mixed = grad_low.astype(jnp.float32) + grad_from_mlp
    grad_mixed_low = grad_mixed.astype(jnp.bfloat16)
    grad_w_out_text = matmul_left_t(cross_context_low, grad_mixed_low)
    grad_cross_ctx = split_heads(
        matmul_right_t(grad_mixed_low, w_out_text)
        .astype(jnp.bfloat16)
        .reshape(images_here, rows_here, width)
    )
    grad_cross_probs = jnp.einsum(
        "iqhd,ikhd->ihqk", grad_cross_ctx, values_sel, preferred_element_type=jnp.float32
    )
    grad_values_sel = jnp.einsum(
        "ihqk,iqhd->ikhd", cross_probs_low, grad_cross_ctx, preferred_element_type=jnp.float32
    )
    grad_cross_scores = cross_probs * (
        grad_cross_probs - jnp.sum(cross_probs * grad_cross_probs, -1, keepdims=True)
    )
    grad_scores_low = grad_cross_scores.astype(jnp.bfloat16)
    grad_cross_query = (
        jnp.einsum("ihqk,ikhd->iqhd", grad_scores_low, keys_sel, preferred_element_type=jnp.float32)
        * scale_factor
    )
    grad_cross_query_low = grad_cross_query.astype(jnp.bfloat16).reshape(flat_rows, width)
    grad_keys_sel = (
        jnp.einsum(
            "ihqk,iqhd->ikhd", grad_scores_low, cross_low, preferred_element_type=jnp.float32
        )
        * scale_factor
    )
    grad_w_query_text = matmul_left_t(cross_normed_low, grad_cross_query_low)
    grad_cross_normed = matmul_right_t(grad_cross_query_low, w_query_text)
    grad_from_cross, grad_gain_cross = norm_back(
        grad_cross_normed, unit_cross, inverse_cross, gain_cross
    )
    grad_hidden = grad_mixed + grad_from_cross
    placing = (jnp.arange(image_total, dtype=jnp.int32)[:, None] == slots[None, :]).astype(
        jnp.float32
    )
    joined_text = jnp.concatenate(
        [
            grad_keys_sel.reshape(images_here, prompt_rows, width),
            grad_values_sel.reshape(images_here, prompt_rows, width),
        ],
        -1,
    )
    text_term = jnp.einsum("si,ipd->spd", placing, joined_text, precision=HIGHEST)
    text_grad = lax.psum_scatter(
        text_term.astype(jnp.bfloat16), "grp", scatter_dimension=0, tiled=True
    )
    share_rows = text_flat.shape[0] // row_count
    text_total = (
        lax.psum(text_grad, "row").astype(jnp.float32).reshape(-1, 2 * width).astype(jnp.bfloat16)
    )
    text_share = lax.dynamic_slice_in_dim(text_total, row_index * share_rows, share_rows, 0)
    text_grad_rows = (
        matmul_right_t(text_total[:, :width], w_key_text)
        + matmul_right_t(text_total[:, width:], w_value_text)
    ).astype(jnp.bfloat16)
    text_part = lax.dynamic_slice_in_dim(text_flat, row_index * share_rows, share_rows, 0)
    grad_w_key_text = matmul_left_t(text_part, text_share[:, :width])
    grad_w_value_text = matmul_left_t(text_part, text_share[:, width:])
    grad_text = text_grad_rows.reshape(text_rows.shape)
    grad_hidden_low = grad_hidden.astype(jnp.bfloat16)
    grad_w_out = matmul_left_t(context_low, grad_hidden_low)
    grad_context = (
        matmul_right_t(grad_hidden_low, w_out)
        .astype(jnp.bfloat16)
        .reshape(images_here, rows_here, width)
    )
    grad_context_heads = split_heads(grad_context)
    context_heads = split_heads(context.reshape(images_here, rows_here, width))
    delta = jnp.einsum(
        "iqhd,iqhd->ihq", grad_context_heads.astype(jnp.float32), context_heads, precision=HIGHEST
    )
    zero_query = jnp.zeros((images_here, rows_here, HEADS, HEAD_DIM), jnp.float32)

    def block_terms(block):
        start = block * block_size
        key_heads = split_heads(lax.dynamic_slice_in_dim(keys_all, start, block_size, 1))
        value_heads = split_heads(lax.dynamic_slice_in_dim(values_all, start, block_size, 1))
        block_pos = start + jnp.arange(block_size, dtype=jnp.int32)
        allowed = (block_pos[None, :] <= query_pos[:, None])[None, None]
        scores = (
            jnp.einsum(
                "iqhd,ikhd->ihqk", query_heads, key_heads, preferred_element_type=jnp.float32
            )
            * scale_factor
        )
        probs = jnp.where(allowed, jnp.exp(scores - log_totals[..., None]), 0.0)
        grad_probs = jnp.einsum(
            "iqhd,ikhd->ihqk", grad_context_heads, value_heads, preferred_element_type=jnp.float32
        )
        grad_scores = (probs * (grad_probs - delta[..., None])).astype(jnp.bfloat16)
        return (grad_scores, probs.astype(jnp.bfloat16), key_heads)

    def step_keys(block, carry):
        grad_query, term_buffer = carry
        grad_scores, probs_low, key_heads = block_terms(block)
        grad_query = (
            grad_query
            + jnp.einsum(
                "ihqk,ikhd->iqhd", grad_scores, key_heads, preferred_element_type=jnp.float32
            )
            * scale_factor
        )
        grad_key_part = (
            jnp.einsum(
                "ihqk,iqhd->ikhd", grad_scores, query_heads, preferred_element_type=jnp.float32
            )
            * scale_factor
        )
        grad_value_part = jnp.einsum(
            "ihqk,iqhd->ikhd", probs_low, grad_context_heads, preferred_element_type=jnp.float32
        )
        joined = jnp.concatenate(
            [
                grad_key_part.reshape(images_here, block_size, width),
                grad_value_part.reshape(images_here, block_size, width),
            ],
            -1,
        )
        term_buffer = lax.dynamic_update_slice_in_dim(term_buffer, joined, block * block_size, 1)
        return (grad_query, term_buffer)

    start_buffer = jnp.zeros((images_here, length, 2 * width), jnp.float32)
    grad_query, term_buffer = lax.fori_loop(0, block_count, step_keys, (zero_query, start_buffer))
    grad_kv = lax.psum_scatter(
        term_buffer.astype(jnp.bfloat16), "row", scatter_dimension=1, tiled=True
    ).astype(jnp.float32)
    grad_query_low = grad_query.reshape(flat_rows, width).astype(jnp.bfloat16)
    grad_kv_low = grad_kv.reshape(flat_rows, 2 * width).astype(jnp.bfloat16)
    grad_w_query = matmul_left_t(normed_low, grad_query_low)
    grad_w_key = matmul_left_t(normed_low, grad_kv_low[:, :width])
    grad_w_value = matmul_left_t(normed_low, grad_kv_low[:, width:])
    grad_normed_self = (
        matmul_right_t(grad_query_low, w_query)
        + matmul_right_t(grad_kv_low[:, :width], w_key)
        + matmul_right_t(grad_kv_low[:, width:], w_value)
    )
    grad_from_self, grad_gain_self = norm_back(grad_normed_self, unit_self, inverse_self, gain_self)
    grad_image = (grad_hidden + grad_from_self).astype(jnp.bfloat16).reshape(image_rows.shape)
    shares = (
        lax.psum_scatter(
            grad_gain_self.astype(jnp.bfloat16), "row", scatter_dimension=0, tiled=True
        ).astype(jnp.float32),
        lax.psum_scatter(
            grad_w_query.astype(jnp.bfloat16), "row", scatter_dimension=0, tiled=True
        ).astype(jnp.float32),
        lax.psum_scatter(
            grad_w_key.astype(jnp.bfloat16), "row", scatter_dimension=0, tiled=True
        ).astype(jnp.float32),
        lax.psum_scatter(
            grad_w_value.astype(jnp.bfloat16), "row", scatter_dimension=0, tiled=True
        ).astype(jnp.float32),
        lax.psum_scatter(
            grad_w_out.astype(jnp.bfloat16), "row", scatter_dimension=0, tiled=True
        ).astype(jnp.float32),
        lax.psum_scatter(
            grad_gain_cross.astype(jnp.bfloat16), "row", scatter_dimension=0, tiled=True
        ).astype(jnp.float32),
        lax.psum_scatter(
            grad_w_query_text.astype(jnp.bfloat16), "row", scatter_dimension=0, tiled=True
        ).astype(jnp.float32),
        lax.psum_scatter(
            grad_w_key_text.astype(jnp.bfloat16), "row", scatter_dimension=0, tiled=True
        ).astype(jnp.float32),
        lax.psum_scatter(
            grad_w_value_text.astype(jnp.bfloat16), "row", scatter_dimension=0, tiled=True
        ).astype(jnp.float32),
        lax.psum_scatter(
            grad_w_out_text.astype(jnp.bfloat16), "row", scatter_dimension=0, tiled=True
        ).astype(jnp.float32),
        lax.psum_scatter(
            grad_gain_mlp.astype(jnp.bfloat16), "row", scatter_dimension=0, tiled=True
        ).astype(jnp.float32),
        lax.psum_scatter(
            grad_w_in.astype(jnp.bfloat16), "row", scatter_dimension=0, tiled=True
        ).astype(jnp.float32),
        lax.psum_scatter(
            grad_w_mlp_out.astype(jnp.bfloat16), "row", scatter_dimension=0, tiled=True
        ).astype(jnp.float32),
    )
    summed = (
        lax.psum(shares[0].astype(jnp.bfloat16), "grp").astype(jnp.float32),
        lax.psum(shares[1].astype(jnp.bfloat16), "grp").astype(jnp.float32),
        lax.psum(shares[2].astype(jnp.bfloat16), "grp").astype(jnp.float32),
        lax.psum(shares[3].astype(jnp.bfloat16), "grp").astype(jnp.float32),
        lax.psum(shares[4].astype(jnp.bfloat16), "grp").astype(jnp.float32),
        lax.psum(shares[5].astype(jnp.bfloat16), "grp").astype(jnp.float32),
        lax.psum(shares[6].astype(jnp.bfloat16), "grp").astype(jnp.float32),
        lax.psum(shares[7].astype(jnp.bfloat16), "grp").astype(jnp.float32),
        lax.psum(shares[8].astype(jnp.bfloat16), "grp").astype(jnp.float32),
        lax.psum(shares[9].astype(jnp.bfloat16), "grp").astype(jnp.float32),
        lax.psum(shares[10].astype(jnp.bfloat16), "grp").astype(jnp.float32),
        lax.psum(shares[11].astype(jnp.bfloat16), "grp").astype(jnp.float32),
        lax.psum(shares[12].astype(jnp.bfloat16), "grp").astype(jnp.float32),
    )
    return (
        out_block,
        grad_image,
        grad_text,
        summed[0],
        summed[1],
        summed[2],
        summed[3],
        summed[4],
        summed[5],
        summed[6],
        summed[7],
        summed[8],
        summed[9],
        summed[10],
        summed[11],
        summed[12],
    )


AXES = ("row", "grp")
SMALL_COST = pl.CostEstimate(flops=0, bytes_accessed=0, transcendentals=0)
BF16 = jnp.bfloat16
F32 = jnp.float32
TEAM = 4
LINES = 4


def fits(mesh):
    return mesh.shape["row"] == 2 * LINES and mesh.shape["grp"] == 4


def moves(change):
    pairs = []
    for place in range(32):
        z, y, x, c = place // 8, place // 4 % 2, place // 2 % 2, place % 2
        z2, y2, x2, c2 = change(z, y, x, c)
        pairs.append((place, z2 * 8 + y2 * 4 + x2 * 2 + c2))
    return pairs


def move(values, change):
    return lax.ppermute(values, AXES, moves(change))


def to_member(values, member):
    flip_y, flip_c = member & 1, member >> 1
    return move(values, lambda z, y, x, c: (z, y ^ flip_y, x, c ^ flip_c))


def team_gather(values):
    side = to_member(values, 1)
    return [values, side, to_member(values, 2), to_member(side, 2)]


def hand_out(step):
    def change(z, y, x, c):
        which = z ^ step
        return (2 * c + (which & 1), y, x, which >> 1)

    return change


def hand_back(step):
    def change(z, y, x, c):
        return (step ^ ((z & 1) | (c << 1)), y, x, z >> 1)

    return change


def ring_groups():
    order = [(0, 0), (0, 1), (0, 2), (0, 3), (1, 3), (1, 2), (1, 1), (1, 0)]
    return [
        [z * 8 + y * 4 + x * 2 + c for x, z in order] for y in range(2) for c in range(2)
    ]


def line_groups():
    return [[z * 8 + place for z in range(LINES)] for place in range(8)]


def ring_sum(blocks):
    flat = blocks.reshape(-1, blocks.shape[-1])
    return lax.psum_scatter(
        flat, AXES, scatter_dimension=0, axis_index_groups=ring_groups(), tiled=True
    )


def lane_mask(rows, head):
    lane = lax.broadcasted_iota(jnp.int32, (rows, 128), 1)
    return (lane >= HEAD_DIM) if head else (lane < HEAD_DIM)


def only(values, head):
    return jnp.where(lane_mask(values.shape[0], head), values, jnp.zeros_like(values))


def dot_nt(left, right):
    return lax.dot_general(
        left, right, (((1,), (1,)), ((), ())), preferred_element_type=F32
    )


def dot_nn(left, right):
    return lax.dot_general(
        left, right, (((1,), (0,)), ((), ())), preferred_element_type=F32
    )


def dot_tn(left, right):
    return lax.dot_general(
        left, right, (((0,), (0,)), ((), ())), preferred_element_type=F32
    )


CHUNK = 64


def self_forward_kernel(table, *refs):
    parts, outs, lse_ref = refs[:TEAM], refs[TEAM : 2 * TEAM], refs[2 * TEAM]
    all_qkv, all_out = refs[2 * TEAM + 1 :]
    length, heads_width = all_out.shape
    chunks = parts[0].shape[0] // CHUNK
    for member in range(TEAM):
        for piece in range(chunks):
            at = pl.multiple_of(table[member * chunks + piece] * CHUNK, CHUNK)
            all_qkv[pl.ds(at, CHUNK), :] = parts[member][piece * CHUNK : (piece + 1) * CHUNK, :]
    block = 256
    pairs = heads_width // 128
    scale_factor = HEAD_DIM ** (-0.5)
    diagonal = lax.broadcasted_iota(jnp.int32, (block, block), 1) <= lax.broadcasted_iota(
        jnp.int32, (block, block), 0
    )
    for pair in range(pairs):
        q_cols = slice(128 * pair, 128 * pair + 128)
        k_cols = slice(heads_width + 128 * pair, heads_width + 128 * pair + 128)
        v_cols = slice(2 * heads_width + 128 * pair, 2 * heads_width + 128 * pair + 128)
        for block_at in range(length // block):
            rows = slice(block * block_at, block * (block_at + 1))
            q_block = all_qkv[rows, q_cols]
            joined = jnp.zeros((block, 128), F32)
            for head in range(2):
                q_one = only(q_block, head)
                near = dot_nt(q_one, all_qkv[rows, k_cols]) * scale_factor
                near = jnp.where(diagonal, near, NEG_LARGE)
                scores = near
                if block_at:
                    far = dot_nt(q_one, all_qkv[0 : block * block_at, k_cols]) * scale_factor
                    scores = jnp.concatenate([far, near], 1)
                largest = jnp.max(scores, -1, keepdims=True)
                expos = jnp.exp(scores - largest)
                denominator = jnp.sum(expos, -1, keepdims=True)
                probs_low = (expos / denominator).astype(BF16)
                mixed = dot_nn(probs_low, all_qkv[0 : block * (block_at + 1), v_cols])
                joined = jnp.where(lane_mask(block, head), mixed, joined)
                total = largest + jnp.log(denominator)
                lse_ref[2 * pair + head : 2 * pair + head + 1, rows] = jnp.transpose(
                    jnp.broadcast_to(total, (block, 128))
                )[0:1, :]
            all_out[rows, q_cols] = joined.astype(BF16)
    for member in range(TEAM):
        for piece in range(chunks):
            at = pl.multiple_of(table[member * chunks + piece] * CHUNK, CHUNK)
            outs[member][piece * CHUNK : (piece + 1) * CHUNK, :] = all_out[pl.ds(at, CHUNK), :]


def in_vmem(count):
    return [pl.BlockSpec(memory_space=pltpu.VMEM)] * count


def self_forward(table, parts):
    rows, width = parts[0].shape
    heads_width, length = width // 3, rows * TEAM
    outs = pl.pallas_call(
        self_forward_kernel,
        in_specs=[pl.BlockSpec(memory_space=pltpu.SMEM)] + in_vmem(TEAM),
        out_specs=in_vmem(TEAM + 1),
        out_shape=[jax.ShapeDtypeStruct((rows, heads_width), BF16)] * TEAM
        + [jax.ShapeDtypeStruct((8, length), F32)],
        scratch_shapes=[
            pltpu.VMEM((length, width), BF16),
            pltpu.VMEM((length, heads_width), BF16),
        ],
        name="self_forward",
        cost_estimate=SMALL_COST,
    )(table, *parts)
    return outs[:TEAM], outs[TEAM]


def self_backward_kernel(table, *refs):
    parts, hidden, oparts = refs[:TEAM], refs[TEAM : 2 * TEAM], refs[2 * TEAM : 3 * TEAM]
    lse_ref, w_ref = refs[3 * TEAM : 3 * TEAM + 2]
    outs = refs[3 * TEAM + 2 : 4 * TEAM + 2]
    all_qkv, all_do, delta_ref, sum_q, sum_k, sum_v = refs[4 * TEAM + 2 :]
    length, heads_width = all_do.shape
    chunks = parts[0].shape[0] // CHUNK
    head_row = lax.broadcasted_iota(jnp.int32, (8, heads_width), 0)
    head_col = lax.broadcasted_iota(jnp.int32, (8, heads_width), 1) // HEAD_DIM
    pick = (head_row == head_col).astype(F32)
    block = 256
    for member in range(TEAM):
        grad_out = dot_nt(hidden[member][...], w_ref[...]).astype(BF16)
        products = grad_out.astype(F32) * oparts[member][...].astype(F32)
        for piece in range(chunks):
            at = pl.multiple_of(table[member * chunks + piece] * CHUNK, CHUNK)
            here = slice(piece * CHUNK, (piece + 1) * CHUNK)
            all_qkv[pl.ds(at, CHUNK), :] = parts[member][here, :]
            all_do[pl.ds(at, CHUNK), :] = grad_out[here, :]
            sum_q[pl.ds(at, CHUNK), :] = products[here, :]
    for block_at in range(length // block):
        rows = slice(block * block_at, block * (block_at + 1))
        delta_ref[:, rows] = lax.dot_general(
            pick,
            sum_q[rows, :],
            (((1,), (1,)), ((), ())),
            precision=HIGHEST,
            preferred_element_type=F32,
        )
    pairs = heads_width // 128
    scale_factor = HEAD_DIM ** (-0.5)
    diagonal = lax.broadcasted_iota(jnp.int32, (block, block), 0) <= lax.broadcasted_iota(
        jnp.int32, (block, block), 1
    )
    for pair in range(pairs):
        q_cols = slice(128 * pair, 128 * pair + 128)
        k_cols = slice(heads_width + 128 * pair, heads_width + 128 * pair + 128)
        v_cols = slice(2 * heads_width + 128 * pair, 2 * heads_width + 128 * pair + 128)
        for block_at in range(length // block):
            rows = slice(block * block_at, block * (block_at + 1))
            seen = slice(0, block * (block_at + 1))
            q_block = all_qkv[rows, q_cols]
            do_block = all_do[rows, q_cols]
            sum_q_block = jnp.zeros((block, 128), F32)
            for head in range(2):
                q_one, do_one = only(q_block, head), only(do_block, head)
                total = lse_ref[2 * pair + head : 2 * pair + head + 1, rows]
                delta = delta_ref[2 * pair + head : 2 * pair + head + 1, rows]
                scores = dot_nt(all_qkv[seen, k_cols], q_one) * scale_factor
                probs = jnp.exp(scores - total)
                near = jnp.where(diagonal, probs[block * block_at :, :], 0.0)
                if block_at:
                    probs = jnp.concatenate([probs[: block * block_at, :], near], 0)
                else:
                    probs = near
                grad_probs = dot_nt(all_qkv[seen, v_cols], do_one)
                grad_scores = (probs * (grad_probs - delta)).astype(BF16)
                term_v = dot_nn(probs.astype(BF16), do_one)
                term_k = dot_nn(grad_scores, q_one) * scale_factor
                if head == 0:
                    term_v_both, term_k_both = term_v, term_k
                else:
                    term_v_both, term_k_both = term_v_both + term_v, term_k_both + term_k
                term_q = dot_tn(grad_scores, all_qkv[seen, k_cols]) * scale_factor
                sum_q_block = jnp.where(lane_mask(block, head), term_q, sum_q_block)
            sum_q[rows, q_cols] = sum_q_block
            if block_at:
                before = slice(0, block * block_at)
                sum_k[before, q_cols] += term_k_both[before, :]
                sum_v[before, q_cols] += term_v_both[before, :]
            sum_k[rows, q_cols] = term_k_both[block * block_at :, :]
            sum_v[rows, q_cols] = term_v_both[block * block_at :, :]
    for member in range(TEAM):
        for piece in range(chunks):
            at = pl.multiple_of(table[member * chunks + piece] * CHUNK, CHUNK)
            here = slice(piece * CHUNK, (piece + 1) * CHUNK)
            outs[member][here, 0:heads_width] = sum_q[pl.ds(at, CHUNK), :].astype(BF16)
            outs[member][here, heads_width : 2 * heads_width] = sum_k[
                pl.ds(at, CHUNK), :
            ].astype(BF16)
            outs[member][here, 2 * heads_width : 3 * heads_width] = sum_v[
                pl.ds(at, CHUNK), :
            ].astype(BF16)


def whole_spec(values):
    return pl.BlockSpec(values.shape, lambda *_: (0,) * len(values.shape))


def self_backward(table, parts, hidden, oparts, lse, w_out):
    rows, width = parts[0].shape
    heads_width, length = width // 3, rows * TEAM
    last = TEAM * LINES
    out = jax.ShapeDtypeStruct((rows, width), BF16)
    return pl.pallas_call(
        self_backward_kernel,
        grid_spec=pltpu.PrefetchScalarGridSpec(
            num_scalar_prefetch=1,
            grid=(1,),
            in_specs=[whole_spec(v) for v in (*parts, *hidden, *oparts, lse)]
            + [pl.BlockSpec((heads_width, w_out.shape[1]), lambda i, t: (t[last], 0))],
            out_specs=[whole_spec(out)] * TEAM,
            scratch_shapes=[
                pltpu.VMEM((length, width), BF16),
                pltpu.VMEM((length, heads_width), BF16),
                pltpu.VMEM((8, length), F32),
                pltpu.VMEM((length, heads_width), F32),
                pltpu.VMEM((length, heads_width), F32),
                pltpu.VMEM((length, heads_width), F32),
            ],
        ),
        out_shape=[out] * TEAM,
        name="self_backward",
        cost_estimate=SMALL_COST,
    )(table, *parts, *hidden, *oparts, lse, w_out)


def cross_probs_of(query_one, key_pair, allowed):
    scores = dot_nt(query_one, key_pair) * HEAD_DIM ** (-0.5)
    scores = jnp.where(allowed, scores, NEG_LARGE)
    expos = jnp.exp(scores - jnp.max(scores, -1, keepdims=True))
    return expos / jnp.sum(expos, -1, keepdims=True)


def cross_forward_kernel(count, c_ref, k_ref, v_ref, o_ref):
    rows, width = c_ref.shape
    allowed = lax.broadcasted_iota(jnp.int32, (rows, k_ref.shape[0]), 1) < count[0]
    for pair in range(width // 128):
        cols = slice(128 * pair, 128 * pair + 128)
        joined = jnp.zeros((rows, 128), F32)
        for head in range(2):
            probs = cross_probs_of(only(c_ref[:, cols], head), k_ref[:, cols], allowed)
            mixed = dot_nn(probs.astype(BF16), v_ref[:, cols])
            joined = jnp.where(lane_mask(rows, head), mixed, joined)
        o_ref[:, cols] = joined.astype(BF16)


def cross_forward(count, cross, keys, values):
    return pl.pallas_call(
        cross_forward_kernel,
        in_specs=[pl.BlockSpec(memory_space=pltpu.SMEM)] + in_vmem(3),
        out_specs=pl.BlockSpec(memory_space=pltpu.VMEM),
        out_shape=jax.ShapeDtypeStruct(cross.shape, BF16),
        name="cross_forward",
        cost_estimate=SMALL_COST,
    )(count, cross, keys, values)


def cross_backward_kernel(count, c_ref, k_ref, v_ref, do_ref, dc_ref, near_ref, far_ref):
    rows, width = c_ref.shape
    half = width // 2
    scale_factor = HEAD_DIM ** (-0.5)
    allowed = lax.broadcasted_iota(jnp.int32, (rows, k_ref.shape[0]), 1) < count[0]

    @pl.loop(0, width // 128)
    def _(step):
        for at in range(1):
            first = (step + at) * 128
            cols = pl.ds(pl.multiple_of(first, 128), 128)
            joined = jnp.zeros((rows, 128), F32)
            sum_k = jnp.zeros((k_ref.shape[0], 128), F32)
            sum_v = jnp.zeros((k_ref.shape[0], 128), F32)
            for head in range(2):
                c_one, do_one = only(c_ref[:, cols], head), only(do_ref[:, cols], head)
                probs = cross_probs_of(c_one, k_ref[:, cols], allowed)
                grad_probs = dot_nt(do_one, v_ref[:, cols])
                inner = jnp.sum(probs * grad_probs, -1, keepdims=True)
                grad_scores = (probs * (grad_probs - inner)).astype(BF16)
                term_c = dot_nn(grad_scores, k_ref[:, cols]) * scale_factor
                joined = jnp.where(lane_mask(rows, head), term_c, joined)
                sum_k += dot_tn(grad_scores, c_one) * scale_factor
                sum_v += dot_tn(probs.astype(BF16), do_one)
            dc_ref[:, cols] = joined.astype(BF16)
            side = (first >= half).astype(jnp.int32)
            within = first - half * side
            key_cols = pl.ds(pl.multiple_of(within, 128), 128)
            value_cols = pl.ds(pl.multiple_of(half + within, 128), 128)

            def keep(ref, sums=(sum_k, sum_v), cols=(key_cols, value_cols)):
                for values, where in zip(sums, cols):
                    ref[:, where] = values.astype(BF16)

            pl.when(count[1] == side)(functools.partial(keep, near_ref))
            pl.when(count[1] != side)(functools.partial(keep, far_ref))


def cross_backward(count, cross, keys, values, grad_ctx):
    side = jax.ShapeDtypeStruct((keys.shape[0], cross.shape[1]), BF16)
    return pl.pallas_call(
        cross_backward_kernel,
        in_specs=[pl.BlockSpec(memory_space=pltpu.SMEM)] + in_vmem(4),
        out_specs=in_vmem(3),
        out_shape=[jax.ShapeDtypeStruct(cross.shape, BF16), side, side],
        name="cross_backward",
        cost_estimate=SMALL_COST,
    )(count, cross, keys, values, grad_ctx)


GELU_SCALE = (2.0 / jnp.pi) ** 0.5
GELU_CUBE = 0.044715


def gelu_both(values):
    square = values * values
    slope = jnp.tanh(GELU_SCALE * (values + GELU_CUBE * (square * values)))
    half_up = 0.5 * (1.0 + slope)
    steep = GELU_SCALE * (1.0 + 3.0 * GELU_CUBE * square)
    return (values * half_up, half_up + 0.5 * values * (1.0 - slope * slope) * steep)


def norm_back_rows(grad_normed, values, gain):
    centered = values - jnp.mean(values, -1, keepdims=True)
    inverse = lax.rsqrt(jnp.mean(centered * centered, -1, keepdims=True) + EPSILON)
    unit_rows = centered * inverse
    grad_unit = grad_normed * gain
    first_mean = jnp.mean(grad_unit, -1, keepdims=True)
    second_mean = jnp.mean(grad_unit * unit_rows, -1, keepdims=True)
    return inverse * (grad_unit - first_mean - unit_rows * second_mean)


def sort_chunks(table, first, count, source, target):
    for piece in range(count):
        at = pl.multiple_of(table[first + piece] * CHUNK, CHUNK)
        target[piece * CHUNK : (piece + 1) * CHUNK, :] = source[pl.ds(at, CHUNK), :]


def mlp_rows_kernel(
    table, m_ref, g_ref, mixed_ref, gain_ref, in_ref, out_ref, *refs
):
    block_refs, (grad_ref, low_ref, total, back, grad_rows) = refs[:LINES], refs[LINES:]
    step = pl.program_id(0)

    @pl.when(step == 0)
    def _():
        sort_chunks(table, 0, LINES, g_ref, grad_rows)

    block = in_ref.shape[1]
    acts, grads = [], []
    for first in (0, block // 2):
        here = slice(first, first + block // 2)
        activated, slope = gelu_both(dot_nn(m_ref[...], in_ref[:, here]))
        acts.append(activated.astype(BF16))
        grads.append((dot_nt(grad_rows[...], out_ref[here, :]) * slope).astype(BF16))
    term = dot_nn(jnp.concatenate(acts, 1), out_ref[...])
    back_term = dot_nt(jnp.concatenate(grads, 1), in_ref[...])

    @pl.when(step == 0)
    def _():
        total[...] = mixed_ref[...] + term
        back[...] = back_term

    @pl.when(step > 0)
    def _():
        total[...] += term
        back[...] += back_term

    @pl.when(step == pl.num_programs(0) - 1)
    def _():
        for line in range(LINES):
            block_refs[line][...] = total[line * CHUNK : (line + 1) * CHUNK, :].astype(BF16)
        grad_mixed = grad_rows[...].astype(F32) + norm_back_rows(
            back[...], mixed_ref[...], gain_ref[...]
        )
        grad_ref[...] = grad_mixed
        low_ref[...] = grad_mixed.astype(BF16)


def mlp_rows(table, mlp_low, grad_low, mixed, gain, w_in, w_mlp_out):
    rows, width = mlp_low.shape
    hidden_width = w_in.shape[1]
    block = hidden_width // LINES
    whole = pl.BlockSpec((rows, width), lambda i, t: (0, 0))
    return pl.pallas_call(
        mlp_rows_kernel,
        grid_spec=pltpu.PrefetchScalarGridSpec(
            num_scalar_prefetch=1,
            grid=(hidden_width // block,),
            in_specs=[
                whole,
                pl.BlockSpec(grad_low.shape, lambda i, t: (0, 0)),
                whole,
                pl.BlockSpec((1, width), lambda i, t: (0, 0)),
                pl.BlockSpec((width, block), lambda i, t: (0, i)),
                pl.BlockSpec((block, width), lambda i, t: (i, 0)),
            ],
            out_specs=[pl.BlockSpec((rows // LINES, width), lambda i, t: (0, 0))] * LINES
            + [whole, whole],
            scratch_shapes=[
                pltpu.VMEM((rows, width), F32),
                pltpu.VMEM((rows, width), F32),
                pltpu.VMEM((rows, width), BF16),
            ],
        ),
        out_shape=[jax.ShapeDtypeStruct((rows // LINES, width), BF16)] * LINES
        + [
            jax.ShapeDtypeStruct((rows, width), F32),
            jax.ShapeDtypeStruct((rows, width), BF16),
        ],
        name="mlp_rows",
        cost_estimate=SMALL_COST,
    )(table, mlp_low, grad_low, mixed, gain, w_in, w_mlp_out)


def mlp_team_kernel(table, *refs):
    parts, grad_parts = refs[:TEAM], refs[TEAM : 2 * TEAM]
    in_ref, out_ref, sum_ref, m_all, g_all = refs[2 * TEAM :]
    step = pl.program_id(0)
    block = in_ref.shape[1]
    rows = parts[0].shape[0]

    @pl.when(step == 0)
    def _():
        for member in range(TEAM):
            here = pl.ds(member * rows, rows)
            sort_chunks(table, 1 + member * LINES, LINES, grad_parts[member], g_all.at[here])
            m_all[here, :] = parts[member][...]

    activated, slope = gelu_both(dot_nn(m_all[...], in_ref[...]))
    grad_pre = (dot_nt(g_all[...], out_ref[...]) * slope).astype(BF16)
    part_in = dot_tn(m_all[...], grad_pre).astype(BF16)
    part_out = dot_tn(activated.astype(BF16), g_all[...]).astype(BF16)
    right = step // 2
    cols = pl.ds(pl.multiple_of((step % 2) * block, block), block)
    for line in range(LINES):
        place = jnp.where(right == 0, line, 2 * LINES - 1 - line)
        sum_ref[place, 0:block, cols] = part_in[line * block : (line + 1) * block, :]
    half = part_out.shape[1] // 2
    sum_ref[step, block : 2 * block, :] = part_out[:, :half]
    sum_ref[2 * LINES - 1 - step, block : 2 * block, :] = part_out[:, half:]


def mlp_team(table, parts, grad_parts, w_in, w_mlp_out):
    rows, width = TEAM * parts[0].shape[0], parts[0].shape[1]
    block = w_in.shape[1] // (LINES * TEAM)
    return pl.pallas_call(
        mlp_team_kernel,
        grid_spec=pltpu.PrefetchScalarGridSpec(
            num_scalar_prefetch=1,
            grid=(LINES,),
            in_specs=[pl.BlockSpec(parts[0].shape, lambda i, t: (0, 0))] * (2 * TEAM)
            + [
                pl.BlockSpec((width, block), lambda i, t: (0, i * TEAM + t[0])),
                pl.BlockSpec((block, width), lambda i, t: (i * TEAM + t[0], 0)),
            ],
            out_specs=pl.BlockSpec((2 * LINES, 2 * block, width // 2), lambda i, t: (0, 0, 0)),
            scratch_shapes=[pltpu.VMEM((rows, width), BF16), pltpu.VMEM((rows, width), BF16)],
        ),
        out_shape=jax.ShapeDtypeStruct((2 * LINES, 2 * block, width // 2), BF16),
        name="mlp_team",
        cost_estimate=SMALL_COST,
    )(table, *parts, *grad_parts, w_in, w_mlp_out)


def small_sums_kernel(core, *refs):
    lefts, rights = refs[:TEAM], refs[TEAM : TEAM + 7]
    text_ref, grad_ref, sum_ref, left_all, right_all = refs[TEAM + 7 :]
    step = pl.program_id(0)
    rows, half = lefts[0].shape[1], right_all.shape[2]
    quarter = sum_ref.shape[2]
    block = text_ref.shape[1]
    cols = pl.ds(pl.multiple_of(core[0] * half, half), half)

    @pl.when(step == 0)
    def _():
        for member in range(TEAM):
            here = slice(member * rows, (member + 1) * rows)
            for at in range(2):
                left_all[at, here, :] = lefts[member][at]
            right_all[1, here, :] = rights[3 + member][:, cols]
        right_all[0, 0:rows, :] = rights[0][:, cols]
        right_all[0, rows : 2 * rows, :] = rights[1][:, cols]
        right_all[0, 2 * rows :, :] = rights[2][...]

    mine = pl.ds(pl.multiple_of(step * block, block), block)
    pairs = [(left_all[at, :, mine], right_all[at]) for at in range(2)]
    pairs += [(text_ref[...], grad_ref[:, at * half : (at + 1) * half]) for at in range(2)]
    for at, (left, right) in enumerate(pairs):
        part = dot_tn(left, right).astype(BF16)
        sum_ref[step, at * block : (at + 1) * block, :] = part[:, :quarter]
        sum_ref[2 * LINES - 1 - step, at * block : (at + 1) * block, :] = part[:, quarter:]


def small_sums(core, lefts, rights, text_left, text_right):
    rows, half = rights[0].shape[0], rights[0].shape[1] // 2
    block, quarter = text_left.shape[1] // LINES, half // 2
    return pl.pallas_call(
        small_sums_kernel,
        grid_spec=pltpu.PrefetchScalarGridSpec(
            num_scalar_prefetch=1,
            grid=(LINES,),
            in_specs=[pl.BlockSpec((2,) + v.shape[1:], lambda i, t: (0, 0, 0)) for v in lefts]
            + [whole_spec(v) for v in rights]
            + [pl.BlockSpec((text_left.shape[0], block), lambda i, t: (0, i))]
            + [whole_spec(text_right)],
            out_specs=pl.BlockSpec((2 * LINES, 4 * block, quarter), lambda i, t: (0, 0, 0)),
            scratch_shapes=[
                pltpu.VMEM((2, TEAM * rows, LINES * block), BF16),
                pltpu.VMEM((2, TEAM * rows, half), BF16),
            ],
        ),
        out_shape=jax.ShapeDtypeStruct((2 * LINES, 4 * block, quarter), BF16),
        name="small_sums",
        cost_estimate=SMALL_COST,
    )(core, *lefts, *rights, text_left, text_right)


def qkv_products_kernel(core, *refs):
    lefts, rights = refs[:TEAM], refs[TEAM : 2 * TEAM]
    cross_lefts, cross_rights = refs[2 * TEAM : 3 * TEAM], refs[3 * TEAM : 3 * TEAM + 3]
    sum_ref, left_all, right_all, cross_left, cross_right = refs[3 * TEAM + 3 :]
    step = pl.program_id(0)
    rows, lanes = lefts[0].shape[0], sum_ref.shape[2]
    block = left_all.shape[1] // LINES

    @pl.when(step == 0)
    def _():
        for member in range(TEAM):
            here = slice(member * rows, (member + 1) * rows)
            left_all[here, :] = lefts[member][...]
            right_all[here, :] = rights[member][...]
            cross_left[here, :] = cross_lefts[member][0]
        half = cross_right.shape[1]
        cols = pl.ds(pl.multiple_of(core[0] * half, half), half)
        cross_right[0:rows, :] = cross_rights[0][:, cols]
        cross_right[rows : 2 * rows, :] = cross_rights[1][:, cols]
        cross_right[2 * rows :, :] = cross_rights[2][...]

    left = left_all[:, pl.ds(pl.multiple_of(step * block, block), block)]
    part = dot_tn(left, right_all[...]).astype(BF16)
    small = cross_left[:, pl.ds(pl.multiple_of(step * lanes, lanes), lanes)]
    cross = dot_tn(small, cross_right[...]).astype(BF16)
    for right, to in enumerate((step, 2 * LINES - 1 - step)):
        for side in range(2):
            for at in range(3):
                first = (3 * side + at) * lanes
                col = (3 * right + at) * lanes
                sum_ref[to, first : first + lanes, :] = part[
                    side * lanes : (side + 1) * lanes, col : col + lanes
                ]
        for at in range(2):
            first, col = (6 + at) * lanes, (2 * right + at) * lanes
            sum_ref[to, first : first + lanes, :] = cross[:, col : col + lanes]


def qkv_products_of(core, lefts, rights, cross_lefts, cross_rights):
    (rows, width), (_, wide) = lefts[0].shape, rights[0].shape
    lanes = width // (2 * LINES)
    half = cross_rights[0].shape[1] // 2
    return pl.pallas_call(
        qkv_products_kernel,
        grid_spec=pltpu.PrefetchScalarGridSpec(
            num_scalar_prefetch=1,
            grid=(LINES,),
            in_specs=[whole_spec(v) for v in (*lefts, *rights)]
            + [pl.BlockSpec((1,) + v.shape[1:], lambda i, t: (2, 0, 0)) for v in cross_lefts]
            + [whole_spec(v) for v in cross_rights],
            out_specs=pl.BlockSpec((2 * LINES, 8 * lanes, lanes), lambda i, t: (0, 0, 0)),
            scratch_shapes=[
                pltpu.VMEM((TEAM * rows, width), BF16),
                pltpu.VMEM((TEAM * rows, wide), BF16),
                pltpu.VMEM((TEAM * rows, LINES * lanes), BF16),
                pltpu.VMEM((TEAM * rows, half), BF16),
            ],
        ),
        out_shape=jax.ShapeDtypeStruct((2 * LINES, 8 * lanes, lanes), BF16),
        name="qkv_products",
        cost_estimate=SMALL_COST,
    )(core, *lefts, *rights, *cross_lefts, *cross_rights)


def place_of(place, piece):
    return (place[0] ^ (piece & 1), place[1] ^ (piece >> 1))


def gain_row(total, gain_ref):
    wide = jnp.transpose(jnp.broadcast_to(total, (total.shape[0], 128)))
    return wide[0:1, :] / gain_ref[...]


def mlp_spread_kernel(place, *refs):
    wholes, (side_ref, core_ref, far_ref), (gain_in, w_ref) = refs[:2], refs[2:5], refs[5:7]
    in_ref, out_ref, gain_ref = refs[7:]
    rows, block = in_ref.shape[0], wholes[0].shape[1] // 2
    tall = out_ref.shape[0] // 2
    mine = pl.ds(pl.multiple_of(place[2] * rows, rows), rows)
    for flip_x in range(2):
        right = place[0] ^ flip_x
        tiles = (
            (0, 0, wholes[flip_x][mine, :]),
            (1, 0, side_ref[flip_x]),
            (0, 1, core_ref[flip_x, :rows, :]),
            (1, 1, far_ref[flip_x]),
        )
        for flip_y, flip_c, tile in tiles:
            for low_line in range(2):
                at = ((2 * right + low_line) * 2 + (place[2] ^ flip_y)) * 2 + (place[1] ^ flip_c)
                in_ref[:, pl.ds(pl.multiple_of(at * block, block), block)] = tile[
                    :, low_line * block : (low_line + 1) * block
                ].astype(F32)
        for flip_c, tile in ((0, wholes[flip_x][2 * rows :, :]), (1, core_ref[flip_x, rows:, :])):
            out_ref[
                pl.ds(pl.multiple_of((place[1] ^ flip_c) * tall, tall), tall),
                pl.ds(pl.multiple_of(right * 2 * block, 2 * block), 2 * block),
            ] = tile.astype(F32)
    total = jnp.sum(in_ref[...] * w_ref[...].astype(F32), -1, keepdims=True)
    gain_ref[...] = gain_row(total, gain_in)


def small_spread_kernel(place, *refs):
    pieces, outs = refs[:4], refs[4:]
    rows, quarter = outs[0].shape[0], pieces[0].shape[1]
    for piece in range(4):
        right, core = place_of(place, piece)
        at = pl.multiple_of((2 * core + right) * quarter, quarter)
        for which in range(4):
            outs[which][:, pl.ds(at, quarter)] = pieces[piece][
                which * rows : (which + 1) * rows, :
            ].astype(F32)


def qkv_spread_kernel(place, *refs):
    wholes, (side_ref, core_ref, far_ref) = refs[:2], refs[2:5]
    gains, w_refs, outs, gain_outs = refs[5:7], refs[7:11], refs[11:15], refs[15:]
    rows, part = outs[0].shape[0], outs[0].shape[1] // TEAM
    lanes = wholes[0].shape[1]

    def tile(flip_x, flip_y, flip_c, at):
        here = slice(at * rows, (at + 1) * rows)
        if flip_c:
            return far_ref[flip_x, here, :] if flip_y else core_ref[flip_x, here, :]
        if flip_y:
            return side_ref[flip_x, here, :]
        first = pl.multiple_of((3 * place[2] + at) * rows, rows)
        return wholes[flip_x][pl.ds(first, rows), :]

    straight = place[0] == 0
    for flip_c in range(2):
        core = place[1] ^ flip_c
        for flip_y in range(2):
            tiles = [[tile(flip_x, flip_y, flip_c, at) for flip_x in (0, 1)] for at in range(3)]
            left = [jnp.where(straight, one, two).astype(F32) for one, two in tiles]
            right = [jnp.where(straight, two, one).astype(F32) for one, two in tiles]
            columns = left + right
            for at in range(6):
                to = (2 * (place[2] ^ flip_y) + core) * part + (at % 2) * lanes
                outs[at // 2][:, pl.ds(pl.multiple_of(to, lanes), lanes)] = columns[at]
        for flip_x in range(2):
            for at in range(2):
                to = core * 2 * part + (place[0] ^ flip_x) * part + at * lanes
                if flip_c:
                    values = core_ref[flip_x, (3 + at) * rows : (4 + at) * rows, :]
                else:
                    values = wholes[flip_x][(6 + at) * rows : (7 + at) * rows, :]
                outs[3][:, pl.ds(pl.multiple_of(to, lanes), lanes)] = values.astype(F32)
    totals = [
        jnp.sum(outs[which][...] * w_refs[which][...].astype(F32), -1, keepdims=True)
        for which in range(4)
    ]
    gain_outs[0][...] = gain_row(totals[0] + totals[1] + totals[2], gains[0])
    gain_outs[1][...] = gain_row(totals[3], gains[1])


def spread(kernel, place, pieces, gains, weights, shapes, name):
    block = shapes[0][0] if not gains else gains[0].shape[1] // (2 * LINES)
    shapes = shapes + [(1, block)] * len(gains)
    return pl.pallas_call(
        kernel,
        grid_spec=pltpu.PrefetchScalarGridSpec(
            num_scalar_prefetch=1,
            grid=(1,),
            in_specs=[whole_spec(v) for v in pieces]
            + [pl.BlockSpec((1, block), lambda i, p: (0, p[3]))] * len(gains)
            + [pl.BlockSpec((block, w.shape[1]), lambda i, p: (p[3], 0)) for w in weights],
            out_specs=[pl.BlockSpec(shape, lambda i, p: (0, 0)) for shape in shapes],
        ),
        out_shape=[jax.ShapeDtypeStruct(shape, F32) for shape in shapes],
        name=name,
        cost_estimate=SMALL_COST,
    )(place, *pieces, *gains, *weights)


def text_share_kernel(place, total_ref, key_ref, value_ref, own_ref, far_ref, part_ref):
    half, share = key_ref.shape[1], own_ref.shape[0]
    rows = total_ref[pl.ds(pl.multiple_of(place[2] * 2 * share, 2 * share), 2 * share), :]
    part_ref[...] = dot_nt(rows[:, :half], key_ref[...]) + dot_nt(rows[:, half:], value_ref[...])
    own_ref[...] = part_ref[pl.ds(pl.multiple_of(place[1] * share, share), share), :]
    away = (1 - place[1]) * share
    far_ref[...] = part_ref[pl.ds(pl.multiple_of(away, share), share), :].astype(BF16)


def text_share(place, total, w_key_text, w_value_text):
    prompt_rows, width = total.shape
    share, half = prompt_rows // TEAM, width // 2
    side = pl.BlockSpec((width, half), lambda i, p: (0, p[1]))
    out = pl.BlockSpec((share, width), lambda i, p: (0, 0))
    return pl.pallas_call(
        text_share_kernel,
        grid_spec=pltpu.PrefetchScalarGridSpec(
            num_scalar_prefetch=1,
            grid=(1,),
            in_specs=[pl.BlockSpec((prompt_rows, width), lambda i, p: (0, 0)), side, side],
            out_specs=[out, out],
            scratch_shapes=[pltpu.VMEM((2 * share, width), F32)],
        ),
        out_shape=[
            jax.ShapeDtypeStruct((share, width), F32),
            jax.ShapeDtypeStruct((share, width), BF16),
        ],
        name="text_share",
        cost_estimate=SMALL_COST,
    )(place, total, w_key_text, w_value_text)


def text_choose_kernel(owners, shares_ref, near_ref, far_ref):
    count = near_ref.shape[0]
    for each in range(count):
        near_ref[each] = shares_ref[owners[each]]
        far_ref[each] = shares_ref[owners[count + each]]


def text_choose(owners, shares):
    shape = (owners.shape[0] // 2,) + shares.shape[1:]
    return pl.pallas_call(
        text_choose_kernel,
        in_specs=[pl.BlockSpec(memory_space=pltpu.SMEM)] + in_vmem(1),
        out_specs=in_vmem(2),
        out_shape=[jax.ShapeDtypeStruct(shape, BF16)] * 2,
        name="text_choose",
        cost_estimate=SMALL_COST,
    )(owners, shares)


def text_place_kernel(place, *refs):
    pieces, out_ref = refs[:4], refs[4]
    share = pieces[0].shape[1]
    for piece in range(4):
        at = (2 * (place[2] ^ (piece & 1)) + (place[1] ^ (piece >> 1))) * share
        for each in range(out_ref.shape[0]):
            out_ref[each, pl.ds(pl.multiple_of(at, share), share), :] = pieces[piece][each]


def text_place(place, pieces):
    count, share, width = pieces[0].shape
    return pl.pallas_call(
        text_place_kernel,
        in_specs=[pl.BlockSpec(memory_space=pltpu.SMEM)] + in_vmem(4),
        out_specs=in_vmem(1)[0],
        out_shape=jax.ShapeDtypeStruct((count, TEAM * share, width), BF16),
        name="text_place",
        cost_estimate=SMALL_COST,
    )(place, *pieces)


def input_grad_kernel(turn, *refs):
    parts, (q_ref, k_ref, v_ref) = refs[:TEAM], refs[TEAM : TEAM + 3]
    rows_ref, gain_ref, hidden_ref = refs[TEAM + 3 : TEAM + 6]
    blocks, refs = refs[TEAM + 6 : TEAM + 6 + LINES], refs[TEAM + 6 + LINES :]
    outs, (kept, total) = refs[:LINES], refs[LINES:]
    step = pl.program_id(0)
    part = q_ref.shape[1]

    @pl.when(step == 0)
    def _():
        for member in range(TEAM):
            kept[member] = parts[member][...]
        total[...] = jnp.zeros_like(total)

    grads = kept[step]
    for at, w_ref in enumerate((q_ref, k_ref, v_ref)):
        total[...] += dot_nt(grads[:, at * part : (at + 1) * part], w_ref[...])

    @pl.when(step == TEAM - 1)
    def _():
        grad = hidden_ref[...] + norm_back_rows(
            total[...], rows_ref[...].astype(F32), gain_ref[...]
        )
        for line in range(LINES):
            outs[line][0] = grad[line * CHUNK : (line + 1) * CHUNK, :].astype(BF16)
            outs[line][1] = blocks[line][...]


def input_grad(turn, parts, weights, rows_low, gain, grad_hidden, block_out):
    rows, width = rows_low.shape
    wide = parts[0].shape[1]
    part = wide // 3
    out = jax.ShapeDtypeStruct((2, rows // LINES, width), BF16)
    return pl.pallas_call(
        input_grad_kernel,
        grid_spec=pltpu.PrefetchScalarGridSpec(
            num_scalar_prefetch=1,
            grid=(TEAM,),
            in_specs=[whole_spec(v) for v in parts]
            + [pl.BlockSpec((width, part), lambda i, t: (0, t[i]))] * 3
            + [whole_spec(v) for v in (rows_low, gain, grad_hidden, *block_out)],
            out_specs=[whole_spec(out)] * LINES,
            scratch_shapes=[
                pltpu.VMEM((TEAM, rows, wide), BF16),
                pltpu.VMEM((rows, width), F32),
            ],
        ),
        out_shape=[out] * LINES,
        name="input_grad",
        cost_estimate=SMALL_COST,
    )(turn, *parts, *weights, rows_low, gain, grad_hidden, *block_out)


def return_place_kernel(place, *refs):
    pieces, outs = refs[:LINES], refs[LINES:]
    tall = pieces[0].shape[1]
    for step in range(LINES):
        which = place[4] ^ step
        at = pl.multiple_of((which >> 1) * tall, tall)
        for each in range(2):
            outs[each][which & 1, pl.ds(at, tall), :] = pieces[step][each]


def return_place(place, pieces):
    _, tall, width = pieces[0].shape
    return pl.pallas_call(
        return_place_kernel,
        in_specs=[pl.BlockSpec(memory_space=pltpu.SMEM)] + in_vmem(LINES),
        out_specs=in_vmem(2),
        out_shape=[jax.ShapeDtypeStruct((2, 2 * tall, width), BF16)] * 2,
        name="return_place",
        cost_estimate=SMALL_COST,
    )(place, *pieces)


def across(values):
    return move(values, lambda z, y, x, c: (z, y, 1 - x, c))


def together(*values):
    return lax.optimization_barrier(values)


def after(values, *others):
    return lax.optimization_barrier((values, others))[0]


def low(values):
    return values.astype(BF16)


def in_order(first, own, other):
    return jnp.where(first == 0, jnp.stack([own, other]), jnp.stack([other, own]))


def on_device(
    image_rows,
    text_rows,
    prompt_len,
    prompt_slot,
    gain_self,
    w_query,
    w_key,
    w_value,
    w_out,
    gain_cross,
    w_query_text,
    w_key_text,
    w_value_text,
    w_out_text,
    gain_mlp,
    w_in,
    w_mlp_out,
    grad_out,
):
    width = image_rows.shape[-1]
    hidden_width = w_in.shape[-1]
    prompt_rows = text_rows.shape[1]
    rows_here = image_rows.shape[1]
    half_rows = rows_here // 2
    part, half = width // TEAM, width // 2
    block = width // (2 * LINES)
    row_index, group_index = lax.axis_index("row"), lax.axis_index("grp")
    z, y, x, c = row_index >> 1, row_index & 1, group_index >> 1, group_index & 1
    mine = 2 * y + c

    def take(values, start, size, dim):
        return lax.dynamic_slice_in_dim(values, start, size, dim, allow_negative_indices=False)

    def pick_row(values, index, dim=0):
        return lax.dynamic_index_in_dim(
            values, index, dim, keepdims=False, allow_negative_indices=False
        )

    def line_columns(values):
        pairs = [values[:, b * block : (b + 1) * block] for b in range(2 * LINES)]
        near = [jnp.where(y == 0, pairs[2 * b], pairs[2 * b + 1]) for b in range(LINES)]
        far = [jnp.where(y == 0, pairs[2 * b + 1], pairs[2 * b]) for b in range(LINES)]
        return jnp.concatenate(near, 1), jnp.concatenate(far, 1)

    def line_stack(arrays):
        sides = [line_columns(values) for values in arrays]
        return jnp.stack([s[0] for s in sides]), jnp.stack([s[1] for s in sides])

    def hand_rows(values):
        pieces = []
        for step in range(LINES):
            which = z ^ step
            piece = lax.dynamic_slice(
                values,
                (which & 1, (which >> 1) * half_rows, 0),
                (1, half_rows, width),
                allow_negative_indices=False,
            )[0]
            pieces.append(move(piece, hand_out(step)))
        return jnp.concatenate(pieces, 0)

    def natural(parts):
        odd, high = c == 1, y == 1
        parts = [parts[0], parts[2], parts[1], parts[3]]
        parts = [jnp.where(odd, parts[m ^ 1], parts[m]) for m in range(TEAM)]
        return jnp.concatenate([jnp.where(high, parts[m ^ 2], parts[m]) for m in range(TEAM)], 1)

    def side_rows(values, far_values, rows):
        both = jnp.stack([values, far_values])
        first, second, rest = both[:, :rows], both[:, rows : 2 * rows], both[:, 2 * rows :]
        kept = jnp.where(y == 0, first, second)
        return jnp.where(y == 0, second, first), jnp.concatenate([kept, rest], 1)

    def right_parts(values, side):
        parts = (values, side)
        away = [jnp.where(c == 0, v[:, half:], v[:, :half]) for v in parts]
        return [values, side, to_member(jnp.concatenate(away, 0), 2)]

    member = np.repeat(np.arange(TEAM), LINES)
    core_of = c ^ (member >> 1)
    line_of = np.tile(np.arange(LINES), TEAM) ^ ((z & 1) | (core_of << 1))
    table = (line_of * 2 + (y ^ (member & 1))) * 2 + core_of
    table = jnp.concatenate([table, mine[None]]).astype(jnp.int32)
    grad_table = jnp.concatenate([mine[None], line_of]).astype(jnp.int32)
    turn = (mine ^ np.array([0, 2, 1, 3])).astype(jnp.int32)
    place = jnp.stack([x, c, y, row_index, z]).astype(jnp.int32)
    slots = np.arange(prompt_slot.shape[0])
    wanted = text_rows.shape[0] * group_index + np.arange(text_rows.shape[0])
    wanted = jnp.concatenate([wanted, wanted ^ 2])
    owners = jnp.sum(jnp.where(prompt_slot[None, :] == wanted[:, None], slots[None, :], 0), 1)
    apart = (owners & 3) ^ z
    owners = (((apart & 1) << 2) | (apart & 2) | ((owners >> 2) ^ x)).astype(jnp.int32)

    image = 4 * x + z
    slot = pick_row(prompt_slot, image)
    count = take(prompt_len, slot, 1, 0)

    start = part * mine
    w_qkv = jnp.concatenate([take(w, start, part, 1) for w in (w_query, w_key, w_value)], 1)
    rows_low, w_qkv, count = together(hand_rows(image_rows), w_qkv, count)
    count_core = jnp.concatenate([count, c[None]])
    inputs = rows_low.astype(F32)
    text_across = across(text_rows)
    wanted_x, wanted_c = slot >> 2, (slot >> 1) & 1
    text_mine = pick_row(jnp.where(wanted_x == x, text_rows, text_across), slot & 1)
    text_mine = jnp.where(wanted_c == c, text_mine, to_member(text_mine, 2))
    grad_rows = lax.all_gather(
        after(grad_out, rows_low), AXES, axis=0, axis_index_groups=line_groups()
    )
    normed_self, _, _ = norm_rows(inputs, gain_self)
    normed_parts = team_gather(low(normed_self))
    qkv_parts = [low(matmul(a, w_qkv)) for a in normed_parts]
    out_parts, log_totals = self_forward(table, qkv_parts)
    got = [out_parts[0]] + [to_member(out_parts[k], k) for k in range(1, TEAM)]
    text_now = after(text_mine, out_parts[0])
    text_key = low(matmul(text_now, w_key_text))
    text_value = low(matmul(text_now, w_value_text))

    context_low = natural(after(got, text_key, text_value))
    hidden = inputs + matmul(context_low, w_out)
    normed_cross, unit_cross, inverse_cross = norm_rows(hidden, gain_cross)
    cross_normed_low = low(normed_cross)
    cross_low = low(matmul(cross_normed_low, w_query_text))
    cross_context_low = cross_forward(count, cross_low, text_key, text_value)
    grad_rows = after(grad_rows, cross_low)
    image_side = z & 1

    def half_image(core):
        return lax.dynamic_slice(
            grad_rows,
            (0, image_side, half_rows * core, 0),
            (LINES, 1, half_rows, width),
            allow_negative_indices=False,
        ).reshape(-1, width)

    grad_far = to_member(half_image(1 - c), 2)
    grad_low = jnp.where(c == z >> 1, half_image(c), grad_far)
    grad_side, grad_core = to_member(grad_low, 1), to_member(grad_low, 2)
    mixed = hidden + matmul(cross_context_low, w_out_text)
    normed_mlp, _, _ = norm_rows(mixed, gain_mlp)
    mlp_low = low(normed_mlp)
    mlp_side, mlp_core = to_member(mlp_low, 1), to_member(mlp_low, 2)
    left_rows = [cross_context_low, context_low, cross_normed_low]
    left_far = line_stack(after(left_rows, mlp_low))[1]
    left_side = to_member(left_far, 1)

    *block_out, grad_mixed, grad_mixed_low = mlp_rows(
        grad_table[1:], mlp_low, grad_low, mixed, gain_mlp.reshape(1, width), w_in, w_mlp_out
    )
    mlp_side, mlp_core, grad_side, grad_core = after(
        (mlp_side, mlp_core, grad_side, grad_core), grad_mixed_low
    )
    mlp_parts = [mlp_low, mlp_side, mlp_core, to_member(mlp_side, 2)]
    grad_parts = [grad_low, grad_side, grad_core, to_member(grad_side, 2)]
    mlp_blocks = mlp_team(grad_table, after(mlp_parts, left_far), grad_parts, w_in, w_mlp_out)
    mlp_blocks, left_side = lax.optimization_barrier((mlp_blocks, left_side))
    mlp_sum = ring_sum(mlp_blocks)

    grad_mixed_low = after(grad_mixed_low, mlp_blocks)
    mixed_side = to_member(grad_mixed_low, 1)
    grad_cross_ctx = low(matmul_right_t(grad_mixed_low, w_out_text))
    grad_cross_low, kv_near, kv_far = cross_backward(
        count_core, cross_low, text_key, text_value, grad_cross_ctx
    )
    grad_cross_low, kv_near, kv_far, mixed_side = together(
        grad_cross_low, kv_near, kv_far, mixed_side
    )
    kv_near = low(kv_near.astype(F32) + to_member(kv_far, 2).astype(F32))
    kv_side = to_member(kv_near, 1)
    grad_cross_normed = matmul_right_t(after(grad_cross_low, kv_near), w_query_text)
    grad_from_cross, _ = norm_back(grad_cross_normed, unit_cross, inverse_cross, gain_cross)
    grad_hidden = grad_mixed + grad_from_cross
    grad_hidden_low = low(grad_hidden)
    text_total = low(kv_near.astype(F32) + after(kv_side, grad_hidden_low).astype(F32))
    hidden_side = to_member(after(grad_hidden_low, text_total), 1)
    hidden_core = to_member(grad_hidden_low, 2)
    left_rows, left_side, mixed_side, text_left = after(
        (left_rows, left_side, mixed_side, text_mine), text_total
    )
    left_near = line_stack(left_rows)[0]
    mixed_parts = right_parts(grad_mixed_low, mixed_side)
    lefts = [left_near, left_side, to_member(left_near, 2), to_member(left_side, 2)]
    text_left = line_columns(text_left)[0]
    share_own, share_far = text_share(
        place, after(text_total, text_left, mixed_parts[1]), w_key_text, w_value_text
    )
    share_own, share_far, hidden_side, lefts = together(share_own, share_far, hidden_side, lefts)
    share_far = to_member(share_far, 2)
    hidden_parts = [grad_hidden_low, hidden_side, hidden_core, to_member(hidden_side, 2)]
    cross_side = to_member(after(grad_cross_low, hidden_side), 1)
    split = width // 4
    small_blocks = small_sums(
        c.reshape(1), lefts, mixed_parts + hidden_parts, text_left, text_total
    )
    small_blocks, share_far = together(small_blocks, share_far)
    small_sum = ring_sum(small_blocks)

    shares = low(share_own + share_far.astype(F32))[None]
    grad_qkv_parts = self_backward(
        table,
        qkv_parts,
        after(hidden_parts, small_blocks, mlp_sum, shares),
        out_parts,
        log_totals,
        w_out,
    )
    grad_qkv_parts, cross_side, shares_two = together(
        grad_qkv_parts, cross_side, across(shares)
    )
    got_grads = [grad_qkv_parts[0]] + [
        to_member(grad_qkv_parts[k], k) for k in range(1, TEAM)
    ]
    cross_parts = right_parts(grad_cross_low, cross_side)
    qkv_products = qkv_products_of(
        c.reshape(1), normed_parts, after(grad_qkv_parts, shares_two), lefts, cross_parts
    )
    shares = jnp.concatenate([shares, shares_two], 0)
    qkv_products, got_grads, shares_two, mlp_across = together(
        qkv_products,
        got_grads,
        move(shares, lambda z, y, x, c: (z ^ 2, y, x, c)),
        across(mlp_sum),
    )
    mlp_send, mlp_keep = side_rows(mlp_sum, mlp_across, block)
    shares = jnp.concatenate([shares, shares_two], 0)
    qkv_sum = ring_sum(qkv_products)
    back_pieces = input_grad(
        turn,
        after(got_grads, small_sum, shares),
        (w_query, w_key, w_value),
        rows_low,
        gain_self.reshape(1, width),
        grad_hidden,
        block_out,
    )
    back_pieces, mlp_parts = together(
        back_pieces, [to_member(mlp_send, 1), to_member(mlp_keep, 2), to_member(mlp_send, 3)]
    )
    back = [move(back_pieces[step], hand_back(step)) for step in range(LINES)]
    grad_w_in, grad_w_mlp_out, grad_gain_mlp = spread(
        mlp_spread_kernel,
        place,
        [mlp_sum, mlp_across, *mlp_parts],
        [gain_mlp.reshape(1, width)],
        [w_in],
        [(block, hidden_width), (2 * split, width)],
        "mlp_spread",
    )
    grad_w_in, small_across, shares_two = together(
        grad_w_in, across(small_sum), move(shares, lambda z, y, x, c: (z ^ 1, y, x, c))
    )
    small_core, small_far = to_member(small_sum, 2), to_member(small_across, 2)
    near, far = text_choose(owners, jnp.concatenate([shares, shares_two], 0))
    small_all = spread(
        small_spread_kernel,
        place,
        after([small_sum, small_across, small_core, small_far], near),
        [],
        [],
        [(block, width)] * 4,
        "small_spread",
    )
    qkv_done = after(qkv_sum, near)
    small_all, back[0], back[1], text_back, qkv_across = together(
        small_all,
        back[0],
        back[1],
        [near, to_member(near, 1), to_member(far, 2), to_member(far, 3)],
        across(qkv_done),
    )
    qkv_send, qkv_keep = side_rows(qkv_done, qkv_across, 3 * block)
    grad_text = text_place(place, after(text_back, qkv_send, qkv_keep))
    grad_text, back, qkv_parts_back = together(
        grad_text,
        back,
        [to_member(qkv_send, 1), to_member(qkv_keep, 2), to_member(qkv_send, 3)],
    )
    grad_image, out_block = return_place(place, back)
    grad_w_query, grad_w_key, grad_w_value, grad_w_query_text, gain_one, gain_two = spread(
        qkv_spread_kernel,
        place,
        [qkv_done, qkv_across, *qkv_parts_back],
        [gain_self.reshape(1, width), gain_cross.reshape(1, width)],
        [w_query, w_key, w_value, w_query_text],
        [(block, width)] * 4,
        "qkv_spread",
    )
    return (
        out_block,
        grad_image,
        grad_text,
        gain_one.reshape(block),
        grad_w_query,
        grad_w_key,
        grad_w_value,
        small_all[1],
        gain_two.reshape(block),
        grad_w_query_text,
        small_all[2],
        small_all[3],
        small_all[0],
        grad_gain_mlp.reshape(block),
        grad_w_in,
        grad_w_mlp_out,
    )


def solution(mesh):
    placed = (
        P("grp", "row", None),
        P("grp", None, None),
        P(),
        P(),
        P(),
        P(),
        P(),
        P(),
        P(),
        P(),
        P(),
        P(),
        P(),
        P(),
        P(),
        P(),
        P(),
        P("grp", "row", None),
    )
    return jax.shard_map(
        on_device if fits(mesh) else on_device_plain,
        mesh=mesh,
        in_specs=placed,
        out_specs=(
            P("grp", "row", None),
            P("grp", "row", None),
            P("grp", None, None),
            P("row"),
            P("row", None),
            P("row", None),
            P("row", None),
            P("row", None),
            P("row"),
            P("row", None),
            P("row", None),
            P("row", None),
            P("row", None),
            P("row"),
            P("row", None),
            P("row", None),
        ),
        check_vma=False,
    )
```
